32 devices in a mesh: wshard: 8 (over z, x), seq: 4 (over y, core).
Axes of the slice: x: 2, y: 2, z: 4, core: 2. Of those that a mesh axis runs over, the one named last changes fastest.
Arguments:
- hidden: bfloat16 [8, 2048, 1536], P('wshard', 'seq'), may hold values from -6 to 6
- segments: int32 [8, 2048], P('wshard'), may hold values from 0 to 3, never falling along the last dimension, each value on 1 to 1024 neighbouring positions
- norm_gain: bfloat16 [1536], P('wshard'), may hold values from 0.099609375 to 1.8984375
- in_weight: bfloat16 [1536, 6448], P('wshard'), may hold values from -0.15625 to 0.15625
- conv_weight: float32 [4, 3328], replicated, may hold values from -3 to 3
- conv_bias: float32 [3328], replicated, may hold values from -3 to 3
- step_bias: float32 [48], replicated, may hold values from -6 to -2
- decay_log: float32 [48], replicated, may hold values from 0 to 2.5
- skip_scale: float32 [48], replicated, may hold values from 0.5 to 1.5
- gate_gain: bfloat16 [3072], P('wshard'), may hold values from 0.099609375 to 1.8984375
- out_weight: bfloat16 [3072, 1536], P('wshard'), may hold values from -0.109375 to 0.109375
- cotangent: bfloat16 [8, 2048, 1536], P('wshard', 'seq'), may hold values from -6 to 6
Outputs:
- layer_output: float32 [8, 2048, 1536], P('wshard', 'seq')
- hidden_grad: float32 [8, 2048, 1536], P('wshard', 'seq')
- norm_gain_grad: float32 [1536], P('wshard')
- in_weight_grad: float32 [1536, 6448], P('wshard')
- conv_weight_grad: float32 [4, 3328], replicated
- conv_bias_grad: float32 [3328], replicated
- step_bias_grad: float32 [48], replicated
- decay_log_grad: float32 [48], replicated
- skip_scale_grad: float32 [48], replicated
- gate_gain_grad: float32 [3072], P('wshard')
- out_weight_grad: float32 [3072, 1536], P('wshard')
The draws below stay inside these ranges and needn't reach their ends.
Inputs may be any that keep to these rules, and one draw needn't show every extreme that they name: `segments`: within each sequence document numbers never fall; each document spans 1 to 1024 consecutive tokens, one of them exactly that many.
All inputs are finite; a program needn't handle non-finite values.
Results may differ from the reference program's by a relative error of at most 0.011.
Values may be sent and summed in bfloat16 or wider, within the bound.
A program may use at most 256 MiB of HBM per device.

```python
import math
import jax
import jax.numpy as jnp
import numpy as np
from jax import lax

D = 1536
H = 48
CONV = 4
STRETCH = 256
LEN = 2048
E = 3072
PROJ = 6448
CH = 3328
SEQS = 8


def raised(values, stream_key, source, target, shards_of, factor):
    def block_of(position):
        return (jnp.arange(values.shape[position]) // (values.shape[position] // shards_of)).reshape((-1,) + (1,) * (values.ndim - 1 - position))

    first = jax.random.permutation(stream_key, shards_of)[block_of(target)]
    second = (block_of(target) + shards_of // 2) % shards_of
    return jnp.where((block_of(source) == first) | (block_of(source) == second), factor * values, values)


def block_scale(stream_key, shape, cuts, least, largest):
    def one(position, parts):
        heights = jax.random.uniform(jax.random.fold_in(jax.random.fold_in(stream_key, 6), position), (parts,), jnp.float32, least / len(cuts), largest / len(cuts))
        return jnp.repeat(jnp.exp(heights), shape[position] // parts).reshape((-1,) + (1,) * (len(shape) - position - 1))

    gain = one(*cuts[0])
    for cut in cuts[1:]:
        gain = gain * one(*cut)
    return gain


def split_up(count, total, reach, skew):
    weights = [(1 << 20) // math.isqrt(rank ** skew) + 1 for rank in range(2, count + 1)]
    spare, holding = total - reach - (count - 1), [1] * (count - 1)
    while spare > 0:
        candidates = [i for i in range(count - 1) if holding[i] < reach]
        mass, left = sum([weights[i] for i in candidates]), spare
        for i in candidates:
            addition = min(reach - holding[i], max(1, left * weights[i] // mass), spare)
            holding[i] = holding[i] + addition
            spare = spare - addition
    return np.array([reach] + holding)


def uneven_parts(own_key, number_of, total, most, lean):
    if number_of == 2:
        one = jax.random.randint(own_key, (), max(1, total - most), min(most, total - 1) + 1)
        return jnp.stack([one, total - one])
    sizes = jnp.asarray(split_up(number_of, total, most, lean), jnp.int32)
    pairs = (number_of - 1) // 2
    giver, sink = sizes[1:1 + 2 * pairs:2], sizes[2:2 + 2 * pairs:2]
    slack = jnp.minimum(giver - 1, most - sink)
    passed = jax.random.randint(jax.random.fold_in(own_key, 1), (pairs,), 0, 1 << 20) % (slack + 1)
    sizes = sizes.at[1:1 + 2 * pairs:2].set(giver - passed).at[2:2 + 2 * pairs:2].set(sink + passed)
    return sizes[jax.random.permutation(jax.random.fold_in(own_key, 2), number_of)]


def noise(stream_key, shape, width, limit, split=(), kind=jnp.bfloat16):
    loudness = block_scale(stream_key, shape, split, -0.22, 0.18) if split else 1.0
    array = jax.random.normal(stream_key, shape, jnp.float32) * width * loudness
    return jnp.minimum(jnp.maximum(array, -limit), limit).astype(kind)


def bell_draw_with(stream_key, shape, width, bound, split, heavy, held_as=jnp.bfloat16):
    result = width * jax.random.normal(stream_key, shape, jnp.float32)
    if split:
        result = result * block_scale(stream_key, shape, split, -0.22, 0.18)
    return jnp.clip(raised(result, jax.random.fold_in(stream_key, 3), *heavy), -bound, bound).astype(held_as)


def setup_inputs(seed: int = 0) -> dict:
    streams_of = jax.random.split(jax.random.key(seed), 13)
    hidden = bell_draw_with(streams_of[0], (SEQS, LEN, D), 1.0, 6.0, ((0, 8), (1, 4)), (0, 2, 8, 2.0))
    segments = jax.vmap(lambda own: jnp.searchsorted(jnp.cumsum(uneven_parts(own, 4, LEN, LEN // 2, 0)), jnp.arange(LEN), side="right"))(jax.random.split(streams_of[1], SEQS)).reshape((SEQS, LEN)).astype(jnp.int32)
    norm_gain = jnp.clip(1.0 + 0.18 * jax.random.normal(streams_of[2], (D,), jnp.float32), 0.099609375, 1.8984375).astype(jnp.bfloat16)
    in_weight = noise(streams_of[3], (D, PROJ), D ** -0.5, 0.15625, ((0, 8),))
    conv_weight = noise(streams_of[4], (CONV, CH), CONV ** -0.5, 3.0, (), jnp.float32)
    conv_bias = noise(streams_of[5], (CH,), 0.5, 3.0, (), jnp.float32)
    step_bias = jnp.clip(jax.random.uniform(streams_of[6], (H,), jnp.float32, -6.0, -2.0), -6.0, -2.0)
    decay_log = jnp.clip(jax.random.uniform(streams_of[7], (H,), jnp.float32, 0.0, 2.5), 0.0, 2.5)
    skip_scale = jnp.clip(jax.random.uniform(streams_of[8], (H,), jnp.float32, 0.5, 1.5), 0.5, 1.5)
    gate_gain = jnp.clip(1.0 + 0.18 * jax.random.normal(streams_of[9], (E,), jnp.float32), 0.099609375, 1.8984375).astype(jnp.bfloat16)
    out_weight = noise(streams_of[10], (E, D), E ** -0.5, 0.109375, ((0, 8),))
    cotangent = noise(streams_of[11], (SEQS, LEN, D), 1.0, 6.0, ((0, 8), (1, 4)))
    return {"hidden": hidden, "segments": segments, "norm_gain": norm_gain, "in_weight": in_weight, "conv_weight": conv_weight, "conv_bias": conv_bias, "step_bias": step_bias, "decay_log": decay_log, "skip_scale": skip_scale, "gate_gain": gate_gain, "out_weight": out_weight, "cotangent": cotangent}


eps = 1e-05
precise = lax.Precision.HIGHEST

@jax.custom_vjp
def low(v):
    return lax.optimization_barrier(v.astype(jnp.bfloat16)).astype(jnp.float32)

@jax.custom_vjp
def low_back(v):
    return v

def low_keep(v):
    return (low(v), None)

def low_pass(kept, grad):
    return (grad,)

def back_keep(v):
    return (v, None)

def back_low(kept, grad):
    return (low(grad),)
low.defvjp(low_keep, low_pass)
low_back.defvjp(back_keep, back_low)

def causal_conv(values, kernel, offsets, seg_ids):
    tap_count = kernel.shape[0]
    length_here = values.shape[0]
    padded = jnp.pad(values, ((tap_count - 1, 0), (0, 0)))
    seg_padded = jnp.concatenate([jnp.full((tap_count - 1,), -1, jnp.int32), seg_ids.astype(jnp.int32)])
    summed = jnp.zeros_like(values) + offsets[None, :]
    for offset in range(tap_count):
        same_doc = (seg_padded[offset:offset + length_here] == seg_ids.astype(jnp.int32)).astype(values.dtype)
        summed = summed + kernel[offset][None, :] * padded[offset:offset + length_here] * same_doc[:, None]
    return jax.nn.silu(summed)

def block_step(state, pieces):
    x_block, b_block, c_block, rate_block, step_block, seg_block, seg_before = pieces
    block_len = x_block.shape[0]
    cumul = jnp.cumsum(rate_block, axis=0)
    causal = jnp.arange(block_len)[:, None] >= jnp.arange(block_len)[None, :]
    allowed = (causal & (seg_block[:, None] == seg_block[None, :]))[:, :, None]
    spread = cumul[:, None, :] - cumul[None, :, :]
    decay = jnp.where(allowed, jnp.exp(jnp.where(allowed, spread, 0.0)), 0.0)
    affinity = jnp.dot(c_block, b_block.T, precision=precise)
    weighted = affinity[:, :, None] * decay * step_block[None, :, :]
    within = jnp.einsum('ijh,jhp->ihp', weighted, x_block, precision=precise)
    carried = (seg_block == seg_before).astype(rate_block.dtype)
    entering = jnp.einsum('in,hnp->ihp', c_block, state, precision=precise) * (jnp.exp(cumul) * carried[:, None])[:, :, None]
    last_cum = cumul[block_len - 1]
    same_last = (seg_block == seg_block[block_len - 1]).astype(rate_block.dtype)
    to_end = jnp.exp(last_cum[None, :] - cumul) * same_last[:, None] * step_block
    retained = jnp.exp(last_cum) * (seg_block[block_len - 1] == seg_before).astype(rate_block.dtype)
    new_state = state * retained[:, None, None] + jnp.einsum('jn,jh,jhp->hnp', b_block, to_end, x_block, precision=precise)
    return (new_state, within + entering)

def state_scan(x_heads, b_vals, c_vals, decay_rates, step_sizes, seg_ids):
    length_here, head_count, head_dim = x_heads.shape
    blocks = length_here // STRETCH
    seg_blocks = seg_ids.astype(jnp.int32).reshape(blocks, STRETCH)
    seg_prior = jnp.concatenate([jnp.full((1,), -1, jnp.int32), seg_blocks[:-1, STRETCH - 1]])
    start_state = jnp.zeros((head_count, b_vals.shape[1], head_dim), x_heads.dtype)
    pieces = (x_heads.reshape(blocks, STRETCH, head_count, head_dim), b_vals.reshape(blocks, STRETCH, b_vals.shape[1]), c_vals.reshape(blocks, STRETCH, c_vals.shape[1]), decay_rates.reshape(blocks, STRETCH, head_count), step_sizes.reshape(blocks, STRETCH, head_count), seg_blocks, seg_prior)
    _, results = lax.scan(jax.checkpoint(block_step), start_state, pieces)
    return results.reshape(length_here, head_count, head_dim)

def mixer(x_raw, bc_raw, dt_raw, conv_weight, conv_bias, step_bias, decay_log, skip_scale, seg_ids, head_start, chan_start):
    channels = x_raw.shape[1]
    head_count = dt_raw.shape[1]
    head_dim = channels // head_count
    state_dim = bc_raw.shape[1] // 2
    inner_width = conv_weight.shape[1] - 2 * state_dim
    x_conv = causal_conv(x_raw, lax.dynamic_slice_in_dim(conv_weight, chan_start, channels, 1), lax.dynamic_slice_in_dim(conv_bias, chan_start, channels, 0), seg_ids)
    bc_conv = causal_conv(bc_raw, conv_weight[:, inner_width:], conv_bias[inner_width:], seg_ids)
    x_heads = x_conv.reshape(-1, head_count, head_dim)
    step_sizes = jax.nn.softplus(dt_raw + lax.dynamic_slice_in_dim(step_bias, head_start, head_count, 0)[None, :])
    decay_rates = -jnp.exp(lax.dynamic_slice_in_dim(decay_log, head_start, head_count, 0))
    scanned = state_scan(x_heads, bc_conv[:, :state_dim], bc_conv[:, state_dim:], step_sizes * decay_rates[None, :], step_sizes, seg_ids)
    skipped = scanned + lax.dynamic_slice_in_dim(skip_scale, head_start, head_count, 0)[None, :, None] * x_heads
    return skipped.reshape(-1, channels)

def layer(params, hidden_seq, seg_ids):
    norm_gain, in_weight, conv_weight, conv_bias, step_bias, decay_log, skip_scale, gate_gain, out_weight = params
    inner_width = out_weight.shape[0]
    state_dim = (conv_weight.shape[1] - inner_width) // 2
    scale = lax.rsqrt(lax.optimization_barrier(jnp.mean(hidden_seq * hidden_seq, axis=-1, keepdims=True)) + eps)
    normed = low(hidden_seq * scale * norm_gain[None, :])
    projected = low_back(jnp.dot(normed, in_weight, precision=precise))
    gate_part = projected[:, :inner_width]
    x_part = low_back(low(projected[:, inner_width:2 * inner_width]))
    bc_part = low_back(low(projected[:, 2 * inner_width:2 * inner_width + 2 * state_dim]))
    dt_part = low_back(low(projected[:, 2 * inner_width + 2 * state_dim:]))
    mixed = low_back(low(mixer(x_part, bc_part, dt_part, conv_weight, conv_bias, step_bias, decay_log, skip_scale, seg_ids, 0, 0)))
    gated = mixed * jax.nn.silu(gate_part)
    gate_scale = lax.rsqrt(lax.optimization_barrier(jnp.mean(gated * gated, axis=-1, keepdims=True)) + eps)
    gated_normed = low(gated * gate_scale * gate_gain[None, :])
    return hidden_seq + jnp.dot(gated_normed, out_weight, precision=precise)

def reference(hidden, segments, norm_gain, in_weight, conv_weight, conv_bias, step_bias, decay_log, skip_scale, gate_gain, out_weight, cotangent):
    params = (norm_gain.astype(jnp.float32), in_weight.astype(jnp.float32), conv_weight.astype(jnp.float32), conv_bias.astype(jnp.float32), step_bias.astype(jnp.float32), decay_log.astype(jnp.float32), skip_scale.astype(jnp.float32), gate_gain.astype(jnp.float32), out_weight.astype(jnp.float32))

    def one_sequence(grad_sums, items):
        hidden_seq, seg_ids, cot_seq = items

        def apply_layer(param_set, hidden_in):
            return layer(param_set, hidden_in, seg_ids)
        output_seq, pullback = jax.vjp(apply_layer, params, hidden_seq)
        param_grads, hidden_back = pullback(cot_seq)
        return (jax.tree.map(jnp.add, grad_sums, param_grads), (output_seq, hidden_back))
    start_grads = jax.tree.map(jnp.zeros_like, params)
    grad_sums, (outputs, hidden_grads) = lax.scan(one_sequence, start_grads, (hidden.astype(jnp.float32), segments, cotangent.astype(jnp.float32)))
    return (outputs, hidden_grads, grad_sums[0], grad_sums[1], grad_sums[2], grad_sums[3], grad_sums[4], grad_sums[5], grad_sums[6], grad_sums[7], grad_sums[8])
```

```python
import jax
import jax.numpy as jnp
from jax import lax
from jax.experimental import pallas as pl
from jax.experimental.pallas import tpu as pltpu
from jax.sharding import PartitionSpec as P

D = 1536
H = 48
P_SIZE = 64
N = 128
E = 3072

eps = 1e-05
f32, bf16 = jnp.float32, jnp.bfloat16
Q = 128
NEG = -1e30


def dot(a, b):
    return jnp.dot(a, b, preferred_element_type=f32)


def dot_nt(a, b):
    return lax.dot_general(a, b, (((1,), (1,)), ((), ())), preferred_element_type=f32)


def dot3(tri, v):
    hi = v.astype(bf16)
    rest = v - hi.astype(f32)
    mid = rest.astype(bf16)
    low = (rest - mid.astype(f32)).astype(bf16)
    return dot(tri, hi) + dot(tri, mid) + dot(tri, low)


def sigmoid(v):
    return 1.0 / (1.0 + jnp.exp(-v))


def spread_col(v, col):
    return jnp.broadcast_to(v[:, col : col + 1], (Q, 128))


def softplus(v):
    return jnp.maximum(v, 0.0) + jnp.log1p(jnp.exp(-jnp.abs(v)))


def chunk_masks(segc, segr):
    row = lax.broadcasted_iota(jnp.int32, (Q, Q), 0)
    col = lax.broadcasted_iota(jnp.int32, (Q, Q), 1)
    return row, col, segc == segr


def conv_pre(useen, flags, wk, bias, lanes):
    now = useen[8 : 8 + Q, lanes]
    pre = bias[:, lanes] + wk[3:4, lanes] * now
    shifted = [now]
    for j in (1, 2, 3):
        moved = useen[8 - j : 8 - j + Q, lanes] * flags[j]
        shifted.append(moved)
        pre = pre + wk[3 - j : 4 - j, lanes] * moved
    return pre, shifted


def fwd_kernel(u_ref, dt_ref, tok_ref, segc_ref, segr_ref, wk_ref, bias_ref, head_ref, skip_ref,
               mixed_ref, save_ref, state, useen, act):
    step_no = pl.program_id(0)
    width = u_ref.shape[1]
    xw = width - 256
    pairs = xw // 128

    @pl.when(step_no == 0)
    def _():
        state[...] = jnp.zeros_like(state)
        useen[0:8, :] = jnp.zeros((8, width), f32)

    useen[8 : 8 + Q, :] = u_ref[...].astype(f32)
    flags = [None] + [spread_col(tok_ref[...], j) for j in range(3)]
    carried = spread_col(tok_ref[...], 3)
    samelast = spread_col(tok_ref[...], 4)
    for p in range(width // 128):
        lanes = slice(128 * p, 128 * p + 128)
        pre, _ = conv_pre(useen, flags, wk_ref, bias_ref, lanes)
        act[:, lanes] = pre * sigmoid(pre)
    tail = useen[Q : Q + 8, :]
    useen[0:8, :] = tail

    step = softplus(dt_ref[...].astype(f32) + head_ref[0:1, :])
    row = lax.broadcasted_iota(jnp.int32, (Q, Q), 0)
    col = lax.broadcasted_iota(jnp.int32, (Q, Q), 1)
    tri = jnp.where(row >= col, 1.0, 0.0).astype(bf16)
    decay = dot3(tri, step * head_ref[1:2, :])
    decay_t = decay.T
    madd = jnp.where((row >= col) & (segc_ref[...] == segr_ref[0]), 0.0, NEG)
    b_now = act[:, xw : xw + 128]
    c_low = act[:, xw + 128 : xw + 256].astype(bf16)
    gram = dot_nt(c_low, b_now.astype(bf16))
    b_t = b_now.T.astype(bf16)
    left = lax.broadcasted_iota(jnp.int32, (Q, 128), 1) < 64
    for p in range(pairs):
        lanes = slice(128 * p, 128 * p + 128)
        d0, d1 = spread_col(decay, 2 * p), spread_col(decay, 2 * p + 1)
        dp = jnp.where(left, d0, d1)
        sp = jnp.where(left, spread_col(step, 2 * p), spread_col(step, 2 * p + 1))
        xs = act[:, lanes]
        xp = xs * sp
        m0 = gram * jnp.exp(d0 - decay_t[2 * p : 2 * p + 1, :] + madd)
        m1 = gram * jnp.exp(d1 - decay_t[2 * p + 1 : 2 * p + 2, :] + madd)
        both = jnp.concatenate([m0.astype(bf16), m1.astype(bf16)], axis=1)
        stacked = jnp.concatenate(
            [jnp.where(left, xp, 0.0).astype(bf16), jnp.where(left, 0.0, xp).astype(bf16)], axis=0
        )
        st = state[:, lanes]
        st_low = st.astype(bf16)
        save_ref[0, :, lanes] = st_low
        y = dot(both, stacked) + dot(c_low, st_low) * (jnp.exp(dp) * carried)
        mixed_ref[:, lanes] = (y + skip_ref[:, lanes] * xs).astype(bf16)
        last = dp[Q - 1 : Q, :]
        to_end = (xp * (jnp.exp(last - dp) * samelast)).astype(bf16)
        state[:, lanes] = st * (jnp.exp(last) * carried[Q - 1 : Q, :]) + dot(b_t, to_end)


def mixer_fwd(u, dt, tok, segc, segr, wk, bias, head, skip):
    length, width = u.shape
    xw = width - 256
    n = length // Q
    whole = lambda shape: pl.BlockSpec(shape, lambda i: (0,) * len(shape))
    return pl.pallas_call(
        fwd_kernel,
        grid=(n,),
        in_specs=[
            pl.BlockSpec((Q, width), lambda i: (i, 0)),
            pl.BlockSpec((Q, 128), lambda i: (i, 0)),
            pl.BlockSpec((Q, 8), lambda i: (i, 0)),
            pl.BlockSpec((Q, 1), lambda i: (i, 0)),
            pl.BlockSpec((1, 1, Q), lambda i: (i, 0, 0)),
            whole((4, width)),
            whole((1, width)),
            whole((2, 128)),
            whole((1, xw)),
        ],
        out_specs=[
            pl.BlockSpec((Q, xw), lambda i: (i, 0)),
            pl.BlockSpec((1, 128, xw), lambda i: (i, 0, 0)),
        ],
        out_shape=[
            jax.ShapeDtypeStruct((length, xw), bf16),
            jax.ShapeDtypeStruct((n, 128, xw), bf16),
        ],
        scratch_shapes=[
            pltpu.VMEM((128, xw), f32),
            pltpu.VMEM((Q + 8, width), f32),
            pltpu.VMEM((Q, width), f32),
        ],
        compiler_params=pltpu.CompilerParams(vmem_limit_bytes=48 * 2**20),
        name="mixer_forward",
    )(u, dt, tok, segc, segr, wk, bias, head, skip)


def bwd_kernel(u_ref, halo_ref, dt_ref, tok_ref, segc_ref, segr_ref, wk_ref, bias_ref, head_ref, skip_ref,
               save_ref, dy_ref, spot_ref,
               du_ref, ddt_ref, wgrad_ref, hgrad_ref, sgrad_ref,
               dstate, useen, act, slope, dpre, keep_y, keep_x, prod_a, prod_b, rows_a, held):
    step_no = pl.program_id(0)
    width = u_ref.shape[1]
    xw = width - 256
    pairs = xw // 128

    @pl.when(step_no == 0)
    def _():
        dstate[...] = jnp.zeros_like(dstate)
        dpre[Q : Q + 8, :] = jnp.zeros((8, width), f32)
        wgrad_ref[...] = jnp.zeros_like(wgrad_ref)
        hgrad_ref[...] = jnp.zeros_like(hgrad_ref)
        sgrad_ref[...] = jnp.zeros_like(sgrad_ref)
        rows_a[...] = jnp.zeros_like(rows_a)

    useen[0:8, :] = halo_ref[...].astype(f32)[8:16, :]
    useen[8 : 8 + Q, :] = u_ref[...].astype(f32)
    tok = tok_ref[...]
    flags = [None] + [spread_col(tok, j) for j in range(3)]
    carried = spread_col(tok, 3)
    samelast = spread_col(tok, 4)
    for p in range(width // 128):
        lanes = slice(128 * p, 128 * p + 128)
        pre, _ = conv_pre(useen, flags, wk_ref, bias_ref, lanes)
        sg = sigmoid(pre)
        act[:, lanes] = pre * sg
        slope[:, lanes] = sg * (1.0 + pre * (1.0 - sg))

    raw = dt_ref[...].astype(f32) + head_ref[0:1, :]
    step = softplus(raw)
    rate = head_ref[1:2, :]
    row = lax.broadcasted_iota(jnp.int32, (Q, Q), 0)
    col = lax.broadcasted_iota(jnp.int32, (Q, Q), 1)
    tri = jnp.where(row >= col, 1.0, 0.0).astype(bf16)
    upper = jnp.where(row <= col, 1.0, 0.0).astype(bf16)
    below = jnp.where(row > col, 1.0, 0.0).astype(bf16)
    decay = dot3(tri, step * rate)
    decay_t = decay.T
    madd = jnp.where((row <= col) & (segc_ref[...] == segr_ref[0]), 0.0, NEG)
    b_now, c_now = act[:, xw : xw + 128], act[:, xw + 128 : xw + 256]
    b_low, c_low = b_now.astype(bf16), c_now.astype(bf16)
    c_t = c_now.T.astype(bf16)
    gram = dot_nt(b_low, c_low)
    left = lax.broadcasted_iota(jnp.int32, (Q, 128), 1) < 64
    lane = lax.broadcasted_iota(jnp.int32, (Q, 128), 1)
    dgram = jnp.zeros((Q, Q), f32)
    cols_b = jnp.zeros((Q, 128), f32)
    for p in range(pairs):
        lanes = slice(128 * p, 128 * p + 128)
        d0, d1 = spread_col(decay, 2 * p), spread_col(decay, 2 * p + 1)
        dp = jnp.where(left, d0, d1)
        sp = jnp.where(left, spread_col(step, 2 * p), spread_col(step, 2 * p + 1))
        xs = act[:, lanes]
        xp = xs * sp
        dy_low = dy_ref[:, lanes]
        dy = dy_low.astype(f32)
        stacked = jnp.concatenate(
            [jnp.where(left, dy, 0.0).astype(bf16), jnp.where(left, 0.0, dy).astype(bf16)], axis=0
        )
        pair = dot_nt(xp.astype(bf16), stacked)
        mts = []
        for k, dk in ((0, d0), (1, d1)):
            h = 2 * p + k
            e = jnp.exp(decay_t[h : h + 1, :] - dk + madd)
            f = e * pair[:, 128 * k : 128 * k + 128]
            dgram = dgram + f
            w = gram * f
            mts.append((gram * e).astype(bf16))
            rows_a[h : h + 1, :] = jnp.sum(w, axis=0, keepdims=True)
            cols_b = jnp.where(lane == h, jnp.sum(w, axis=1, keepdims=True), cols_b)
        within = dot(jnp.concatenate(mts, axis=1), stacked)
        grow = jnp.exp(dp) * carried
        dy_in = dy * grow
        dy_in_low = dy_in.astype(bf16)
        keep_y[:, lanes] = dy_in_low
        st = save_ref[0, :, lanes]
        prod_a[:, lanes] = (dy_in * dot(c_low, st)).astype(bf16)
        last = dp[Q - 1 : Q, :]
        fade = jnp.exp(last - dp) * samelast
        ds = dstate[:, lanes]
        ds_low = ds.astype(bf16)
        xe = xp * fade
        keep_x[:, lanes] = xe.astype(bf16)
        later = dot(b_low, ds_low)
        prod_b[:, lanes] = (xe * later).astype(bf16)
        retain = jnp.exp(last) * carried[Q - 1 : Q, :]
        held[0:1, lanes] = jnp.sum(ds * st.astype(f32), axis=0, keepdims=True) * retain
        dxs = sp * (within + later * fade) + skip_ref[:, lanes] * dy
        skp = xs * dy
        sgrad_ref[:, lanes] += jnp.sum(skp.reshape(Q // 8, 8, 128), axis=0)
        dpre[0:Q, lanes] = dxs * slope[:, lanes]
        dstate[:, lanes] = ds * retain + dot(c_t, dy_in_low)
        if p == 0:
            db_in, dc_in = dot_nt(keep_x[:, lanes], ds_low), dot_nt(dy_in_low, st)
        else:
            db_in, dc_in = db_in + dot_nt(keep_x[:, lanes], ds_low), dc_in + dot_nt(dy_in_low, st)

    dg_low = dgram.astype(bf16)
    db = dot(dg_low, c_low) + db_in
    dc = dot(dgram.T.astype(bf16), b_low) + dc_in
    dpre[0:Q, xw : xw + 128] = db * slope[:, xw : xw + 128]
    dpre[0:Q, xw + 128 : xw + 256] = dc * slope[:, xw + 128 : xw + 256]

    spot = spot_ref[...]
    a_in = dot(prod_a[...], spot)
    b_in = dot(prod_b[...], spot)
    hv = jnp.broadcast_to(held[0:1, :], (8, xw))
    h_hi = hv.astype(bf16)
    h_lo = (hv - h_hi.astype(f32)).astype(bf16)
    through = (dot(h_hi, spot) + dot(h_lo, spot))[0:1, :]
    a_own = rows_a[...].T
    cross = dot3(upper, a_own - cols_b + a_in) + dot3(below, b_in) + through
    total = cols_b + b_in
    sg = sigmoid(raw)
    ratio = jnp.where(step > 1e-30, sg / jnp.maximum(step, 1e-30), 1.0)
    draw = total * ratio + rate * cross * sg
    ddt_ref[...] = draw.astype(bf16)
    hgrad_ref[0:8, :] += jnp.sum(draw.reshape(Q // 8, 8, 128), axis=0)
    hgrad_ref[8:16, :] += jnp.sum((step * cross).reshape(Q // 8, 8, 128), axis=0)

    for p in range(width // 128):
        lanes = slice(128 * p, 128 * p + 128)
        own = dpre[0:Q, lanes]
        du = wk_ref[3:4, lanes] * own
        wgrad_ref[24:32, lanes] += jnp.sum((own * useen[8 : 8 + Q, lanes]).reshape(Q // 8, 8, 128), axis=0)
        wgrad_ref[32:40, lanes] += jnp.sum(own.reshape(Q // 8, 8, 128), axis=0)
        for j in (1, 2, 3):
            du = du + wk_ref[3 - j : 4 - j, lanes] * (dpre[j : j + Q, lanes] * spread_col(tok, 4 + j))
            moved = own * (useen[8 - j : 8 - j + Q, lanes] * flags[j])
            k = 3 - j
            wgrad_ref[8 * k : 8 * k + 8, lanes] += jnp.sum(moved.reshape(Q // 8, 8, 128), axis=0)
        du_ref[:, lanes] = du.astype(bf16)
    first = dpre[0:8, :]
    dpre[Q : Q + 8, :] = first


def mixer_bwd(u, dt, tok, segc, segr, wk, bias, head, skip, save, dy, spot):
    length, width = u.shape
    xw = width - 256
    n = length // Q
    whole = lambda shape: pl.BlockSpec(shape, lambda i: (0,) * len(shape))
    back = lambda i: (n - 1 - i, 0)
    return pl.pallas_call(
        bwd_kernel,
        grid=(n,),
        in_specs=[
            pl.BlockSpec((Q, width), back),
            pl.BlockSpec((16, width), lambda i: (jnp.maximum((n - 1 - i) * (Q // 16) - 1, 0), 0)),
            pl.BlockSpec((Q, 128), back),
            pl.BlockSpec((Q, 8), back),
            pl.BlockSpec((Q, 1), back),
            pl.BlockSpec((1, 1, Q), lambda i: (n - 1 - i, 0, 0)),
            whole((4, width)),
            whole((1, width)),
            whole((2, 128)),
            whole((1, xw)),
            pl.BlockSpec((1, 128, xw), lambda i: (n - 1 - i, 0, 0)),
            pl.BlockSpec((Q, xw), back),
            whole((xw, 128)),
        ],
        out_specs=[
            pl.BlockSpec((Q, width), back),
            pl.BlockSpec((Q, 128), back),
            whole((40, width)),
            whole((16, 128)),
            whole((8, xw)),
        ],
        out_shape=[
            jax.ShapeDtypeStruct((length, width), bf16),
            jax.ShapeDtypeStruct((length, 128), bf16),
            jax.ShapeDtypeStruct((40, width), f32),
            jax.ShapeDtypeStruct((16, 128), f32),
            jax.ShapeDtypeStruct((8, xw), f32),
        ],
        scratch_shapes=[
            pltpu.VMEM((128, xw), f32),
            pltpu.VMEM((Q + 8, width), f32),
            pltpu.VMEM((Q, width), f32),
            pltpu.VMEM((Q, width), f32),
            pltpu.VMEM((Q + 8, width), f32),
            pltpu.VMEM((Q, xw), bf16),
            pltpu.VMEM((Q, xw), bf16),
            pltpu.VMEM((Q, xw), bf16),
            pltpu.VMEM((Q, xw), bf16),
            pltpu.VMEM((128, 128), f32),
            pltpu.VMEM((8, xw), f32),
        ],
        compiler_params=pltpu.CompilerParams(vmem_limit_bytes=48 * 2**20),
        name="mixer_backward",
    )(u, u, dt, tok, segc, segr, wk, bias, head, skip, save, dy, spot)


def token_facts(seg):
    length = seg.shape[0]
    facts = []
    for j in (1, 2, 3):
        before = jnp.concatenate([jnp.full((j,), -1, jnp.int32), seg[:-j]])
        facts.append(before == seg)
    by = seg.reshape(length // Q, Q)
    ends = by[:, Q - 1]
    prior = jnp.concatenate([jnp.full((1,), -1, jnp.int32), ends[:-1]])
    facts.append((by == prior[:, None]).reshape(length))
    facts.append((by == ends[:, None]).reshape(length))
    for j in (1, 2, 3):
        after = jnp.concatenate([seg[j:], jnp.full((j,), -1, jnp.int32)])
        facts.append(after == seg)
    return jnp.stack(facts, axis=1).astype(f32)


def over_rows(left, right):
    return lax.dot_general(
        left, right, (((0,), (0,)), ((), ())), preferred_element_type=jnp.float32
    )


def own_columns(weight, group, groups):
    heads = H // groups
    wide = heads * P_SIZE
    dt = lax.dynamic_slice_in_dim(weight, 2 * E + 2 * N + group * heads, heads, 1)
    return jnp.concatenate(
        [
            lax.dynamic_slice_in_dim(weight, group * wide, wide, 1),
            lax.dynamic_slice_in_dim(weight, E + group * wide, wide, 1),
            weight[:, 2 * E : 2 * E + 2 * N],
            jnp.pad(dt, ((0, 0), (0, 128 - heads))),
        ],
        axis=1,
    )


def shards(
    hidden,
    segments,
    norm_gain,
    in_weight,
    conv_weight,
    conv_bias,
    step_bias,
    decay_log,
    skip_scale,
    gate_gain,
    out_weight,
    cotangent,
):
    group = lax.axis_index("seq")
    groups = lax.axis_size("seq")
    heads = H // groups
    wide = heads * P_SIZE
    piece = hidden.shape[1]
    length = segments.shape[1]
    hidden_own, cot_own = hidden[0], cotangent[0]
    hidden_all = lax.all_gather(hidden_own, "seq", axis=0, tiled=True)
    in_gain = norm_gain.astype(f32)[:, None]
    in_scaled = (in_weight.astype(f32) * in_gain).astype(bf16)
    in_own = lax.all_gather(own_columns(in_scaled, group, groups), "wshard", axis=0, tiled=True)
    out_gain = gate_gain.astype(f32)[:, None]
    out_scaled = (out_weight.astype(f32) * out_gain).astype(bf16)
    out_cols = lax.all_to_all(out_scaled, "wshard", split_axis=1, concat_axis=0, tiled=True)
    out_own = lax.all_gather(
        lax.dynamic_slice_in_dim(out_cols, group * wide, wide, 0), "wshard", axis=1, tiled=True
    )
    cot_all = lax.all_gather(cot_own, "seq", axis=0, tiled=True)

    hidden_wide = hidden_all.astype(f32)
    scale = lax.rsqrt(jnp.mean(hidden_wide * hidden_wide, axis=-1, keepdims=True) + eps)
    gate = jnp.dot(hidden_all, in_own[:, :wide], preferred_element_type=f32) * scale
    u = (
        jnp.dot(hidden_all, in_own[:, wide : 2 * wide + 2 * N], preferred_element_type=f32) * scale
    ).astype(bf16)
    dt = (
        jnp.dot(hidden_all, in_own[:, 2 * wide + 2 * N :], preferred_element_type=f32) * scale
    ).astype(bf16)

    seg = segments[0]
    tok = token_facts(seg)
    segc, segr = seg[:, None], seg.reshape(length // Q, 1, Q)
    own_chan = lambda v: jnp.concatenate(
        [lax.dynamic_slice_in_dim(v, group * wide, wide, v.ndim - 1), v[..., E:]], axis=-1
    )
    own_head = lambda v: lax.dynamic_slice_in_dim(v, group * heads, heads, 0)
    taps, bias = own_chan(conv_weight), own_chan(conv_bias)[None]
    rate = -jnp.exp(own_head(decay_log))
    head = jnp.pad(jnp.stack([own_head(step_bias), rate]), ((0, 0), (0, 128 - heads)))
    skip = jnp.repeat(own_head(skip_scale), P_SIZE)[None]
    spot = (jnp.arange(wide)[:, None] // P_SIZE == jnp.arange(128)[None]).astype(bf16)
    mixed, save = mixer_fwd(u, dt, tok, segc, segr, taps, bias, head, skip)

    mixed_wide = mixed.astype(f32)
    sg = jax.nn.sigmoid(gate)
    silu = gate * sg
    g = mixed_wide * silu
    g_low = g.astype(bf16)
    a = lax.dot_general(cot_all, out_own, (((1,), (1,)), ((), ())), preferred_element_type=f32)
    sums = lax.psum(jnp.stack([jnp.sum(g * g, axis=1), jnp.sum(a * g, axis=1)]), "seq")
    r = lax.rsqrt(sums[0] / E + eps)[:, None]
    pull = (r * r * r) * (sums[1] / E)[:, None]
    d_g = r * a - g * pull
    gate_gain_part = jnp.sum(a * (g * r), axis=0)
    d_mixed = (d_g * silu).astype(bf16)
    d_gate = (d_g * mixed_wide * (sg * (1.0 + gate * (1.0 - sg))) * scale).astype(bf16)
    partial = (jnp.dot(g_low, out_own, preferred_element_type=f32) * r).astype(bf16)
    out_sum = lax.psum_scatter(partial, "seq", scatter_dimension=0, tiled=True)
    layer_output = hidden_own.astype(f32) + out_sum.astype(f32)
    cot_r = (cot_all.astype(f32) * r).astype(bf16)
    out_part = over_rows(g_low, cot_r).astype(bf16)
    out_part = lax.psum_scatter(out_part, "wshard", scatter_dimension=1, tiled=True)
    out_part = lax.all_gather(out_part, "seq", axis=0, tiled=True)
    out_part = lax.all_to_all(out_part, "wshard", split_axis=0, concat_axis=1, tiled=True)
    out_weight_grad = out_part.astype(f32) * out_gain

    du, ddt, taps_sum, head_sum, skip_sum = mixer_bwd(
        u, dt, tok, segc, segr, taps, bias, head, skip, save, d_mixed, spot
    )
    du = (du.astype(f32) * scale).astype(bf16)
    ddt = (ddt.astype(f32) * scale).astype(bf16)
    d_proj = jnp.concatenate([d_gate, du, ddt], axis=1)
    in_part = over_rows(hidden_all, d_proj).astype(bf16)
    b_part = lax.dot_general(
        d_proj, in_own, (((1,), (1,)), ((), ())), preferred_element_type=f32
    ).astype(bf16)
    b_sum = lax.psum_scatter(b_part, "seq", scatter_dimension=0, tiled=True).astype(f32)
    own_wide = hidden_own.astype(f32)
    own_scale = lax.rsqrt(jnp.mean(own_wide * own_wide, axis=-1, keepdims=True) + eps)
    hidden_grad = (
        cot_own.astype(f32)
        + b_sum
        - own_wide * (own_scale * own_scale) * jnp.mean(b_sum * own_wide, axis=-1, keepdims=True)
    )
    norm_part = jnp.sum(b_sum * own_wide, axis=0)

    in_part = lax.psum_scatter(in_part, "wshard", scatter_dimension=0, tiled=True)
    in_all = lax.all_gather(in_part, "seq", axis=0, tiled=False).astype(f32)
    side = lambda lo, hi: jnp.concatenate([in_all[i, :, lo:hi] for i in range(groups)], axis=1)
    in_weight_grad = (
        jnp.concatenate(
            [
                side(0, wide),
                side(wide, 2 * wide),
                jnp.sum(in_all[:, :, 2 * wide : 2 * wide + 2 * N], axis=0),
                side(2 * wide + 2 * N, 2 * wide + 2 * N + heads),
            ],
            axis=1,
        )
        * in_gain
    )

    taps_sum = jnp.sum(taps_sum.reshape(5, 8, -1), axis=1)
    head_sum = jnp.sum(head_sum.reshape(2, 8, -1), axis=1)[:, :heads]
    head_sum = head_sum * jnp.stack([jnp.ones_like(rate), rate])
    skip_sum = jnp.sum(skip_sum, axis=0).reshape(heads, P_SIZE).sum(axis=1)
    place = lambda v, size, at: lax.dynamic_update_slice_in_dim(
        jnp.zeros(v.shape[:-1] + (size,), f32), v, at, v.ndim - 1
    )
    chan_sums = jnp.concatenate([place(taps_sum[:, :wide], E, group * wide), taps_sum[:, wide:]], axis=1)
    flat = jnp.concatenate(
        [
            chan_sums.reshape(-1),
            place(jnp.concatenate([head_sum, skip_sum[None]]), H, group * heads).reshape(-1),
            place(gate_gain_part, E, group * wide),
            norm_part,
        ]
    )
    flat = lax.psum(flat, ("wshard", "seq"))
    channels = E + 2 * N
    chan_sums = flat[: 5 * channels].reshape(5, channels)
    at = 5 * channels
    head_sums = flat[at : at + 3 * H].reshape(3, H)
    at = at + 3 * H
    shard = lax.axis_index("wshard")
    gate_rows, norm_rows = out_weight.shape[0], in_weight.shape[0]
    gate_gain_grad = lax.dynamic_slice_in_dim(flat[at : at + E], shard * gate_rows, gate_rows, 0) / gate_gain.astype(f32)
    norm_gain_grad = lax.dynamic_slice_in_dim(flat[at + E :], shard * norm_rows, norm_rows, 0) / norm_gain.astype(f32)
    return (
        layer_output[None],
        hidden_grad[None],
        norm_gain_grad,
        in_weight_grad,
        chan_sums[:4],
        chan_sums[4],
        head_sums[0],
        head_sums[1],
        head_sums[2],
        gate_gain_grad,
        out_weight_grad,
    )


def solution(mesh):
    in_specs = (
        P("wshard", "seq", None),
        P("wshard", None),
        P("wshard"),
        P("wshard", None),
        P(),
        P(),
        P(),
        P(),
        P(),
        P("wshard"),
        P("wshard", None),
        P("wshard", "seq", None),
    )
    out_specs = (
        P("wshard", "seq", None),
        P("wshard", "seq", None),
        P("wshard"),
        P("wshard", None),
        P(),
        P(),
        P(),
        P(),
        P(),
        P("wshard"),
        P("wshard", None),
    )
    return jax.shard_map(shards, mesh=mesh, in_specs=in_specs, out_specs=out_specs, check_vma=False)
```

```python
import functools

import jax
import jax.numpy as jnp
from jax import lax
from jax.experimental import pallas as pl
from jax.experimental.pallas import tpu as pltpu
from jax.sharding import PartitionSpec as P

D = 1536
H = 48
P_SIZE = 64
N = 128
E = 3072

eps = 1e-05
f32, bf16 = jnp.float32, jnp.bfloat16
Q = 128
NEG = -1e30


def dot(a, b):
    return jnp.dot(a, b, preferred_element_type=f32)


def dot_nt(a, b):
    return lax.dot_general(a, b, (((1,), (1,)), ((), ())), preferred_element_type=f32)


def dot3(tri, v):
    hi = v.astype(bf16)
    rest = v - hi.astype(f32)
    mid = rest.astype(bf16)
    low = (rest - mid.astype(f32)).astype(bf16)
    return dot(tri, hi) + dot(tri, mid) + dot(tri, low)


def sigmoid(v):
    return 1.0 / (1.0 + jnp.exp(-v))


def spread_col(v, col):
    return jnp.broadcast_to(v[:, col : col + 1], (Q, 128))


def softplus(v):
    return jnp.maximum(v, 0.0) + jnp.log1p(jnp.exp(-jnp.abs(v)))


def chunk_masks(segc, segr):
    row = lax.broadcasted_iota(jnp.int32, (Q, Q), 0)
    col = lax.broadcasted_iota(jnp.int32, (Q, Q), 1)
    return row, col, segc == segr


def conv_pre(useen, flags, wk, bias, lanes):
    now = useen[8 : 8 + Q, lanes]
    pre = bias[:, lanes] + wk[3:4, lanes] * now
    shifted = [now]
    for j in (1, 2, 3):
        moved = useen[8 - j : 8 - j + Q, lanes] * flags[j]
        shifted.append(moved)
        pre = pre + wk[3 - j : 4 - j, lanes] * moved
    return pre, shifted


class NoTraffic:
    inputs, outputs, scratch, collective_id = (), (), (), None

    def __init__(self, *refs):
        pass

    def step(self, i, last):
        pass


def fwd_kernel(traffic, hid_ref, main_ref, bc_ref, wdt_ref, tok_ref, segc_ref, segr_ref, wk_ref, bias_ref, head_ref, skip_ref, *rest):
    n_in, n_out = len(traffic.inputs), len(traffic.outputs)
    extra_in, rest = rest[:n_in], rest[n_in:]
    u_ref, dt_ref, gate_ref, scale_ref, mixed_ref, save_ref = rest[:6]
    extra_out, rest = rest[6 : 6 + n_out], rest[6 + n_out :]
    state, useen, act, next_u, next_dt = rest[:5]
    step_no = pl.program_id(0)
    traffic(*extra_in, *extra_out, *rest[5:]).step(step_no, pl.num_programs(0) - 1)
    width = wk_ref.shape[1]
    xw = width - 256
    pairs = xw // 128

    @pl.when(step_no == 0)
    def _():
        next_u[...] = jnp.zeros_like(next_u)
        next_dt[...] = jnp.zeros_like(next_dt)

    @pl.when(step_no <= 1)
    def _():
        state[...] = jnp.zeros_like(state)
        useen[0:8, :] = jnp.zeros((8, width), f32)

    useen[8 : 8 + Q, :] = next_u[...]
    dt_now = next_dt[...]

    low = hid_ref[...]
    total = jnp.zeros((Q, 128), f32)
    for k in range(low.shape[1] // 128):
        part = low[:, 128 * k : 128 * k + 128].astype(f32)
        total = total + part * part
    scale = lax.rsqrt(jnp.sum(total, axis=1, keepdims=True) / low.shape[1] + eps)
    scale_ref[...] = scale
    for k in range(xw // 256):
        gate_ref[:, 256 * k : 256 * k + 256] = dot(low, main_ref[:, 256 * k : 256 * k + 256]) * scale
    for k in range(xw // 256):
        got = (dot(low, main_ref[:, xw + 256 * k : xw + 256 * k + 256]) * scale).astype(bf16)
        u_ref[:, 256 * k : 256 * k + 256] = got
        next_u[:, 256 * k : 256 * k + 256] = got.astype(f32)
    got = (dot(low, bc_ref[...]) * scale).astype(bf16)
    u_ref[:, xw : xw + 256] = got
    next_u[:, xw : xw + 256] = got.astype(f32)
    got = (dot(low, wdt_ref[...]) * scale).astype(bf16)
    dt_ref[...] = got
    next_dt[...] = got.astype(f32)

    flags = [None] + [spread_col(tok_ref[...], j) for j in range(3)]
    carried = spread_col(tok_ref[...], 3)
    samelast = spread_col(tok_ref[...], 4)
    for p in range(width // 128):
        lanes = slice(128 * p, 128 * p + 128)
        pre, _ = conv_pre(useen, flags, wk_ref, bias_ref, lanes)
        act[:, lanes] = pre * sigmoid(pre)
    tail = useen[Q : Q + 8, :]
    useen[0:8, :] = tail

    step = softplus(dt_now + head_ref[0:1, :])
    row = lax.broadcasted_iota(jnp.int32, (Q, Q), 0)
    col = lax.broadcasted_iota(jnp.int32, (Q, Q), 1)
    tri = jnp.where(row >= col, 1.0, 0.0).astype(bf16)
    decay = dot3(tri, step * head_ref[1:2, :])
    decay_t = decay.T
    madd = jnp.where((row >= col) & (segc_ref[...] == segr_ref[0]), 0.0, NEG)
    b_now = act[:, xw : xw + 128]
    c_low = act[:, xw + 128 : xw + 256].astype(bf16)
    gram = dot_nt(c_low, b_now.astype(bf16))
    b_t = b_now.T.astype(bf16)
    left = lax.broadcasted_iota(jnp.int32, (Q, 128), 1) < 64
    for p in range(pairs):
        lanes = slice(128 * p, 128 * p + 128)
        d0, d1 = spread_col(decay, 2 * p), spread_col(decay, 2 * p + 1)
        dp = jnp.where(left, d0, d1)
        sp = jnp.where(left, spread_col(step, 2 * p), spread_col(step, 2 * p + 1))
        xs = act[:, lanes]
        xp = xs * sp
        m0 = gram * jnp.exp(d0 - decay_t[2 * p : 2 * p + 1, :] + madd)
        m1 = gram * jnp.exp(d1 - decay_t[2 * p + 1 : 2 * p + 2, :] + madd)
        both = jnp.concatenate([m0.astype(bf16), m1.astype(bf16)], axis=1)
        stacked = jnp.concatenate(
            [jnp.where(left, xp, 0.0).astype(bf16), jnp.where(left, 0.0, xp).astype(bf16)], axis=0
        )
        st = state[:, lanes]
        st_low = st.astype(bf16)
        save_ref[0, :, lanes] = st_low
        y = dot(both, stacked) + dot(c_low, st_low) * (jnp.exp(dp) * carried)
        mixed_ref[:, lanes] = (y + skip_ref[:, lanes] * xs).astype(bf16)
        last = dp[Q - 1 : Q, :]
        to_end = (xp * (jnp.exp(last - dp) * samelast)).astype(bf16)
        state[:, lanes] = st * (jnp.exp(last) * carried[Q - 1 : Q, :]) + dot(b_t, to_end)


def mixer_fwd(traffic, extra, hid, main, bc, wdt, tok, segc, segr, wk, bias, head, skip):
    length, depth = hid.shape
    width = wk.shape[1]
    xw = width - 256
    n = length // Q
    whole = lambda shape: pl.BlockSpec(shape, lambda i: (0,) * len(shape), pipeline_mode=pl.Buffered(1))
    ahead = lambda i: (jnp.minimum(i, n - 1), 0)
    now = lambda i: (jnp.maximum(i - 1, 0), 0)
    now3 = lambda i: (jnp.maximum(i - 1, 0), 0, 0)
    return pl.pallas_call(
        functools.partial(fwd_kernel, traffic),
        grid=(n + 1,),
        in_specs=[
            pl.BlockSpec((Q, depth), ahead),
            whole(main.shape),
            whole(bc.shape),
            whole(wdt.shape),
            pl.BlockSpec((Q, 8), now),
            pl.BlockSpec((Q, 1), now),
            pl.BlockSpec((1, 1, Q), now3),
            whole((4, width)),
            whole((1, width)),
            whole((2, 128)),
            whole((1, xw)),
        ]
        + [pl.BlockSpec(memory_space=pl.ANY)] * len(extra),
        out_specs=[
            pl.BlockSpec((Q, width), ahead),
            pl.BlockSpec((Q, 128), ahead),
            pl.BlockSpec((Q, xw), ahead),
            pl.BlockSpec((Q, 1), ahead),
            pl.BlockSpec((Q, xw), now),
            pl.BlockSpec((1, 128, xw), now3),
        ]
        + [pl.BlockSpec(memory_space=pl.ANY)] * len(traffic.outputs),
        out_shape=[
            jax.ShapeDtypeStruct((length, width), bf16),
            jax.ShapeDtypeStruct((length, 128), bf16),
            jax.ShapeDtypeStruct((length, xw), f32),
            jax.ShapeDtypeStruct((length, 1), f32),
            jax.ShapeDtypeStruct((length, xw), bf16),
            jax.ShapeDtypeStruct((n, 128, xw), bf16),
            *traffic.outputs,
        ],
        scratch_shapes=[
            pltpu.VMEM((128, xw), f32),
            pltpu.VMEM((Q + 8, width), f32),
            pltpu.VMEM((Q, width), f32),
            pltpu.VMEM((Q, width), f32),
            pltpu.VMEM((Q, 128), f32),
            *traffic.scratch,
        ],
        compiler_params=pltpu.CompilerParams(
            vmem_limit_bytes=48 * 2**20,
            collective_id=traffic.collective_id,
            has_side_effects=traffic.collective_id is not None,
        ),
        name="mixer_forward",
    )(hid, main, bc, wdt, tok, segc, segr, wk, bias, head, skip, *extra)


def bwd_kernel(traffic, u_ref, halo_ref, dt_ref, tok_ref, segc_ref, segr_ref, wk_ref, bias_ref, head_ref, skip_ref,
               save_ref, dy_ref, spot_ref, *rest):
    n_in, n_out = len(traffic.inputs), len(traffic.outputs)
    extra_in, rest = rest[:n_in], rest[n_in:]
    du_ref, ddt_ref, wgrad_ref, hgrad_ref, sgrad_ref = rest[:5]
    extra_out, rest = rest[5 : 5 + n_out], rest[5 + n_out :]
    dstate, useen, act, slope, dpre, keep_y, keep_x, prod_a, prod_b, rows_a, held = rest[:11]
    step_no = pl.program_id(0)
    traffic(*extra_in, *extra_out, *rest[11:]).step(step_no, pl.num_programs(0) - 1)
    width = u_ref.shape[1]
    xw = width - 256
    pairs = xw // 128

    @pl.when(step_no == 0)
    def _():
        dstate[...] = jnp.zeros_like(dstate)
        dpre[Q : Q + 8, :] = jnp.zeros((8, width), f32)
        wgrad_ref[...] = jnp.zeros_like(wgrad_ref)
        hgrad_ref[...] = jnp.zeros_like(hgrad_ref)
        sgrad_ref[...] = jnp.zeros_like(sgrad_ref)
        rows_a[...] = jnp.zeros_like(rows_a)

    useen[0:8, :] = halo_ref[...].astype(f32)[8:16, :]
    useen[8 : 8 + Q, :] = u_ref[...].astype(f32)
    tok = tok_ref[...]
    flags = [None] + [spread_col(tok, j) for j in range(3)]
    carried = spread_col(tok, 3)
    samelast = spread_col(tok, 4)
    for p in range(width // 128):
        lanes = slice(128 * p, 128 * p + 128)
        pre, _ = conv_pre(useen, flags, wk_ref, bias_ref, lanes)
        sg = sigmoid(pre)
        act[:, lanes] = pre * sg
        slope[:, lanes] = sg * (1.0 + pre * (1.0 - sg))

    raw = dt_ref[...].astype(f32) + head_ref[0:1, :]
    step = softplus(raw)
    rate = head_ref[1:2, :]
    row = lax.broadcasted_iota(jnp.int32, (Q, Q), 0)
    col = lax.broadcasted_iota(jnp.int32, (Q, Q), 1)
    tri = jnp.where(row >= col, 1.0, 0.0).astype(bf16)
    upper = jnp.where(row <= col, 1.0, 0.0).astype(bf16)
    below = jnp.where(row > col, 1.0, 0.0).astype(bf16)
    decay = dot3(tri, step * rate)
    decay_t = decay.T
    madd = jnp.where((row <= col) & (segc_ref[...] == segr_ref[0]), 0.0, NEG)
    b_now, c_now = act[:, xw : xw + 128], act[:, xw + 128 : xw + 256]
    b_low, c_low = b_now.astype(bf16), c_now.astype(bf16)
    c_t = c_now.T.astype(bf16)
    gram = dot_nt(b_low, c_low)
    left = lax.broadcasted_iota(jnp.int32, (Q, 128), 1) < 64
    lane = lax.broadcasted_iota(jnp.int32, (Q, 128), 1)
    dgram = jnp.zeros((Q, Q), f32)
    cols_b = jnp.zeros((Q, 128), f32)
    for p in range(pairs):
        lanes = slice(128 * p, 128 * p + 128)
        d0, d1 = spread_col(decay, 2 * p), spread_col(decay, 2 * p + 1)
        dp = jnp.where(left, d0, d1)
        sp = jnp.where(left, spread_col(step, 2 * p), spread_col(step, 2 * p + 1))
        xs = act[:, lanes]
        xp = xs * sp
        dy_low = dy_ref[:, lanes]
        dy = dy_low.astype(f32)
        stacked = jnp.concatenate(
            [jnp.where(left, dy, 0.0).astype(bf16), jnp.where(left, 0.0, dy).astype(bf16)], axis=0
        )
        pair = dot_nt(xp.astype(bf16), stacked)
        mts = []
        for k, dk in ((0, d0), (1, d1)):
            h = 2 * p + k
            e = jnp.exp(decay_t[h : h + 1, :] - dk + madd)
            f = e * pair[:, 128 * k : 128 * k + 128]
            dgram = dgram + f
            w = gram * f
            mts.append((gram * e).astype(bf16))
            rows_a[h : h + 1, :] = jnp.sum(w, axis=0, keepdims=True)
            cols_b = jnp.where(lane == h, jnp.sum(w, axis=1, keepdims=True), cols_b)
        within = dot(jnp.concatenate(mts, axis=1), stacked)
        grow = jnp.exp(dp) * carried
        dy_in = dy * grow
        dy_in_low = dy_in.astype(bf16)
        keep_y[:, lanes] = dy_in_low
        st = save_ref[0, :, lanes]
        prod_a[:, lanes] = (dy_in * dot(c_low, st)).astype(bf16)
        last = dp[Q - 1 : Q, :]
        fade = jnp.exp(last - dp) * samelast
        ds = dstate[:, lanes]
        ds_low = ds.astype(bf16)
        xe = xp * fade
        keep_x[:, lanes] = xe.astype(bf16)
        later = dot(b_low, ds_low)
        prod_b[:, lanes] = (xe * later).astype(bf16)
        retain = jnp.exp(last) * carried[Q - 1 : Q, :]
        held[0:1, lanes] = jnp.sum(ds * st.astype(f32), axis=0, keepdims=True) * retain
        dxs = sp * (within + later * fade) + skip_ref[:, lanes] * dy
        skp = xs * dy
        sgrad_ref[:, lanes] += jnp.sum(skp.reshape(Q // 8, 8, 128), axis=0)
        dpre[0:Q, lanes] = dxs * slope[:, lanes]
        dstate[:, lanes] = ds * retain + dot(c_t, dy_in_low)
        if p == 0:
            db_in, dc_in = dot_nt(keep_x[:, lanes], ds_low), dot_nt(dy_in_low, st)
        else:
            db_in, dc_in = db_in + dot_nt(keep_x[:, lanes], ds_low), dc_in + dot_nt(dy_in_low, st)

    dg_low = dgram.astype(bf16)
    db = dot(dg_low, c_low) + db_in
    dc = dot(dgram.T.astype(bf16), b_low) + dc_in
    dpre[0:Q, xw : xw + 128] = db * slope[:, xw : xw + 128]
    dpre[0:Q, xw + 128 : xw + 256] = dc * slope[:, xw + 128 : xw + 256]

    spot = spot_ref[...]
    a_in = dot(prod_a[...], spot)
    b_in = dot(prod_b[...], spot)
    hv = jnp.broadcast_to(held[0:1, :], (8, xw))
    h_hi = hv.astype(bf16)
    h_lo = (hv - h_hi.astype(f32)).astype(bf16)
    through = (dot(h_hi, spot) + dot(h_lo, spot))[0:1, :]
    a_own = rows_a[...].T
    cross = dot3(upper, a_own - cols_b + a_in) + dot3(below, b_in) + through
    total = cols_b + b_in
    sg = sigmoid(raw)
    ratio = jnp.where(step > 1e-30, sg / jnp.maximum(step, 1e-30), 1.0)
    draw = total * ratio + rate * cross * sg
    ddt_ref[...] = draw.astype(bf16)
    hgrad_ref[0:8, :] += jnp.sum(draw.reshape(Q // 8, 8, 128), axis=0)
    hgrad_ref[8:16, :] += jnp.sum((step * cross).reshape(Q // 8, 8, 128), axis=0)

    for p in range(width // 128):
        lanes = slice(128 * p, 128 * p + 128)
        own = dpre[0:Q, lanes]
        du = wk_ref[3:4, lanes] * own
        wgrad_ref[24:32, lanes] += jnp.sum((own * useen[8 : 8 + Q, lanes]).reshape(Q // 8, 8, 128), axis=0)
        wgrad_ref[32:40, lanes] += jnp.sum(own.reshape(Q // 8, 8, 128), axis=0)
        for j in (1, 2, 3):
            du = du + wk_ref[3 - j : 4 - j, lanes] * (dpre[j : j + Q, lanes] * spread_col(tok, 4 + j))
            moved = own * (useen[8 - j : 8 - j + Q, lanes] * flags[j])
            k = 3 - j
            wgrad_ref[8 * k : 8 * k + 8, lanes] += jnp.sum(moved.reshape(Q // 8, 8, 128), axis=0)
        du_ref[:, lanes] = du.astype(bf16)
    first = dpre[0:8, :]
    dpre[Q : Q + 8, :] = first


def mixer_bwd(traffic, extra, u, dt, tok, segc, segr, wk, bias, head, skip, save, dy, spot):
    length, width = u.shape
    xw = width - 256
    n = length // Q
    whole = lambda shape: pl.BlockSpec(shape, lambda i: (0,) * len(shape))
    back = lambda i: (n - 1 - i, 0)
    return pl.pallas_call(
        functools.partial(bwd_kernel, traffic),
        grid=(n,),
        in_specs=[
            pl.BlockSpec((Q, width), back),
            pl.BlockSpec((16, width), lambda i: (jnp.maximum((n - 1 - i) * (Q // 16) - 1, 0), 0)),
            pl.BlockSpec((Q, 128), back),
            pl.BlockSpec((Q, 8), back),
            pl.BlockSpec((Q, 1), back),
            pl.BlockSpec((1, 1, Q), lambda i: (n - 1 - i, 0, 0)),
            whole((4, width)),
            whole((1, width)),
            whole((2, 128)),
            whole((1, xw)),
            pl.BlockSpec((1, 128, xw), lambda i: (n - 1 - i, 0, 0)),
            pl.BlockSpec((Q, xw), back),
            whole((xw, 128)),
        ]
        + [pl.BlockSpec(memory_space=pl.ANY)] * len(extra),
        out_specs=[
            pl.BlockSpec((Q, width), back),
            pl.BlockSpec((Q, 128), back),
            whole((40, width)),
            whole((16, 128)),
            whole((8, xw)),
        ]
        + [pl.BlockSpec(memory_space=pl.ANY)] * len(traffic.outputs),
        out_shape=[
            jax.ShapeDtypeStruct((length, width), bf16),
            jax.ShapeDtypeStruct((length, 128), bf16),
            jax.ShapeDtypeStruct((40, width), f32),
            jax.ShapeDtypeStruct((16, 128), f32),
            jax.ShapeDtypeStruct((8, xw), f32),
            *traffic.outputs,
        ],
        scratch_shapes=[
            pltpu.VMEM((128, xw), f32),
            pltpu.VMEM((Q + 8, width), f32),
            pltpu.VMEM((Q, width), f32),
            pltpu.VMEM((Q, width), f32),
            pltpu.VMEM((Q + 8, width), f32),
            pltpu.VMEM((Q, xw), bf16),
            pltpu.VMEM((Q, xw), bf16),
            pltpu.VMEM((Q, xw), bf16),
            pltpu.VMEM((Q, xw), bf16),
            pltpu.VMEM((128, 128), f32),
            pltpu.VMEM((8, xw), f32),
            *traffic.scratch,
        ],
        compiler_params=pltpu.CompilerParams(
            vmem_limit_bytes=48 * 2**20,
            collective_id=traffic.collective_id,
            has_side_effects=traffic.collective_id is not None,
        ),
        name="mixer_backward",
    )(u, u, dt, tok, segc, segr, wk, bias, head, skip, save, dy, spot, *extra)


def token_facts(seg):
    length = seg.shape[0]
    facts = []
    for j in (1, 2, 3):
        before = jnp.concatenate([jnp.full((j,), -1, jnp.int32), seg[:-j]])
        facts.append(before == seg)
    by = seg.reshape(length // Q, Q)
    ends = by[:, Q - 1]
    prior = jnp.concatenate([jnp.full((1,), -1, jnp.int32), ends[:-1]])
    facts.append((by == prior[:, None]).reshape(length))
    facts.append((by == ends[:, None]).reshape(length))
    for j in (1, 2, 3):
        after = jnp.concatenate([seg[j:], jnp.full((j,), -1, jnp.int32)])
        facts.append(after == seg)
    return jnp.stack(facts, axis=1).astype(f32)


MESH = pl.DeviceIdType.MESH
ANY = pl.ANY
PARTS = 4


def remote(src, dst, send_sem, recv_sem, device):
    return pltpu.make_async_remote_copy(
        src_ref=src, dst_ref=dst, send_sem=send_sem, recv_sem=recv_sem, device_id=device, device_id_type=MESH
    )


class Place:
    def __init__(self):
        self.w, self.s = lax.axis_index("wshard"), lax.axis_index("seq")
        self.z, self.x = self.w // 2, lax.rem(self.w, 2)
        self.y, self.c = self.s // 2, lax.rem(self.s, 2)
        self.s_sib = 2 * self.y + 1 - self.c
        self.s_far = 2 * (1 - self.y) + self.c
        self.s_diag = 2 * (1 - self.y) + 1 - self.c
        self.side = (2 * self.z + 1 - self.x, self.s)
        self.up = (lax.rem(self.w + 2, 8), self.s)
        self.down = (lax.rem(self.w + 6, 8), self.s)
        self.sib = (self.w, self.s_sib)
        self.far = (self.w, self.s_far)

    def greet(self, everyone=False):
        barrier = pltpu.get_barrier_semaphore()
        others = [(lax.rem(self.w + k, 8), self.s) for k in range(1, 8)] if everyone else []
        if everyone:
            others += [(self.w, lax.rem(self.s + k, 4)) for k in range(1, 4)]
        else:
            others = [self.side, self.up, self.down, self.sib, self.far]
        for other in others:
            pl.semaphore_signal(barrier, inc=1, device_id=other, device_id_type=MESH)
        pl.semaphore_wait(barrier, len(others))


def dma(*shape):
    return pltpu.SemaphoreType.DMA(shape)


def gather_pieces_start(at, own, full, sems):
    send, recv, local = sems
    rows = own.shape[0] // PARTS
    pltpu.make_async_copy(own, full.at[at.s], local).start()
    for k in range(PARTS):
        part = pl.ds(k * rows, rows)
        remote(own.at[part], full.at[at.s, part], send.at[1, k], recv.at[1, k], at.far).start()
    for k in range(PARTS):
        part = pl.ds(k * rows, rows)
        remote(own.at[part], full.at[at.s, part], send.at[0, k], recv.at[0, k], at.sib).start()


def gather_pieces_pass(at, own, full, sems):
    send, recv, _ = sems
    rows = own.shape[0] // PARTS
    for k in range(PARTS):
        part = pl.ds(k * rows, rows)
        theirs = full.at[at.s_far, part]
        remote(theirs, theirs, send.at[1, k], recv.at[1, k], at.far).wait_recv()
        remote(theirs, theirs, send.at[2, k], recv.at[2, k], at.sib).start()


def gather_pieces_end(at, own, full, sems):
    send, recv, local = sems
    rows = own.shape[0] // PARTS
    pltpu.make_async_copy(own, full.at[at.s], local).wait()
    for k in range(PARTS):
        part = pl.ds(k * rows, rows)
        sib, diag, far = full.at[at.s_sib, part], full.at[at.s_diag, part], full.at[at.s_far, part]
        remote(own.at[part], full.at[at.s, part], send.at[0, k], recv.at[0, k], at.sib).wait_send()
        remote(own.at[part], full.at[at.s, part], send.at[1, k], recv.at[1, k], at.far).wait_send()
        remote(far, far, send.at[2, k], recv.at[2, k], at.sib).wait_send()
        remote(sib, sib, send.at[0, k], recv.at[0, k], at.sib).wait_recv()
        remote(diag, diag, send.at[2, k], recv.at[2, k], at.sib).wait_recv()


def gather_shards(at, main, com, main_all, com_all, sems, between):
    send, recv, csend, crecv, psend, precv, local = sems
    half = com.shape[0] // 2
    mine = pl.ds(pl.multiple_of(at.c * half, half), half)
    pltpu.make_async_copy(main, main_all.at[at.w], local.at[0]).start()
    pltpu.make_async_copy(com, com_all.at[at.w], local.at[1]).start()

    def hop(zp, way, device):
        w = 2 * zp + at.x
        return (
            remote(main_all.at[w], main_all.at[w], send.at[way, zp], recv.at[w], device),
            remote(com_all.at[w, mine], com_all.at[w, mine], csend.at[way, zp], crecv.at[w], device),
        )

    def first(way, device):
        return (
            remote(main, main_all.at[at.w], send.at[way, at.z], recv.at[at.w], device),
            remote(com.at[mine], com_all.at[at.w, mine], csend.at[way, at.z], crecv.at[at.w], device),
        )

    def begin(copies):
        for copy in copies:
            copy.start()

    begin(first(0, at.side))

    @pl.when(at.z < 3)
    def _():
        begin(first(1, at.up))

    @pl.when(at.z > 0)
    def _():
        begin(first(2, at.down))

    def arrived(w):
        remote(main_all.at[w], main_all.at[w], send.at[0, 0], recv.at[w], at.side).wait_recv()
        held = com_all.at[w, mine]
        remote(held, held, csend.at[0, 0], crecv.at[w], at.side).wait_recv()
        remote(held, held, psend.at[w], precv.at[w], at.sib).start()

    for d in (1, 2, 3):
        if d == 3:
            between()

        @pl.when(at.z - d >= 0)
        def _():
            zp = at.z - d
            arrived(2 * zp + at.x)

            @pl.when(at.z < 3)
            def _():
                begin(hop(zp, 1, at.up))

            begin(hop(zp, 0, at.side))

        @pl.when(at.z + d <= 3)
        def _():
            zp = at.z + d
            arrived(2 * zp + at.x)

            @pl.when(at.z > 0)
            def _():
                begin(hop(zp, 2, at.down))

            begin(hop(zp, 0, at.side))

    for zp in range(4):
        arrived(2 * zp + 1 - at.x)
    pltpu.make_async_copy(main, main_all.at[at.w], local.at[0]).wait()
    pltpu.make_async_copy(com, com_all.at[at.w], local.at[1]).wait()
    other = pl.ds(pl.multiple_of((1 - at.c) * half, half), half)
    for zp in range(4):
        for copy in hop(zp, 0, at.side):
            copy.wait_send()

        @pl.when((at.z < 3) & (zp <= at.z))
        def _():
            for copy in hop(zp, 1, at.up):
                copy.wait_send()

        @pl.when((at.z > 0) & (zp >= at.z))
        def _():
            for copy in hop(zp, 2, at.down):
                copy.wait_send()

    for k in range(1, 8):
        w = lax.rem(at.w + k, 8)
        sent, got = com_all.at[w, mine], com_all.at[w, other]
        remote(sent, sent, psend.at[w], precv.at[w], at.sib).wait_send()
        remote(got, got, psend.at[w], precv.at[w], at.sib).wait_recv()


def gather_kernel(hid, main, com, hid_all, main_all, com_all, *sems):
    at = Place()
    at.greet()
    gather_pieces_start(at, hid, hid_all, sems[0:3])
    pass_on = lambda: gather_pieces_pass(at, hid, hid_all, sems[0:3])
    gather_shards(at, main, com, main_all, com_all, sems[3:10], pass_on)
    gather_pieces_end(at, hid, hid_all, sems[0:3])


def gather_first(hid, main, com):
    shape = lambda n, v: jax.ShapeDtypeStruct((n,) + v.shape, v.dtype)
    return pl.pallas_call(
        gather_kernel,
        in_specs=[pl.BlockSpec(memory_space=ANY)] * 3,
        out_specs=[pl.BlockSpec(memory_space=ANY)] * 3,
        out_shape=[shape(4, hid), shape(8, main), shape(8, com)],
        scratch_shapes=[dma(3, PARTS), dma(3, PARTS), dma()]
        + [dma(3, 4), dma(8), dma(3, 4), dma(8), dma(8), dma(8), dma(2)],
        compiler_params=pltpu.CompilerParams(collective_id=1, has_side_effects=True),
        name="gather_first",
    )(hid, main, com)


SLICES = 8


def each_slice(body):
    def run(k, _):
        body(k)
        return 0

    lax.fori_loop(0, SLICES, run, 0)


def forward_traffic(cot, rows):
    class Traffic:
        inputs = (cot, rows)
        outputs = (
            jax.ShapeDtypeStruct((4,) + cot.shape, cot.dtype),
            jax.ShapeDtypeStruct((2,) + rows.shape, rows.dtype),
        )
        scratch = (dma(3, SLICES), dma(3, SLICES), dma(), dma(3, SLICES), dma(2, SLICES), dma())
        collective_id = 2

        def __init__(self, own, row_own, full, row_full, send, recv, local, rsend, rrecv, rlocal):
            self.at = at = Place()
            self.own, self.full, self.row_own, self.row_full = own, full, row_own, row_full
            self.rrecv = rrecv
            cut, rcut = own.shape[0] // SLICES, row_own.shape[0] // SLICES
            part = lambda k: pl.ds(pl.multiple_of(k * cut, cut), cut)
            rpart = lambda k: pl.ds(pl.multiple_of(k * rcut, rcut), rcut)
            piece = lambda s, k: full.at[s, part(k)]
            self.keep = pltpu.make_async_copy(own, full.at[at.s], local)
            self.rkeep = pltpu.make_async_copy(row_own, row_full.at[at.x], rlocal)
            self.to_sib = lambda k: remote(own.at[part(k)], piece(at.s, k), send.at[0, k], recv.at[0, k], at.sib)
            self.to_far = lambda k: remote(own.at[part(k)], piece(at.s, k), send.at[1, k], recv.at[1, k], at.far)
            self.pass_on = lambda k: remote(piece(at.s_far, k), piece(at.s_far, k), send.at[2, k], recv.at[2, k], at.sib)
            here = lambda k, n, device: remote(
                row_full.at[at.x, rpart(k)], row_full.at[at.x, rpart(k)], rsend.at[n, k], rrecv.at[at.x, k], device
            )
            self.rows = (lambda k: here(k, 0, at.side), lambda k: here(k, 1, at.up), lambda k: here(k, 2, at.down))
            got = lambda s, n, k: remote(piece(s, k), piece(s, k), send.at[n, k], recv.at[n, k], at.sib)
            self.from_sib = lambda k: got(at.s_sib, 0, k)
            self.from_far = lambda k: got(at.s_far, 1, k)
            self.from_diag = lambda k: got(at.s_diag, 2, k)
            other = lambda k: row_full.at[1 - at.x, rpart(k)]
            self.from_side = lambda k: remote(other(k), other(k), rsend.at[0, k], rrecv.at[1 - at.x, k], at.side)

        def step(self, i, last):
            at = self.at
            upward, downward = (at.z >= at.s) & (at.z < 3), (at.z <= at.s) & (at.z > 0)
            side, up, down = self.rows

            @pl.when(i == 0)
            def _():
                at.greet()
                self.keep.start()
                each_slice(lambda k: self.to_sib(k).start())

                @pl.when(at.z == at.s)
                def _():
                    self.rkeep.start()
                    self.rkeep.wait()

            k = i - 1

            @pl.when((k >= 0) & (k < SLICES))
            def _():
                self.to_far(k).start()

            @pl.when((k >= SLICES) & (k < 2 * SLICES))
            def _():
                self.from_far(k - SLICES).wait_recv()
                self.pass_on(k - SLICES).start()

            far_away = jnp.where(at.z > at.s, at.z - at.s, at.s - at.z)
            r = i - 1 - 2 * far_away

            @pl.when((r >= 0) & (r < SLICES))
            def _():
                @pl.when(at.z != at.s)
                def _():
                    side(r).wait_recv()

                side(r).start()

                @pl.when(upward)
                def _():
                    up(r).start()

                @pl.when(downward)
                def _():
                    down(r).start()

            @pl.when(i == last)
            def _():
                self.keep.wait()

                def finish(k):
                    self.to_sib(k).wait_send()
                    self.to_far(k).wait_send()
                    self.pass_on(k).wait_send()
                    self.from_sib(k).wait_recv()
                    self.from_diag(k).wait_recv()
                    side(k).wait_send()
                    self.from_side(k).wait_recv()

                    @pl.when(upward)
                    def _():
                        up(k).wait_send()

                    @pl.when(downward)
                    def _():
                        down(k).wait_send()

                each_slice(finish)

    return Traffic


def add_into(dst, src, rows):
    def body(i, _):
        part = pl.ds(pl.multiple_of(i * 16, 16), 16)
        dst[part, :] = (dst[part, :].astype(f32) + src[part, :].astype(f32)).astype(bf16)
        return 0

    lax.fori_loop(0, rows // 16, body, 0)


def backward_traffic(layer, rows):
    piece, cols = layer.shape[1:]
    rrows = rows.shape[1]

    class Traffic:
        inputs = (layer, rows)
        outputs = (jax.ShapeDtypeStruct((piece, cols), f32), jax.ShapeDtypeStruct((rrows, cols), bf16))
        scratch = (
            *[pltpu.VMEM((piece, cols), bf16)] * 5,
            pltpu.VMEM((piece, cols), f32),
            *[pltpu.VMEM((rrows, cols), bf16)] * 4,
            dma(3, SLICES),
            dma(3, SLICES),
            dma(3),
            dma(3, SLICES),
            dma(3, SLICES),
            dma(2),
        )
        collective_id = 3

        def __init__(
            self, layer, rows, out, rows_out,
            own_v, far_v, sib_v, pass_v, got_v, sum_v, acc, side_v, low_v, high_v,
            send, recv, local, rsend, rrecv, rlocal,
        ):
            self.at = at = Place()
            cut, rcut = piece // SLICES, rrows // SLICES
            part = lambda k: pl.ds(pl.multiple_of(k * cut, cut), cut)
            rpart = lambda k: pl.ds(pl.multiple_of(k * rcut, rcut), rcut)
            self.own, self.sib, self.passed, self.got, self.sum = own_v, sib_v, pass_v, got_v, sum_v
            self.part, self.rpart, self.cut, self.rcut = part, rpart, cut, rcut
            self.far_v, self.acc, self.side_v, self.low_v, self.high_v = far_v, acc, side_v, low_v, high_v
            self.load_far = pltpu.make_async_copy(layer.at[at.s_far], far_v, local.at[0])
            self.load_own = pltpu.make_async_copy(layer.at[at.s], own_v, local.at[1])
            self.store = pltpu.make_async_copy(sum_v, out, local.at[2])
            self.to_pass = lambda k: remote(
                layer.at[at.s_diag, part(k)], pass_v.at[part(k)], send.at[0, k], recv.at[0, k], at.sib
            )
            self.to_sib = lambda k: remote(
                layer.at[at.s_sib, part(k)], sib_v.at[part(k)], send.at[1, k], recv.at[1, k], at.sib
            )
            self.to_far = lambda k: remote(
                far_v.at[part(k)], got_v.at[part(k)], send.at[2, k], recv.at[2, k], at.far
            )
            self.load_acc = pltpu.make_async_copy(rows.at[at.x], acc, rlocal.at[0])
            self.store_acc = pltpu.make_async_copy(acc, rows_out, rlocal.at[1])
            self.to_side = lambda k: remote(
                rows.at[1 - at.x, rpart(k)], side_v.at[rpart(k)], rsend.at[0, k], rrecv.at[0, k], at.side
            )
            self.to_up = lambda k: remote(
                acc.at[rpart(k)], low_v.at[rpart(k)], rsend.at[1, k], rrecv.at[1, k], at.up
            )
            self.to_down = lambda k: remote(
                acc.at[rpart(k)], high_v.at[rpart(k)], rsend.at[2, k], rrecv.at[2, k], at.down
            )

        def step(self, i, last):
            at = self.at

            @pl.when(i == 0)
            def _():
                at.greet()
                self.load_far.start()
                self.load_own.start()
                self.load_acc.start()
                each_slice(lambda k: self.to_pass(k).start())
                each_slice(lambda k: self.to_sib(k).start())

            @pl.when(i < SLICES)
            def _():
                self.to_side(i).start()

            @pl.when(i == 1)
            def _():
                self.load_far.wait()
                self.load_own.wait()
                self.load_acc.wait()

            k = i - 1

            @pl.when((k >= 0) & (k < SLICES))
            def _():
                self.to_pass(k).wait_recv()
                add_into(self.far_v.at[self.part(k)], self.passed.at[self.part(k)], self.cut)
                self.to_far(k).start()

            m = i - SLICES

            @pl.when((m >= 0) & (m < SLICES))
            def _():
                self.to_sib(m).wait_recv()
                self.to_far(m).wait_recv()
                p = self.part(m)
                self.sum[p, :] = (
                    self.own[p, :].astype(f32) + self.sib[p, :].astype(f32) + self.got[p, :].astype(f32)
                )

            ends = jnp.where(at.z > 3 - at.z, at.z, 3 - at.z)
            chain = jnp.where(at.z < at.s, at.z, jnp.where(at.z > at.s, 3 - at.z, ends))
            r = i - 2 - 2 * chain

            @pl.when((r >= 0) & (r < SLICES))
            def _():
                acc = self.acc.at[self.rpart(r)]
                self.to_side(r).wait_recv()
                add_into(acc, self.side_v.at[self.rpart(r)], self.rcut)

                @pl.when((at.z <= at.s) & (at.z > 0))
                def _():
                    self.to_up(r).wait_recv()
                    add_into(acc, self.low_v.at[self.rpart(r)], self.rcut)

                @pl.when((at.z >= at.s) & (at.z < 3))
                def _():
                    self.to_down(r).wait_recv()
                    add_into(acc, self.high_v.at[self.rpart(r)], self.rcut)

                @pl.when(at.z < at.s)
                def _():
                    self.to_up(r).start()

                @pl.when(at.z > at.s)
                def _():
                    self.to_down(r).start()

            @pl.when(i == last)
            def _():
                self.store.start()
                self.store_acc.start()

                def finish(k):
                    self.to_pass(k).wait_send()
                    self.to_sib(k).wait_send()
                    self.to_far(k).wait_send()
                    self.to_side(k).wait_send()

                    @pl.when(at.z < at.s)
                    def _():
                        self.to_up(k).wait_send()

                    @pl.when(at.z > at.s)
                    def _():
                        self.to_down(k).wait_send()

                each_slice(finish)
                self.store.wait()
                self.store_acc.wait()

    return Traffic


def reduce_pieces_start(at, partial, bufs, sems):
    own_v, far_v, from_sib, pass_sib, from_far = bufs
    send, recv, local = sems
    rows = partial.shape[1] // PARTS
    pltpu.make_async_copy(partial.at[at.s_far], far_v, local.at[0]).start()
    pltpu.make_async_copy(partial.at[at.s], own_v, local.at[1]).start()
    for k in range(PARTS):
        part = pl.ds(k * rows, rows)
        remote(partial.at[at.s_diag, part], pass_sib.at[part], send.at[0, k], recv.at[0, k], at.sib).start()
    for k in range(PARTS):
        part = pl.ds(k * rows, rows)
        remote(partial.at[at.s_sib, part], from_sib.at[part], send.at[1, k], recv.at[1, k], at.sib).start()


def reduce_pieces_pass(at, partial, bufs, sems):
    own_v, far_v, from_sib, pass_sib, from_far = bufs
    send, recv, local = sems
    rows = partial.shape[1] // PARTS
    pltpu.make_async_copy(partial.at[at.s_far], far_v, local.at[0]).wait()
    for k in range(PARTS):
        part = pl.ds(k * rows, rows)
        got = pass_sib.at[part]
        remote(got, got, send.at[0, k], recv.at[0, k], at.sib).wait_recv()
        add_into(far_v.at[part], got, rows)
        remote(far_v.at[part], from_far.at[part], send.at[2, k], recv.at[2, k], at.far).start()


def reduce_pieces_end(at, partial, bufs, sems, out):
    own_v, far_v, from_sib, pass_sib, from_far = bufs
    send, recv, local = sems
    rows = partial.shape[1] // PARTS
    pltpu.make_async_copy(partial.at[at.s], own_v, local.at[1]).wait()
    for k in range(PARTS):
        part = pl.ds(k * rows, rows)
        sib, far = from_sib.at[part], from_far.at[part]
        remote(sib, sib, send.at[1, k], recv.at[1, k], at.sib).wait_recv()
        remote(far, far, send.at[2, k], recv.at[2, k], at.far).wait_recv()

        def body(i, _):
            r = pl.ds(pl.multiple_of(k * rows + i * 16, 16), 16)
            out[r, :] = own_v[r, :].astype(f32) + from_sib[r, :].astype(f32) + from_far[r, :].astype(f32)
            return 0

        lax.fori_loop(0, rows // 16, body, 0)
        remote(partial.at[at.s_diag, part], pass_sib.at[part], send.at[0, k], recv.at[0, k], at.sib).wait_send()
        remote(partial.at[at.s_sib, part], from_sib.at[part], send.at[1, k], recv.at[1, k], at.sib).wait_send()
        remote(far_v.at[part], from_far.at[part], send.at[2, k], recv.at[2, k], at.far).wait_send()


def far_first(at, i):
    inner = (at.z == 1) | (at.z == 2)
    if i >= 2:
        i = jnp.where(inner, 5 - i, i)
    return jnp.where(at.z < 2, 3 - i, i)


class ReduceShards:
    def __init__(self, at, partial, cuts, acc, from_side, from_down, from_up, sems):
        self.at, self.partial, self.cuts, self.acc = at, partial, cuts, acc
        self.from_side, self.from_down, self.from_up = from_side, from_down, from_up
        self.send, self.recv_side, self.recv_down, self.recv_up = sems
        self.rows = acc.shape[1] // cuts

    def unit(self, j):
        zp, cut = far_first(self.at, j // self.cuts), j % self.cuts
        return zp, zp * self.cuts + cut, pl.ds(cut * self.rows, self.rows)

    def side_copy(self, j):
        at = self.at
        zp, n, part = self.unit(j)
        return remote(
            self.partial.at[2 * zp + 1 - at.x, part], self.from_side.at[zp, part],
            self.send.at[0, n], self.recv_side.at[n], at.side,
        )

    def up_copy(self, j):
        zp, n, part = self.unit(j)
        return remote(
            self.acc.at[zp, part], self.from_down.at[zp, part], self.send.at[1, n], self.recv_down.at[n], self.at.up
        )

    def down_copy(self, j):
        zp, n, part = self.unit(j)
        return remote(
            self.acc.at[zp, part], self.from_up.at[zp, part], self.send.at[2, n], self.recv_up.at[n], self.at.down
        )

    def start(self):
        self.side_copy(0).start()
        self.side_copy(1).start()

    def step(self, j):
        at = self.at
        zp, _, part = self.unit(j)
        self.side_copy(j).wait()
        if j + 2 < 4 * self.cuts:
            self.side_copy(j + 2).start()
        acc = self.acc.at[zp, part]
        add_into(acc, self.from_side.at[zp, part], self.rows)

        @pl.when((at.z > 0) & (zp >= at.z))
        def _():
            self.up_copy(j).wait_recv()
            add_into(acc, self.from_down.at[zp, part], self.rows)

        @pl.when((at.z < 3) & (zp <= at.z))
        def _():
            self.down_copy(j).wait_recv()
            add_into(acc, self.from_up.at[zp, part], self.rows)

        @pl.when(zp > at.z)
        def _():
            self.up_copy(j).start()

        @pl.when(zp < at.z)
        def _():
            self.down_copy(j).start()

    def end(self):
        at = self.at
        for j in range(4 * self.cuts):
            zp = self.unit(j)[0]

            @pl.when(zp > at.z)
            def _():
                self.up_copy(j).wait_send()

            @pl.when(zp < at.z)
            def _():
                self.down_copy(j).wait_send()


def spread_start(at, rows, out, sems):
    send, recv, local = sems

    @pl.when(at.s == at.z)
    def _():
        copy = pltpu.make_async_copy(rows, out, local)
        copy.start()
        remote(rows, out, send.at[1], recv, at.far).start()
        remote(rows, out, send.at[0], recv, at.sib).start()
        copy.wait()


def spread_pass(at, rows, out, sems):
    send, recv, local = sems

    @pl.when(at.s_far == at.z)
    def _():
        remote(out, out, send.at[1], recv, at.far).wait_recv()
        remote(out, out, send.at[0], recv, at.sib).start()


def spread_end(at, rows, out, sems):
    send, recv, local = sems

    @pl.when(at.s == at.z)
    def _():
        remote(rows, out, send.at[1], recv, at.far).wait_send()
        remote(rows, out, send.at[0], recv, at.sib).wait_send()

    @pl.when(at.s_far == at.z)
    def _():
        remote(out, out, send.at[0], recv, at.sib).wait_send()

    @pl.when((at.s_sib == at.z) | (at.s_diag == at.z))
    def _():
        remote(out, out, send.at[0], recv, at.sib).wait_recv()


def small_start(at, small, got, sems):
    send, recv = sems
    for k in range(1, 8):
        peer = (lax.rem(at.w + k, 8), at.s)
        remote(small, got.at[k], send.at[k], recv.at[k], peer).start()


def small_pass(at, small, got, total, full, sems, more):
    send, recv = sems
    send2, recv2, local = more
    value = small[...]
    for k in range(1, 8):
        remote(small, got.at[k], send.at[k], recv.at[k], at.side).wait_recv()
        value = value + got[k]
    total[...] = value
    pltpu.make_async_copy(total, full.at[at.s], local).start()
    for k, s in enumerate((at.s_sib, at.s_far, at.s_diag)):
        remote(total, full.at[at.s], send2.at[k], recv2.at[k], (at.w, s)).start()


def small_end(at, small, got, total, full, sems, more):
    send, recv = sems
    send2, recv2, local = more
    pltpu.make_async_copy(total, full.at[at.s], local).wait()
    for k in range(1, 8):
        remote(small, got.at[k], send.at[k], recv.at[k], at.side).wait_send()
    for k, s in enumerate((at.s_sib, at.s_far, at.s_diag)):
        remote(total, full.at[at.s], send2.at[k], recv2.at[k], (at.w, s)).wait_send()
        remote(total, full.at[s], send2.at[k], recv2.at[k], (at.w, s)).wait_recv()


def reduce_kernel(back, main, com, rows, small,
                  back_sum, main_out, com_out, rows_out, small_out,
                  b0, b1, b2, b3, b4,
                  macc, mside, mlow, mhigh, mown, cown, csib, cacc, cside, clow, chigh, cfar, csum,
                  sgot, stotal, *sems):
    at = Place()
    sems = list(sems)
    take = lambda n: [sems.pop(0) for _ in range(n)]
    bsem, msem, csem, cx, rsem, ssem, smore, asem, mlocal = (
        take(3), take(4), take(4), take(5), take(3), take(2), take(3), take(3), take(1)[0]
    )
    bbuf = (b0, b1, b2, b3, b4)
    half = com.shape[1] // 2
    mine = pl.ds(pl.multiple_of(at.c * half, half), half)
    other = pl.ds(pl.multiple_of((1 - at.c) * half, half), half)
    big = ReduceShards(at, main, 2, macc, mside, mlow, mhigh, msem)
    few = ReduceShards(at, cown, 1, cacc, cside, clow, chigh, csem)
    at.greet(everyone=True)

    csib_copy = remote(com.at[:, other], csib, cx[0], cx[1], at.sib)
    csib_copy.start()
    own_copy = pltpu.make_async_copy(com.at[:, mine], cown, mlocal.at[4])
    own_copy.start()
    big.start()
    reduce_pieces_start(at, back, bbuf, bsem)
    for zp in range(4):
        pltpu.make_async_copy(main.at[2 * zp + at.x], macc.at[zp], mlocal.at[zp]).start()
    small_start(at, small, sgot, ssem)
    own_copy.wait()
    csib_copy.wait_recv()
    for w in range(8):
        add_into(cown.at[w], csib.at[w], half)
    few.start()
    for zp in range(4):
        cacc[zp] = cown[2 * zp + at.x]
    reduce_pieces_pass(at, back, bbuf, bsem)
    spread_start(at, rows, rows_out, rsem)
    for zp in range(4):
        pltpu.make_async_copy(main.at[2 * zp + at.x], macc.at[zp], mlocal.at[zp]).wait()
    for j in range(8):
        big.step(j)
        if j % 2 == 0:
            few.step(j // 2)
        if j == 2:
            small_pass(at, small, sgot, stotal, small_out, ssem, smore)
    mown[...] = macc[at.z]
    gather_pieces_start(at, mown, main_out, asem)
    csum[...] = cacc[at.z].astype(f32)
    far_copy = remote(csum, cfar, cx[2].at[0], cx[3].at[0], at.far)
    far_copy.start()
    reduce_pieces_end(at, back, bbuf, bsem, back_sum)
    spread_pass(at, rows, rows_out, rsem)
    far_copy.wait()
    csum[...] = csum[...] + cfar[...]
    com_copy = remote(csum, com_out.at[mine], cx[2].at[1], cx[3].at[1], at.sib)
    com_copy.start()
    keep_copy = pltpu.make_async_copy(csum, com_out.at[mine], cx[4])
    keep_copy.start()
    gather_pieces_pass(at, mown, main_out, asem)
    big.end()
    few.end()
    csib_copy.wait_send()
    gather_pieces_end(at, mown, main_out, asem)
    keep_copy.wait()
    com_copy.wait_send()
    got = com_out.at[other]
    remote(csum, got, cx[2].at[1], cx[3].at[1], at.sib).wait_recv()
    small_end(at, small, sgot, stotal, small_out, ssem, smore)
    spread_end(at, rows, rows_out, rsem)


def reduce_last(back, main, com, rows, small):
    piece, cols = back.shape[1:]
    mrows, mcols = main.shape[1:]
    half, ccols = com.shape[1] // 2, com.shape[2]
    vm = pltpu.VMEM
    shards4 = lambda cuts: [dma(3, 4 * cuts), dma(4 * cuts), dma(4 * cuts), dma(4 * cuts)]
    return pl.pallas_call(
        reduce_kernel,
        in_specs=[pl.BlockSpec(memory_space=ANY)] * 4 + [pl.BlockSpec(memory_space=pltpu.VMEM)],
        out_specs=[pl.BlockSpec(memory_space=pltpu.VMEM)] + [pl.BlockSpec(memory_space=ANY)] * 4,
        out_shape=[
            jax.ShapeDtypeStruct((piece, cols), f32),
            jax.ShapeDtypeStruct((4, mrows, mcols), bf16),
            jax.ShapeDtypeStruct((2 * half, ccols), f32),
            jax.ShapeDtypeStruct(rows.shape, bf16),
            jax.ShapeDtypeStruct((4,) + small.shape, f32),
        ],
        scratch_shapes=[vm((piece, cols), bf16)] * 5
        + [vm((4, mrows, mcols), bf16)] * 4
        + [vm((mrows, mcols), bf16)]
        + [vm((8, half, ccols), bf16)] * 2
        + [vm((4, half, ccols), bf16)] * 4
        + [vm((half, ccols), f32)] * 2
        + [vm((8,) + small.shape, f32), vm(small.shape, f32)]
        + [dma(3, PARTS), dma(3, PARTS), dma(2)]
        + shards4(2)
        + shards4(1)
        + [dma(), dma(), dma(2), dma(2), dma()]
        + [dma(2), dma(), dma()]
        + [dma(8), dma(8)]
        + [dma(3), dma(3), dma()]
        + [dma(3, PARTS), dma(3, PARTS), dma()]
        + [dma(5)],
        compiler_params=pltpu.CompilerParams(
            collective_id=4, has_side_effects=True, vmem_limit_bytes=56 * 2**20
        ),
        name="reduce_last",
    )(back, main, com, rows, small)


def over_rows(left, right):
    return lax.dot_general(
        left, right, (((0,), (0,)), ((), ())), preferred_element_type=jnp.float32
    )


def gather_plain(hid, main, com):
    hid_all = lax.all_gather(hid, "seq", axis=0)
    main_all = lax.all_gather(main, "wshard", axis=0)
    return hid_all, main_all, lax.all_gather(com, "wshard", axis=0)


def gather_more_plain(cot, rows, wide):
    cot_all = lax.all_gather(cot, "seq", axis=0)
    cols = lax.all_to_all(rows, "wshard", split_axis=1, concat_axis=0, tiled=True)
    own = lax.dynamic_slice_in_dim(cols, lax.axis_index("seq") * wide, wide, 0)
    return cot_all, lax.all_gather(own, "wshard", axis=1, tiled=True)


def reduce_scattered(v, axis):
    return lax.psum_scatter(v, axis, scatter_dimension=0, tiled=False)


def reduce_first_plain(layer, rows):
    layer_sum = reduce_scattered(layer, "seq").astype(f32)
    rows = rows.reshape(-1, rows.shape[-1])
    part = lax.psum_scatter(rows, "wshard", scatter_dimension=1, tiled=True)
    part = lax.all_gather(part, "seq", axis=0, tiled=True)
    return layer_sum, lax.all_to_all(part, "wshard", split_axis=0, concat_axis=1, tiled=True)


def reduce_plain(back, main, com, rows, small):
    back_sum = reduce_scattered(back, "seq").astype(f32)
    main_out = lax.all_gather(reduce_scattered(main, "wshard"), "seq", axis=0)
    com_all = lax.all_gather(reduce_scattered(com, "wshard"), "seq", axis=0)
    small_out = lax.all_gather(lax.psum(small, "wshard"), "seq", axis=0)
    return back_sum, main_out, jnp.sum(com_all.astype(f32), axis=0), rows, small_out


def shards(
    hidden,
    segments,
    norm_gain,
    in_weight,
    conv_weight,
    conv_bias,
    step_bias,
    decay_log,
    skip_scale,
    gate_gain,
    out_weight,
    cotangent,
):
    group = lax.axis_index("seq")
    groups, owners = lax.axis_size("seq"), lax.axis_size("wshard")
    direct = (groups, owners) == (4, 8)
    heads = H // groups
    wide = heads * P_SIZE
    length = segments.shape[1]
    hidden_own, cot_own = hidden[0], cotangent[0]
    in_gain = norm_gain.astype(f32)[:, None]
    in_scaled = (in_weight.astype(f32) * in_gain).astype(bf16)
    main = jnp.concatenate(
        [
            lax.dynamic_slice_in_dim(in_scaled, group * wide, wide, 1),
            lax.dynamic_slice_in_dim(in_scaled, E + group * wide, wide, 1),
        ],
        axis=1,
    )
    com = jnp.pad(in_scaled[:, 2 * E :], ((0, 0), (0, 128 - H)))
    out_gain = gate_gain.astype(f32)[:, None]
    out_scaled = (out_weight.astype(f32) * out_gain).astype(bf16)
    gather = gather_first if direct else gather_plain
    hidden_all, w_main, w_com = gather(hidden_own, main, com)
    hidden_all = hidden_all.reshape(length, D)
    w_main, w_com = w_main.reshape(D, 2 * wide), w_com.reshape(D, -1)
    w_bc = w_com[:, : 2 * N]
    w_dt = jnp.pad(
        lax.dynamic_slice_in_dim(w_com, 2 * N + group * heads, heads, 1), ((0, 0), (0, 128 - heads))
    )

    seg = segments[0]
    tok = token_facts(seg)
    segc, segr = seg[:, None], seg.reshape(length // Q, 1, Q)
    own_chan = lambda v: jnp.concatenate(
        [lax.dynamic_slice_in_dim(v, group * wide, wide, v.ndim - 1), v[..., E:]], axis=-1
    )
    own_head = lambda v: lax.dynamic_slice_in_dim(v, group * heads, heads, 0)
    taps, bias = own_chan(conv_weight), own_chan(conv_bias)[None]
    rate = -jnp.exp(own_head(decay_log))
    head = jnp.pad(jnp.stack([own_head(step_bias), rate]), ((0, 0), (0, 128 - heads)))
    skip = jnp.repeat(own_head(skip_scale), P_SIZE)[None]
    spot = (jnp.arange(wide)[:, None] // P_SIZE == jnp.arange(128)[None]).astype(bf16)
    beside, more = (forward_traffic(cot_own, out_scaled), (cot_own, out_scaled)) if direct else (NoTraffic, ())
    u, dt, gate, scale, mixed, save, *got = mixer_fwd(
        beside, more, hidden_all, w_main, w_bc, w_dt, tok, segc, segr, taps, bias, head, skip
    )
    cot_all, w_out = got if direct else gather_more_plain(cot_own, out_scaled, wide)
    cot_all, w_out = cot_all.reshape(length, D), w_out.reshape(wide, D)

    mixed_wide = mixed.astype(f32)
    sg = jax.nn.sigmoid(gate)
    silu = gate * sg
    g = mixed_wide * silu
    g_low = g.astype(bf16)
    a = lax.dot_general(cot_all, w_out, (((1,), (1,)), ((), ())), preferred_element_type=f32)
    sums = lax.psum(jnp.stack([jnp.sum(g * g, axis=1), jnp.sum(a * g, axis=1)]), "seq")
    r = lax.rsqrt(sums[0] / E + eps)[:, None]
    pull = (r * r * r) * (sums[1] / E)[:, None]
    d_g = r * a - g * pull
    d_mixed = (d_g * silu).astype(bf16)
    d_gate = (d_g * mixed_wide * (sg * (1.0 + gate * (1.0 - sg))) * scale).astype(bf16)
    layer_part = (jnp.dot(g_low, w_out, preferred_element_type=f32) * r).astype(bf16)
    cot_r = (cot_all.astype(f32) * r).astype(bf16)
    out_part = over_rows(g_low, cot_r).astype(bf16)

    layer_part, out_part = layer_part.reshape(groups, -1, D), out_part.reshape(2, -1, D)
    beside, more = (backward_traffic(layer_part, out_part), (layer_part, out_part)) if direct else (NoTraffic, ())
    du, ddt, taps_sum, head_sum, skip_sum, *got = mixer_bwd(
        beside, more, u, dt, tok, segc, segr, taps, bias, head, skip, save, d_mixed, spot
    )
    layer_sum, out_sum = got if direct else reduce_first_plain(layer_part, out_part)
    du = (du.astype(f32) * scale).astype(bf16)
    ddt = (ddt.astype(f32) * scale).astype(bf16)
    d_main = jnp.concatenate([d_gate, du[:, :wide]], axis=1)
    d_com = jnp.concatenate([du[:, wide:], ddt], axis=1)
    main_part = over_rows(hidden_all, d_main).astype(bf16)
    com_part = over_rows(hidden_all, d_com).astype(bf16)
    com_part = jnp.concatenate(
        [
            com_part[:, : 2 * N],
            lax.dynamic_update_slice_in_dim(
                jnp.zeros((D, 128), bf16), com_part[:, 2 * N : 2 * N + heads], group * heads, 1
            ),
        ],
        axis=1,
    )
    w_rest = jnp.concatenate([w_bc, w_dt], axis=1)
    nt = lambda p, q: lax.dot_general(p, q, (((1,), (1,)), ((), ())), preferred_element_type=f32)
    back_part = (nt(d_main, w_main) + nt(d_com, w_rest)).astype(bf16)

    head_sum = jnp.sum(head_sum.reshape(2, 8, -1), axis=1)[:, :heads]
    head_sum = head_sum * jnp.stack([jnp.ones_like(rate), rate])
    skip_sum = jnp.sum(skip_sum, axis=0).reshape(heads, P_SIZE).sum(axis=1)
    small = jnp.concatenate(
        [
            jnp.sum(taps_sum.reshape(5, 8, -1), axis=1),
            jnp.pad(jnp.concatenate([head_sum, skip_sum[None]]), ((0, 0), (0, wide + 2 * N - heads))),
        ]
    )
    reduce = reduce_last if direct else reduce_plain
    back_sum, main_out, com_out, out_sum, small_out = reduce(
        back_part.reshape(groups, -1, D),
        main_part.reshape(owners, -1, 2 * wide),
        com_part.reshape(owners, D // owners, -1),
        out_sum,
        small,
    )

    own_wide = hidden_own.astype(f32)
    layer_output = own_wide + layer_sum
    own_scale = lax.rsqrt(jnp.mean(own_wide * own_wide, axis=-1, keepdims=True) + eps)
    hidden_grad = (
        cot_own.astype(f32)
        + back_sum
        - own_wide * (own_scale * own_scale) * jnp.mean(back_sum * own_wide, axis=-1, keepdims=True)
    )
    main_out = main_out.astype(f32)
    in_sum = jnp.concatenate(
        [main_out[i, :, :wide] for i in range(groups)]
        + [main_out[i, :, wide:] for i in range(groups)]
        + [com_out[:, : 2 * N + H]],
        axis=1,
    )
    in_weight_grad = in_sum * in_gain
    norm_gain_grad = jnp.sum(in_sum * in_weight.astype(f32), axis=1)
    out_sum = out_sum.astype(f32)
    out_weight_grad = out_sum * out_gain
    gate_gain_grad = jnp.sum(out_sum * out_weight.astype(f32), axis=1)
    side = lambda lo, hi: jnp.concatenate([small_out[i, lo:hi, :wide] for i in range(groups)], axis=1)
    chan = jnp.concatenate([side(0, 5), jnp.sum(small_out[:, :5, wide:], axis=0)], axis=1)
    per_head = lambda k: small_out[:, k, :heads].reshape(H)
    return (
        layer_output[None],
        hidden_grad[None],
        norm_gain_grad,
        in_weight_grad,
        chan[:4],
        chan[4],
        per_head(5),
        per_head(6),
        per_head(7),
        gate_gain_grad,
        out_weight_grad,
    )


def solution(mesh):
    in_specs = (
        P("wshard", "seq", None),
        P("wshard", None),
        P("wshard"),
        P("wshard", None),
        P(),
        P(),
        P(),
        P(),
        P(),
        P("wshard"),
        P("wshard", None),
        P("wshard", "seq", None),
    )
    out_specs = (
        P("wshard", "seq", None),
        P("wshard", "seq", None),
        P("wshard"),
        P("wshard", None),
        P(),
        P(),
        P(),
        P(),
        P(),
        P("wshard"),
        P("wshard", None),
    )
    return jax.shard_map(shards, mesh=mesh, in_specs=in_specs, out_specs=out_specs, check_vma=False)
```

```python
import functools

import jax
import jax.numpy as jnp
from jax import lax
from jax.experimental import pallas as pl
from jax.experimental.pallas import tpu as pltpu
from jax.sharding import PartitionSpec as P

D = 1536
H = 48
P_SIZE = 64
N = 128
E = 3072

eps = 1e-05
f32, bf16 = jnp.float32, jnp.bfloat16
Q = 128
NEG = -1e30


def dot(a, b):
    return jnp.dot(a, b, preferred_element_type=f32)


def dot_nt(a, b):
    return lax.dot_general(a, b, (((1,), (1,)), ((), ())), preferred_element_type=f32)


def dot3(tri, v):
    hi = v.astype(bf16)
    rest = v - hi.astype(f32)
    mid = rest.astype(bf16)
    low = (rest - mid.astype(f32)).astype(bf16)
    return dot(tri, hi) + dot(tri, mid) + dot(tri, low)


def sigmoid(v):
    return 1.0 / (1.0 + jnp.exp(-v))


def spread_col(v, col):
    return jnp.broadcast_to(v[:, col : col + 1], (Q, 128))


def softplus(v):
    return jnp.maximum(v, 0.0) + jnp.log1p(jnp.exp(-jnp.abs(v)))


def conv_pre(useen, flags, wk, bias, lanes, chans):
    pre = bias[:, chans] + wk[3:4, chans] * useen[8 : 8 + Q, lanes]
    for j in (1, 2, 3):
        pre = pre + wk[3 - j : 4 - j, chans] * (useen[8 - j : 8 - j + Q, lanes] * flags[j])
    return pre


class Facts:
    def __init__(self, chunk, seg_ref, par_ref, xw):
        self.group = lax.axis_index("seq")
        self.heads = xw // P_SIZE
        self.xw = xw
        near = seg_ref[pl.ds(pl.multiple_of(chunk * Q, 8), Q + 16), :]
        now = near[8 : 8 + Q]
        same = lambda other: jnp.broadcast_to(jnp.where(other == now, 1.0, 0.0), (Q, 128))
        self.before = [None] + [same(near[8 - j : 8 - j + Q]) for j in (1, 2, 3)]
        self.after = lambda j: same(near[8 + j : 8 + j + Q])
        self.carried = same(near[7:8])
        self.samelast = same(near[7 + Q : 8 + Q])
        self.now = now
        self.turn = self.heads * self.group
        lane = lax.broadcasted_iota(jnp.int32, (8, 128), 1)
        par = self.own(par_ref[...])
        self.bias = par[0:1]
        self.rate = jnp.where(lane < self.heads, -jnp.exp(par), 0.0)[1:2]

    def own(self, v):
        lane = lax.broadcasted_iota(jnp.int32, v.shape, 1)
        return jnp.where(lane < self.heads, pltpu.roll(v, lax.rem(128 - self.turn, 128), 1), 0.0)

    def back(self, v):
        return pltpu.roll(v, self.turn, 1)

    def chans(self, p):
        if p < self.xw // 128:
            return pl.ds(pl.multiple_of(self.group * self.xw + 128 * p, 128), 128)
        at = E + 128 * (p - self.xw // 128)
        return slice(at, at + 128)


class NoTraffic:
    inputs, outputs, scratch, collective_id = (), (), (), None

    def __init__(self, *refs):
        pass

    def step(self, i, last):
        pass


def fwd_kernel(traffic, hid_ref, main_ref, com_ref, seg_ref, segr_ref, wk_ref, bias_ref, par_ref, skip_ref, *rest):
    n_in, n_out = len(traffic.inputs), len(traffic.outputs)
    extra_in, rest = rest[:n_in], rest[n_in:]
    u_ref, dt_ref, gate_ref, scale_ref, mixed_ref, save_ref = rest[:6]
    extra_out, rest = rest[6 : 6 + n_out], rest[6 + n_out :]
    state, useen, act, next_u, next_dt = rest[:5]
    step_no = pl.program_id(0)
    traffic(*extra_in, *extra_out, *rest[5:]).step(step_no, pl.num_programs(0) - 1)
    xw = mixed_ref.shape[1]
    width = xw + 256
    pairs = xw // 128
    facts = Facts(jnp.maximum(step_no - 1, 0), seg_ref, par_ref, xw)

    @pl.when(step_no == 0)
    def _():
        next_u[...] = jnp.zeros_like(next_u)
        next_dt[...] = jnp.zeros_like(next_dt)

    @pl.when(step_no <= 1)
    def _():
        state[...] = jnp.zeros_like(state)
        useen[0:8, :] = jnp.zeros((8, width), f32)

    useen[8 : 8 + Q, :] = next_u[...]
    dt_now = next_dt[...]

    low = hid_ref[...]
    total = jnp.zeros((Q, 128), f32)
    for k in range(low.shape[1] // 128):
        part = low[:, 128 * k : 128 * k + 128].astype(f32)
        total = total + part * part
    scale = lax.rsqrt(jnp.sum(total, axis=1, keepdims=True) / low.shape[1] + eps)
    scale_ref[...] = scale
    for k in range(xw // 256):
        gate_ref[:, 256 * k : 256 * k + 256] = dot(low, main_ref[:, 256 * k : 256 * k + 256]) * scale
    for k in range(xw // 256):
        got = (dot(low, main_ref[:, xw + 256 * k : xw + 256 * k + 256]) * scale).astype(bf16)
        u_ref[:, 256 * k : 256 * k + 256] = got
        next_u[:, 256 * k : 256 * k + 256] = got.astype(f32)
    got = (dot(low, com_ref[:, 0:256]) * scale).astype(bf16)
    u_ref[:, xw : xw + 256] = got
    next_u[:, xw : xw + 256] = got.astype(f32)
    got = facts.own((dot(low, com_ref[:, 256:384]) * scale).astype(bf16).astype(f32))
    dt_ref[...] = got.astype(bf16)
    next_dt[...] = got

    carried, samelast = facts.carried, facts.samelast
    for p in range(width // 128):
        lanes = slice(128 * p, 128 * p + 128)
        pre = conv_pre(useen, facts.before, wk_ref, bias_ref, lanes, facts.chans(p))
        act[:, lanes] = pre * sigmoid(pre)
    tail = useen[Q : Q + 8, :]
    useen[0:8, :] = tail

    step = softplus(dt_now + facts.bias)
    row = lax.broadcasted_iota(jnp.int32, (Q, Q), 0)
    col = lax.broadcasted_iota(jnp.int32, (Q, Q), 1)
    tri = jnp.where(row >= col, 1.0, 0.0).astype(bf16)
    decay = dot3(tri, step * facts.rate)
    decay_t = decay.T
    madd = jnp.where((row >= col) & (facts.now == segr_ref[0]), 0.0, NEG)
    b_now = act[:, xw : xw + 128]
    c_low = act[:, xw + 128 : xw + 256].astype(bf16)
    gram = dot_nt(c_low, b_now.astype(bf16))
    b_t = b_now.T.astype(bf16)
    left = lax.broadcasted_iota(jnp.int32, (Q, 128), 1) < 64
    for p in range(pairs):
        lanes = slice(128 * p, 128 * p + 128)
        d0, d1 = spread_col(decay, 2 * p), spread_col(decay, 2 * p + 1)
        dp = jnp.where(left, d0, d1)
        sp = jnp.where(left, spread_col(step, 2 * p), spread_col(step, 2 * p + 1))
        xs = act[:, lanes]
        xp = xs * sp
        m0 = gram * jnp.exp(d0 - decay_t[2 * p : 2 * p + 1, :] + madd)
        m1 = gram * jnp.exp(d1 - decay_t[2 * p + 1 : 2 * p + 2, :] + madd)
        both = jnp.concatenate([m0.astype(bf16), m1.astype(bf16)], axis=1)
        stacked = jnp.concatenate(
            [jnp.where(left, xp, 0.0).astype(bf16), jnp.where(left, 0.0, xp).astype(bf16)], axis=0
        )
        st = state[:, lanes]
        st_low = st.astype(bf16)
        save_ref[0, :, lanes] = st_low
        y = dot(both, stacked) + dot(c_low, st_low) * (jnp.exp(dp) * carried)
        mixed_ref[:, lanes] = (y + skip_ref[:, facts.chans(p)] * xs).astype(bf16)
        last = dp[Q - 1 : Q, :]
        to_end = (xp * (jnp.exp(last - dp) * samelast)).astype(bf16)
        state[:, lanes] = st * (jnp.exp(last) * carried[Q - 1 : Q, :]) + dot(b_t, to_end)


def mixer_fwd(traffic, extra, hid, main, com, seg, segr, wk, bias, par, skip):
    length, depth = hid.shape
    xw = main.shape[1] // 2
    width = xw + 256
    n = length // Q
    whole = lambda shape: pl.BlockSpec(shape, lambda i: (0,) * len(shape), pipeline_mode=pl.Buffered(1))
    ahead = lambda i: (jnp.minimum(i, n - 1), 0)
    now = lambda i: (jnp.maximum(i - 1, 0), 0)
    now3 = lambda i: (jnp.maximum(i - 1, 0), 0, 0)
    return pl.pallas_call(
        functools.partial(fwd_kernel, traffic),
        grid=(n + 1,),
        in_specs=[
            pl.BlockSpec((Q, depth), ahead),
            whole(main.shape),
            whole(com.shape),
            whole(seg.shape),
            pl.BlockSpec((1, 1, Q), now3),
            whole(wk.shape),
            whole(bias.shape),
            whole(par.shape),
            whole(skip.shape),
        ]
        + [pl.BlockSpec(memory_space=pl.ANY)] * len(extra),
        out_specs=[
            pl.BlockSpec((Q, width), ahead),
            pl.BlockSpec((Q, 128), ahead),
            pl.BlockSpec((Q, xw), ahead),
            pl.BlockSpec((Q, 1), ahead),
            pl.BlockSpec((Q, xw), now),
            pl.BlockSpec((1, 128, xw), now3),
        ]
        + [pl.BlockSpec(memory_space=pl.ANY)] * len(traffic.outputs),
        out_shape=[
            jax.ShapeDtypeStruct((length, width), bf16),
            jax.ShapeDtypeStruct((length, 128), bf16),
            jax.ShapeDtypeStruct((length, xw), f32),
            jax.ShapeDtypeStruct((length, 1), f32),
            jax.ShapeDtypeStruct((length, xw), bf16),
            jax.ShapeDtypeStruct((n, 128, xw), bf16),
            *traffic.outputs,
        ],
        scratch_shapes=[
            pltpu.VMEM((128, xw), f32),
            pltpu.VMEM((Q + 8, width), f32),
            pltpu.VMEM((Q, width), f32),
            pltpu.VMEM((Q, width), f32),
            pltpu.VMEM((Q, 128), f32),
            *traffic.scratch,
        ],
        compiler_params=pltpu.CompilerParams(
            vmem_limit_bytes=48 * 2**20,
            collective_id=traffic.collective_id,
            has_side_effects=traffic.collective_id is not None,
        ),
        name="mixer_forward",
    )(hid, main, com, seg, segr, wk, bias, par, skip, *extra)


def bwd_kernel(traffic, u_ref, halo_ref, dt_ref, scale_ref, seg_ref, segr_ref, wk_ref, bias_ref, par_ref, skip_ref,
               save_ref, dy_ref, *rest):
    n_in, n_out = len(traffic.inputs), len(traffic.outputs)
    extra_in, rest = rest[:n_in], rest[n_in:]
    du_ref, ddt_ref, small_ref = rest[:3]
    extra_out, rest = rest[3 : 3 + n_out], rest[3 + n_out :]
    dstate, useen, act, slope, dpre, keep_y, keep_x, prod_a, prod_b, rows_a, held = rest[:11]
    wgrad_ref, hgrad_ref, sgrad_ref, spot_ref = rest[11:15]
    step_no = pl.program_id(0)
    last_step = pl.num_programs(0) - 1
    traffic(*extra_in, *extra_out, *rest[15:]).step(step_no, last_step)
    width = u_ref.shape[1]
    xw = width - 256
    pairs = xw // 128

    @pl.when(step_no == 0)
    def _():
        dstate[...] = jnp.zeros_like(dstate)
        dpre[Q : Q + 8, :] = jnp.zeros((8, width), f32)
        wgrad_ref[...] = jnp.zeros_like(wgrad_ref)
        hgrad_ref[...] = jnp.zeros_like(hgrad_ref)
        sgrad_ref[...] = jnp.zeros_like(sgrad_ref)
        rows_a[...] = jnp.zeros_like(rows_a)
        head_of = lax.broadcasted_iota(jnp.int32, (xw, 128), 0) // P_SIZE
        mark = head_of == lax.broadcasted_iota(jnp.int32, (xw, 128), 1)
        spot_ref[...] = jnp.where(mark, 1.0, 0.0).astype(bf16)

    useen[0:8, :] = halo_ref[...].astype(f32)[8:16, :]
    useen[8 : 8 + Q, :] = u_ref[...].astype(f32)
    facts = Facts(last_step - step_no, seg_ref, par_ref, xw)
    flags, carried, samelast = facts.before, facts.carried, facts.samelast
    for p in range(width // 128):
        lanes = slice(128 * p, 128 * p + 128)
        pre = conv_pre(useen, flags, wk_ref, bias_ref, lanes, facts.chans(p))
        sg = sigmoid(pre)
        act[:, lanes] = pre * sg
        slope[:, lanes] = sg * (1.0 + pre * (1.0 - sg))

    raw = dt_ref[...].astype(f32) + facts.bias
    step = softplus(raw)
    rate = facts.rate
    row = lax.broadcasted_iota(jnp.int32, (Q, Q), 0)
    col = lax.broadcasted_iota(jnp.int32, (Q, Q), 1)
    tri = jnp.where(row >= col, 1.0, 0.0).astype(bf16)
    upper = jnp.where(row <= col, 1.0, 0.0).astype(bf16)
    below = jnp.where(row > col, 1.0, 0.0).astype(bf16)
    decay = dot3(tri, step * rate)
    decay_t = decay.T
    madd = jnp.where((row <= col) & (facts.now == segr_ref[0]), 0.0, NEG)
    b_now, c_now = act[:, xw : xw + 128], act[:, xw + 128 : xw + 256]
    b_low, c_low = b_now.astype(bf16), c_now.astype(bf16)
    c_t = c_now.T.astype(bf16)
    gram = dot_nt(b_low, c_low)
    left = lax.broadcasted_iota(jnp.int32, (Q, 128), 1) < 64
    lane = lax.broadcasted_iota(jnp.int32, (Q, 128), 1)
    dgram = jnp.zeros((Q, Q), f32)
    cols_b = jnp.zeros((Q, 128), f32)
    for p in range(pairs):
        lanes = slice(128 * p, 128 * p + 128)
        d0, d1 = spread_col(decay, 2 * p), spread_col(decay, 2 * p + 1)
        dp = jnp.where(left, d0, d1)
        sp = jnp.where(left, spread_col(step, 2 * p), spread_col(step, 2 * p + 1))
        xs = act[:, lanes]
        xp = xs * sp
        dy_low = dy_ref[:, lanes]
        dy = dy_low.astype(f32)
        stacked = jnp.concatenate(
            [jnp.where(left, dy, 0.0).astype(bf16), jnp.where(left, 0.0, dy).astype(bf16)], axis=0
        )
        pair = dot_nt(xp.astype(bf16), stacked)
        mts = []
        for k, dk in ((0, d0), (1, d1)):
            h = 2 * p + k
            e = jnp.exp(decay_t[h : h + 1, :] - dk + madd)
            f = e * pair[:, 128 * k : 128 * k + 128]
            dgram = dgram + f
            w = gram * f
            mts.append((gram * e).astype(bf16))
            rows_a[h : h + 1, :] = jnp.sum(w, axis=0, keepdims=True)
            cols_b = jnp.where(lane == h, jnp.sum(w, axis=1, keepdims=True), cols_b)
        within = dot(jnp.concatenate(mts, axis=1), stacked)
        grow = jnp.exp(dp) * carried
        dy_in = dy * grow
        dy_in_low = dy_in.astype(bf16)
        keep_y[:, lanes] = dy_in_low
        st = save_ref[0, :, lanes]
        prod_a[:, lanes] = (dy_in * dot(c_low, st)).astype(bf16)
        last = dp[Q - 1 : Q, :]
        fade = jnp.exp(last - dp) * samelast
        ds = dstate[:, lanes]
        ds_low = ds.astype(bf16)
        xe = xp * fade
        keep_x[:, lanes] = xe.astype(bf16)
        later = dot(b_low, ds_low)
        prod_b[:, lanes] = (xe * later).astype(bf16)
        retain = jnp.exp(last) * carried[Q - 1 : Q, :]
        held[0:1, lanes] = jnp.sum(ds * st.astype(f32), axis=0, keepdims=True) * retain
        dxs = sp * (within + later * fade) + skip_ref[:, facts.chans(p)] * dy
        skp = xs * dy
        sgrad_ref[:, lanes] += jnp.sum(skp.reshape(Q // 8, 8, 128), axis=0)
        dpre[0:Q, lanes] = dxs * slope[:, lanes]
        dstate[:, lanes] = ds * retain + dot(c_t, dy_in_low)
        if p == 0:
            db_in, dc_in = dot_nt(keep_x[:, lanes], ds_low), dot_nt(dy_in_low, st)
        else:
            db_in, dc_in = db_in + dot_nt(keep_x[:, lanes], ds_low), dc_in + dot_nt(dy_in_low, st)

    dg_low = dgram.astype(bf16)
    db = dot(dg_low, c_low) + db_in
    dc = dot(dgram.T.astype(bf16), b_low) + dc_in
    dpre[0:Q, xw : xw + 128] = db * slope[:, xw : xw + 128]
    dpre[0:Q, xw + 128 : xw + 256] = dc * slope[:, xw + 128 : xw + 256]

    spot = spot_ref[...]
    a_in = dot(prod_a[...], spot)
    b_in = dot(prod_b[...], spot)
    hv = jnp.broadcast_to(held[0:1, :], (8, xw))
    h_hi = hv.astype(bf16)
    h_lo = (hv - h_hi.astype(f32)).astype(bf16)
    through = (dot(h_hi, spot) + dot(h_lo, spot))[0:1, :]
    a_own = rows_a[...].T
    cross = dot3(upper, a_own - cols_b + a_in) + dot3(below, b_in) + through
    total = cols_b + b_in
    sg = sigmoid(raw)
    ratio = jnp.where(step > 1e-30, sg / jnp.maximum(step, 1e-30), 1.0)
    draw = total * ratio + rate * cross * sg
    scale = jnp.broadcast_to(scale_ref[...], (Q, 128))
    ddt_ref[...] = facts.back(draw * scale).astype(bf16)
    hgrad_ref[0:8, :] += jnp.sum(draw.reshape(Q // 8, 8, 128), axis=0)
    hgrad_ref[8:16, :] += jnp.sum((step * cross).reshape(Q // 8, 8, 128), axis=0)

    ahead = [None] + [facts.after(j) for j in (1, 2, 3)]
    for p in range(width // 128):
        lanes = slice(128 * p, 128 * p + 128)
        own = dpre[0:Q, lanes]
        chans = facts.chans(p)
        du = wk_ref[3:4, chans] * own
        wgrad_ref[24:32, lanes] += jnp.sum((own * useen[8 : 8 + Q, lanes]).reshape(Q // 8, 8, 128), axis=0)
        wgrad_ref[32:40, lanes] += jnp.sum(own.reshape(Q // 8, 8, 128), axis=0)
        for j in (1, 2, 3):
            du = du + wk_ref[3 - j : 4 - j, chans] * (dpre[j : j + Q, lanes] * ahead[j])
            moved = own * (useen[8 - j : 8 - j + Q, lanes] * flags[j])
            k = 3 - j
            wgrad_ref[8 * k : 8 * k + 8, lanes] += jnp.sum(moved.reshape(Q // 8, 8, 128), axis=0)
        du_ref[:, lanes] = (du * scale).astype(bf16)
    first = dpre[0:8, :]
    dpre[Q : Q + 8, :] = first

    @pl.when(step_no == last_step)
    def _():
        small_ref[...] = jnp.zeros_like(small_ref)
        for k in range(5):
            small_ref[k : k + 1, :] = jnp.sum(wgrad_ref[8 * k : 8 * k + 8, :], axis=0, keepdims=True)
        small_ref[5:6, 0:128] = jnp.sum(hgrad_ref[0:8, :], axis=0, keepdims=True)
        small_ref[6:7, 0:128] = rate * jnp.sum(hgrad_ref[8:16, :], axis=0, keepdims=True)
        skips = sgrad_ref[...]
        hi = skips.astype(bf16)
        mid = (skips - hi.astype(f32)).astype(bf16)
        by_head = dot(hi, spot_ref[...]) + dot(mid, spot_ref[...])
        small_ref[7:8, 0:128] = jnp.sum(by_head, axis=0, keepdims=True)


def mixer_bwd(traffic, extra, u, dt, scale, seg, segr, wk, bias, par, skip, save, dy):
    length, width = u.shape
    xw = width - 256
    n = length // Q
    whole = lambda shape: pl.BlockSpec(shape, lambda i: (0,) * len(shape))
    back = lambda i: (n - 1 - i, 0)
    return pl.pallas_call(
        functools.partial(bwd_kernel, traffic),
        grid=(n,),
        in_specs=[
            pl.BlockSpec((Q, width), back),
            pl.BlockSpec((16, width), lambda i: (jnp.maximum((n - 1 - i) * (Q // 16) - 1, 0), 0)),
            pl.BlockSpec((Q, 128), back),
            pl.BlockSpec((Q, 1), back),
            whole(seg.shape),
            pl.BlockSpec((1, 1, Q), lambda i: (n - 1 - i, 0, 0)),
            whole(wk.shape),
            whole(bias.shape),
            whole(par.shape),
            whole(skip.shape),
            pl.BlockSpec((1, 128, xw), lambda i: (n - 1 - i, 0, 0)),
            pl.BlockSpec((Q, xw), back),
        ]
        + [pl.BlockSpec(memory_space=pl.ANY)] * len(extra),
        out_specs=[
            pl.BlockSpec((Q, width), back),
            pl.BlockSpec((Q, 128), back),
            whole((8, width)),
        ]
        + [pl.BlockSpec(memory_space=pl.ANY)] * len(traffic.outputs),
        out_shape=[
            jax.ShapeDtypeStruct((length, width), bf16),
            jax.ShapeDtypeStruct((length, 128), bf16),
            jax.ShapeDtypeStruct((8, width), f32),
            *traffic.outputs,
        ],
        scratch_shapes=[
            pltpu.VMEM((128, xw), f32),
            pltpu.VMEM((Q + 8, width), f32),
            pltpu.VMEM((Q, width), f32),
            pltpu.VMEM((Q, width), f32),
            pltpu.VMEM((Q + 8, width), f32),
            pltpu.VMEM((Q, xw), bf16),
            pltpu.VMEM((Q, xw), bf16),
            pltpu.VMEM((Q, xw), bf16),
            pltpu.VMEM((Q, xw), bf16),
            pltpu.VMEM((128, 128), f32),
            pltpu.VMEM((8, xw), f32),
            pltpu.VMEM((40, width), f32),
            pltpu.VMEM((16, 128), f32),
            pltpu.VMEM((8, xw), f32),
            pltpu.VMEM((xw, 128), bf16),
            *traffic.scratch,
        ],
        compiler_params=pltpu.CompilerParams(
            vmem_limit_bytes=48 * 2**20,
            collective_id=traffic.collective_id,
            has_side_effects=traffic.collective_id is not None,
        ),
        name="mixer_backward",
    )(u, u, dt, scale, seg, segr, wk, bias, par, skip, save, dy, *extra)


MESH = pl.DeviceIdType.MESH
ANY = pl.ANY
PARTS = 4


def remote(src, dst, send_sem, recv_sem, device):
    return pltpu.make_async_remote_copy(
        src_ref=src, dst_ref=dst, send_sem=send_sem, recv_sem=recv_sem, device_id=device, device_id_type=MESH
    )


class Place:
    def __init__(self):
        self.w, self.s = lax.axis_index("wshard"), lax.axis_index("seq")
        self.z, self.x = self.w // 2, lax.rem(self.w, 2)
        self.y, self.c = self.s // 2, lax.rem(self.s, 2)
        self.s_sib = 2 * self.y + 1 - self.c
        self.s_far = 2 * (1 - self.y) + self.c
        self.s_diag = 2 * (1 - self.y) + 1 - self.c
        self.side = (2 * self.z + 1 - self.x, self.s)
        self.up = (lax.rem(self.w + 2, 8), self.s)
        self.down = (lax.rem(self.w + 6, 8), self.s)
        self.sib = (self.w, self.s_sib)
        self.far = (self.w, self.s_far)

    def greet(self, everyone=False):
        barrier = pltpu.get_barrier_semaphore()
        others = [(lax.rem(self.w + k, 8), self.s) for k in range(1, 8)] if everyone else []
        if everyone:
            others += [(self.w, lax.rem(self.s + k, 4)) for k in range(1, 4)]
        else:
            others = [self.side, self.up, self.down, self.sib, self.far]
        for other in others:
            pl.semaphore_signal(barrier, inc=1, device_id=other, device_id_type=MESH)
        pl.semaphore_wait(barrier, len(others))


def dma(*shape):
    return pltpu.SemaphoreType.DMA(shape)


def gather_pieces_start(at, own, slot, sems):
    send, recv, local = sems
    rows = own.shape[0] // PARTS
    pltpu.make_async_copy(own, slot(at.s), local).start()
    for k in range(PARTS):
        part = pl.ds(k * rows, rows)
        remote(own.at[part], slot(at.s).at[part], send.at[1, k], recv.at[1, k], at.far).start()
    for k in range(PARTS):
        part = pl.ds(k * rows, rows)
        remote(own.at[part], slot(at.s).at[part], send.at[0, k], recv.at[0, k], at.sib).start()


def gather_pieces_pass(at, own, slot, sems):
    send, recv, _ = sems
    rows = own.shape[0] // PARTS
    for k in range(PARTS):
        part = pl.ds(k * rows, rows)
        theirs = slot(at.s_far).at[part]
        remote(theirs, theirs, send.at[1, k], recv.at[1, k], at.far).wait_recv()
        remote(theirs, theirs, send.at[2, k], recv.at[2, k], at.sib).start()


def gather_pieces_end(at, own, slot, sems):
    send, recv, local = sems
    rows = own.shape[0] // PARTS
    pltpu.make_async_copy(own, slot(at.s), local).wait()
    for k in range(PARTS):
        part = pl.ds(k * rows, rows)
        sib, diag, far = slot(at.s_sib).at[part], slot(at.s_diag).at[part], slot(at.s_far).at[part]
        remote(own.at[part], slot(at.s).at[part], send.at[0, k], recv.at[0, k], at.sib).wait_send()
        remote(own.at[part], slot(at.s).at[part], send.at[1, k], recv.at[1, k], at.far).wait_send()
        remote(far, far, send.at[2, k], recv.at[2, k], at.sib).wait_send()
        remote(sib, sib, send.at[0, k], recv.at[0, k], at.sib).wait_recv()
        remote(diag, diag, send.at[2, k], recv.at[2, k], at.sib).wait_recv()


CUTS = 2


def gather_shards(at, main, com, main_all, com_all, sems, between):
    send, recv, csend, crecv, psend, precv, local = sems
    half, cut = com.shape[0] // 2, main.shape[0] // CUTS
    mine = pl.ds(pl.multiple_of(at.c * half, half), half)
    keep = pltpu.make_async_copy(main, main_all.at[at.w], local.at[0])
    com_keep = pltpu.make_async_copy(com, com_all.at[at.w], local.at[1])
    keep.start()
    com_keep.start()

    def hop(zp, q, way, device, own=False):
        w, n, part = 2 * zp + at.x, zp * CUTS + q, pl.ds(q * cut, cut)
        slot, com_slot = main_all.at[w, part], com_all.at[w, mine]
        copies = [remote(main.at[part] if own else slot, slot, send.at[way, n], recv.at[w * CUTS + q], device)]
        if q == 0:
            copies.append(remote(com.at[mine] if own else com_slot, com_slot, csend.at[way, zp], crecv.at[w], device))
        return copies

    def begin(copies):
        for copy in copies:
            copy.start()

    def sent(copies):
        for copy in copies:
            copy.wait_send()

    def all_ways(act, q):
        act(hop(at.z, q, 0, at.side, True))

        @pl.when(at.z < 3)
        def _():
            act(hop(at.z, q, 1, at.up, True))

        @pl.when(at.z > 0)
        def _():
            act(hop(at.z, q, 2, at.down, True))

    def arrived(w, q):
        slot = main_all.at[w, pl.ds(q * cut, cut)]
        remote(slot, slot, send.at[0, 0], recv.at[w * CUTS + q], at.side).wait_recv()
        if q == 0:
            held = com_all.at[w, mine]
            remote(held, held, csend.at[0, 0], crecv.at[w], at.side).wait_recv()
            remote(held, held, psend.at[w], precv.at[w], at.sib).start()

    for q in range(CUTS):
        if q > 0:
            all_ways(sent, q - 1)
        all_ways(begin, q)
    for d in (1, 2, 3):
        if d == 3:
            between()
        for q in range(CUTS):

            @pl.when(at.z - d >= 0)
            def _():
                zp = at.z - d
                arrived(2 * zp + at.x, q)

                @pl.when(at.z < 3)
                def _():
                    begin(hop(zp, q, 1, at.up))

                begin(hop(zp, q, 0, at.side))

            @pl.when(at.z + d <= 3)
            def _():
                zp = at.z + d
                arrived(2 * zp + at.x, q)

                @pl.when(at.z > 0)
                def _():
                    begin(hop(zp, q, 2, at.down))

                begin(hop(zp, q, 0, at.side))

    for zp in range(4):
        for q in range(CUTS):
            arrived(2 * zp + 1 - at.x, q)
    keep.wait()
    com_keep.wait()
    all_ways(sent, CUTS - 1)
    for zp in range(4):
        for q in range(CUTS):

            @pl.when(at.z != zp)
            def _():
                sent(hop(zp, q, 0, at.side))

            @pl.when((at.z < 3) & (zp < at.z))
            def _():
                sent(hop(zp, q, 1, at.up))

            @pl.when((at.z > 0) & (zp > at.z))
            def _():
                sent(hop(zp, q, 2, at.down))

    other = pl.ds(pl.multiple_of((1 - at.c) * half, half), half)
    for k in range(1, 8):
        w = lax.rem(at.w + k, 8)
        gone, got = com_all.at[w, mine], com_all.at[w, other]
        remote(gone, gone, psend.at[w], precv.at[w], at.sib).wait_send()
        remote(got, got, psend.at[w], precv.at[w], at.sib).wait_recv()


def gather_kernel(hid, main, com, hid_all, main_all, com_all, *sems):
    at = Place()
    at.greet()
    slot = lambda s: hid_all.at[s]
    gather_pieces_start(at, hid, slot, sems[0:3])
    pass_on = lambda: gather_pieces_pass(at, hid, slot, sems[0:3])
    gather_shards(at, main, com, main_all, com_all, sems[3:10], pass_on)
    gather_pieces_end(at, hid, slot, sems[0:3])


def gather_first(hid, main, com):
    shape = lambda n, v: jax.ShapeDtypeStruct((n,) + v.shape, v.dtype)
    return pl.pallas_call(
        gather_kernel,
        in_specs=[pl.BlockSpec(memory_space=ANY)] * 3,
        out_specs=[pl.BlockSpec(memory_space=ANY)] * 3,
        out_shape=[shape(4, hid), shape(8, main), shape(8, com)],
        scratch_shapes=[dma(3, PARTS), dma(3, PARTS), dma()]
        + [dma(3, 4 * CUTS), dma(8 * CUTS), dma(3, 4), dma(8), dma(8), dma(8), dma(2)],
        compiler_params=pltpu.CompilerParams(collective_id=1, has_side_effects=True),
        name="gather_first",
    )(hid, main, com)


SLICES = 8


def each_slice(body):
    def run(k, _):
        body(k)
        return 0

    lax.fori_loop(0, SLICES, run, 0)


def forward_traffic(cot, rows):
    class Traffic:
        inputs = (cot, rows)
        outputs = (
            jax.ShapeDtypeStruct((4,) + cot.shape, cot.dtype),
            jax.ShapeDtypeStruct((2,) + rows.shape, rows.dtype),
        )
        scratch = (dma(3, SLICES), dma(3, SLICES), dma(), dma(3, SLICES), dma(2, SLICES), dma())
        collective_id = 2

        def __init__(self, own, row_own, full, row_full, send, recv, local, rsend, rrecv, rlocal):
            self.at = at = Place()
            self.own, self.full, self.row_own, self.row_full = own, full, row_own, row_full
            self.rrecv = rrecv
            cut, rcut = own.shape[0] // SLICES, row_own.shape[0] // SLICES
            part = lambda k: pl.ds(pl.multiple_of(k * cut, cut), cut)
            rpart = lambda k: pl.ds(pl.multiple_of(k * rcut, rcut), rcut)
            piece = lambda s, k: full.at[s, part(k)]
            self.keep = pltpu.make_async_copy(own, full.at[at.s], local)
            self.rkeep = pltpu.make_async_copy(row_own, row_full.at[at.x], rlocal)
            self.to_sib = lambda k: remote(own.at[part(k)], piece(at.s, k), send.at[0, k], recv.at[0, k], at.sib)
            self.to_far = lambda k: remote(own.at[part(k)], piece(at.s, k), send.at[1, k], recv.at[1, k], at.far)
            self.pass_on = lambda k: remote(piece(at.s_far, k), piece(at.s_far, k), send.at[2, k], recv.at[2, k], at.sib)
            here = lambda k, n, device: remote(
                row_full.at[at.x, rpart(k)], row_full.at[at.x, rpart(k)], rsend.at[n, k], rrecv.at[at.x, k], device
            )
            self.rows = (lambda k: here(k, 0, at.side), lambda k: here(k, 1, at.up), lambda k: here(k, 2, at.down))
            got = lambda s, n, k: remote(piece(s, k), piece(s, k), send.at[n, k], recv.at[n, k], at.sib)
            self.from_sib = lambda k: got(at.s_sib, 0, k)
            self.from_far = lambda k: got(at.s_far, 1, k)
            self.from_diag = lambda k: got(at.s_diag, 2, k)
            other = lambda k: row_full.at[1 - at.x, rpart(k)]
            self.from_side = lambda k: remote(other(k), other(k), rsend.at[0, k], rrecv.at[1 - at.x, k], at.side)

        def step(self, i, last):
            at = self.at
            upward, downward = (at.z >= at.s) & (at.z < 3), (at.z <= at.s) & (at.z > 0)
            side, up, down = self.rows

            @pl.when(i == 0)
            def _():
                at.greet()
                self.keep.start()
                each_slice(lambda k: self.to_sib(k).start())

                @pl.when(at.z == at.s)
                def _():
                    self.rkeep.start()
                    self.rkeep.wait()

            k = i - 1

            @pl.when((k >= 0) & (k < SLICES))
            def _():
                self.to_far(k).start()

            @pl.when((k >= SLICES) & (k < 2 * SLICES))
            def _():
                self.from_far(k - SLICES).wait_recv()
                self.pass_on(k - SLICES).start()

            far_away = jnp.where(at.z > at.s, at.z - at.s, at.s - at.z)
            r = i - 1 - 2 * far_away

            @pl.when((r >= 0) & (r < SLICES))
            def _():
                @pl.when(at.z != at.s)
                def _():
                    side(r).wait_recv()

                side(r).start()

                @pl.when(upward)
                def _():
                    up(r).start()

                @pl.when(downward)
                def _():
                    down(r).start()

            @pl.when(i == last)
            def _():
                self.keep.wait()

                def finish(k):
                    self.to_sib(k).wait_send()
                    self.to_far(k).wait_send()
                    self.pass_on(k).wait_send()
                    self.from_sib(k).wait_recv()
                    self.from_diag(k).wait_recv()
                    side(k).wait_send()
                    self.from_side(k).wait_recv()

                    @pl.when(upward)
                    def _():
                        up(k).wait_send()

                    @pl.when(downward)
                    def _():
                        down(k).wait_send()

                each_slice(finish)

    return Traffic


def add_into(dst, src, rows):
    def body(i, _):
        part = pl.ds(pl.multiple_of(i * 16, 16), 16)
        dst[part, :] = (dst[part, :].astype(f32) + src[part, :].astype(f32)).astype(bf16)
        return 0

    lax.fori_loop(0, rows // 16, body, 0)


def far_first(at, i):
    inner = (at.z == 1) | (at.z == 2)
    i = jnp.where(inner & (i >= 2), 5 - i, i)
    return jnp.where(at.z < 2, 3 - i, i)


class ReduceShards:
    def __init__(self, at, partial, cuts, acc, from_side, from_down, from_up, sems):
        self.at, self.partial, self.cuts, self.acc = at, partial, cuts, acc
        self.from_side, self.from_down, self.from_up = from_side, from_down, from_up
        self.send, self.recv_side, self.recv_down, self.recv_up = sems
        self.rows = acc.shape[1] // cuts

    def unit(self, j):
        if isinstance(j, int):
            shard, cut = j // self.cuts, j % self.cuts
        else:
            shard, cut = lax.div(j, self.cuts), lax.rem(j, self.cuts)
        zp = far_first(self.at, shard)
        return zp, zp * self.cuts + cut, pl.ds(pl.multiple_of(cut * self.rows, self.rows), self.rows)

    def side_copy(self, j):
        at = self.at
        zp, n, part = self.unit(j)
        return remote(
            self.partial(zp).at[part], self.from_side.at[zp, part],
            self.send.at[0, n], self.recv_side.at[n], at.side,
        )

    def up_copy(self, j):
        zp, n, part = self.unit(j)
        return remote(
            self.acc.at[zp, part], self.from_down.at[zp, part], self.send.at[1, n], self.recv_down.at[n], self.at.up
        )

    def down_copy(self, j):
        zp, n, part = self.unit(j)
        return remote(
            self.acc.at[zp, part], self.from_up.at[zp, part], self.send.at[2, n], self.recv_up.at[n], self.at.down
        )

    def start(self):
        self.side_copy(0).start()
        self.side_copy(1).start()

    def step(self, j):
        at = self.at
        zp, _, part = self.unit(j)
        self.side_copy(j).wait()
        acc = self.acc.at[zp, part]
        add_into(acc, self.from_side.at[zp, part], self.rows)

        @pl.when((at.z > 0) & (zp >= at.z))
        def _():
            self.up_copy(j).wait_recv()
            add_into(acc, self.from_down.at[zp, part], self.rows)

        @pl.when((at.z < 3) & (zp <= at.z))
        def _():
            self.down_copy(j).wait_recv()
            add_into(acc, self.from_up.at[zp, part], self.rows)

        @pl.when(zp > at.z)
        def _():
            self.up_copy(j).start()

        @pl.when(zp < at.z)
        def _():
            self.down_copy(j).start()

    def end(self):
        at = self.at
        for j in range(4 * self.cuts):
            zp = self.unit(j)[0]

            @pl.when(zp > at.z)
            def _():
                self.up_copy(j).wait_send()

            @pl.when(zp < at.z)
            def _():
                self.down_copy(j).wait_send()


def backward_traffic(layer, rows, gate):
    piece, cols = layer.shape[1:]
    rrows = rows.shape[1]
    grows, gcols = gate.shape[1:]

    class Traffic:
        inputs = (layer, rows, gate)
        outputs = (
            jax.ShapeDtypeStruct((piece, cols), f32),
            jax.ShapeDtypeStruct((rrows, cols), bf16),
            jax.ShapeDtypeStruct((grows, gcols), bf16),
        )
        scratch = (
            *[pltpu.VMEM((piece, cols), bf16)] * 5,
            pltpu.VMEM((piece, cols), f32),
            *[pltpu.VMEM((rrows, cols), bf16)] * 4,
            dma(3, SLICES),
            dma(3, SLICES),
            dma(3),
            dma(3, SLICES),
            dma(3, SLICES),
            dma(2),
            dma(2, SLICES),
            dma(2, SLICES),
            *[pltpu.VMEM((4, grows, gcols), bf16)] * 4,
            dma(3, 8),
            dma(8),
            dma(8),
            dma(8),
            dma(5),
        )
        collective_id = 3

        def __init__(
            self, layer, rows, gate, out, rows_out, gate_out,
            own_v, far_v, sib_v, pass_v, got_v, sum_v, acc, side_v, low_v, high_v,
            send, recv, local, rsend, rrecv, rlocal, fsend, frecv,
            gacc, gside, glow, ghigh, gsend, grecv_side, grecv_low, grecv_high, glocal,
        ):
            self.at = at = Place()
            cut, rcut = piece // SLICES, rrows // SLICES
            part = lambda k: pl.ds(pl.multiple_of(k * cut, cut), cut)
            rpart = lambda k: pl.ds(pl.multiple_of(k * rcut, rcut), rcut)
            self.own, self.sib, self.passed, self.got, self.sum = own_v, sib_v, pass_v, got_v, sum_v
            self.part, self.rpart, self.cut, self.rcut = part, rpart, cut, rcut
            self.far_v, self.acc, self.side_v, self.low_v, self.high_v = far_v, acc, side_v, low_v, high_v
            self.load_far = pltpu.make_async_copy(layer.at[at.s_far], far_v, local.at[0])
            self.load_own = pltpu.make_async_copy(layer.at[at.s], own_v, local.at[1])
            self.store = pltpu.make_async_copy(sum_v, out, local.at[2])
            self.to_pass = lambda k: remote(
                layer.at[at.s_diag, part(k)], pass_v.at[part(k)], send.at[0, k], recv.at[0, k], at.sib
            )
            self.to_sib = lambda k: remote(
                layer.at[at.s_sib, part(k)], sib_v.at[part(k)], send.at[1, k], recv.at[1, k], at.sib
            )
            self.to_far = lambda k: remote(
                far_v.at[part(k)], got_v.at[part(k)], send.at[2, k], recv.at[2, k], at.far
            )
            self.load_acc = pltpu.make_async_copy(rows.at[at.x], acc, rlocal.at[0])
            self.store_acc = pltpu.make_async_copy(acc, rows_out, rlocal.at[1])
            spread = lambda k, n, device: remote(
                acc.at[rpart(k)], rows_out.at[rpart(k)], fsend.at[n, k], frecv.at[n, k], device
            )
            self.spread_far = lambda k: spread(k, 0, at.far)
            self.spread_sib = lambda k: spread(k, 1, at.sib)
            self.spread_on = lambda k: remote(
                rows_out.at[rpart(k)], rows_out.at[rpart(k)], fsend.at[1, k], frecv.at[1, k], at.sib
            )
            self.gates = ReduceShards(
                at, lambda zp: gate.at[2 * zp + 1 - at.x], 2, gacc, gside, glow, ghigh,
                (gsend, grecv_side, grecv_low, grecv_high),
            )
            self.load_gate = [
                pltpu.make_async_copy(gate.at[2 * zp + at.x], gacc.at[zp], glocal.at[zp]) for zp in range(4)
            ]
            self.store_gate = pltpu.make_async_copy(gacc.at[at.z], gate_out, glocal.at[4])
            self.to_side = lambda k: remote(
                rows.at[1 - at.x, rpart(k)], side_v.at[rpart(k)], rsend.at[0, k], rrecv.at[0, k], at.side
            )
            self.to_up = lambda k: remote(
                acc.at[rpart(k)], low_v.at[rpart(k)], rsend.at[1, k], rrecv.at[1, k], at.up
            )
            self.to_down = lambda k: remote(
                acc.at[rpart(k)], high_v.at[rpart(k)], rsend.at[2, k], rrecv.at[2, k], at.down
            )

        def step(self, i, last):
            at = self.at

            @pl.when(i == 0)
            def _():
                at.greet()
                self.load_far.start()
                self.load_own.start()
                self.load_acc.start()
                for copy in self.load_gate:
                    copy.start()
                each_slice(lambda k: self.to_pass(k).start())
                each_slice(lambda k: self.to_sib(k).start())

            @pl.when(i < SLICES)
            def _():
                self.to_side(i).start()

            @pl.when(i == 1)
            def _():
                self.load_far.wait()
                self.load_own.wait()
                self.load_acc.wait()
                for copy in self.load_gate:
                    copy.wait()

            k = i - 1

            @pl.when((k >= 0) & (k < SLICES))
            def _():
                self.to_pass(k).wait_recv()
                add_into(self.far_v.at[self.part(k)], self.passed.at[self.part(k)], self.cut)
                self.to_far(k).start()

            m = i - SLICES

            @pl.when((m >= 0) & (m < SLICES))
            def _():
                self.to_sib(m).wait_recv()
                self.to_far(m).wait_recv()
                p = self.part(m)
                self.sum[p, :] = (
                    self.own[p, :].astype(f32) + self.sib[p, :].astype(f32) + self.got[p, :].astype(f32)
                )

            ends = jnp.where(at.z > 3 - at.z, at.z, 3 - at.z)
            chain = jnp.where(at.z < at.s, at.z, jnp.where(at.z > at.s, 3 - at.z, ends))
            r = i - 2 - 2 * chain

            @pl.when((r >= 0) & (r < SLICES))
            def _():
                acc = self.acc.at[self.rpart(r)]
                self.to_side(r).wait_recv()
                add_into(acc, self.side_v.at[self.rpart(r)], self.rcut)

                @pl.when((at.z <= at.s) & (at.z > 0))
                def _():
                    self.to_up(r).wait_recv()
                    add_into(acc, self.low_v.at[self.rpart(r)], self.rcut)

                @pl.when((at.z >= at.s) & (at.z < 3))
                def _():
                    self.to_down(r).wait_recv()
                    add_into(acc, self.high_v.at[self.rpart(r)], self.rcut)

                @pl.when(at.z < at.s)
                def _():
                    self.to_up(r).start()

                @pl.when(at.z > at.s)
                def _():
                    self.to_down(r).start()

                @pl.when(at.z == at.s)
                def _():
                    self.spread_far(r).start()
                    self.spread_sib(r).start()

            g = i - 6

            @pl.when((g >= 0) & (g < 8))
            def _():
                self.gates.side_copy(g).start()

            inner = jnp.where((at.z == 1) | (at.z == 2), 1, 0)
            g = i - 8 - inner

            @pl.when((g >= 0) & (g < 8))
            def _():
                self.gates.step(g)

            @pl.when(i == last)
            def _():
                @pl.when(inner == 1)
                def _():
                    self.gates.step(jnp.int32(7))

                self.store.start()
                self.store_gate.start()

                @pl.when(at.s == at.z)
                def _():
                    self.store_acc.start()

                def forward(k):
                    @pl.when(at.s_far == at.z)
                    def _():
                        self.spread_far(k).wait_recv()
                        self.spread_on(k).start()

                each_slice(forward)

                def finish(k):
                    @pl.when(at.s == at.z)
                    def _():
                        self.spread_far(k).wait_send()
                        self.spread_sib(k).wait_send()

                    @pl.when(at.s_far == at.z)
                    def _():
                        self.spread_on(k).wait_send()

                    @pl.when((at.s_sib == at.z) | (at.s_diag == at.z))
                    def _():
                        self.spread_on(k).wait_recv()

                    self.to_pass(k).wait_send()
                    self.to_sib(k).wait_send()
                    self.to_far(k).wait_send()
                    self.to_side(k).wait_send()

                    @pl.when(at.z < at.s)
                    def _():
                        self.to_up(k).wait_send()

                    @pl.when(at.z > at.s)
                    def _():
                        self.to_down(k).wait_send()

                each_slice(finish)
                self.gates.end()
                self.store.wait()
                self.store_gate.wait()

                @pl.when(at.s == at.z)
                def _():
                    self.store_acc.wait()

    return Traffic


def small_start(at, small, got, sems):
    send, recv = sems
    for k in range(1, 8):
        peer = (lax.rem(at.w + k, 8), at.s)
        remote(small, got.at[k], send.at[k], recv.at[k], peer).start()


def small_pass(at, small, got, total, full, sems, more):
    send, recv = sems
    send2, recv2, local = more
    value = small[...]
    for k in range(1, 8):
        remote(small, got.at[k], send.at[k], recv.at[k], at.side).wait_recv()
        value = value + got[k]
    total[...] = value
    pltpu.make_async_copy(total, full.at[at.s], local).start()
    for k, s in enumerate((at.s_sib, at.s_far, at.s_diag)):
        remote(total, full.at[at.s], send2.at[k], recv2.at[k], (at.w, s)).start()


def small_end(at, small, got, total, full, sems, more):
    send, recv = sems
    send2, recv2, local = more
    pltpu.make_async_copy(total, full.at[at.s], local).wait()
    for k in range(1, 8):
        remote(small, got.at[k], send.at[k], recv.at[k], at.side).wait_send()
    for k, s in enumerate((at.s_sib, at.s_far, at.s_diag)):
        remote(total, full.at[at.s], send2.at[k], recv2.at[k], (at.w, s)).wait_send()
        remote(total, full.at[s], send2.at[k], recv2.at[k], (at.w, s)).wait_recv()


def last_kernel(hid, d_gate, d_u, d_dt, w_main, w_com, gate_sum, small,
                back_sum, in_sum, sums_out,
                hid_v, dg_v, du_v, dt_v, wm_v, wc_v,
                b_diag, b_sib, b_far, b_own, from_sib, pass_sib, from_far,
                part_v, mside, mlow, mhigh, macc, mown, csib, cown, cacc, cside, clow, chigh, cfar, csum,
                sgot, stotal, sfull, *sems):
    at = Place()
    sems = list(sems)
    take = lambda n: [sems.pop(0) for _ in range(n)]
    load, bsem, msem, csem, cx, ssem, smore, asem, gsem = (
        take(6), take(2), take(4), take(4), take(7), take(2), take(3), take(3), take(3)
    )
    piece = hid_v.shape[0] // 4
    shard = hid_v.shape[1] // 8
    wide = dg_v.shape[1]
    half = shard // 2
    mine = pl.ds(pl.multiple_of(at.c * half, half), half)
    other = pl.ds(pl.multiple_of((1 - at.c) * half, half), half)
    at.greet(everyone=True)

    order = (at.s_diag, at.s_far, at.s_sib, at.s)
    rows_of = lambda s: pl.ds(pl.multiple_of(s * piece, piece), piece)
    weights = [
        pltpu.make_async_copy(w_main, wm_v, load[0].at[0]),
        pltpu.make_async_copy(w_com, wc_v, load[0].at[1]),
    ]
    loads = []
    for k, s in enumerate(order):
        r = rows_of(s)
        loads.append(
            [
                pltpu.make_async_copy(d_gate.at[r], dg_v.at[r], load[1].at[k]),
                pltpu.make_async_copy(d_u.at[r], du_v.at[r], load[2].at[k]),
                pltpu.make_async_copy(d_dt.at[r], dt_v.at[r], load[3].at[k]),
            ]
        )
    hid_load = pltpu.make_async_copy(hid, hid_v, load[4])
    for copy in loads[0] + weights + loads[1] + loads[2] + loads[3] + [hid_load]:
        copy.start()
    gate_slot = lambda s: in_sum.at[:, pl.ds(pl.multiple_of(s * wide, 128), wide)]
    x_slot = lambda s: in_sum.at[:, pl.ds(pl.multiple_of(E + s * wide, 128), wide)]
    gather_pieces_start(at, gate_sum, gate_slot, gsem)
    small_start(at, small, sgot, ssem)

    send, recv = bsem
    rows = piece // PARTS
    parts = [pl.ds(k * rows, rows) for k in range(PARTS)]
    to_pass = [remote(b_diag.at[p], pass_sib.at[p], send.at[0, k], recv.at[0, k], at.sib) for k, p in enumerate(parts)]
    to_sib = [remote(b_sib.at[p], from_sib.at[p], send.at[1, k], recv.at[1, k], at.sib) for k, p in enumerate(parts)]
    to_far = [remote(b_far.at[p], from_far.at[p], send.at[2, k], recv.at[2, k], at.far) for k, p in enumerate(parts)]

    def back_piece(s, out):
        base = s * piece

        def body(t, _):
            tile = pl.ds(pl.multiple_of(base + t * 256, 256), 256)
            place = pl.ds(pl.multiple_of(t * 256, 256), 256)
            for n in range(hid_v.shape[1] // 256):
                col = slice(256 * n, 256 * n + 256)
                total = dot_nt(dg_v[tile, :], wm_v[col, 0:wide])
                total = total + dot_nt(du_v[tile, 0:wide], wm_v[col, wide : 2 * wide])
                total = total + dot_nt(du_v[tile, wide : wide + 256], wc_v[col, 0:256])
                total = total + dot_nt(dt_v[tile, :], wc_v[col, 256:384])
                out[place, col] = total.astype(bf16)
            return 0

        lax.fori_loop(0, piece // 256, body, 0)

    big = ReduceShards(at, lambda zp: part_v.at[zp, 1 - at.x, :, pl.ds(0, wide)], 1, macc, mside, mlow, mhigh, msem)
    few = ReduceShards(at, lambda zp: cown.at[zp, 1 - at.x], 1, cacc, cside, clow, chigh, csem)
    com_cols = pl.ds(wide, 384)
    com_to_sib = lambda zp: remote(
        part_v.at[zp, :, other, com_cols], csib.at[zp], cx[0].at[zp], cx[1].at[zp], at.sib
    )

    def shard_pair(i):
        zp = far_first(at, i)
        lanes = pl.ds(pl.multiple_of(zp * 2 * shard, 128), 2 * shard)
        left = hid_v[:, lanes]
        tn = lambda right: lax.dot_general(left, right, (((0,), (0,)), ((), ())), preferred_element_type=f32)
        for n in range((wide + 256) // 256):
            col = slice(256 * n, 256 * n + 256)
            got = tn(du_v[:, col]).astype(bf16)
            part_v[zp, 0, :, col] = got[0:shard]
            part_v[zp, 1, :, col] = got[shard : 2 * shard]
        col = slice(wide + 256, wide + 384)
        got = tn(dt_v[...]).astype(bf16)
        part_v[zp, 0, :, col] = got[0:shard]
        part_v[zp, 1, :, col] = got[shard : 2 * shard]
        macc[zp] = part_v[zp, at.x, :, 0:wide]
        big.side_copy(i).start()
        com_to_sib(zp).start()

    def com_pair(i):
        zp = far_first(at, i)
        com_to_sib(zp).wait_recv()
        for x in range(2):
            cown[zp, x] = part_v[zp, x, mine, com_cols]
            add_into(cown.at[zp, x], csib.at[zp, x], half)
        cacc[zp] = cown[zp, at.x]
        few.side_copy(i).start()

    for copy in loads[0] + weights:
        copy.wait()
    back_piece(at.s_diag, b_diag)
    for copy in to_pass:
        copy.start()
    for copy in loads[1] + loads[2] + loads[3] + [hid_load]:
        copy.wait()
    shard_pair(0)
    back_piece(at.s_far, b_far)
    for k, p in enumerate(parts):
        to_pass[k].wait_recv()
        add_into(b_far.at[p], pass_sib.at[p], rows)
        to_far[k].start()
    com_pair(0)
    shard_pair(1)
    shard_pair(2)
    com_pair(1)
    big.step(0)
    few.step(0)
    gather_pieces_pass(at, gate_sum, gate_slot, gsem)
    shard_pair(3)
    com_pair(2)
    back_piece(at.s_sib, b_sib)
    for copy in to_sib:
        copy.start()
    com_pair(3)
    big.step(1)
    few.step(1)
    back_piece(at.s, b_own)
    big.step(2)
    few.step(2)
    small_pass(at, small, sgot, stotal, sfull, ssem, smore)
    big.step(3)
    few.step(3)
    mown[...] = macc[at.z]
    gather_pieces_start(at, mown, x_slot, asem)
    csum[...] = cacc[at.z]
    far_copy = remote(csum, cfar, cx[2], cx[3], at.far)
    far_copy.start()
    for k, p in enumerate(parts):
        to_sib[k].wait_recv()
        to_far[k].wait_recv()

        def body(i, _):
            r = pl.ds(pl.multiple_of(k * rows + i * 16, 16), 16)
            back_sum[r, :] = b_own[r, :].astype(f32) + from_sib[r, :].astype(f32) + from_far[r, :].astype(f32)
            return 0

        lax.fori_loop(0, rows // 16, body, 0)
    far_copy.wait()
    add_into(csum, cfar, half)
    com_out = in_sum.at[mine, pl.ds(2 * E, 384)]
    com_copy = remote(csum, com_out, cx[4], cx[5], at.sib)
    com_copy.start()
    keep_copy = pltpu.make_async_copy(csum, com_out, cx[6])
    keep_copy.start()
    gather_pieces_pass(at, mown, x_slot, asem)
    small_end(at, small, sgot, stotal, sfull, ssem, smore)
    sums_out[...] = jnp.zeros_like(sums_out)
    bc, heads = jnp.zeros((8, 256), f32), jnp.zeros((8, 128), f32)
    for s in range(4):
        sums_out[:, wide * s : wide * s + wide] = sfull[s, :, 0:wide]
        bc = bc + sfull[s, :, wide : wide + 256]
        shift = (wide // P_SIZE) * s
        own = sfull[s, :, 0:128]
        heads = heads + (pltpu.roll(own, shift, 1) if shift else own)
    sums_out[:, E : E + 256] = bc
    sums_out[:, E + 256 : E + 384] = heads
    for copy in to_pass + to_sib + to_far:
        copy.wait_send()
    for zp in range(4):
        com_to_sib(zp).wait_send()
    big.end()
    few.end()
    gather_pieces_end(at, gate_sum, gate_slot, gsem)
    gather_pieces_end(at, mown, x_slot, asem)
    keep_copy.wait()
    com_copy.wait_send()
    got = in_sum.at[other, pl.ds(2 * E, 384)]
    remote(csum, got, cx[4], cx[5], at.sib).wait_recv()


def finish_last(hid, d_gate, d_u, d_dt, w_main, w_com, gate_sum, small):
    length, depth = hid.shape
    piece, shard, half = length // 4, depth // 8, depth // 16
    wide = d_gate.shape[1]
    vm = pltpu.VMEM
    shards4 = [dma(3, 4), dma(4), dma(4), dma(4)]
    return pl.pallas_call(
        last_kernel,
        in_specs=[pl.BlockSpec(memory_space=ANY)] * 7 + [pl.BlockSpec(memory_space=pltpu.VMEM)],
        out_specs=[
            pl.BlockSpec(memory_space=pltpu.VMEM),
            pl.BlockSpec(memory_space=ANY),
            pl.BlockSpec(memory_space=pltpu.VMEM),
        ],
        out_shape=[
            jax.ShapeDtypeStruct((piece, depth), f32),
            jax.ShapeDtypeStruct((shard, 2 * E + 384), bf16),
            jax.ShapeDtypeStruct((8, E + 384), f32),
        ],
        scratch_shapes=[vm(v.shape, bf16) for v in (hid, d_gate, d_u, d_dt, w_main, w_com)]
        + [vm((piece, depth), bf16)] * 7
        + [vm((4, 2, shard, wide + 384), bf16)]
        + [vm((4, shard, wide), bf16)] * 4
        + [vm((shard, wide), bf16)]
        + [vm((4, 2, half, 384), bf16)] * 2
        + [vm((4, half, 384), bf16)] * 4
        + [vm((half, 384), bf16)] * 2
        + [vm((8,) + small.shape, f32), vm(small.shape, f32), vm((4,) + small.shape, f32)]
        + [dma(2), dma(4), dma(4), dma(4), dma(), dma()]
        + [dma(3, PARTS), dma(3, PARTS)]
        + shards4
        + shards4
        + [dma(4), dma(4), dma(), dma(), dma(), dma(), dma()]
        + [dma(8), dma(8)]
        + [dma(3), dma(3), dma()]
        + [dma(3, PARTS), dma(3, PARTS), dma()]
        + [dma(3, PARTS), dma(3, PARTS), dma()],
        compiler_params=pltpu.CompilerParams(
            collective_id=4, has_side_effects=True, vmem_limit_bytes=60 * 2**20
        ),
        name="finish_last",
    )(hid, d_gate, d_u, d_dt, w_main, w_com, gate_sum, small)


def over_rows(left, right):
    return lax.dot_general(
        left, right, (((0,), (0,)), ((), ())), preferred_element_type=jnp.float32
    )


def gather_plain(hid, main, com):
    hid_all = lax.all_gather(hid, "seq", axis=0)
    main_all = lax.all_gather(main, "wshard", axis=0)
    return hid_all, main_all, lax.all_gather(com, "wshard", axis=0)


def gather_more_plain(cot, rows, wide):
    cot_all = lax.all_gather(cot, "seq", axis=0)
    cols = lax.all_to_all(rows, "wshard", split_axis=1, concat_axis=0, tiled=True)
    own = lax.dynamic_slice_in_dim(cols, lax.axis_index("seq") * wide, wide, 0)
    return cot_all, lax.all_gather(own, "wshard", axis=1, tiled=True)


def reduce_scattered(v, axis):
    return lax.psum_scatter(v, axis, scatter_dimension=0, tiled=False)


def reduce_first_plain(layer, rows, gate):
    layer_sum = reduce_scattered(layer, "seq").astype(f32)
    rows = rows.reshape(-1, rows.shape[-1])
    part = lax.psum_scatter(rows, "wshard", scatter_dimension=1, tiled=True)
    part = lax.all_gather(part, "seq", axis=0, tiled=True)
    part = lax.all_to_all(part, "wshard", split_axis=0, concat_axis=1, tiled=True)
    return layer_sum, part, reduce_scattered(gate, "wshard")


def finish_plain(hid, d_gate, d_u, d_dt, w_main, w_com, gate_sum, small):
    groups, owners = lax.axis_size("seq"), lax.axis_size("wshard")
    wide = d_gate.shape[1]
    rest = jnp.concatenate([d_u, d_dt], axis=1)
    nt = lambda p, q: lax.dot_general(p, q, (((1,), (1,)), ((), ())), preferred_element_type=f32)
    back = nt(d_gate, w_main[:, :wide]) + nt(rest, jnp.concatenate([w_main[:, wide:], w_com], axis=1))
    back_sum = reduce_scattered(back.astype(bf16).reshape(groups, -1, D), "seq").astype(f32)
    part = reduce_scattered(over_rows(hid, rest).astype(bf16).reshape(owners, -1, rest.shape[1]), "wshard")
    part = lax.all_gather(jnp.concatenate([gate_sum, part], axis=1), "seq", axis=0)
    in_sum = jnp.concatenate(
        [part[i, :, :wide] for i in range(groups)]
        + [part[i, :, wide : 2 * wide] for i in range(groups)]
        + [jnp.sum(part[:, :, 2 * wide :].astype(f32), axis=0).astype(bf16)],
        axis=1,
    )
    full = lax.all_gather(lax.psum(small, "wshard"), "seq", axis=0)
    turned = [jnp.roll(full[i, :, :128], i * (wide // P_SIZE), axis=1) for i in range(groups)]
    sums = jnp.concatenate(
        [full[i, :, :wide] for i in range(groups)] + [jnp.sum(full[:, :, wide:], axis=0), sum(turned)], axis=1
    )
    return back_sum, in_sum, sums


def shards(
    hidden,
    segments,
    norm_gain,
    in_weight,
    conv_weight,
    conv_bias,
    step_bias,
    decay_log,
    skip_scale,
    gate_gain,
    out_weight,
    cotangent,
):
    group = lax.axis_index("seq")
    groups, owners = lax.axis_size("seq"), lax.axis_size("wshard")
    direct = (groups, owners) == (4, 8)
    heads = H // groups
    wide = heads * P_SIZE
    length = segments.shape[1]
    hidden_own, cot_own = hidden[0], cotangent[0]
    in_gain = norm_gain.astype(f32)[:, None]
    in_scaled = (in_weight.astype(f32) * in_gain).astype(bf16)
    main = jnp.concatenate(
        [
            lax.dynamic_slice_in_dim(in_scaled, group * wide, wide, 1),
            lax.dynamic_slice_in_dim(in_scaled, E + group * wide, wide, 1),
        ],
        axis=1,
    )
    com = jnp.pad(in_scaled[:, 2 * E :], ((0, 0), (0, 128 - H)))
    out_gain = gate_gain.astype(f32)[:, None]
    out_scaled = (out_weight.astype(f32) * out_gain).astype(bf16)
    gather = gather_first if direct else gather_plain
    hidden_all, w_main, w_com = gather(hidden_own, main, com)
    hidden_all = hidden_all.reshape(length, D)
    w_main, w_com = w_main.reshape(D, 2 * wide), w_com.reshape(D, -1)

    seg = segments[0]
    seg_col = jnp.pad(seg, (8, 8), constant_values=-1)[:, None]
    segr = seg.reshape(length // Q, 1, Q)
    par = jnp.pad(jnp.stack([step_bias, decay_log]), ((0, 6), (0, 128 - H)))
    skip = jnp.repeat(skip_scale, P_SIZE)[None]
    facts = (seg_col, segr, conv_weight, conv_bias[None], par, skip)
    beside, more = (forward_traffic(cot_own, out_scaled), (cot_own, out_scaled)) if direct else (NoTraffic, ())
    u, dt, gate, scale, mixed, save, *got = mixer_fwd(beside, more, hidden_all, w_main, w_com, *facts)
    cot_all, w_out = got if direct else gather_more_plain(cot_own, out_scaled, wide)
    cot_all, w_out = cot_all.reshape(length, D), w_out.reshape(wide, D)

    mixed_wide = mixed.astype(f32)
    sg = jax.nn.sigmoid(gate)
    silu = gate * sg
    g = mixed_wide * silu
    g_low = g.astype(bf16)
    a = lax.dot_general(cot_all, w_out, (((1,), (1,)), ((), ())), preferred_element_type=f32)
    sums = lax.psum(jnp.stack([jnp.sum(g * g, axis=1), jnp.sum(a * g, axis=1)]), "seq")
    r = lax.rsqrt(sums[0] / E + eps)[:, None]
    pull = (r * r * r) * (sums[1] / E)[:, None]
    d_g = r * a - g * pull
    d_mixed = (d_g * silu).astype(bf16)
    d_gate = (d_g * mixed_wide * (sg * (1.0 + gate * (1.0 - sg))) * scale).astype(bf16)
    layer_part = (jnp.dot(g_low, w_out, preferred_element_type=f32) * r).astype(bf16)
    cot_r = (cot_all.astype(f32) * r).astype(bf16)
    out_part = over_rows(g_low, cot_r).astype(bf16)

    gate_part = over_rows(hidden_all, d_gate).astype(bf16)

    layer_part, out_part = layer_part.reshape(groups, -1, D), out_part.reshape(2, -1, D)
    gate_part = gate_part.reshape(owners, -1, wide)
    more = (layer_part, out_part, gate_part) if direct else ()
    beside = backward_traffic(*more) if direct else NoTraffic
    du, ddt, small, *got = mixer_bwd(beside, more, u, dt, scale, *facts, save, d_mixed)
    layer_sum, out_sum, gate_sum = got if direct else reduce_first_plain(*(layer_part, out_part, gate_part))
    finish = finish_last if direct else finish_plain
    back_sum, in_sum, sums = finish(hidden_all, d_gate, du, ddt, w_main, w_com, gate_sum, small)

    own_wide = hidden_own.astype(f32)
    layer_output = own_wide + layer_sum
    own_scale = lax.rsqrt(jnp.mean(own_wide * own_wide, axis=-1, keepdims=True) + eps)
    hidden_grad = (
        cot_own.astype(f32)
        + back_sum
        - own_wide * (own_scale * own_scale) * jnp.mean(back_sum * own_wide, axis=-1, keepdims=True)
    )
    in_sum = in_sum[:, : 2 * E + 2 * N + H].astype(f32)
    in_weight_grad = in_sum * in_gain
    norm_gain_grad = jnp.sum(in_sum * in_weight.astype(f32), axis=1)
    out_sum = out_sum.astype(f32)
    out_weight_grad = out_sum * out_gain
    gate_gain_grad = jnp.sum(out_sum * out_weight.astype(f32), axis=1)
    chan, per_head = sums[:, : E + 2 * N], sums[:, E + 2 * N : E + 2 * N + H]
    return (
        layer_output[None],
        hidden_grad[None],
        norm_gain_grad,
        in_weight_grad,
        chan[:4],
        chan[4],
        per_head[5],
        per_head[6],
        per_head[7],
        gate_gain_grad,
        out_weight_grad,
    )


def solution(mesh):
    in_specs = (
        P("wshard", "seq", None),
        P("wshard", None),
        P("wshard"),
        P("wshard", None),
        P(),
        P(),
        P(),
        P(),
        P(),
        P("wshard"),
        P("wshard", None),
        P("wshard", "seq", None),
    )
    out_specs = (
        P("wshard", "seq", None),
        P("wshard", "seq", None),
        P("wshard"),
        P("wshard", None),
        P(),
        P(),
        P(),
        P(),
        P(),
        P("wshard"),
        P("wshard", None),
    )
    return jax.shard_map(shards, mesh=mesh, in_specs=in_specs, out_specs=out_specs, check_vma=False)
```

```python
import functools

import jax
import jax.numpy as jnp
from jax import lax
from jax.experimental import pallas as pl
from jax.experimental.pallas import tpu as pltpu
from jax.sharding import PartitionSpec as P

D = 1536
H = 48
P_SIZE = 64
N = 128
E = 3072

eps = 1e-05
f32, bf16 = jnp.float32, jnp.bfloat16
Q = 128
NEG = -1e30


def dot(a, b):
    return jnp.dot(a, b, preferred_element_type=f32)


def dot_nt(a, b):
    return lax.dot_general(a, b, (((1,), (1,)), ((), ())), preferred_element_type=f32)


def dot3(tri, v):
    hi = v.astype(bf16)
    rest = v - hi.astype(f32)
    mid = rest.astype(bf16)
    low = (rest - mid.astype(f32)).astype(bf16)
    return dot(tri, hi) + dot(tri, mid) + dot(tri, low)


def sigmoid(v):
    return 1.0 / (1.0 + jnp.exp(-v))


def spread_col(v, col):
    return jnp.broadcast_to(v[:, col : col + 1], (Q, 128))


def softplus(v):
    return jnp.maximum(v, 0.0) + jnp.log1p(jnp.exp(-jnp.abs(v)))


def conv_pre(useen, flags, wk, bias, lanes, chans):
    pre = bias[:, chans] + wk[3:4, chans] * useen[8 : 8 + Q, lanes]
    for j in (1, 2, 3):
        pre = pre + wk[3 - j : 4 - j, chans] * (useen[8 - j : 8 - j + Q, lanes] * flags[j])
    return pre


class Facts:
    def __init__(self, chunk, seg_ref, par_ref, xw):
        self.group = lax.axis_index("seq")
        self.heads = xw // P_SIZE
        self.xw = xw
        near = seg_ref[pl.ds(pl.multiple_of(chunk * Q, 8), Q + 16), :]
        now = near[8 : 8 + Q]
        same = lambda other: jnp.broadcast_to(jnp.where(other == now, 1.0, 0.0), (Q, 128))
        self.before = [None] + [same(near[8 - j : 8 - j + Q]) for j in (1, 2, 3)]
        self.after = lambda j: same(near[8 + j : 8 + j + Q])
        self.carried = same(near[7:8])
        self.samelast = same(near[7 + Q : 8 + Q])
        self.now = now
        self.turn = self.heads * self.group
        lane = lax.broadcasted_iota(jnp.int32, (8, 128), 1)
        par = self.own(par_ref[...])
        self.bias = par[0:1]
        self.rate = jnp.where(lane < self.heads, -jnp.exp(par), 0.0)[1:2]

    def own(self, v):
        lane = lax.broadcasted_iota(jnp.int32, v.shape, 1)
        return jnp.where(lane < self.heads, pltpu.roll(v, lax.rem(128 - self.turn, 128), 1), 0.0)

    def back(self, v):
        return pltpu.roll(v, self.turn, 1)

    def chans(self, p):
        if p < self.xw // 128:
            return pl.ds(pl.multiple_of(self.group * self.xw + 128 * p, 128), 128)
        at = E + 128 * (p - self.xw // 128)
        return slice(at, at + 128)


class NoTraffic:
    inputs, outputs, scratch, collective_id = (), (), (), None

    def __init__(self, *refs):
        pass

    def step(self, i, last):
        pass


def fwd_kernel(traffic, hid_ref, main_ref, com_ref, seg_ref, segr_ref, wk_ref, bias_ref, par_ref, skip_ref, *rest):
    n_in, n_out = len(traffic.inputs), len(traffic.outputs)
    extra_in, rest = rest[:n_in], rest[n_in:]
    u_ref, dt_ref, gate_ref, scale_ref, mixed_ref, save_ref = rest[:6]
    extra_out, rest = rest[6 : 6 + n_out], rest[6 + n_out :]
    state, useen, act, next_u, next_dt = rest[:5]
    step_no = pl.program_id(0)
    traffic(*extra_in, *extra_out, *rest[5:]).step(step_no, pl.num_programs(0) - 1)
    xw = mixed_ref.shape[1]
    width = xw + 256
    pairs = xw // 128
    facts = Facts(jnp.maximum(step_no - 1, 0), seg_ref, par_ref, xw)

    @pl.when(step_no == 0)
    def _():
        next_u[...] = jnp.zeros_like(next_u)
        next_dt[...] = jnp.zeros_like(next_dt)

    @pl.when(step_no <= 1)
    def _():
        state[...] = jnp.zeros_like(state)
        useen[0:8, :] = jnp.zeros((8, width), f32)

    useen[8 : 8 + Q, :] = next_u[...]
    dt_now = next_dt[...]

    low = hid_ref[...]
    total = jnp.zeros((Q, 128), f32)
    for k in range(low.shape[1] // 128):
        part = low[:, 128 * k : 128 * k + 128].astype(f32)
        total = total + part * part
    scale = lax.rsqrt(jnp.sum(total, axis=1, keepdims=True) / low.shape[1] + eps)
    scale_ref[...] = scale
    for k in range(xw // 256):
        gate_ref[:, 256 * k : 256 * k + 256] = dot(low, main_ref[:, 256 * k : 256 * k + 256]) * scale
    for k in range(xw // 256):
        got = (dot(low, main_ref[:, xw + 256 * k : xw + 256 * k + 256]) * scale).astype(bf16)
        u_ref[:, 256 * k : 256 * k + 256] = got
        next_u[:, 256 * k : 256 * k + 256] = got.astype(f32)
    got = (dot(low, com_ref[:, 0:256]) * scale).astype(bf16)
    u_ref[:, xw : xw + 256] = got
    next_u[:, xw : xw + 256] = got.astype(f32)
    got = facts.own((dot(low, com_ref[:, 256:384]) * scale).astype(bf16).astype(f32))
    dt_ref[...] = got.astype(bf16)
    next_dt[...] = got

    carried, samelast = facts.carried, facts.samelast
    for p in range(width // 128):
        lanes = slice(128 * p, 128 * p + 128)
        pre = conv_pre(useen, facts.before, wk_ref, bias_ref, lanes, facts.chans(p))
        act[:, lanes] = pre * sigmoid(pre)
    tail = useen[Q : Q + 8, :]
    useen[0:8, :] = tail

    step = softplus(dt_now + facts.bias)
    row = lax.broadcasted_iota(jnp.int32, (Q, Q), 0)
    col = lax.broadcasted_iota(jnp.int32, (Q, Q), 1)
    tri = jnp.where(row >= col, 1.0, 0.0).astype(bf16)
    decay = dot3(tri, step * facts.rate)
    decay_t = decay.T
    madd = jnp.where((row >= col) & (facts.now == segr_ref[0]), 0.0, NEG)
    b_now = act[:, xw : xw + 128]
    c_low = act[:, xw + 128 : xw + 256].astype(bf16)
    gram = dot_nt(c_low, b_now.astype(bf16))
    b_t = b_now.T.astype(bf16)
    left = lax.broadcasted_iota(jnp.int32, (Q, 128), 1) < 64
    for p in range(pairs):
        lanes = slice(128 * p, 128 * p + 128)
        d0, d1 = spread_col(decay, 2 * p), spread_col(decay, 2 * p + 1)
        dp = jnp.where(left, d0, d1)
        sp = jnp.where(left, spread_col(step, 2 * p), spread_col(step, 2 * p + 1))
        xs = act[:, lanes]
        xp = xs * sp
        m0 = gram * jnp.exp(d0 - decay_t[2 * p : 2 * p + 1, :] + madd)
        m1 = gram * jnp.exp(d1 - decay_t[2 * p + 1 : 2 * p + 2, :] + madd)
        both = jnp.concatenate([m0.astype(bf16), m1.astype(bf16)], axis=1)
        stacked = jnp.concatenate(
            [jnp.where(left, xp, 0.0).astype(bf16), jnp.where(left, 0.0, xp).astype(bf16)], axis=0
        )
        st = state[:, lanes]
        st_low = st.astype(bf16)
        save_ref[0, :, lanes] = st_low
        y = dot(both, stacked) + dot(c_low, st_low) * (jnp.exp(dp) * carried)
        mixed_ref[:, lanes] = (y + skip_ref[:, facts.chans(p)] * xs).astype(bf16)
        last = dp[Q - 1 : Q, :]
        to_end = (xp * (jnp.exp(last - dp) * samelast)).astype(bf16)
        state[:, lanes] = st * (jnp.exp(last) * carried[Q - 1 : Q, :]) + dot(b_t, to_end)


def mixer_fwd(traffic, extra, hid, main, com, seg, segr, wk, bias, par, skip):
    length, depth = hid.shape
    xw = main.shape[1] // 2
    width = xw + 256
    n = length // Q
    whole = lambda shape: pl.BlockSpec(shape, lambda i: (0,) * len(shape), pipeline_mode=pl.Buffered(1))
    ahead = lambda i: (jnp.minimum(i, n - 1), 0)
    now = lambda i: (jnp.maximum(i - 1, 0), 0)
    now3 = lambda i: (jnp.maximum(i - 1, 0), 0, 0)
    return pl.pallas_call(
        functools.partial(fwd_kernel, traffic),
        grid=(n + 1,),
        in_specs=[
            pl.BlockSpec((Q, depth), ahead),
            whole(main.shape),
            whole(com.shape),
            whole(seg.shape),
            pl.BlockSpec((1, 1, Q), now3),
            whole(wk.shape),
            whole(bias.shape),
            whole(par.shape),
            whole(skip.shape),
        ]
        + [pl.BlockSpec(memory_space=pl.ANY)] * len(extra),
        out_specs=[
            pl.BlockSpec((Q, width), ahead),
            pl.BlockSpec((Q, 128), ahead),
            pl.BlockSpec((Q, xw), ahead),
            pl.BlockSpec((Q, 1), ahead),
            pl.BlockSpec((Q, xw), now),
            pl.BlockSpec((1, 128, xw), now3),
        ]
        + [pl.BlockSpec(memory_space=pl.ANY)] * len(traffic.outputs),
        out_shape=[
            jax.ShapeDtypeStruct((length, width), bf16),
            jax.ShapeDtypeStruct((length, 128), bf16),
            jax.ShapeDtypeStruct((length, xw), f32),
            jax.ShapeDtypeStruct((length, 1), f32),
            jax.ShapeDtypeStruct((length, xw), bf16),
            jax.ShapeDtypeStruct((n, 128, xw), bf16),
            *traffic.outputs,
        ],
        scratch_shapes=[
            pltpu.VMEM((128, xw), f32),
            pltpu.VMEM((Q + 8, width), f32),
            pltpu.VMEM((Q, width), f32),
            pltpu.VMEM((Q, width), f32),
            pltpu.VMEM((Q, 128), f32),
            *traffic.scratch,
        ],
        compiler_params=pltpu.CompilerParams(
            vmem_limit_bytes=48 * 2**20,
            collective_id=traffic.collective_id,
            has_side_effects=traffic.collective_id is not None,
        ),
        name="mixer_forward",
    )(hid, main, com, seg, segr, wk, bias, par, skip, *extra)


def bwd_kernel(traffic, u_ref, halo_ref, dt_ref, scale_ref, seg_ref, segr_ref, wk_ref, bias_ref, par_ref, skip_ref,
               save_ref, dy_ref, *rest):
    n_in, n_out = len(traffic.inputs), len(traffic.outputs)
    extra_in, rest = rest[:n_in], rest[n_in:]
    du_ref, ddt_ref, small_ref = rest[:3]
    extra_out, rest = rest[3 : 3 + n_out], rest[3 + n_out :]
    dstate, useen, act, slope, dpre, keep_y, keep_x, prod_a, prod_b, rows_a, held = rest[:11]
    wgrad_ref, hgrad_ref, sgrad_ref, spot_ref = rest[11:15]
    step_no = pl.program_id(0)
    last_step = pl.num_programs(0) - 1
    traffic(*extra_in, *extra_out, *rest[15:]).step(step_no, last_step)
    width = u_ref.shape[1]
    xw = width - 256
    pairs = xw // 128

    @pl.when(step_no == 0)
    def _():
        dstate[...] = jnp.zeros_like(dstate)
        dpre[Q : Q + 8, :] = jnp.zeros((8, width), f32)
        wgrad_ref[...] = jnp.zeros_like(wgrad_ref)
        hgrad_ref[...] = jnp.zeros_like(hgrad_ref)
        sgrad_ref[...] = jnp.zeros_like(sgrad_ref)
        rows_a[...] = jnp.zeros_like(rows_a)
        head_of = lax.broadcasted_iota(jnp.int32, (xw, 128), 0) // P_SIZE
        mark = head_of == lax.broadcasted_iota(jnp.int32, (xw, 128), 1)
        spot_ref[...] = jnp.where(mark, 1.0, 0.0).astype(bf16)

    useen[0:8, :] = halo_ref[...].astype(f32)[8:16, :]
    useen[8 : 8 + Q, :] = u_ref[...].astype(f32)
    facts = Facts(last_step - step_no, seg_ref, par_ref, xw)
    flags, carried, samelast = facts.before, facts.carried, facts.samelast
    for p in range(width // 128):
        lanes = slice(128 * p, 128 * p + 128)
        pre = conv_pre(useen, flags, wk_ref, bias_ref, lanes, facts.chans(p))
        sg = sigmoid(pre)
        act[:, lanes] = pre * sg
        slope[:, lanes] = sg * (1.0 + pre * (1.0 - sg))

    raw = dt_ref[...].astype(f32) + facts.bias
    step = softplus(raw)
    rate = facts.rate
    row = lax.broadcasted_iota(jnp.int32, (Q, Q), 0)
    col = lax.broadcasted_iota(jnp.int32, (Q, Q), 1)
    tri = jnp.where(row >= col, 1.0, 0.0).astype(bf16)
    upper = jnp.where(row <= col, 1.0, 0.0).astype(bf16)
    below = jnp.where(row > col, 1.0, 0.0).astype(bf16)
    decay = dot3(tri, step * rate)
    decay_t = decay.T
    madd = jnp.where((row <= col) & (facts.now == segr_ref[0]), 0.0, NEG)
    b_now, c_now = act[:, xw : xw + 128], act[:, xw + 128 : xw + 256]
    b_low, c_low = b_now.astype(bf16), c_now.astype(bf16)
    c_t = c_now.T.astype(bf16)
    gram = dot_nt(b_low, c_low)
    left = lax.broadcasted_iota(jnp.int32, (Q, 128), 1) < 64
    lane = lax.broadcasted_iota(jnp.int32, (Q, 128), 1)
    dgram = jnp.zeros((Q, Q), f32)
    cols_b = jnp.zeros((Q, 128), f32)
    for p in range(pairs):
        lanes = slice(128 * p, 128 * p + 128)
        d0, d1 = spread_col(decay, 2 * p), spread_col(decay, 2 * p + 1)
        dp = jnp.where(left, d0, d1)
        sp = jnp.where(left, spread_col(step, 2 * p), spread_col(step, 2 * p + 1))
        xs = act[:, lanes]
        xp = xs * sp
        dy_low = dy_ref[:, lanes]
        dy = dy_low.astype(f32)
        stacked = jnp.concatenate(
            [jnp.where(left, dy, 0.0).astype(bf16), jnp.where(left, 0.0, dy).astype(bf16)], axis=0
        )
        pair = dot_nt(xp.astype(bf16), stacked)
        mts = []
        for k, dk in ((0, d0), (1, d1)):
            h = 2 * p + k
            e = jnp.exp(decay_t[h : h + 1, :] - dk + madd)
            f = e * pair[:, 128 * k : 128 * k + 128]
            dgram = dgram + f
            w = gram * f
            mts.append((gram * e).astype(bf16))
            rows_a[h : h + 1, :] = jnp.sum(w, axis=0, keepdims=True)
            cols_b = jnp.where(lane == h, jnp.sum(w, axis=1, keepdims=True), cols_b)
        within = dot(jnp.concatenate(mts, axis=1), stacked)
        grow = jnp.exp(dp) * carried
        dy_in = dy * grow
        dy_in_low = dy_in.astype(bf16)
        keep_y[:, lanes] = dy_in_low
        st = save_ref[0, :, lanes]
        prod_a[:, lanes] = (dy_in * dot(c_low, st)).astype(bf16)
        last = dp[Q - 1 : Q, :]
        fade = jnp.exp(last - dp) * samelast
        ds = dstate[:, lanes]
        ds_low = ds.astype(bf16)
        xe = xp * fade
        keep_x[:, lanes] = xe.astype(bf16)
        later = dot(b_low, ds_low)
        prod_b[:, lanes] = (xe * later).astype(bf16)
        retain = jnp.exp(last) * carried[Q - 1 : Q, :]
        held[0:1, lanes] = jnp.sum(ds * st.astype(f32), axis=0, keepdims=True) * retain
        dxs = sp * (within + later * fade) + skip_ref[:, facts.chans(p)] * dy
        skp = xs * dy
        sgrad_ref[:, lanes] += jnp.sum(skp.reshape(Q // 8, 8, 128), axis=0)
        dpre[0:Q, lanes] = dxs * slope[:, lanes]
        dstate[:, lanes] = ds * retain + dot(c_t, dy_in_low)
        if p == 0:
            db_in, dc_in = dot_nt(keep_x[:, lanes], ds_low), dot_nt(dy_in_low, st)
        else:
            db_in, dc_in = db_in + dot_nt(keep_x[:, lanes], ds_low), dc_in + dot_nt(dy_in_low, st)

    dg_low = dgram.astype(bf16)
    db = dot(dg_low, c_low) + db_in
    dc = dot(dgram.T.astype(bf16), b_low) + dc_in
    dpre[0:Q, xw : xw + 128] = db * slope[:, xw : xw + 128]
    dpre[0:Q, xw + 128 : xw + 256] = dc * slope[:, xw + 128 : xw + 256]

    spot = spot_ref[...]
    a_in = dot(prod_a[...], spot)
    b_in = dot(prod_b[...], spot)
    hv = jnp.broadcast_to(held[0:1, :], (8, xw))
    h_hi = hv.astype(bf16)
    h_lo = (hv - h_hi.astype(f32)).astype(bf16)
    through = (dot(h_hi, spot) + dot(h_lo, spot))[0:1, :]
    a_own = rows_a[...].T
    cross = dot3(upper, a_own - cols_b + a_in) + dot3(below, b_in) + through
    total = cols_b + b_in
    sg = sigmoid(raw)
    ratio = jnp.where(step > 1e-30, sg / jnp.maximum(step, 1e-30), 1.0)
    draw = total * ratio + rate * cross * sg
    scale = jnp.broadcast_to(scale_ref[...], (Q, 128))
    ddt_ref[...] = facts.back(draw * scale).astype(bf16)
    hgrad_ref[0:8, :] += jnp.sum(draw.reshape(Q // 8, 8, 128), axis=0)
    hgrad_ref[8:16, :] += jnp.sum((step * cross).reshape(Q // 8, 8, 128), axis=0)

    ahead = [None] + [facts.after(j) for j in (1, 2, 3)]
    for p in range(width // 128):
        lanes = slice(128 * p, 128 * p + 128)
        own = dpre[0:Q, lanes]
        chans = facts.chans(p)
        du = wk_ref[3:4, chans] * own
        wgrad_ref[24:32, lanes] += jnp.sum((own * useen[8 : 8 + Q, lanes]).reshape(Q // 8, 8, 128), axis=0)
        wgrad_ref[32:40, lanes] += jnp.sum(own.reshape(Q // 8, 8, 128), axis=0)
        for j in (1, 2, 3):
            du = du + wk_ref[3 - j : 4 - j, chans] * (dpre[j : j + Q, lanes] * ahead[j])
            moved = own * (useen[8 - j : 8 - j + Q, lanes] * flags[j])
            k = 3 - j
            wgrad_ref[8 * k : 8 * k + 8, lanes] += jnp.sum(moved.reshape(Q // 8, 8, 128), axis=0)
        du_ref[:, lanes] = (du * scale).astype(bf16)
    first = dpre[0:8, :]
    dpre[Q : Q + 8, :] = first

    @pl.when(step_no == last_step)
    def _():
        small_ref[...] = jnp.zeros_like(small_ref)
        for k in range(5):
            small_ref[k : k + 1, :] = jnp.sum(wgrad_ref[8 * k : 8 * k + 8, :], axis=0, keepdims=True)
        small_ref[5:6, 0:128] = jnp.sum(hgrad_ref[0:8, :], axis=0, keepdims=True)
        small_ref[6:7, 0:128] = rate * jnp.sum(hgrad_ref[8:16, :], axis=0, keepdims=True)
        skips = sgrad_ref[...]
        hi = skips.astype(bf16)
        mid = (skips - hi.astype(f32)).astype(bf16)
        by_head = dot(hi, spot_ref[...]) + dot(mid, spot_ref[...])
        small_ref[7:8, 0:128] = jnp.sum(by_head, axis=0, keepdims=True)


def mixer_bwd(traffic, extra, u, dt, scale, seg, segr, wk, bias, par, skip, save, dy):
    length, width = u.shape
    xw = width - 256
    n = length // Q
    whole = lambda shape: pl.BlockSpec(shape, lambda i: (0,) * len(shape))
    back = lambda i: (n - 1 - i, 0)
    return pl.pallas_call(
        functools.partial(bwd_kernel, traffic),
        grid=(n,),
        in_specs=[
            pl.BlockSpec((Q, width), back),
            pl.BlockSpec((16, width), lambda i: (jnp.maximum((n - 1 - i) * (Q // 16) - 1, 0), 0)),
            pl.BlockSpec((Q, 128), back),
            pl.BlockSpec((Q, 1), back),
            whole(seg.shape),
            pl.BlockSpec((1, 1, Q), lambda i: (n - 1 - i, 0, 0)),
            whole(wk.shape),
            whole(bias.shape),
            whole(par.shape),
            whole(skip.shape),
            pl.BlockSpec((1, 128, xw), lambda i: (n - 1 - i, 0, 0)),
            pl.BlockSpec((Q, xw), back),
        ]
        + [pl.BlockSpec(memory_space=pl.ANY)] * len(extra),
        out_specs=[
            pl.BlockSpec((Q, width), back),
            pl.BlockSpec((Q, 128), back),
            whole((8, width)),
        ]
        + [pl.BlockSpec(memory_space=pl.ANY)] * len(traffic.outputs),
        out_shape=[
            jax.ShapeDtypeStruct((length, width), bf16),
            jax.ShapeDtypeStruct((length, 128), bf16),
            jax.ShapeDtypeStruct((8, width), f32),
            *traffic.outputs,
        ],
        scratch_shapes=[
            pltpu.VMEM((128, xw), f32),
            pltpu.VMEM((Q + 8, width), f32),
            pltpu.VMEM((Q, width), f32),
            pltpu.VMEM((Q, width), f32),
            pltpu.VMEM((Q + 8, width), f32),
            pltpu.VMEM((Q, xw), bf16),
            pltpu.VMEM((Q, xw), bf16),
            pltpu.VMEM((Q, xw), bf16),
            pltpu.VMEM((Q, xw), bf16),
            pltpu.VMEM((128, 128), f32),
            pltpu.VMEM((8, xw), f32),
            pltpu.VMEM((40, width), f32),
            pltpu.VMEM((16, 128), f32),
            pltpu.VMEM((8, xw), f32),
            pltpu.VMEM((xw, 128), bf16),
            *traffic.scratch,
        ],
        compiler_params=pltpu.CompilerParams(
            vmem_limit_bytes=48 * 2**20,
            collective_id=traffic.collective_id,
            has_side_effects=traffic.collective_id is not None,
        ),
        name="mixer_backward",
    )(u, u, dt, scale, seg, segr, wk, bias, par, skip, save, dy, *extra)


MESH = pl.DeviceIdType.MESH
ANY = pl.ANY
PARTS = 4


def remote(src, dst, send_sem, recv_sem, device):
    return pltpu.make_async_remote_copy(
        src_ref=src, dst_ref=dst, send_sem=send_sem, recv_sem=recv_sem, device_id=device, device_id_type=MESH
    )


class Place:
    def __init__(self):
        self.w, self.s = lax.axis_index("wshard"), lax.axis_index("seq")
        self.z, self.x = self.w // 2, lax.rem(self.w, 2)
        self.y, self.c = self.s // 2, lax.rem(self.s, 2)
        self.s_sib = 2 * self.y + 1 - self.c
        self.s_far = 2 * (1 - self.y) + self.c
        self.s_diag = 2 * (1 - self.y) + 1 - self.c
        self.side = (2 * self.z + 1 - self.x, self.s)
        self.up = (lax.rem(self.w + 2, 8), self.s)
        self.down = (lax.rem(self.w + 6, 8), self.s)
        self.sib = (self.w, self.s_sib)
        self.far = (self.w, self.s_far)

    def greet(self, everyone=False):
        barrier = pltpu.get_barrier_semaphore()
        others = [(lax.rem(self.w + k, 8), self.s) for k in range(1, 8)] if everyone else []
        if everyone:
            others += [(self.w, lax.rem(self.s + k, 4)) for k in range(1, 4)]
        else:
            others = [self.side, self.up, self.down, self.sib, self.far]
        for other in others:
            pl.semaphore_signal(barrier, inc=1, device_id=other, device_id_type=MESH)
        pl.semaphore_wait(barrier, len(others))


def dma(*shape):
    return pltpu.SemaphoreType.DMA(shape)


def gather_pieces_start(at, own, slot, sems, stage=None):
    send, recv, local = sems[:3]
    rows = own.shape[0] // PARTS
    for k in range(PARTS):
        part = pl.ds(k * rows, rows)
        remote(own.at[part], slot(at.s).at[part], send.at[1, k], recv.at[1, k], at.far).start()
    for k in range(PARTS):
        part = pl.ds(k * rows, rows)
        remote(own.at[part], slot(at.s).at[part], send.at[0, k], recv.at[0, k], at.sib).start()
    if stage is not None:
        copy = pltpu.make_async_copy(own, stage, local)
        copy.start()
        copy.wait()
    pltpu.make_async_copy(own if stage is None else stage, slot(at.s), local).start()


def gather_pieces_pass(at, own, slot, sems):
    send, recv, _ = sems
    rows = own.shape[0] // PARTS
    for k in range(PARTS):
        part = pl.ds(k * rows, rows)
        theirs = slot(at.s_far).at[part]
        remote(theirs, theirs, send.at[1, k], recv.at[1, k], at.far).wait_recv()
        remote(theirs, theirs, send.at[2, k], recv.at[2, k], at.sib).start()


def gather_pieces_end(at, own, slot, sems):
    send, recv, local = sems
    rows = own.shape[0] // PARTS
    pltpu.make_async_copy(own, slot(at.s), local).wait()
    for k in range(PARTS):
        part = pl.ds(k * rows, rows)
        sib, diag, far = slot(at.s_sib).at[part], slot(at.s_diag).at[part], slot(at.s_far).at[part]
        remote(own.at[part], slot(at.s).at[part], send.at[0, k], recv.at[0, k], at.sib).wait_send()
        remote(own.at[part], slot(at.s).at[part], send.at[1, k], recv.at[1, k], at.far).wait_send()
        remote(far, far, send.at[2, k], recv.at[2, k], at.sib).wait_send()
        remote(sib, sib, send.at[0, k], recv.at[0, k], at.sib).wait_recv()
        remote(diag, diag, send.at[2, k], recv.at[2, k], at.sib).wait_recv()


CUTS = 2


def gather_shards(at, main, com, main_all, com_all, stage, sems, between):
    send, recv, csend, crecv, psend, precv, local = sems
    half, cut = com.shape[0] // 2, main.shape[0] // CUTS
    mine = pl.ds(pl.multiple_of(at.c * half, half), half)
    load = pltpu.make_async_copy(main, stage[0], local.at[0])
    com_load = pltpu.make_async_copy(com, stage[1], local.at[1])
    keep = pltpu.make_async_copy(stage[0], main_all.at[at.w], local.at[0])
    com_keep = pltpu.make_async_copy(stage[1], com_all.at[at.w], local.at[1])

    def hop(zp, q, way, device, own=False):
        w, n, part = 2 * zp + at.x, zp * CUTS + q, pl.ds(q * cut, cut)
        slot, com_slot = main_all.at[w, part], com_all.at[w, mine]
        copies = [remote(main.at[part] if own else slot, slot, send.at[way, n], recv.at[w * CUTS + q], device)]
        if q == 0:
            copies.append(remote(com.at[mine] if own else com_slot, com_slot, csend.at[way, zp], crecv.at[w], device))
        return copies

    def begin(copies):
        for copy in copies:
            copy.start()

    def sent(copies):
        for copy in copies:
            copy.wait_send()

    def all_ways(act, q):
        act(hop(at.z, q, 0, at.side, True))

        @pl.when(at.z < 3)
        def _():
            act(hop(at.z, q, 1, at.up, True))

        @pl.when(at.z > 0)
        def _():
            act(hop(at.z, q, 2, at.down, True))

    def arrived(w, q):
        slot = main_all.at[w, pl.ds(q * cut, cut)]
        remote(slot, slot, send.at[0, 0], recv.at[w * CUTS + q], at.side).wait_recv()
        if q == 0:
            held = com_all.at[w, mine]
            remote(held, held, csend.at[0, 0], crecv.at[w], at.side).wait_recv()
            remote(held, held, psend.at[w], precv.at[w], at.sib).start()

    for q in range(CUTS):
        if q > 0:
            all_ways(sent, q - 1)
        all_ways(begin, q)
        if q == 0:
            load.start()
            com_load.start()
            load.wait()
            com_load.wait()
            keep.start()
            com_keep.start()
    for d in (1, 2, 3):
        if d == 3:
            between()
        for q in range(CUTS):

            @pl.when(at.z - d >= 0)
            def _():
                zp = at.z - d
                arrived(2 * zp + at.x, q)

                @pl.when(at.z < 3)
                def _():
                    begin(hop(zp, q, 1, at.up))

                begin(hop(zp, q, 0, at.side))

            @pl.when(at.z + d <= 3)
            def _():
                zp = at.z + d
                arrived(2 * zp + at.x, q)

                @pl.when(at.z > 0)
                def _():
                    begin(hop(zp, q, 2, at.down))

                begin(hop(zp, q, 0, at.side))

    for zp in range(4):
        for q in range(CUTS):
            arrived(2 * zp + 1 - at.x, q)
    keep.wait()
    com_keep.wait()
    all_ways(sent, CUTS - 1)
    for zp in range(4):
        for q in range(CUTS):

            @pl.when(at.z != zp)
            def _():
                sent(hop(zp, q, 0, at.side))

            @pl.when((at.z < 3) & (zp < at.z))
            def _():
                sent(hop(zp, q, 1, at.up))

            @pl.when((at.z > 0) & (zp > at.z))
            def _():
                sent(hop(zp, q, 2, at.down))

    other = pl.ds(pl.multiple_of((1 - at.c) * half, half), half)
    for k in range(1, 8):
        w = lax.rem(at.w + k, 8)
        gone, got = com_all.at[w, mine], com_all.at[w, other]
        remote(gone, gone, psend.at[w], precv.at[w], at.sib).wait_send()
        remote(got, got, psend.at[w], precv.at[w], at.sib).wait_recv()


def gather_kernel(hid, main, com, hid_all, main_all, com_all, hid_v, main_v, com_v, *sems):
    at = Place()
    at.greet()
    slot = lambda s: hid_all.at[s]
    gather_pieces_start(at, hid, slot, sems[0:3], hid_v)
    pass_on = lambda: gather_pieces_pass(at, hid, slot, sems[0:3])
    gather_shards(at, main, com, main_all, com_all, (main_v, com_v), sems[3:10], pass_on)
    gather_pieces_end(at, hid, slot, sems[0:3])


def gather_first(hid, main, com):
    shape = lambda n, v: jax.ShapeDtypeStruct((n,) + v.shape, v.dtype)
    return pl.pallas_call(
        gather_kernel,
        in_specs=[pl.BlockSpec(memory_space=ANY)] * 3,
        out_specs=[pl.BlockSpec(memory_space=ANY)] * 3,
        out_shape=[shape(4, hid), shape(8, main), shape(8, com)],
        scratch_shapes=[pltpu.VMEM(v.shape, v.dtype) for v in (hid, main, com)]
        + [dma(3, PARTS), dma(3, PARTS), dma()]
        + [dma(3, 4 * CUTS), dma(8 * CUTS), dma(3, 4), dma(8), dma(8), dma(8), dma(2)],
        compiler_params=pltpu.CompilerParams(collective_id=1, has_side_effects=True),
        name="gather_first",
    )(hid, main, com)


SLICES = 8


def each_slice(body):
    def run(k, _):
        body(k)
        return 0

    lax.fori_loop(0, SLICES, run, 0)


def forward_traffic(cot, rows):
    class Traffic:
        inputs = (cot, rows)
        outputs = (
            jax.ShapeDtypeStruct((4,) + cot.shape, cot.dtype),
            jax.ShapeDtypeStruct((2,) + rows.shape, rows.dtype),
        )
        scratch = (
            pltpu.VMEM(cot.shape, cot.dtype),
            pltpu.VMEM(rows.shape, rows.dtype),
            dma(3, SLICES),
            dma(3, SLICES),
            dma(),
            dma(3, SLICES),
            dma(2, SLICES),
            dma(),
        )
        collective_id = 2

        def __init__(self, own, row_own, full, row_full, stage, rstage, send, recv, local, rsend, rrecv, rlocal):
            self.at = at = Place()
            self.own, self.full, self.row_own, self.row_full = own, full, row_own, row_full
            self.rrecv = rrecv
            cut, rcut = own.shape[0] // SLICES, row_own.shape[0] // SLICES
            part = lambda k: pl.ds(pl.multiple_of(k * cut, cut), cut)
            rpart = lambda k: pl.ds(pl.multiple_of(k * rcut, rcut), rcut)
            piece = lambda s, k: full.at[s, part(k)]
            self.load = pltpu.make_async_copy(own, stage, local)
            self.keep = pltpu.make_async_copy(stage, full.at[at.s], local)
            self.rload = pltpu.make_async_copy(row_own, rstage, rlocal)
            self.rkeep = pltpu.make_async_copy(rstage, row_full.at[at.x], rlocal)
            self.to_sib = lambda k: remote(own.at[part(k)], piece(at.s, k), send.at[0, k], recv.at[0, k], at.sib)
            self.to_far = lambda k: remote(own.at[part(k)], piece(at.s, k), send.at[1, k], recv.at[1, k], at.far)
            self.pass_on = lambda k: remote(piece(at.s_far, k), piece(at.s_far, k), send.at[2, k], recv.at[2, k], at.sib)
            here = lambda k, n, device: remote(
                row_full.at[at.x, rpart(k)], row_full.at[at.x, rpart(k)], rsend.at[n, k], rrecv.at[at.x, k], device
            )
            self.rows = (lambda k: here(k, 0, at.side), lambda k: here(k, 1, at.up), lambda k: here(k, 2, at.down))
            got = lambda s, n, k: remote(piece(s, k), piece(s, k), send.at[n, k], recv.at[n, k], at.sib)
            self.from_sib = lambda k: got(at.s_sib, 0, k)
            self.from_far = lambda k: got(at.s_far, 1, k)
            self.from_diag = lambda k: got(at.s_diag, 2, k)
            other = lambda k: row_full.at[1 - at.x, rpart(k)]
            self.from_side = lambda k: remote(other(k), other(k), rsend.at[0, k], rrecv.at[1 - at.x, k], at.side)

        def step(self, i, last):
            at = self.at
            upward, downward = (at.z >= at.s) & (at.z < 3), (at.z <= at.s) & (at.z > 0)
            side, up, down = self.rows

            @pl.when(i == 0)
            def _():
                at.greet()
                self.load.start()
                each_slice(lambda k: self.to_sib(k).start())

                @pl.when(at.z == at.s)
                def _():
                    self.rload.start()
                    self.rload.wait()
                    self.rkeep.start()
                    self.rkeep.wait()

                self.load.wait()
                self.keep.start()

            k = i - 1

            @pl.when((k >= 0) & (k < SLICES))
            def _():
                self.to_far(k).start()

            @pl.when((k >= SLICES) & (k < 2 * SLICES))
            def _():
                self.from_far(k - SLICES).wait_recv()
                self.pass_on(k - SLICES).start()

            far_away = jnp.where(at.z > at.s, at.z - at.s, at.s - at.z)
            v = 3 * i - 6 * far_away + 1
            r = jnp.where(v >= 0, lax.div(v, 4), -1)

            @pl.when((r >= 0) & (r < SLICES) & (4 * r < v))
            def _():
                @pl.when(at.z != at.s)
                def _():
                    side(r).wait_recv()

                side(r).start()

                @pl.when(upward)
                def _():
                    up(r).start()

                @pl.when(downward)
                def _():
                    down(r).start()

            @pl.when(i == last)
            def _():
                self.keep.wait()

                def finish(k):
                    self.to_sib(k).wait_send()
                    self.to_far(k).wait_send()
                    self.pass_on(k).wait_send()
                    self.from_sib(k).wait_recv()
                    self.from_diag(k).wait_recv()
                    side(k).wait_send()
                    self.from_side(k).wait_recv()

                    @pl.when(upward)
                    def _():
                        up(k).wait_send()

                    @pl.when(downward)
                    def _():
                        down(k).wait_send()

                each_slice(finish)

    return Traffic


def add_into(dst, src, rows):
    step = next(n for n in (64, 48, 32, 16) if rows % n == 0)

    def body(i, _):
        part = pl.ds(pl.multiple_of(i * step, 16), step)
        dst[part, :] = (dst[part, :].astype(f32) + src[part, :].astype(f32)).astype(bf16)
        return 0

    lax.fori_loop(0, rows // step, body, 0)


def far_first(at, i):
    inner = (at.z == 1) | (at.z == 2)
    i = jnp.where(inner & (i >= 2), 5 - i, i)
    return jnp.where(at.z < 2, 3 - i, i)


class ReduceShards:
    def __init__(self, at, partial, cuts, acc, from_side, from_down, from_up, sems):
        self.at, self.partial, self.cuts, self.acc = at, partial, cuts, acc
        self.from_side, self.from_down, self.from_up = from_side, from_down, from_up
        self.send, self.recv_side, self.recv_down, self.recv_up = sems
        self.rows = acc.shape[1] // cuts

    def unit(self, j):
        if isinstance(j, int):
            shard, cut = j // self.cuts, j % self.cuts
        else:
            shard, cut = lax.div(j, self.cuts), lax.rem(j, self.cuts)
        zp = far_first(self.at, shard)
        return zp, zp * self.cuts + cut, pl.ds(pl.multiple_of(cut * self.rows, self.rows), self.rows)

    def side_copy(self, j):
        at = self.at
        zp, n, part = self.unit(j)
        return remote(
            self.partial(zp).at[part], self.from_side.at[zp, part],
            self.send.at[0, n], self.recv_side.at[n], at.side,
        )

    def up_copy(self, j):
        zp, n, part = self.unit(j)
        return remote(
            self.acc.at[zp, part], self.from_down.at[zp, part], self.send.at[1, n], self.recv_down.at[n], self.at.up
        )

    def down_copy(self, j):
        zp, n, part = self.unit(j)
        return remote(
            self.acc.at[zp, part], self.from_up.at[zp, part], self.send.at[2, n], self.recv_up.at[n], self.at.down
        )

    def start(self):
        self.side_copy(0).start()
        self.side_copy(1).start()

    def step(self, j):
        at = self.at
        zp, _, part = self.unit(j)
        self.side_copy(j).wait()
        acc = self.acc.at[zp, part]
        add_into(acc, self.from_side.at[zp, part], self.rows)

        @pl.when((at.z > 0) & (zp >= at.z))
        def _():
            self.up_copy(j).wait_recv()
            add_into(acc, self.from_down.at[zp, part], self.rows)

        @pl.when((at.z < 3) & (zp <= at.z))
        def _():
            self.down_copy(j).wait_recv()
            add_into(acc, self.from_up.at[zp, part], self.rows)

        @pl.when(zp > at.z)
        def _():
            self.up_copy(j).start()

        @pl.when(zp < at.z)
        def _():
            self.down_copy(j).start()

    def end(self):
        at = self.at
        for j in range(4 * self.cuts):
            zp = self.unit(j)[0]

            @pl.when(zp > at.z)
            def _():
                self.up_copy(j).wait_send()

            @pl.when(zp < at.z)
            def _():
                self.down_copy(j).wait_send()


def backward_traffic(layer, rows, gate):
    piece, cols = layer.shape[1:]
    rrows = rows.shape[1]
    grows, gcols = gate.shape[1:]

    class Traffic:
        inputs = (layer, rows, gate)
        outputs = (
            jax.ShapeDtypeStruct((piece, cols), f32),
            jax.ShapeDtypeStruct((rrows, cols), bf16),
            jax.ShapeDtypeStruct((grows, gcols), bf16),
        )
        scratch = (
            *[pltpu.VMEM((piece, cols), bf16)] * 5,
            pltpu.VMEM((piece, cols), f32),
            *[pltpu.VMEM((rrows, cols), bf16)] * 4,
            dma(3, SLICES),
            dma(3, SLICES),
            dma(3),
            dma(3, SLICES),
            dma(3, SLICES),
            dma(2),
            dma(2, SLICES),
            dma(2, SLICES),
            *[pltpu.VMEM((4, grows, gcols), bf16)] * 4,
            dma(3, 8),
            dma(8),
            dma(8),
            dma(8),
            dma(5),
        )
        collective_id = 3

        def __init__(
            self, layer, rows, gate, out, rows_out, gate_out,
            own_v, far_v, sib_v, pass_v, got_v, sum_v, acc, side_v, low_v, high_v,
            send, recv, local, rsend, rrecv, rlocal, fsend, frecv,
            gacc, gside, glow, ghigh, gsend, grecv_side, grecv_low, grecv_high, glocal,
        ):
            self.at = at = Place()
            cut, rcut = piece // SLICES, rrows // SLICES
            part = lambda k: pl.ds(pl.multiple_of(k * cut, cut), cut)
            rpart = lambda k: pl.ds(pl.multiple_of(k * rcut, rcut), rcut)
            self.own, self.sib, self.passed, self.got, self.sum = own_v, sib_v, pass_v, got_v, sum_v
            self.part, self.rpart, self.cut, self.rcut = part, rpart, cut, rcut
            self.far_v, self.acc, self.side_v, self.low_v, self.high_v = far_v, acc, side_v, low_v, high_v
            self.load_far = pltpu.make_async_copy(layer.at[at.s_far], far_v, local.at[0])
            self.load_own = pltpu.make_async_copy(layer.at[at.s], own_v, local.at[1])
            self.store = pltpu.make_async_copy(sum_v, out, local.at[2])
            self.to_pass = lambda k: remote(
                layer.at[at.s_diag, part(k)], pass_v.at[part(k)], send.at[0, k], recv.at[0, k], at.sib
            )
            self.to_sib = lambda k: remote(
                layer.at[at.s_sib, part(k)], sib_v.at[part(k)], send.at[1, k], recv.at[1, k], at.sib
            )
            self.to_far = lambda k: remote(
                far_v.at[part(k)], got_v.at[part(k)], send.at[2, k], recv.at[2, k], at.far
            )
            self.load_acc = pltpu.make_async_copy(rows.at[at.x], acc, rlocal.at[0])
            self.store_acc = pltpu.make_async_copy(acc, rows_out, rlocal.at[1])
            spread = lambda k, n, device: remote(
                acc.at[rpart(k)], rows_out.at[rpart(k)], fsend.at[n, k], frecv.at[n, k], device
            )
            self.spread_far = lambda k: spread(k, 0, at.far)
            self.spread_sib = lambda k: spread(k, 1, at.sib)
            self.spread_on = lambda k: remote(
                rows_out.at[rpart(k)], rows_out.at[rpart(k)], fsend.at[1, k], frecv.at[1, k], at.sib
            )
            self.gates = ReduceShards(
                at, lambda zp: gate.at[2 * zp + 1 - at.x], 2, gacc, gside, glow, ghigh,
                (gsend, grecv_side, grecv_low, grecv_high),
            )
            self.load_gate = [
                pltpu.make_async_copy(gate.at[2 * zp + at.x], gacc.at[zp], glocal.at[zp]) for zp in range(4)
            ]
            self.store_gate = pltpu.make_async_copy(gacc.at[at.z], gate_out, glocal.at[4])
            self.to_side = lambda k: remote(
                rows.at[1 - at.x, rpart(k)], side_v.at[rpart(k)], rsend.at[0, k], rrecv.at[0, k], at.side
            )
            self.to_up = lambda k: remote(
                acc.at[rpart(k)], low_v.at[rpart(k)], rsend.at[1, k], rrecv.at[1, k], at.up
            )
            self.to_down = lambda k: remote(
                acc.at[rpart(k)], high_v.at[rpart(k)], rsend.at[2, k], rrecv.at[2, k], at.down
            )

        def step(self, i, last):
            at = self.at

            @pl.when(i == 0)
            def _():
                at.greet()
                self.load_far.start()
                self.load_own.start()
                self.load_acc.start()
                for copy in self.load_gate:
                    copy.start()
                each_slice(lambda k: self.to_pass(k).start())
                each_slice(lambda k: self.to_sib(k).start())

            @pl.when(i < SLICES)
            def _():
                self.to_side(i).start()

            @pl.when(i == 1)
            def _():
                self.load_far.wait()
                self.load_own.wait()
                self.load_acc.wait()
                for copy in self.load_gate:
                    copy.wait()

            k = i - 1

            @pl.when((k >= 0) & (k < SLICES))
            def _():
                self.to_pass(k).wait_recv()
                add_into(self.far_v.at[self.part(k)], self.passed.at[self.part(k)], self.cut)
                self.to_far(k).start()

            m = i - SLICES

            @pl.when((m >= 0) & (m < SLICES))
            def _():
                self.to_sib(m).wait_recv()
                self.to_far(m).wait_recv()
                p = self.part(m)
                self.sum[p, :] = (
                    self.own[p, :].astype(f32) + self.sib[p, :].astype(f32) + self.got[p, :].astype(f32)
                )

            ends = jnp.where(at.z > 3 - at.z, at.z, 3 - at.z)
            chain = jnp.where(at.z < at.s, at.z, jnp.where(at.z > at.s, 3 - at.z, ends))
            v = 10 * i - 17 * chain - 26 + 10
            r = jnp.where(v >= 0, lax.div(v, 11), -1)

            @pl.when((r >= 0) & (r < SLICES) & (11 * r < v))
            def _():
                acc = self.acc.at[self.rpart(r)]
                self.to_side(r).wait_recv()
                add_into(acc, self.side_v.at[self.rpart(r)], self.rcut)

                @pl.when((at.z <= at.s) & (at.z > 0))
                def _():
                    self.to_up(r).wait_recv()
                    add_into(acc, self.low_v.at[self.rpart(r)], self.rcut)

                @pl.when((at.z >= at.s) & (at.z < 3))
                def _():
                    self.to_down(r).wait_recv()
                    add_into(acc, self.high_v.at[self.rpart(r)], self.rcut)

                @pl.when(at.z < at.s)
                def _():
                    self.to_up(r).start()

                @pl.when(at.z > at.s)
                def _():
                    self.to_down(r).start()

                @pl.when(at.z == at.s)
                def _():
                    self.spread_far(r).start()
                    self.spread_sib(r).start()

            g = i - (last - 7)

            @pl.when(g >= 0)
            def _():
                self.gates.side_copy(g).start()

            inner = jnp.where((at.z == 1) | (at.z == 2), 1, 0)
            g = i - 11 - inner

            @pl.when(g >= 0)
            def _():
                self.gates.step(g)

            @pl.when(i == last)
            def _():
                def rest(k, _):
                    self.gates.step(k)
                    return 0

                lax.fori_loop(last - 10 - inner, 8, rest, 0)

                self.store.start()
                self.store_gate.start()

                @pl.when(at.s == at.z)
                def _():
                    self.store_acc.start()

                def forward(k):
                    @pl.when(at.s_far == at.z)
                    def _():
                        self.spread_far(k).wait_recv()
                        self.spread_on(k).start()

                each_slice(forward)

                def finish(k):
                    @pl.when(at.s == at.z)
                    def _():
                        self.spread_far(k).wait_send()
                        self.spread_sib(k).wait_send()

                    @pl.when(at.s_far == at.z)
                    def _():
                        self.spread_on(k).wait_send()

                    @pl.when((at.s_sib == at.z) | (at.s_diag == at.z))
                    def _():
                        self.spread_on(k).wait_recv()

                    self.to_pass(k).wait_send()
                    self.to_sib(k).wait_send()
                    self.to_far(k).wait_send()
                    self.to_side(k).wait_send()

                    @pl.when(at.z < at.s)
                    def _():
                        self.to_up(k).wait_send()

                    @pl.when(at.z > at.s)
                    def _():
                        self.to_down(k).wait_send()

                each_slice(finish)
                self.gates.end()
                self.store.wait()
                self.store_gate.wait()

                @pl.when(at.s == at.z)
                def _():
                    self.store_acc.wait()

    return Traffic


def small_start(at, small, got, sems):
    send, recv = sems
    for k in range(1, 8):
        peer = (lax.rem(at.w + k, 8), at.s)
        remote(small, got.at[k], send.at[k], recv.at[k], peer).start()


def small_pass(at, small, got, total, full, sems, more):
    send, recv = sems
    send2, recv2, local = more
    value = small[...]
    for k in range(1, 8):
        remote(small, got.at[k], send.at[k], recv.at[k], at.side).wait_recv()
        value = value + got[k]
    total[...] = value
    pltpu.make_async_copy(total, full.at[at.s], local).start()
    for k, s in enumerate((at.s_sib, at.s_far, at.s_diag)):
        remote(total, full.at[at.s], send2.at[k], recv2.at[k], (at.w, s)).start()


def small_end(at, small, got, total, full, sems, more):
    send, recv = sems
    send2, recv2, local = more
    pltpu.make_async_copy(total, full.at[at.s], local).wait()
    for k in range(1, 8):
        remote(small, got.at[k], send.at[k], recv.at[k], at.side).wait_send()
    for k, s in enumerate((at.s_sib, at.s_far, at.s_diag)):
        remote(total, full.at[at.s], send2.at[k], recv2.at[k], (at.w, s)).wait_send()
        remote(total, full.at[s], send2.at[k], recv2.at[k], (at.w, s)).wait_recv()


def last_kernel(hid, d_gate, d_u, d_dt, w_main, w_com, gate_sum, small,
                back_sum, in_sum, sums_out,
                hid_v, dp_v, w_v,
                b_diag, b_sib, b_far, b_own, from_sib, pass_sib, from_far,
                part_v, mside, mlow, mhigh, macc, mown, csib, cown, cacc, cside, clow, chigh, cfar, csum,
                sgot, stotal, sfull, gate_v, *sems):
    at = Place()
    sems = list(sems)
    take = lambda n: [sems.pop(0) for _ in range(n)]
    load, bsem, msem, csem, cx, ssem, smore, asem, gsem = (
        take(6), take(2), take(4), take(4), take(7), take(2), take(3), take(3), take(3)
    )
    piece = hid_v.shape[0] // 4
    shard = hid_v.shape[1] // 8
    wide = d_gate.shape[1]
    half = shard // 2
    mine = pl.ds(pl.multiple_of(at.c * half, half), half)
    other = pl.ds(pl.multiple_of((1 - at.c) * half, half), half)
    at.greet(everyone=True)

    order = (at.s_diag, at.s_far, at.s_sib, at.s)
    rows_of = lambda s: pl.ds(pl.multiple_of(s * piece, piece), piece)
    weights = [
        pltpu.make_async_copy(w_main, w_v.at[:, pl.ds(0, 2 * wide)], load[0].at[0]),
        pltpu.make_async_copy(w_com, w_v.at[:, pl.ds(2 * wide, 384)], load[0].at[1]),
    ]
    loads = []
    for k, s in enumerate(order):
        r = rows_of(s)
        loads.append(
            [
                pltpu.make_async_copy(d_gate.at[r], dp_v.at[r, pl.ds(0, wide)], load[1].at[k]),
                pltpu.make_async_copy(d_u.at[r], dp_v.at[r, pl.ds(wide, wide + 256)], load[2].at[k]),
                pltpu.make_async_copy(d_dt.at[r], dp_v.at[r, pl.ds(2 * wide + 256, 128)], load[3].at[k]),
            ]
        )
    hid_load = pltpu.make_async_copy(hid, hid_v, load[4])
    soon, later = weights + loads[0] + loads[1], [hid_load] + loads[2] + loads[3]
    for copy in soon + later:
        copy.start()
    gate_slot = lambda s: in_sum.at[:, pl.ds(pl.multiple_of(s * wide, 128), wide)]
    x_slot = lambda s: in_sum.at[:, pl.ds(pl.multiple_of(E + s * wide, 128), wide)]
    gather_pieces_start(at, gate_sum, gate_slot, gsem, gate_v)
    small_start(at, small, sgot, ssem)

    send, recv = bsem
    rows = piece // PARTS
    parts = [pl.ds(k * rows, rows) for k in range(PARTS)]
    to_pass = [remote(b_diag.at[p], pass_sib.at[p], send.at[0, k], recv.at[0, k], at.sib) for k, p in enumerate(parts)]
    to_sib = [remote(b_sib.at[p], from_sib.at[p], send.at[1, k], recv.at[1, k], at.sib) for k, p in enumerate(parts)]
    to_far = [remote(b_far.at[p], from_far.at[p], send.at[2, k], recv.at[2, k], at.far) for k, p in enumerate(parts)]

    def back_tile(s, out, t):
        tile = pl.ds(pl.multiple_of(s * piece + t * 256, 256), 256)
        place = pl.ds(t * 256, 256)

        for n in range(hid_v.shape[1] // 256):
            col = slice(256 * n, 256 * n + 256)
            out[place, col] = dot_nt(dp_v[tile, :], w_v[col, :]).astype(bf16)

    big = ReduceShards(at, lambda zp: part_v.at[zp, 1 - at.x, :, pl.ds(0, wide)], 2, macc, mside, mlow, mhigh, msem)
    few = ReduceShards(at, lambda zp: cown.at[zp, 1 - at.x], 1, cacc, cside, clow, chigh, csem)
    com_cols = pl.ds(wide, 384)
    com_to_sib = lambda zp: remote(
        part_v.at[zp, :, other, com_cols], csib.at[zp], cx[0].at[zp], cx[1].at[zp], at.sib
    )

    def shard_pair(i):
        zp = far_first(at, i)
        lanes = pl.ds(pl.multiple_of(zp * 2 * shard, 128), 2 * shard)
        got = lax.dot_general(
            hid_v[:, lanes], dp_v[:, wide : 2 * wide + 384], (((0,), (0,)), ((), ())), preferred_element_type=f32
        ).astype(bf16)
        part_v[zp, 0] = got[0:shard]
        part_v[zp, 1] = got[shard : 2 * shard]
        macc[zp] = part_v[zp, at.x, :, 0:wide]
        big.side_copy(2 * i).start()
        com_to_sib(zp).start()

    def com_pair(i):
        zp = far_first(at, i)
        com_to_sib(zp).wait_recv()
        for x in range(2):
            cown[zp, x] = part_v[zp, x, mine, com_cols]
            add_into(cown.at[zp, x], csib.at[zp, x], half)
        cacc[zp] = cown[zp, at.x]
        few.side_copy(i).start()

    ends = (at.z == 0) | (at.z == 3)

    def step(j, who):
        @pl.when(who)
        def _():
            big.step(j)
            if j % 2:
                few.step(j // 2)

    tiles = piece // 256
    per = PARTS // tiles
    def far_tile(t):
        back_tile(at.s_far, b_far, t)
        for k in range(t * per, t * per + per):
            to_pass[k].wait_recv()
            add_into(b_far.at[parts[k]], pass_sib.at[parts[k]], rows)
            to_far[k].start()

    for copy in soon:
        copy.wait()
    for t in range(tiles):
        back_tile(at.s_diag, b_diag, t)
        for k in range(t * per, t * per + per):
            to_pass[k].start()
    far_tile(0)
    for copy in later:
        copy.wait()
    def sib_tile(t):
        back_tile(at.s_sib, b_sib, t)
        for k in range(t * per, t * per + per):
            to_sib[k].start()

    shard_pair(0)
    far_tile(1)
    big.side_copy(1).start()
    shard_pair(1)
    com_pair(0)
    shard_pair(2)
    big.side_copy(3).start()
    com_pair(1)
    step(0, ends)
    step(1, ends)
    shard_pair(3)
    big.side_copy(5).start()
    com_pair(2)
    step(0, ~ends)
    step(2, ends)
    gather_pieces_pass(at, gate_sum, gate_slot, gsem)
    sib_tile(0)
    big.side_copy(7).start()
    com_pair(3)
    step(1, ~ends)
    step(3, ends)
    sib_tile(1)
    step(2, ~ends)
    step(4, ends)
    back_tile(at.s, b_own, 0)
    step(3, ~ends)
    step(4, ~ends)
    step(5, ends)
    back_tile(at.s, b_own, 1)
    step(5, ~ends)
    small_pass(at, small, sgot, stotal, sfull, ssem, smore)
    for j in (6, 7):
        big.step(j)
    few.step(3)
    mown[...] = macc[at.z]
    gather_pieces_start(at, mown, x_slot, asem)
    csum[...] = cacc[at.z]
    far_copy = remote(csum, cfar, cx[2], cx[3], at.far)
    far_copy.start()
    for k, p in enumerate(parts):
        to_sib[k].wait_recv()
        to_far[k].wait_recv()

        def body(i, _):
            r = pl.ds(pl.multiple_of(k * rows + i * 32, 32), 32)
            back_sum[r, :] = b_own[r, :].astype(f32) + from_sib[r, :].astype(f32) + from_far[r, :].astype(f32)
            return 0

        lax.fori_loop(0, rows // 32, body, 0)
    far_copy.wait()
    add_into(csum, cfar, half)
    com_out = in_sum.at[mine, pl.ds(2 * E, 384)]
    com_copy = remote(csum, com_out, cx[4], cx[5], at.sib)
    com_copy.start()
    keep_copy = pltpu.make_async_copy(csum, com_out, cx[6])
    keep_copy.start()
    gather_pieces_pass(at, mown, x_slot, asem)
    small_end(at, small, sgot, stotal, sfull, ssem, smore)
    sums_out[...] = jnp.zeros_like(sums_out)
    bc, heads = jnp.zeros((8, 256), f32), jnp.zeros((8, 128), f32)
    for s in range(4):
        sums_out[:, wide * s : wide * s + wide] = sfull[s, :, 0:wide]
        bc = bc + sfull[s, :, wide : wide + 256]
        shift = (wide // P_SIZE) * s
        own = sfull[s, :, 0:128]
        heads = heads + (pltpu.roll(own, shift, 1) if shift else own)
    sums_out[:, E : E + 256] = bc
    sums_out[:, E + 256 : E + 384] = heads
    for copy in to_pass + to_sib + to_far:
        copy.wait_send()
    for zp in range(4):
        com_to_sib(zp).wait_send()
    big.end()
    few.end()
    gather_pieces_end(at, gate_sum, gate_slot, gsem)
    gather_pieces_end(at, mown, x_slot, asem)
    keep_copy.wait()
    com_copy.wait_send()
    got = in_sum.at[other, pl.ds(2 * E, 384)]
    remote(csum, got, cx[4], cx[5], at.sib).wait_recv()


def finish_last(hid, d_gate, d_u, d_dt, w_main, w_com, gate_sum, small):
    length, depth = hid.shape
    piece, shard, half = length // 4, depth // 8, depth // 16
    wide = d_gate.shape[1]
    vm = pltpu.VMEM
    shards4 = lambda cuts: [dma(3, 4 * cuts), dma(4 * cuts), dma(4 * cuts), dma(4 * cuts)]
    return pl.pallas_call(
        last_kernel,
        in_specs=[pl.BlockSpec(memory_space=ANY)] * 7 + [pl.BlockSpec(memory_space=pltpu.VMEM)],
        out_specs=[
            pl.BlockSpec(memory_space=pltpu.VMEM),
            pl.BlockSpec(memory_space=ANY),
            pl.BlockSpec(memory_space=pltpu.VMEM),
        ],
        out_shape=[
            jax.ShapeDtypeStruct((piece, depth), f32),
            jax.ShapeDtypeStruct((shard, 2 * E + 384), bf16),
            jax.ShapeDtypeStruct((8, E + 384), f32),
        ],
        scratch_shapes=[vm(hid.shape, bf16), vm((length, 2 * wide + 384), bf16), vm((depth, 2 * wide + 384), bf16)]
        + [vm((piece, depth), bf16)] * 7
        + [vm((4, 2, shard, wide + 384), bf16)]
        + [vm((4, shard, wide), bf16)] * 4
        + [vm((shard, wide), bf16)]
        + [vm((4, 2, half, 384), bf16)] * 2
        + [vm((4, half, 384), bf16)] * 4
        + [vm((half, 384), bf16)] * 2
        + [vm((8,) + small.shape, f32), vm(small.shape, f32), vm((4,) + small.shape, f32), vm(gate_sum.shape, bf16)]
        + [dma(2), dma(4), dma(4), dma(4), dma(), dma()]
        + [dma(3, PARTS), dma(3, PARTS)]
        + shards4(2)
        + shards4(1)
        + [dma(4), dma(4), dma(), dma(), dma(), dma(), dma()]
        + [dma(8), dma(8)]
        + [dma(3), dma(3), dma()]
        + [dma(3, PARTS), dma(3, PARTS), dma()]
        + [dma(3, PARTS), dma(3, PARTS), dma()],
        compiler_params=pltpu.CompilerParams(
            collective_id=4, has_side_effects=True, vmem_limit_bytes=60 * 2**20
        ),
        name="finish_last",
    )(hid, d_gate, d_u, d_dt, w_main, w_com, gate_sum, small)


def over_rows(left, right):
    return lax.dot_general(
        left, right, (((0,), (0,)), ((), ())), preferred_element_type=jnp.float32
    )


def gather_plain(hid, main, com):
    hid_all = lax.all_gather(hid, "seq", axis=0)
    main_all = lax.all_gather(main, "wshard", axis=0)
    return hid_all, main_all, lax.all_gather(com, "wshard", axis=0)


def gather_more_plain(cot, rows, wide):
    cot_all = lax.all_gather(cot, "seq", axis=0)
    cols = lax.all_to_all(rows, "wshard", split_axis=1, concat_axis=0, tiled=True)
    own = lax.dynamic_slice_in_dim(cols, lax.axis_index("seq") * wide, wide, 0)
    return cot_all, lax.all_gather(own, "wshard", axis=1, tiled=True)


def reduce_scattered(v, axis):
    return lax.psum_scatter(v, axis, scatter_dimension=0, tiled=False)


def reduce_first_plain(layer, rows, gate):
    layer_sum = reduce_scattered(layer, "seq").astype(f32)
    rows = rows.reshape(-1, rows.shape[-1])
    part = lax.psum_scatter(rows, "wshard", scatter_dimension=1, tiled=True)
    part = lax.all_gather(part, "seq", axis=0, tiled=True)
    part = lax.all_to_all(part, "wshard", split_axis=0, concat_axis=1, tiled=True)
    return layer_sum, part, reduce_scattered(gate, "wshard")


def finish_plain(hid, d_gate, d_u, d_dt, w_main, w_com, gate_sum, small):
    groups, owners = lax.axis_size("seq"), lax.axis_size("wshard")
    wide = d_gate.shape[1]
    rest = jnp.concatenate([d_u, d_dt], axis=1)
    nt = lambda p, q: lax.dot_general(p, q, (((1,), (1,)), ((), ())), preferred_element_type=f32)
    back = nt(d_gate, w_main[:, :wide]) + nt(rest, jnp.concatenate([w_main[:, wide:], w_com], axis=1))
    back_sum = reduce_scattered(back.astype(bf16).reshape(groups, -1, D), "seq").astype(f32)
    part = reduce_scattered(over_rows(hid, rest).astype(bf16).reshape(owners, -1, rest.shape[1]), "wshard")
    part = lax.all_gather(jnp.concatenate([gate_sum, part], axis=1), "seq", axis=0)
    in_sum = jnp.concatenate(
        [part[i, :, :wide] for i in range(groups)]
        + [part[i, :, wide : 2 * wide] for i in range(groups)]
        + [jnp.sum(part[:, :, 2 * wide :].astype(f32), axis=0).astype(bf16)],
        axis=1,
    )
    full = lax.all_gather(lax.psum(small, "wshard"), "seq", axis=0)
    turned = [jnp.roll(full[i, :, :128], i * (wide // P_SIZE), axis=1) for i in range(groups)]
    sums = jnp.concatenate(
        [full[i, :, :wide] for i in range(groups)] + [jnp.sum(full[:, :, wide:], axis=0), sum(turned)], axis=1
    )
    return back_sum, in_sum, sums


def shards(
    hidden,
    segments,
    norm_gain,
    in_weight,
    conv_weight,
    conv_bias,
    step_bias,
    decay_log,
    skip_scale,
    gate_gain,
    out_weight,
    cotangent,
):
    group = lax.axis_index("seq")
    groups, owners = lax.axis_size("seq"), lax.axis_size("wshard")
    direct = (groups, owners) == (4, 8)
    heads = H // groups
    wide = heads * P_SIZE
    length = segments.shape[1]
    hidden_own, cot_own = hidden[0], cotangent[0]
    in_gain = norm_gain.astype(f32)[:, None]
    in_scaled = (in_weight.astype(f32) * in_gain).astype(bf16)
    main = jnp.concatenate(
        [
            lax.dynamic_slice_in_dim(in_scaled, group * wide, wide, 1),
            lax.dynamic_slice_in_dim(in_scaled, E + group * wide, wide, 1),
        ],
        axis=1,
    )
    com = jnp.pad(in_scaled[:, 2 * E :], ((0, 0), (0, 128 - H)))
    out_gain = gate_gain.astype(f32)[:, None]
    out_scaled = (out_weight.astype(f32) * out_gain).astype(bf16)
    gather = gather_first if direct else gather_plain
    hidden_all, w_main, w_com = gather(hidden_own, main, com)
    hidden_all = hidden_all.reshape(length, D)
    w_main, w_com = w_main.reshape(D, 2 * wide), w_com.reshape(D, -1)

    seg = segments[0]
    seg_col = jnp.pad(seg, (8, 8), constant_values=-1)[:, None]
    segr = seg.reshape(length // Q, 1, Q)
    par = jnp.pad(jnp.stack([step_bias, decay_log]), ((0, 6), (0, 128 - H)))
    skip = jnp.repeat(skip_scale, P_SIZE)[None]
    facts = (seg_col, segr, conv_weight, conv_bias[None], par, skip)
    beside, more = (forward_traffic(cot_own, out_scaled), (cot_own, out_scaled)) if direct else (NoTraffic, ())
    u, dt, gate, scale, mixed, save, *got = mixer_fwd(beside, more, hidden_all, w_main, w_com, *facts)
    cot_all, w_out = got if direct else gather_more_plain(cot_own, out_scaled, wide)
    cot_all, w_out = cot_all.reshape(length, D), w_out.reshape(wide, D)

    mixed_wide = mixed.astype(f32)
    sg = jax.nn.sigmoid(gate)
    silu = gate * sg
    g = mixed_wide * silu
    g_low = g.astype(bf16)
    a = lax.dot_general(cot_all, w_out, (((1,), (1,)), ((), ())), preferred_element_type=f32)
    sums = lax.psum(jnp.stack([jnp.sum(g * g, axis=1), jnp.sum(a * g, axis=1)]), "seq")
    r = lax.rsqrt(sums[0] / E + eps)[:, None]
    pull = (r * r * r) * (sums[1] / E)[:, None]
    d_g = r * a - g * pull
    d_mixed = (d_g * silu).astype(bf16)
    d_gate = (d_g * mixed_wide * (sg * (1.0 + gate * (1.0 - sg))) * scale).astype(bf16)
    layer_part = (jnp.dot(g_low, w_out, preferred_element_type=f32) * r).astype(bf16)
    cot_r = (cot_all.astype(f32) * r).astype(bf16)
    out_part = over_rows(g_low, cot_r).astype(bf16)

    gate_part = over_rows(hidden_all, d_gate).astype(bf16)

    layer_part, out_part = layer_part.reshape(groups, -1, D), out_part.reshape(2, -1, D)
    gate_part = gate_part.reshape(owners, -1, wide)
    more = (layer_part, out_part, gate_part) if direct else ()
    beside = backward_traffic(*more) if direct else NoTraffic
    du, ddt, small, *got = mixer_bwd(beside, more, u, dt, scale, *facts, save, d_mixed)
    layer_sum, out_sum, gate_sum = got if direct else reduce_first_plain(*(layer_part, out_part, gate_part))
    finish = finish_last if direct else finish_plain
    back_sum, in_sum, sums = finish(hidden_all, d_gate, du, ddt, w_main, w_com, gate_sum, small)

    own_wide = hidden_own.astype(f32)
    layer_output = own_wide + layer_sum
    own_scale = lax.rsqrt(jnp.mean(own_wide * own_wide, axis=-1, keepdims=True) + eps)
    hidden_grad = (
        cot_own.astype(f32)
        + back_sum
        - own_wide * (own_scale * own_scale) * jnp.mean(back_sum * own_wide, axis=-1, keepdims=True)
    )
    in_sum = in_sum[:, : 2 * E + 2 * N + H].astype(f32)
    in_weight_grad = in_sum * in_gain
    norm_gain_grad = jnp.sum(in_sum * in_weight.astype(f32), axis=1)
    out_sum = out_sum.astype(f32)
    out_weight_grad = out_sum * out_gain
    gate_gain_grad = jnp.sum(out_sum * out_weight.astype(f32), axis=1)
    chan, per_head = sums[:, : E + 2 * N], sums[:, E + 2 * N : E + 2 * N + H]
    return (
        layer_output[None],
        hidden_grad[None],
        norm_gain_grad,
        in_weight_grad,
        chan[:4],
        chan[4],
        per_head[5],
        per_head[6],
        per_head[7],
        gate_gain_grad,
        out_weight_grad,
    )


def solution(mesh):
    in_specs = (
        P("wshard", "seq", None),
        P("wshard", None),
        P("wshard"),
        P("wshard", None),
        P(),
        P(),
        P(),
        P(),
        P(),
        P("wshard"),
        P("wshard", None),
        P("wshard", "seq", None),
    )
    out_specs = (
        P("wshard", "seq", None),
        P("wshard", "seq", None),
        P("wshard"),
        P("wshard", None),
        P(),
        P(),
        P(),
        P(),
        P(),
        P("wshard"),
        P("wshard", None),
    )
    return jax.shard_map(shards, mesh=mesh, in_specs=in_specs, out_specs=out_specs, check_vma=False)
```

```python
import functools

import jax
import jax.numpy as jnp
from jax import lax
from jax.experimental import pallas as pl
from jax.experimental.pallas import tpu as pltpu
from jax.sharding import PartitionSpec as P

D = 1536
H = 48
P_SIZE = 64
N = 128
E = 3072

eps = 1e-05
f32, bf16 = jnp.float32, jnp.bfloat16
Q = 128
NEG = -1e30


def dot(a, b):
    return jnp.dot(a, b, preferred_element_type=f32)


def dot_nt(a, b):
    return lax.dot_general(a, b, (((1,), (1,)), ((), ())), preferred_element_type=f32)


def dot3(tri, v):
    hi = v.astype(bf16)
    rest = v - hi.astype(f32)
    mid = rest.astype(bf16)
    low = (rest - mid.astype(f32)).astype(bf16)
    return dot(tri, hi) + dot(tri, mid) + dot(tri, low)


def sigmoid(v):
    return 1.0 / (1.0 + jnp.exp(-v))


def spread_col(v, col):
    return jnp.broadcast_to(v[:, col : col + 1], (Q, 128))


def softplus(v):
    return jnp.maximum(v, 0.0) + jnp.log1p(jnp.exp(-jnp.abs(v)))


def conv_pre(useen, flags, wk, bias, lanes, chans):
    pre = bias[:, chans] + wk[3:4, chans] * useen[8 : 8 + Q, lanes]
    for j in (1, 2, 3):
        pre = pre + wk[3 - j : 4 - j, chans] * (useen[8 - j : 8 - j + Q, lanes] * flags[j])
    return pre


class Facts:
    def __init__(self, chunk, seg_ref, par_ref, xw):
        self.group = lax.axis_index("seq")
        self.heads = xw // P_SIZE
        self.xw = xw
        near = seg_ref[pl.ds(pl.multiple_of(chunk * Q, 8), Q + 16), :]
        now = near[8 : 8 + Q]
        same = lambda other: jnp.broadcast_to(jnp.where(other == now, 1.0, 0.0), (Q, 128))
        self.before = [None] + [same(near[8 - j : 8 - j + Q]) for j in (1, 2, 3)]
        self.after = lambda j: same(near[8 + j : 8 + j + Q])
        self.carried = same(near[7:8])
        self.samelast = same(near[7 + Q : 8 + Q])
        self.now = now
        self.turn = self.heads * self.group
        lane = lax.broadcasted_iota(jnp.int32, (8, 128), 1)
        par = self.own(par_ref[...])
        self.bias = par[0:1]
        self.rate = jnp.where(lane < self.heads, -jnp.exp(par), 0.0)[1:2]

    def own(self, v):
        lane = lax.broadcasted_iota(jnp.int32, v.shape, 1)
        return jnp.where(lane < self.heads, pltpu.roll(v, lax.rem(128 - self.turn, 128), 1), 0.0)

    def back(self, v):
        return pltpu.roll(v, self.turn, 1)

    def chans(self, p):
        if p < self.xw // 128:
            return pl.ds(pl.multiple_of(self.group * self.xw + 128 * p, 128), 128)
        at = E + 128 * (p - self.xw // 128)
        return slice(at, at + 128)


class NoTraffic:
    inputs, outputs, scratch, collective_id = (), (), (), None

    def __init__(self, *refs):
        pass

    def step(self, i, last):
        pass


def fwd_kernel(traffic, hid_ref, gain_ref, main_ref, com_ref, seg_ref, segr_ref, wk_ref, bias_ref, par_ref, skip_ref, *rest):
    n_in, n_out = len(traffic.inputs), len(traffic.outputs)
    extra_in, rest = rest[:n_in], rest[n_in:]
    u_ref, dt_ref, gate_ref, normed_ref, mixed_ref, save_ref = rest[:6]
    extra_out, rest = rest[6 : 6 + n_out], rest[6 + n_out :]
    state, useen, act, next_u, next_dt = rest[:5]
    step_no = pl.program_id(0)
    traffic(*extra_in, *extra_out, *rest[5:]).step(step_no, pl.num_programs(0) - 1)
    xw = mixed_ref.shape[1]
    width = xw + 256
    pairs = xw // 128
    facts = Facts(jnp.maximum(step_no - 1, 0), seg_ref, par_ref, xw)

    @pl.when(step_no == 0)
    def _():
        next_u[...] = jnp.zeros_like(next_u)
        next_dt[...] = jnp.zeros_like(next_dt)

    @pl.when(step_no <= 1)
    def _():
        state[...] = jnp.zeros_like(state)
        useen[0:8, :] = jnp.zeros((8, width), f32)

    useen[8 : 8 + Q, :] = next_u[...]
    dt_now = next_dt[...]

    hid = hid_ref[...].astype(f32)
    depth = hid.shape[1]
    total = jnp.zeros((Q, 128), f32)
    for k in range(depth // 128):
        part = hid[:, 128 * k : 128 * k + 128]
        total = total + part * part
    scale = lax.rsqrt(jnp.sum(total, axis=1, keepdims=True) / depth + eps)
    normed_ref[...] = (hid * scale * gain_ref[...]).astype(bf16)
    low = normed_ref[...]
    for k in range(xw // 256):
        gate_ref[:, 256 * k : 256 * k + 256] = dot(low, main_ref[:, 256 * k : 256 * k + 256])
    for k in range(xw // 256):
        got = dot(low, main_ref[:, xw + 256 * k : xw + 256 * k + 256]).astype(bf16)
        u_ref[:, 256 * k : 256 * k + 256] = got
        next_u[:, 256 * k : 256 * k + 256] = got.astype(f32)
    got = dot(low, com_ref[:, 0:256]).astype(bf16)
    u_ref[:, xw : xw + 256] = got
    next_u[:, xw : xw + 256] = got.astype(f32)
    got = facts.own(dot(low, com_ref[:, 256:384]).astype(bf16).astype(f32))
    dt_ref[...] = got.astype(bf16)
    next_dt[...] = got

    carried, samelast = facts.carried, facts.samelast
    for p in range(width // 128):
        lanes = slice(128 * p, 128 * p + 128)
        pre = conv_pre(useen, facts.before, wk_ref, bias_ref, lanes, facts.chans(p))
        act[:, lanes] = pre * sigmoid(pre)
    tail = useen[Q : Q + 8, :]
    useen[0:8, :] = tail

    step = softplus(dt_now + facts.bias)
    row = lax.broadcasted_iota(jnp.int32, (Q, Q), 0)
    col = lax.broadcasted_iota(jnp.int32, (Q, Q), 1)
    tri = jnp.where(row >= col, 1.0, 0.0).astype(bf16)
    decay = dot3(tri, step * facts.rate)
    decay_t = decay.T
    madd = jnp.where((row >= col) & (facts.now == segr_ref[0]), 0.0, NEG)
    b_now = act[:, xw : xw + 128]
    c_low = act[:, xw + 128 : xw + 256].astype(bf16)
    gram = dot_nt(c_low, b_now.astype(bf16))
    b_t = b_now.T.astype(bf16)
    left = lax.broadcasted_iota(jnp.int32, (Q, 128), 1) < 64
    for p in range(pairs):
        lanes = slice(128 * p, 128 * p + 128)
        d0, d1 = spread_col(decay, 2 * p), spread_col(decay, 2 * p + 1)
        dp = jnp.where(left, d0, d1)
        sp = jnp.where(left, spread_col(step, 2 * p), spread_col(step, 2 * p + 1))
        xs = act[:, lanes]
        xp = xs * sp
        m0 = gram * jnp.exp(d0 - decay_t[2 * p : 2 * p + 1, :] + madd)
        m1 = gram * jnp.exp(d1 - decay_t[2 * p + 1 : 2 * p + 2, :] + madd)
        both = jnp.concatenate([m0.astype(bf16), m1.astype(bf16)], axis=1)
        stacked = jnp.concatenate(
            [jnp.where(left, xp, 0.0).astype(bf16), jnp.where(left, 0.0, xp).astype(bf16)], axis=0
        )
        st = state[:, lanes]
        st_low = st.astype(bf16)
        save_ref[0, :, lanes] = st_low
        y = dot(both, stacked) + dot(c_low, st_low) * (jnp.exp(dp) * carried)
        mixed_ref[:, lanes] = (y + skip_ref[:, facts.chans(p)] * xs).astype(bf16)
        last = dp[Q - 1 : Q, :]
        to_end = (xp * (jnp.exp(last - dp) * samelast)).astype(bf16)
        state[:, lanes] = st * (jnp.exp(last) * carried[Q - 1 : Q, :]) + dot(b_t, to_end)


def mixer_fwd(traffic, extra, hid, gain, main, com, seg, segr, wk, bias, par, skip):
    length, depth = hid.shape
    xw = main.shape[1] // 2
    width = xw + 256
    n = length // Q
    whole = lambda shape: pl.BlockSpec(shape, lambda i: (0,) * len(shape), pipeline_mode=pl.Buffered(1))
    ahead = lambda i: (jnp.minimum(i, n - 1), 0)
    now = lambda i: (jnp.maximum(i - 1, 0), 0)
    now3 = lambda i: (jnp.maximum(i - 1, 0), 0, 0)
    return pl.pallas_call(
        functools.partial(fwd_kernel, traffic),
        grid=(n + 1,),
        in_specs=[
            pl.BlockSpec((Q, depth), ahead),
            whole(gain.shape),
            whole(main.shape),
            whole(com.shape),
            whole(seg.shape),
            pl.BlockSpec((1, 1, Q), now3),
            whole(wk.shape),
            whole(bias.shape),
            whole(par.shape),
            whole(skip.shape),
        ]
        + [pl.BlockSpec(memory_space=pl.ANY)] * len(extra),
        out_specs=[
            pl.BlockSpec((Q, width), ahead),
            pl.BlockSpec((Q, 128), ahead),
            pl.BlockSpec((Q, xw), ahead),
            pl.BlockSpec((Q, depth), ahead),
            pl.BlockSpec((Q, xw), now),
            pl.BlockSpec((1, 128, xw), now3),
        ]
        + [pl.BlockSpec(memory_space=pl.ANY)] * len(traffic.outputs),
        out_shape=[
            jax.ShapeDtypeStruct((length, width), bf16),
            jax.ShapeDtypeStruct((length, 128), bf16),
            jax.ShapeDtypeStruct((length, xw), f32),
            jax.ShapeDtypeStruct((length, depth), bf16),
            jax.ShapeDtypeStruct((length, xw), bf16),
            jax.ShapeDtypeStruct((n, 128, xw), bf16),
            *traffic.outputs,
        ],
        scratch_shapes=[
            pltpu.VMEM((128, xw), f32),
            pltpu.VMEM((Q + 8, width), f32),
            pltpu.VMEM((Q, width), f32),
            pltpu.VMEM((Q, width), f32),
            pltpu.VMEM((Q, 128), f32),
            *traffic.scratch,
        ],
        compiler_params=pltpu.CompilerParams(
            vmem_limit_bytes=48 * 2**20,
            collective_id=traffic.collective_id,
            has_side_effects=traffic.collective_id is not None,
        ),
        name="mixer_forward",
    )(hid, gain, main, com, seg, segr, wk, bias, par, skip, *extra)


def bwd_kernel(traffic, u_ref, halo_ref, dt_ref, seg_ref, segr_ref, wk_ref, bias_ref, par_ref, skip_ref,
               save_ref, dy_ref, *rest):
    n_in, n_out = len(traffic.inputs), len(traffic.outputs)
    extra_in, rest = rest[:n_in], rest[n_in:]
    du_ref, ddt_ref, small_ref = rest[:3]
    extra_out, rest = rest[3 : 3 + n_out], rest[3 + n_out :]
    dstate, useen, act, slope, dpre, keep_y, keep_x, prod_a, prod_b, rows_a, held = rest[:11]
    wgrad_ref, hgrad_ref, sgrad_ref, spot_ref = rest[11:15]
    step_no = pl.program_id(0)
    last_step = pl.num_programs(0) - 1
    traffic(*extra_in, *extra_out, *rest[15:]).step(step_no, last_step)
    width = u_ref.shape[1]
    xw = width - 256
    pairs = xw // 128

    @pl.when(step_no == 0)
    def _():
        dstate[...] = jnp.zeros_like(dstate)
        dpre[Q : Q + 8, :] = jnp.zeros((8, width), f32)
        wgrad_ref[...] = jnp.zeros_like(wgrad_ref)
        hgrad_ref[...] = jnp.zeros_like(hgrad_ref)
        sgrad_ref[...] = jnp.zeros_like(sgrad_ref)
        rows_a[...] = jnp.zeros_like(rows_a)
        head_of = lax.broadcasted_iota(jnp.int32, (xw, 128), 0) // P_SIZE
        mark = head_of == lax.broadcasted_iota(jnp.int32, (xw, 128), 1)
        spot_ref[...] = jnp.where(mark, 1.0, 0.0).astype(bf16)

    useen[0:8, :] = halo_ref[...].astype(f32)[8:16, :]
    useen[8 : 8 + Q, :] = u_ref[...].astype(f32)
    facts = Facts(last_step - step_no, seg_ref, par_ref, xw)
    flags, carried, samelast = facts.before, facts.carried, facts.samelast
    for p in range(width // 128):
        lanes = slice(128 * p, 128 * p + 128)
        pre = conv_pre(useen, flags, wk_ref, bias_ref, lanes, facts.chans(p))
        sg = sigmoid(pre)
        act[:, lanes] = pre * sg
        slope[:, lanes] = sg * (1.0 + pre * (1.0 - sg))

    raw = dt_ref[...].astype(f32) + facts.bias
    step = softplus(raw)
    rate = facts.rate
    row = lax.broadcasted_iota(jnp.int32, (Q, Q), 0)
    col = lax.broadcasted_iota(jnp.int32, (Q, Q), 1)
    tri = jnp.where(row >= col, 1.0, 0.0).astype(bf16)
    upper = jnp.where(row <= col, 1.0, 0.0).astype(bf16)
    below = jnp.where(row > col, 1.0, 0.0).astype(bf16)
    decay = dot3(tri, step * rate)
    decay_t = decay.T
    madd = jnp.where((row <= col) & (facts.now == segr_ref[0]), 0.0, NEG)
    b_now, c_now = act[:, xw : xw + 128], act[:, xw + 128 : xw + 256]
    b_low, c_low = b_now.astype(bf16), c_now.astype(bf16)
    c_t = c_now.T.astype(bf16)
    gram = dot_nt(b_low, c_low)
    left = lax.broadcasted_iota(jnp.int32, (Q, 128), 1) < 64
    lane = lax.broadcasted_iota(jnp.int32, (Q, 128), 1)
    dgram = jnp.zeros((Q, Q), f32)
    cols_b = jnp.zeros((Q, 128), f32)
    for p in range(pairs):
        lanes = slice(128 * p, 128 * p + 128)
        d0, d1 = spread_col(decay, 2 * p), spread_col(decay, 2 * p + 1)
        dp = jnp.where(left, d0, d1)
        sp = jnp.where(left, spread_col(step, 2 * p), spread_col(step, 2 * p + 1))
        xs = act[:, lanes]
        xp = xs * sp
        dy_low = dy_ref[:, lanes]
        dy = dy_low.astype(f32)
        stacked = jnp.concatenate(
            [jnp.where(left, dy, 0.0).astype(bf16), jnp.where(left, 0.0, dy).astype(bf16)], axis=0
        )
        pair = dot_nt(xp.astype(bf16), stacked)
        mts = []
        for k, dk in ((0, d0), (1, d1)):
            h = 2 * p + k
            e = jnp.exp(decay_t[h : h + 1, :] - dk + madd)
            f = e * pair[:, 128 * k : 128 * k + 128]
            dgram = dgram + f
            w = gram * f
            mts.append((gram * e).astype(bf16))
            rows_a[h : h + 1, :] = jnp.sum(w, axis=0, keepdims=True)
            cols_b = jnp.where(lane == h, jnp.sum(w, axis=1, keepdims=True), cols_b)
        within = dot(jnp.concatenate(mts, axis=1), stacked)
        grow = jnp.exp(dp) * carried
        dy_in = dy * grow
        dy_in_low = dy_in.astype(bf16)
        keep_y[:, lanes] = dy_in_low
        st = save_ref[0, :, lanes]
        prod_a[:, lanes] = (dy_in * dot(c_low, st)).astype(bf16)
        last = dp[Q - 1 : Q, :]
        fade = jnp.exp(last - dp) * samelast
        ds = dstate[:, lanes]
        ds_low = ds.astype(bf16)
        xe = xp * fade
        keep_x[:, lanes] = xe.astype(bf16)
        later = dot(b_low, ds_low)
        prod_b[:, lanes] = (xe * later).astype(bf16)
        retain = jnp.exp(last) * carried[Q - 1 : Q, :]
        held[0:1, lanes] = jnp.sum(ds * st.astype(f32), axis=0, keepdims=True) * retain
        dxs = sp * (within + later * fade) + skip_ref[:, facts.chans(p)] * dy
        skp = xs * dy
        sgrad_ref[:, lanes] += jnp.sum(skp.reshape(Q // 8, 8, 128), axis=0)
        dpre[0:Q, lanes] = dxs * slope[:, lanes]
        dstate[:, lanes] = ds * retain + dot(c_t, dy_in_low)
        if p == 0:
            db_in, dc_in = dot_nt(keep_x[:, lanes], ds_low), dot_nt(dy_in_low, st)
        else:
            db_in, dc_in = db_in + dot_nt(keep_x[:, lanes], ds_low), dc_in + dot_nt(dy_in_low, st)

    dg_low = dgram.astype(bf16)
    db = dot(dg_low, c_low) + db_in
    dc = dot(dgram.T.astype(bf16), b_low) + dc_in
    dpre[0:Q, xw : xw + 128] = db * slope[:, xw : xw + 128]
    dpre[0:Q, xw + 128 : xw + 256] = dc * slope[:, xw + 128 : xw + 256]

    spot = spot_ref[...]
    a_in = dot(prod_a[...], spot)
    b_in = dot(prod_b[...], spot)
    hv = jnp.broadcast_to(held[0:1, :], (8, xw))
    h_hi = hv.astype(bf16)
    h_lo = (hv - h_hi.astype(f32)).astype(bf16)
    through = (dot(h_hi, spot) + dot(h_lo, spot))[0:1, :]
    a_own = rows_a[...].T
    cross = dot3(upper, a_own - cols_b + a_in) + dot3(below, b_in) + through
    total = cols_b + b_in
    sg = sigmoid(raw)
    ratio = jnp.where(step > 1e-30, sg / jnp.maximum(step, 1e-30), 1.0)
    draw = total * ratio + rate * cross * sg
    ddt_ref[...] = facts.back(draw).astype(bf16)
    hgrad_ref[0:8, :] += jnp.sum(draw.reshape(Q // 8, 8, 128), axis=0)
    hgrad_ref[8:16, :] += jnp.sum((step * cross).reshape(Q // 8, 8, 128), axis=0)

    ahead = [None] + [facts.after(j) for j in (1, 2, 3)]
    for p in range(width // 128):
        lanes = slice(128 * p, 128 * p + 128)
        own = dpre[0:Q, lanes]
        chans = facts.chans(p)
        du = wk_ref[3:4, chans] * own
        wgrad_ref[24:32, lanes] += jnp.sum((own * useen[8 : 8 + Q, lanes]).reshape(Q // 8, 8, 128), axis=0)
        wgrad_ref[32:40, lanes] += jnp.sum(own.reshape(Q // 8, 8, 128), axis=0)
        for j in (1, 2, 3):
            du = du + wk_ref[3 - j : 4 - j, chans] * (dpre[j : j + Q, lanes] * ahead[j])
            moved = own * (useen[8 - j : 8 - j + Q, lanes] * flags[j])
            k = 3 - j
            wgrad_ref[8 * k : 8 * k + 8, lanes] += jnp.sum(moved.reshape(Q // 8, 8, 128), axis=0)
        du_ref[:, lanes] = du.astype(bf16)
    first = dpre[0:8, :]
    dpre[Q : Q + 8, :] = first

    @pl.when(step_no == last_step)
    def _():
        small_ref[...] = jnp.zeros_like(small_ref)
        for k in range(5):
            small_ref[k : k + 1, :] = jnp.sum(wgrad_ref[8 * k : 8 * k + 8, :], axis=0, keepdims=True)
        small_ref[5:6, 0:128] = jnp.sum(hgrad_ref[0:8, :], axis=0, keepdims=True)
        small_ref[6:7, 0:128] = rate * jnp.sum(hgrad_ref[8:16, :], axis=0, keepdims=True)
        skips = sgrad_ref[...]
        hi = skips.astype(bf16)
        mid = (skips - hi.astype(f32)).astype(bf16)
        by_head = dot(hi, spot_ref[...]) + dot(mid, spot_ref[...])
        small_ref[7:8, 0:128] = jnp.sum(by_head, axis=0, keepdims=True)


def mixer_bwd(traffic, extra, u, dt, seg, segr, wk, bias, par, skip, save, dy):
    length, width = u.shape
    xw = width - 256
    n = length // Q
    whole = lambda shape: pl.BlockSpec(shape, lambda i: (0,) * len(shape))
    back = lambda i: (n - 1 - i, 0)
    return pl.pallas_call(
        functools.partial(bwd_kernel, traffic),
        grid=(n,),
        in_specs=[
            pl.BlockSpec((Q, width), back),
            pl.BlockSpec((16, width), lambda i: (jnp.maximum((n - 1 - i) * (Q // 16) - 1, 0), 0)),
            pl.BlockSpec((Q, 128), back),
            whole(seg.shape),
            pl.BlockSpec((1, 1, Q), lambda i: (n - 1 - i, 0, 0)),
            whole(wk.shape),
            whole(bias.shape),
            whole(par.shape),
            whole(skip.shape),
            pl.BlockSpec((1, 128, xw), lambda i: (n - 1 - i, 0, 0)),
            pl.BlockSpec((Q, xw), back),
        ]
        + [pl.BlockSpec(memory_space=pl.ANY)] * len(extra),
        out_specs=[
            pl.BlockSpec((Q, width), back),
            pl.BlockSpec((Q, 128), back),
            whole((8, width)),
        ]
        + [pl.BlockSpec(memory_space=pl.ANY)] * len(traffic.outputs),
        out_shape=[
            jax.ShapeDtypeStruct((length, width), bf16),
            jax.ShapeDtypeStruct((length, 128), bf16),
            jax.ShapeDtypeStruct((8, width), f32),
            *traffic.outputs,
        ],
        scratch_shapes=[
            pltpu.VMEM((128, xw), f32),
            pltpu.VMEM((Q + 8, width), f32),
            pltpu.VMEM((Q, width), f32),
            pltpu.VMEM((Q, width), f32),
            pltpu.VMEM((Q + 8, width), f32),
            pltpu.VMEM((Q, xw), bf16),
            pltpu.VMEM((Q, xw), bf16),
            pltpu.VMEM((Q, xw), bf16),
            pltpu.VMEM((Q, xw), bf16),
            pltpu.VMEM((128, 128), f32),
            pltpu.VMEM((8, xw), f32),
            pltpu.VMEM((40, width), f32),
            pltpu.VMEM((16, 128), f32),
            pltpu.VMEM((8, xw), f32),
            pltpu.VMEM((xw, 128), bf16),
            *traffic.scratch,
        ],
        compiler_params=pltpu.CompilerParams(
            vmem_limit_bytes=48 * 2**20,
            collective_id=traffic.collective_id,
            has_side_effects=traffic.collective_id is not None,
        ),
        name="mixer_backward",
    )(u, u, dt, seg, segr, wk, bias, par, skip, save, dy, *extra)


MESH = pl.DeviceIdType.MESH
ANY = pl.ANY
PARTS = 4


def remote(src, dst, send_sem, recv_sem, device):
    return pltpu.make_async_remote_copy(
        src_ref=src, dst_ref=dst, send_sem=send_sem, recv_sem=recv_sem, device_id=device, device_id_type=MESH
    )


class Place:
    def __init__(self):
        self.w, self.s = lax.axis_index("wshard"), lax.axis_index("seq")
        self.z, self.x = self.w // 2, lax.rem(self.w, 2)
        self.y, self.c = self.s // 2, lax.rem(self.s, 2)
        self.s_sib = 2 * self.y + 1 - self.c
        self.s_far = 2 * (1 - self.y) + self.c
        self.s_diag = 2 * (1 - self.y) + 1 - self.c
        self.side = (2 * self.z + 1 - self.x, self.s)
        self.up = (lax.rem(self.w + 2, 8), self.s)
        self.down = (lax.rem(self.w + 6, 8), self.s)
        self.sib = (self.w, self.s_sib)
        self.far = (self.w, self.s_far)

    def greet(self, everyone=False, sequence=False):
        barrier = pltpu.get_barrier_semaphore()
        others = [(lax.rem(self.w + k, 8), self.s) for k in range(1, 8)] if everyone else []
        if everyone or sequence:
            others += [(self.w, lax.rem(self.s + k, 4)) for k in range(1, 4)]
        else:
            others = [self.side, self.up, self.down, self.sib, self.far]
        for other in others:
            pl.semaphore_signal(barrier, inc=1, device_id=other, device_id_type=MESH)
        pl.semaphore_wait(barrier, len(others))


def dma(*shape):
    return pltpu.SemaphoreType.DMA(shape)


def gather_pieces_start(at, own, slot, sems, stage=None):
    send, recv, local = sems[:3]
    rows = own.shape[0] // PARTS
    for k in range(PARTS):
        part = pl.ds(k * rows, rows)
        remote(own.at[part], slot(at.s).at[part], send.at[1, k], recv.at[1, k], at.far).start()
    for k in range(PARTS):
        part = pl.ds(k * rows, rows)
        remote(own.at[part], slot(at.s).at[part], send.at[0, k], recv.at[0, k], at.sib).start()
    if stage is not None:
        copy = pltpu.make_async_copy(own, stage, local)
        copy.start()
        copy.wait()
    pltpu.make_async_copy(own if stage is None else stage, slot(at.s), local).start()


def gather_pieces_pass(at, own, slot, sems):
    send, recv, _ = sems
    rows = own.shape[0] // PARTS
    for k in range(PARTS):
        part = pl.ds(k * rows, rows)
        theirs = slot(at.s_far).at[part]
        remote(theirs, theirs, send.at[1, k], recv.at[1, k], at.far).wait_recv()
        remote(theirs, theirs, send.at[2, k], recv.at[2, k], at.sib).start()


def gather_pieces_end(at, own, slot, sems):
    send, recv, local = sems
    rows = own.shape[0] // PARTS
    pltpu.make_async_copy(own, slot(at.s), local).wait()
    for k in range(PARTS):
        part = pl.ds(k * rows, rows)
        sib, diag, far = slot(at.s_sib).at[part], slot(at.s_diag).at[part], slot(at.s_far).at[part]
        remote(own.at[part], slot(at.s).at[part], send.at[0, k], recv.at[0, k], at.sib).wait_send()
        remote(own.at[part], slot(at.s).at[part], send.at[1, k], recv.at[1, k], at.far).wait_send()
        remote(far, far, send.at[2, k], recv.at[2, k], at.sib).wait_send()
        remote(sib, sib, send.at[0, k], recv.at[0, k], at.sib).wait_recv()
        remote(diag, diag, send.at[2, k], recv.at[2, k], at.sib).wait_recv()


CUTS = 2


def gather_shards(at, main, com, main_all, com_all, stage, sems, between):
    send, recv, csend, crecv, psend, precv, local = sems
    half, cut = com.shape[0] // 2, main.shape[0] // CUTS
    mine = pl.ds(pl.multiple_of(at.c * half, half), half)
    load = pltpu.make_async_copy(main, stage[0], local.at[0])
    com_load = pltpu.make_async_copy(com, stage[1], local.at[1])
    keep = pltpu.make_async_copy(stage[0], main_all.at[at.w], local.at[0])
    com_keep = pltpu.make_async_copy(stage[1], com_all.at[at.w], local.at[1])

    def hop(zp, q, way, device, own=False):
        w, n, part = 2 * zp + at.x, zp * CUTS + q, pl.ds(q * cut, cut)
        slot, com_slot = main_all.at[w, part], com_all.at[w, mine]
        copies = [remote(main.at[part] if own else slot, slot, send.at[way, n], recv.at[w * CUTS + q], device)]
        if q == 0:
            copies.append(remote(com.at[mine] if own else com_slot, com_slot, csend.at[way, zp], crecv.at[w], device))
        return copies

    def begin(copies):
        for copy in copies:
            copy.start()

    def sent(copies):
        for copy in copies:
            copy.wait_send()

    def all_ways(act, q):
        act(hop(at.z, q, 0, at.side, True))

        @pl.when(at.z < 3)
        def _():
            act(hop(at.z, q, 1, at.up, True))

        @pl.when(at.z > 0)
        def _():
            act(hop(at.z, q, 2, at.down, True))

    def arrived(w, q):
        slot = main_all.at[w, pl.ds(q * cut, cut)]
        remote(slot, slot, send.at[0, 0], recv.at[w * CUTS + q], at.side).wait_recv()
        if q == 0:
            held = com_all.at[w, mine]
            remote(held, held, csend.at[0, 0], crecv.at[w], at.side).wait_recv()
            remote(held, held, psend.at[w], precv.at[w], at.sib).start()

    for q in range(CUTS):
        if q > 0:
            all_ways(sent, q - 1)
        all_ways(begin, q)
        if q == 0:
            load.start()
            com_load.start()
            load.wait()
            com_load.wait()
            keep.start()
            com_keep.start()
    for d in (1, 2, 3):
        if d == 3:
            between()
        for q in range(CUTS):

            @pl.when(at.z - d >= 0)
            def _():
                zp = at.z - d
                arrived(2 * zp + at.x, q)

                @pl.when(at.z < 3)
                def _():
                    begin(hop(zp, q, 1, at.up))

                begin(hop(zp, q, 0, at.side))

            @pl.when(at.z + d <= 3)
            def _():
                zp = at.z + d
                arrived(2 * zp + at.x, q)

                @pl.when(at.z > 0)
                def _():
                    begin(hop(zp, q, 2, at.down))

                begin(hop(zp, q, 0, at.side))

    for zp in range(4):
        for q in range(CUTS):
            arrived(2 * zp + 1 - at.x, q)
    keep.wait()
    com_keep.wait()
    all_ways(sent, CUTS - 1)
    for zp in range(4):
        for q in range(CUTS):

            @pl.when(at.z != zp)
            def _():
                sent(hop(zp, q, 0, at.side))

            @pl.when((at.z < 3) & (zp < at.z))
            def _():
                sent(hop(zp, q, 1, at.up))

            @pl.when((at.z > 0) & (zp > at.z))
            def _():
                sent(hop(zp, q, 2, at.down))

    other = pl.ds(pl.multiple_of((1 - at.c) * half, half), half)
    for k in range(1, 8):
        w = lax.rem(at.w + k, 8)
        gone, got = com_all.at[w, mine], com_all.at[w, other]
        remote(gone, gone, psend.at[w], precv.at[w], at.sib).wait_send()
        remote(got, got, psend.at[w], precv.at[w], at.sib).wait_recv()


def gather_kernel(hid, main, com, hid_all, main_all, com_all, hid_v, main_v, com_v, *sems):
    at = Place()
    at.greet()
    slot = lambda s: hid_all.at[s]
    gather_pieces_start(at, hid, slot, sems[0:3], hid_v)
    pass_on = lambda: gather_pieces_pass(at, hid, slot, sems[0:3])
    gather_shards(at, main, com, main_all, com_all, (main_v, com_v), sems[3:10], pass_on)
    gather_pieces_end(at, hid, slot, sems[0:3])


def gather_first(hid, main, com):
    shape = lambda n, v: jax.ShapeDtypeStruct((n,) + v.shape, v.dtype)
    return pl.pallas_call(
        gather_kernel,
        in_specs=[pl.BlockSpec(memory_space=ANY)] * 3,
        out_specs=[pl.BlockSpec(memory_space=ANY)] * 3,
        out_shape=[shape(4, hid), shape(8, main), shape(8, com)],
        scratch_shapes=[pltpu.VMEM(v.shape, v.dtype) for v in (hid, main, com)]
        + [dma(3, PARTS), dma(3, PARTS), dma()]
        + [dma(3, 4 * CUTS), dma(8 * CUTS), dma(3, 4), dma(8), dma(8), dma(8), dma(2)],
        compiler_params=pltpu.CompilerParams(collective_id=1, has_side_effects=True),
        name="gather_first",
    )(hid, main, com)


SLICES = 8


def each_slice(body):
    def run(k, _):
        body(k)
        return 0

    lax.fori_loop(0, SLICES, run, 0)


def forward_traffic(cot, rows):
    class Traffic:
        inputs = (cot, rows)
        outputs = (
            jax.ShapeDtypeStruct((4,) + cot.shape, cot.dtype),
            jax.ShapeDtypeStruct((2,) + rows.shape, rows.dtype),
        )
        scratch = (
            pltpu.VMEM(cot.shape, cot.dtype),
            pltpu.VMEM(rows.shape, rows.dtype),
            dma(3, SLICES),
            dma(3, SLICES),
            dma(),
            dma(3, SLICES),
            dma(2, SLICES),
            dma(),
        )
        collective_id = 2

        def __init__(self, own, row_own, full, row_full, stage, rstage, send, recv, local, rsend, rrecv, rlocal):
            self.at = at = Place()
            self.own, self.full, self.row_own, self.row_full = own, full, row_own, row_full
            self.rrecv = rrecv
            cut, rcut = own.shape[0] // SLICES, row_own.shape[0] // SLICES
            part = lambda k: pl.ds(pl.multiple_of(k * cut, cut), cut)
            rpart = lambda k: pl.ds(pl.multiple_of(k * rcut, rcut), rcut)
            piece = lambda s, k: full.at[s, part(k)]
            self.load = pltpu.make_async_copy(own, stage, local)
            self.keep = pltpu.make_async_copy(stage, full.at[at.s], local)
            self.rload = pltpu.make_async_copy(row_own, rstage, rlocal)
            self.rkeep = pltpu.make_async_copy(rstage, row_full.at[at.x], rlocal)
            self.to_sib = lambda k: remote(own.at[part(k)], piece(at.s, k), send.at[0, k], recv.at[0, k], at.sib)
            self.to_far = lambda k: remote(own.at[part(k)], piece(at.s, k), send.at[1, k], recv.at[1, k], at.far)
            self.pass_on = lambda k: remote(piece(at.s_far, k), piece(at.s_far, k), send.at[2, k], recv.at[2, k], at.sib)
            here = lambda k, n, device: remote(
                row_full.at[at.x, rpart(k)], row_full.at[at.x, rpart(k)], rsend.at[n, k], rrecv.at[at.x, k], device
            )
            self.rows = (lambda k: here(k, 0, at.side), lambda k: here(k, 1, at.up), lambda k: here(k, 2, at.down))
            got = lambda s, n, k: remote(piece(s, k), piece(s, k), send.at[n, k], recv.at[n, k], at.sib)
            self.from_sib = lambda k: got(at.s_sib, 0, k)
            self.from_far = lambda k: got(at.s_far, 1, k)
            self.from_diag = lambda k: got(at.s_diag, 2, k)
            other = lambda k: row_full.at[1 - at.x, rpart(k)]
            self.from_side = lambda k: remote(other(k), other(k), rsend.at[0, k], rrecv.at[1 - at.x, k], at.side)

        def step(self, i, last):
            at = self.at
            upward, downward = (at.z >= at.s) & (at.z < 3), (at.z <= at.s) & (at.z > 0)
            side, up, down = self.rows

            @pl.when(i == 0)
            def _():
                at.greet()
                self.load.start()
                each_slice(lambda k: self.to_sib(k).start())

                @pl.when(at.z == at.s)
                def _():
                    self.rload.start()
                    self.rload.wait()
                    self.rkeep.start()
                    self.rkeep.wait()

                self.load.wait()
                self.keep.start()

            k = i - 1

            @pl.when((k >= 0) & (k < SLICES))
            def _():
                self.to_far(k).start()

            @pl.when((k >= SLICES) & (k < 2 * SLICES))
            def _():
                self.from_far(k - SLICES).wait_recv()
                self.pass_on(k - SLICES).start()

            far_away = jnp.where(at.z > at.s, at.z - at.s, at.s - at.z)
            v = 3 * i - 6 * far_away + 1
            r = jnp.where(v >= 0, lax.div(v, 4), -1)

            @pl.when((r >= 0) & (r < SLICES) & (4 * r < v))
            def _():
                @pl.when(at.z != at.s)
                def _():
                    side(r).wait_recv()

                side(r).start()

                @pl.when(upward)
                def _():
                    up(r).start()

                @pl.when(downward)
                def _():
                    down(r).start()

            @pl.when(i == last)
            def _():
                self.keep.wait()

                def finish(k):
                    self.to_sib(k).wait_send()
                    self.to_far(k).wait_send()
                    self.pass_on(k).wait_send()
                    self.from_sib(k).wait_recv()
                    self.from_diag(k).wait_recv()
                    side(k).wait_send()
                    self.from_side(k).wait_recv()

                    @pl.when(upward)
                    def _():
                        up(k).wait_send()

                    @pl.when(downward)
                    def _():
                        down(k).wait_send()

                each_slice(finish)

    return Traffic


def add_into(dst, src, rows):
    step = next(n for n in (64, 48, 32, 16) if rows % n == 0)

    def body(i, _):
        part = pl.ds(pl.multiple_of(i * step, 16), step)
        dst[part, :] = (dst[part, :].astype(f32) + src[part, :].astype(f32)).astype(bf16)
        return 0

    lax.fori_loop(0, rows // step, body, 0)


def far_first(at, i):
    inner = (at.z == 1) | (at.z == 2)
    i = jnp.where(inner & (i >= 2), 5 - i, i)
    return jnp.where(at.z < 2, 3 - i, i)


class ReduceShards:
    def __init__(self, at, partial, cuts, acc, from_side, from_down, from_up, sems):
        self.at, self.partial, self.cuts, self.acc = at, partial, cuts, acc
        self.from_side, self.from_down, self.from_up = from_side, from_down, from_up
        self.send, self.recv_side, self.recv_down, self.recv_up = sems
        self.rows = acc.shape[1] // cuts

    def unit(self, j):
        if isinstance(j, int):
            shard, cut = j // self.cuts, j % self.cuts
        else:
            shard, cut = lax.div(j, self.cuts), lax.rem(j, self.cuts)
        zp = far_first(self.at, shard)
        return zp, zp * self.cuts + cut, pl.ds(pl.multiple_of(cut * self.rows, self.rows), self.rows)

    def side_copy(self, j):
        at = self.at
        zp, n, part = self.unit(j)
        return remote(
            self.partial(zp).at[part], self.from_side.at[zp, part],
            self.send.at[0, n], self.recv_side.at[n], at.side,
        )

    def up_copy(self, j):
        zp, n, part = self.unit(j)
        return remote(
            self.acc.at[zp, part], self.from_down.at[zp, part], self.send.at[1, n], self.recv_down.at[n], self.at.up
        )

    def down_copy(self, j):
        zp, n, part = self.unit(j)
        return remote(
            self.acc.at[zp, part], self.from_up.at[zp, part], self.send.at[2, n], self.recv_up.at[n], self.at.down
        )

    def start(self):
        self.side_copy(0).start()
        self.side_copy(1).start()

    def step(self, j):
        at = self.at
        zp, _, part = self.unit(j)
        self.side_copy(j).wait()
        acc = self.acc.at[zp, part]
        add_into(acc, self.from_side.at[zp, part], self.rows)

        @pl.when((at.z > 0) & (zp >= at.z))
        def _():
            self.up_copy(j).wait_recv()
            add_into(acc, self.from_down.at[zp, part], self.rows)

        @pl.when((at.z < 3) & (zp <= at.z))
        def _():
            self.down_copy(j).wait_recv()
            add_into(acc, self.from_up.at[zp, part], self.rows)

        @pl.when(zp > at.z)
        def _():
            self.up_copy(j).start()

        @pl.when(zp < at.z)
        def _():
            self.down_copy(j).start()

    def end(self):
        at = self.at
        for j in range(4 * self.cuts):
            zp = self.unit(j)[0]

            @pl.when(zp > at.z)
            def _():
                self.up_copy(j).wait_send()

            @pl.when(zp < at.z)
            def _():
                self.down_copy(j).wait_send()


def backward_traffic(layer, rows, gate):
    piece, cols = layer.shape[1:]
    rrows = rows.shape[1]
    grows, gcols = gate.shape[1:]

    class Traffic:
        inputs = (layer, rows, gate)
        outputs = (
            jax.ShapeDtypeStruct((piece, cols), f32),
            jax.ShapeDtypeStruct((rrows, cols), bf16),
            jax.ShapeDtypeStruct((grows, gcols), bf16),
        )
        scratch = (
            *[pltpu.VMEM((piece, cols), bf16)] * 5,
            pltpu.VMEM((piece, cols), f32),
            *[pltpu.VMEM((rrows, cols), bf16)] * 4,
            dma(3, SLICES),
            dma(3, SLICES),
            dma(3),
            dma(3, SLICES),
            dma(3, SLICES),
            dma(2),
            dma(2, SLICES),
            dma(2, SLICES),
            *[pltpu.VMEM((4, grows, gcols), bf16)] * 4,
            dma(3, 8),
            dma(8),
            dma(8),
            dma(8),
            dma(5),
        )
        collective_id = 3

        def __init__(
            self, layer, rows, gate, out, rows_out, gate_out,
            own_v, far_v, sib_v, pass_v, got_v, sum_v, acc, side_v, low_v, high_v,
            send, recv, local, rsend, rrecv, rlocal, fsend, frecv,
            gacc, gside, glow, ghigh, gsend, grecv_side, grecv_low, grecv_high, glocal,
        ):
            self.at = at = Place()
            cut, rcut = piece // SLICES, rrows // SLICES
            part = lambda k: pl.ds(pl.multiple_of(k * cut, cut), cut)
            rpart = lambda k: pl.ds(pl.multiple_of(k * rcut, rcut), rcut)
            self.own, self.sib, self.passed, self.got, self.sum = own_v, sib_v, pass_v, got_v, sum_v
            self.part, self.rpart, self.cut, self.rcut = part, rpart, cut, rcut
            self.far_v, self.acc, self.side_v, self.low_v, self.high_v = far_v, acc, side_v, low_v, high_v
            self.load_far = pltpu.make_async_copy(layer.at[at.s_far], far_v, local.at[0])
            self.load_own = pltpu.make_async_copy(layer.at[at.s], own_v, local.at[1])
            self.store = pltpu.make_async_copy(sum_v, out, local.at[2])
            self.to_pass = lambda k: remote(
                layer.at[at.s_diag, part(k)], pass_v.at[part(k)], send.at[0, k], recv.at[0, k], at.sib
            )
            self.to_sib = lambda k: remote(
                layer.at[at.s_sib, part(k)], sib_v.at[part(k)], send.at[1, k], recv.at[1, k], at.sib
            )
            self.to_far = lambda k: remote(
                far_v.at[part(k)], got_v.at[part(k)], send.at[2, k], recv.at[2, k], at.far
            )
            self.load_acc = pltpu.make_async_copy(rows.at[at.x], acc, rlocal.at[0])
            self.store_acc = pltpu.make_async_copy(acc, rows_out, rlocal.at[1])
            spread = lambda k, n, device: remote(
                acc.at[rpart(k)], rows_out.at[rpart(k)], fsend.at[n, k], frecv.at[n, k], device
            )
            self.spread_far = lambda k: spread(k, 0, at.far)
            self.spread_sib = lambda k: spread(k, 1, at.sib)
            self.spread_on = lambda k: remote(
                rows_out.at[rpart(k)], rows_out.at[rpart(k)], fsend.at[1, k], frecv.at[1, k], at.sib
            )
            self.gates = ReduceShards(
                at, lambda zp: gate.at[2 * zp + 1 - at.x], 2, gacc, gside, glow, ghigh,
                (gsend, grecv_side, grecv_low, grecv_high),
            )
            self.load_gate = [
                pltpu.make_async_copy(gate.at[2 * zp + at.x], gacc.at[zp], glocal.at[zp]) for zp in range(4)
            ]
            self.store_gate = pltpu.make_async_copy(gacc.at[at.z], gate_out, glocal.at[4])
            self.to_side = lambda k: remote(
                rows.at[1 - at.x, rpart(k)], side_v.at[rpart(k)], rsend.at[0, k], rrecv.at[0, k], at.side
            )
            self.to_up = lambda k: remote(
                acc.at[rpart(k)], low_v.at[rpart(k)], rsend.at[1, k], rrecv.at[1, k], at.up
            )
            self.to_down = lambda k: remote(
                acc.at[rpart(k)], high_v.at[rpart(k)], rsend.at[2, k], rrecv.at[2, k], at.down
            )

        def step(self, i, last):
            at = self.at

            @pl.when(i == 0)
            def _():
                at.greet()
                self.load_far.start()
                self.load_own.start()
                self.load_acc.start()
                for copy in self.load_gate:
                    copy.start()
                each_slice(lambda k: self.to_pass(k).start())
                each_slice(lambda k: self.to_sib(k).start())

            @pl.when(i < SLICES)
            def _():
                self.to_side(i).start()

            @pl.when(i == 1)
            def _():
                self.load_far.wait()
                self.load_own.wait()
                self.load_acc.wait()
                for copy in self.load_gate:
                    copy.wait()

            k = i - 1

            @pl.when((k >= 0) & (k < SLICES))
            def _():
                self.to_pass(k).wait_recv()
                add_into(self.far_v.at[self.part(k)], self.passed.at[self.part(k)], self.cut)
                self.to_far(k).start()

            m = i - SLICES

            @pl.when((m >= 0) & (m < SLICES))
            def _():
                self.to_sib(m).wait_recv()
                self.to_far(m).wait_recv()
                p = self.part(m)
                self.sum[p, :] = (
                    self.own[p, :].astype(f32) + self.sib[p, :].astype(f32) + self.got[p, :].astype(f32)
                )

            ends = jnp.where(at.z > 3 - at.z, at.z, 3 - at.z)
            chain = jnp.where(at.z < at.s, at.z, jnp.where(at.z > at.s, 3 - at.z, ends))
            v = 10 * i - 17 * chain - 26 + 10
            r = jnp.where(v >= 0, lax.div(v, 11), -1)

            @pl.when((r >= 0) & (r < SLICES) & (11 * r < v))
            def _():
                acc = self.acc.at[self.rpart(r)]
                self.to_side(r).wait_recv()
                add_into(acc, self.side_v.at[self.rpart(r)], self.rcut)

                @pl.when((at.z <= at.s) & (at.z > 0))
                def _():
                    self.to_up(r).wait_recv()
                    add_into(acc, self.low_v.at[self.rpart(r)], self.rcut)

                @pl.when((at.z >= at.s) & (at.z < 3))
                def _():
                    self.to_down(r).wait_recv()
                    add_into(acc, self.high_v.at[self.rpart(r)], self.rcut)

                @pl.when(at.z < at.s)
                def _():
                    self.to_up(r).start()

                @pl.when(at.z > at.s)
                def _():
                    self.to_down(r).start()

                @pl.when(at.z == at.s)
                def _():
                    self.spread_far(r).start()
                    self.spread_sib(r).start()

            g = i - (last - 7)

            @pl.when(g >= 0)
            def _():
                self.gates.side_copy(g).start()

            inner = jnp.where((at.z == 1) | (at.z == 2), 1, 0)
            g = i - 11 - inner

            @pl.when(g >= 0)
            def _():
                self.gates.step(g)

            @pl.when(i == last)
            def _():
                def rest(k, _):
                    self.gates.step(k)
                    return 0

                lax.fori_loop(last - 10 - inner, 8, rest, 0)

                self.store.start()
                self.store_gate.start()

                @pl.when(at.s == at.z)
                def _():
                    self.store_acc.start()

                def forward(k):
                    @pl.when(at.s_far == at.z)
                    def _():
                        self.spread_far(k).wait_recv()
                        self.spread_on(k).start()

                each_slice(forward)

                def finish(k):
                    @pl.when(at.s == at.z)
                    def _():
                        self.spread_far(k).wait_send()
                        self.spread_sib(k).wait_send()

                    @pl.when(at.s_far == at.z)
                    def _():
                        self.spread_on(k).wait_send()

                    @pl.when((at.s_sib == at.z) | (at.s_diag == at.z))
                    def _():
                        self.spread_on(k).wait_recv()

                    self.to_pass(k).wait_send()
                    self.to_sib(k).wait_send()
                    self.to_far(k).wait_send()
                    self.to_side(k).wait_send()

                    @pl.when(at.z < at.s)
                    def _():
                        self.to_up(k).wait_send()

                    @pl.when(at.z > at.s)
                    def _():
                        self.to_down(k).wait_send()

                each_slice(finish)
                self.gates.end()
                self.store.wait()
                self.store_gate.wait()

                @pl.when(at.s == at.z)
                def _():
                    self.store_acc.wait()

    return Traffic


def mid_kernel(gate, mixed, cot, w_out, normed,
               d_mixed, d_gate, gate_part, out_part, layer_part,
               gate_v, mixed_v, cot_v, normed_v, w_v, a_v, low_v, dg_v, l_v, out_v, stats, got, *sems):
    at = Place()
    load, xsend, xrecv, store = sems
    length, wide = mixed_v.shape
    depth = cot_v.shape[1]
    piece = length // 4
    strips = wide // 128
    tiles = piece // 256
    part = lambda t: pl.ds(pl.multiple_of(t * 256, 256), 256)

    def loads(k):
        r = pl.ds(pl.multiple_of(k * piece, piece), piece)
        pairs = ((cot, cot_v), (gate, gate_v), (mixed, mixed_v))
        return [pltpu.make_async_copy(p.at[r], v.at[r], load.at[3 * k + n]) for n, (p, v) in enumerate(pairs)]

    w_load = pltpu.make_async_copy(w_out, w_v, load.at[12])
    normed_load = pltpu.make_async_copy(normed, normed_v, load.at[13])
    w_load.start()
    for k in range(4):
        for copy in loads(k):
            copy.start()
    normed_load.start()
    at.greet(sequence=True)

    stats[...] = jnp.zeros_like(stats)
    w_load.wait()

    def first(i, _):
        @pl.when(lax.rem(i, tiles) == 0)
        def _():
            for copy in loads(lax.div(i, tiles)):
                copy.wait()

        tile = part(i)
        a_v[tile, :] = dot_nt(cot_v[tile, :], w_v[...])
        sum_g, sum_a = jnp.zeros((256, 128), f32), jnp.zeros((256, 128), f32)
        for n in range(strips):
            col = slice(128 * n, 128 * n + 128)
            gt = gate_v[tile, col]
            g = mixed_v[tile, col].astype(f32) * (gt * sigmoid(gt))
            sum_g = sum_g + g * g
            sum_a = sum_a + a_v[tile, col] * g
        stats[0:1, tile] = jnp.sum(sum_g.T, axis=0, keepdims=True)
        stats[1:2, tile] = jnp.sum(sum_a.T, axis=0, keepdims=True)
        return 0

    lax.fori_loop(0, 4 * tiles, first, 0)

    peers = (at.s_sib, at.s_far, at.s_diag)
    swap = [remote(stats, got.at[k], xsend.at[k], xrecv.at[k], (at.w, s)) for k, s in enumerate(peers)]
    for copy in swap:
        copy.start()
    for copy in swap:
        copy.wait()
    total = stats[...] + got[0] + got[1] + got[2]
    r_row = lax.rsqrt(total[0:1] / E + eps)
    stats[0:1, :] = r_row
    stats[1:2, :] = r_row * r_row * r_row * (total[1:2] / E)

    def column(k, at_row):
        return jnp.broadcast_to(stats[k : k + 1, pl.ds(pl.multiple_of(at_row, 128), 256)], (128, 256)).T

    def second(i, _):
        tile = pl.ds(pl.multiple_of(i * 256, 256), 256)
        r, pull = column(0, i * 256), column(1, i * 256)
        for n in range(strips):
            col = slice(128 * n, 128 * n + 128)
            gt, mx = gate_v[tile, col], mixed_v[tile, col].astype(f32)
            sg = sigmoid(gt)
            silu = gt * sg
            g = mx * silu
            low_v[tile, col] = (g * r).astype(bf16)
            d_g = r * a_v[tile, col] - g * pull
            mixed_v[tile, col] = (d_g * silu).astype(bf16)
            dg_v[tile, col] = (d_g * mx * (sg * (1.0 + gt * (1.0 - sg)))).astype(bf16)
        l_v[tile, :] = dot(low_v[tile, :], w_v[...]).astype(bf16)
        layer_copy(i).start()
        return 0

    layer_copy = lambda i: pltpu.make_async_copy(l_v.at[part(i)], layer_part.at[part(i)], store.at[9 + i])
    lax.fori_loop(0, length // 256, second, 0)
    keep = [pltpu.make_async_copy(mixed_v, d_mixed, store.at[0]), pltpu.make_async_copy(dg_v, d_gate, store.at[1])]
    for copy in keep:
        copy.start()
    normed_load.wait()
    tn = lambda p, q: lax.dot_general(p, q, (((0,), (0,)), ((), ())), preferred_element_type=f32)

    def out_block(n):
        room = out_v.at[part(n)]
        return room, pltpu.make_async_copy(room, out_part.at[part(n)], store.at[2 + n])

    def out_grad(n, _):
        room, copy = out_block(n)
        room[...] = tn(low_v[:, part(n)], cot_v[...]).astype(bf16)
        copy.start()
        return 0

    lax.fori_loop(0, wide // 256, out_grad, 0)
    shard = depth // 4
    block = lambda n: pl.ds(pl.multiple_of(n * shard, shard), shard)
    gate_block = lambda n: pltpu.make_async_copy(low_v.at[block(n)], gate_part.at[block(n)], store.at[5 + n])

    def gate_grad(n, _):
        low_v[block(n), :] = tn(normed_v[:, block(n)], dg_v[...]).astype(bf16)
        gate_block(n).start()
        return 0

    lax.fori_loop(0, 4, gate_grad, 0)

    for copy in keep:
        copy.wait()
    for n in range(wide // 256):
        out_block(n)[1].wait()
    for n in range(4):
        gate_block(n).wait()
    for i in range(length // 256):
        layer_copy(i).wait()


def middle(gate, mixed, cot, w_out, normed):
    length, wide = mixed.shape
    depth = cot.shape[1]
    piece = length // 4
    vm = pltpu.VMEM
    low = lambda *shape: jax.ShapeDtypeStruct(shape, bf16)
    return pl.pallas_call(
        mid_kernel,
        in_specs=[pl.BlockSpec(memory_space=ANY)] * 5,
        out_specs=[pl.BlockSpec(memory_space=ANY)] * 5,
        out_shape=[
            low(length, wide),
            low(length, wide),
            low(depth, wide),
            low(wide, depth),
            low(length, depth),
        ],
        scratch_shapes=[
            vm((length, wide), f32),
            vm((length, wide), bf16),
            vm((length, depth), bf16),
            vm((length, depth), bf16),
            vm((wide, depth), bf16),
            vm((length, wide), f32),
            vm((length, wide), bf16),
            vm((length, wide), bf16),
            vm((length, depth), bf16),
            vm((wide, depth), bf16),
        ]
        + [vm((8, length), f32), vm((3, 8, length), f32)]
        + [dma(14), dma(3), dma(3), dma(17)],
        compiler_params=pltpu.CompilerParams(
            collective_id=5, has_side_effects=True, vmem_limit_bytes=61 * 2**20
        ),
        name="middle",
    )(gate, mixed, cot, w_out, normed)


def small_start(at, small, got, sems):
    send, recv = sems
    for k in range(1, 8):
        peer = (lax.rem(at.w + k, 8), at.s)
        remote(small, got.at[k], send.at[k], recv.at[k], peer).start()


def small_pass(at, small, got, total, full, sems, more):
    send, recv = sems
    send2, recv2, local = more
    value = small[...]
    for k in range(1, 8):
        remote(small, got.at[k], send.at[k], recv.at[k], at.side).wait_recv()
        value = value + got[k]
    total[...] = value
    pltpu.make_async_copy(total, full.at[at.s], local).start()
    for k, s in enumerate((at.s_sib, at.s_far, at.s_diag)):
        remote(total, full.at[at.s], send2.at[k], recv2.at[k], (at.w, s)).start()


def small_end(at, small, got, total, full, sems, more):
    send, recv = sems
    send2, recv2, local = more
    pltpu.make_async_copy(total, full.at[at.s], local).wait()
    for k in range(1, 8):
        remote(small, got.at[k], send.at[k], recv.at[k], at.side).wait_send()
    for k, s in enumerate((at.s_sib, at.s_far, at.s_diag)):
        remote(total, full.at[at.s], send2.at[k], recv2.at[k], (at.w, s)).wait_send()
        remote(total, full.at[s], send2.at[k], recv2.at[k], (at.w, s)).wait_recv()


def last_kernel(hid, d_gate, d_u, d_dt, w_main, w_com, gate_sum, small,
                back_sum, in_sum, sums_out,
                hid_v, dp_v, w_v,
                b_diag, b_sib, b_far, b_own, from_sib, pass_sib, from_far,
                part_v, mside, mlow, mhigh, macc, mown, csib, cown, cacc, cside, clow, chigh, cfar, csum,
                sgot, stotal, sfull, gate_v, *sems):
    at = Place()
    sems = list(sems)
    take = lambda n: [sems.pop(0) for _ in range(n)]
    load, bsem, msem, csem, cx, ssem, smore, asem, gsem = (
        take(6), take(2), take(4), take(4), take(7), take(2), take(3), take(3), take(3)
    )
    piece = hid_v.shape[0] // 4
    shard = hid_v.shape[1] // 8
    wide = d_gate.shape[1]
    half = shard // 2
    mine = pl.ds(pl.multiple_of(at.c * half, half), half)
    other = pl.ds(pl.multiple_of((1 - at.c) * half, half), half)
    at.greet(everyone=True)

    order = (at.s_diag, at.s_far, at.s_sib, at.s)
    rows_of = lambda s: pl.ds(pl.multiple_of(s * piece, piece), piece)
    weights = [
        pltpu.make_async_copy(w_main, w_v.at[:, pl.ds(0, 2 * wide)], load[0].at[0]),
        pltpu.make_async_copy(w_com, w_v.at[:, pl.ds(2 * wide, 384)], load[0].at[1]),
    ]
    loads = []
    for k, s in enumerate(order):
        r = rows_of(s)
        loads.append(
            [
                pltpu.make_async_copy(d_gate.at[r], dp_v.at[r, pl.ds(0, wide)], load[1].at[k]),
                pltpu.make_async_copy(d_u.at[r], dp_v.at[r, pl.ds(wide, wide + 256)], load[2].at[k]),
                pltpu.make_async_copy(d_dt.at[r], dp_v.at[r, pl.ds(2 * wide + 256, 128)], load[3].at[k]),
            ]
        )
    hid_load = pltpu.make_async_copy(hid, hid_v, load[4])
    soon, later = weights + loads[0] + loads[1], [hid_load] + loads[2] + loads[3]
    for copy in soon + later:
        copy.start()
    gate_slot = lambda s: in_sum.at[:, pl.ds(pl.multiple_of(s * wide, 128), wide)]
    x_slot = lambda s: in_sum.at[:, pl.ds(pl.multiple_of(E + s * wide, 128), wide)]
    gather_pieces_start(at, gate_sum, gate_slot, gsem, gate_v)
    small_start(at, small, sgot, ssem)

    send, recv = bsem
    rows = piece // PARTS
    parts = [pl.ds(k * rows, rows) for k in range(PARTS)]
    to_pass = [remote(b_diag.at[p], pass_sib.at[p], send.at[0, k], recv.at[0, k], at.sib) for k, p in enumerate(parts)]
    to_sib = [remote(b_sib.at[p], from_sib.at[p], send.at[1, k], recv.at[1, k], at.sib) for k, p in enumerate(parts)]
    to_far = [remote(b_far.at[p], from_far.at[p], send.at[2, k], recv.at[2, k], at.far) for k, p in enumerate(parts)]

    def back_tile(s, out, t):
        tile = pl.ds(pl.multiple_of(s * piece + t * 256, 256), 256)
        place = pl.ds(t * 256, 256)

        for n in range(hid_v.shape[1] // 256):
            col = slice(256 * n, 256 * n + 256)
            out[place, col] = dot_nt(dp_v[tile, :], w_v[col, :]).astype(bf16)

    big = ReduceShards(at, lambda zp: part_v.at[zp, 1 - at.x, :, pl.ds(0, wide)], 2, macc, mside, mlow, mhigh, msem)
    few = ReduceShards(at, lambda zp: cown.at[zp, 1 - at.x], 1, cacc, cside, clow, chigh, csem)
    com_cols = pl.ds(wide, 384)
    com_to_sib = lambda zp: remote(
        part_v.at[zp, :, other, com_cols], csib.at[zp], cx[0].at[zp], cx[1].at[zp], at.sib
    )

    def shard_pair(i):
        zp = far_first(at, i)
        lanes = pl.ds(pl.multiple_of(zp * 2 * shard, 128), 2 * shard)
        got = lax.dot_general(
            hid_v[:, lanes], dp_v[:, wide : 2 * wide + 384], (((0,), (0,)), ((), ())), preferred_element_type=f32
        ).astype(bf16)
        part_v[zp, 0] = got[0:shard]
        part_v[zp, 1] = got[shard : 2 * shard]
        macc[zp] = part_v[zp, at.x, :, 0:wide]
        big.side_copy(2 * i).start()
        com_to_sib(zp).start()

    def com_pair(i):
        zp = far_first(at, i)
        com_to_sib(zp).wait_recv()
        for x in range(2):
            cown[zp, x] = part_v[zp, x, mine, com_cols]
            add_into(cown.at[zp, x], csib.at[zp, x], half)
        cacc[zp] = cown[zp, at.x]
        few.side_copy(i).start()

    ends = (at.z == 0) | (at.z == 3)

    def step(j, who):
        @pl.when(who)
        def _():
            big.step(j)
            if j % 2:
                few.step(j // 2)

    tiles = piece // 256
    per = PARTS // tiles
    def far_tile(t):
        back_tile(at.s_far, b_far, t)
        for k in range(t * per, t * per + per):
            to_pass[k].wait_recv()
            add_into(b_far.at[parts[k]], pass_sib.at[parts[k]], rows)
            to_far[k].start()

    for copy in soon:
        copy.wait()
    for t in range(tiles):
        back_tile(at.s_diag, b_diag, t)
        for k in range(t * per, t * per + per):
            to_pass[k].start()
    far_tile(0)
    for copy in later:
        copy.wait()
    def sib_tile(t):
        back_tile(at.s_sib, b_sib, t)
        for k in range(t * per, t * per + per):
            to_sib[k].start()

    shard_pair(0)
    far_tile(1)
    big.side_copy(1).start()
    shard_pair(1)
    com_pair(0)
    shard_pair(2)
    big.side_copy(3).start()
    com_pair(1)
    step(0, ends)
    step(1, ends)
    shard_pair(3)
    big.side_copy(5).start()
    com_pair(2)
    step(0, ~ends)
    step(2, ends)
    gather_pieces_pass(at, gate_sum, gate_slot, gsem)
    sib_tile(0)
    big.side_copy(7).start()
    com_pair(3)
    step(1, ~ends)
    step(3, ends)
    sib_tile(1)
    step(2, ~ends)
    step(4, ends)
    back_tile(at.s, b_own, 0)
    step(3, ~ends)
    step(4, ~ends)
    step(5, ends)
    back_tile(at.s, b_own, 1)
    step(5, ~ends)
    small_pass(at, small, sgot, stotal, sfull, ssem, smore)
    for j in (6, 7):
        big.step(j)
    few.step(3)
    mown[...] = macc[at.z]
    gather_pieces_start(at, mown, x_slot, asem)
    csum[...] = cacc[at.z]
    far_copy = remote(csum, cfar, cx[2], cx[3], at.far)
    far_copy.start()
    for k, p in enumerate(parts):
        to_sib[k].wait_recv()
        to_far[k].wait_recv()

        def body(i, _):
            r = pl.ds(pl.multiple_of(k * rows + i * 32, 32), 32)
            back_sum[r, :] = b_own[r, :].astype(f32) + from_sib[r, :].astype(f32) + from_far[r, :].astype(f32)
            return 0

        lax.fori_loop(0, rows // 32, body, 0)
    far_copy.wait()
    add_into(csum, cfar, half)
    com_out = in_sum.at[mine, pl.ds(2 * E, 384)]
    com_copy = remote(csum, com_out, cx[4], cx[5], at.sib)
    com_copy.start()
    keep_copy = pltpu.make_async_copy(csum, com_out, cx[6])
    keep_copy.start()
    gather_pieces_pass(at, mown, x_slot, asem)
    small_end(at, small, sgot, stotal, sfull, ssem, smore)
    sums_out[...] = jnp.zeros_like(sums_out)
    bc, heads = jnp.zeros((8, 256), f32), jnp.zeros((8, 128), f32)
    for s in range(4):
        sums_out[:, wide * s : wide * s + wide] = sfull[s, :, 0:wide]
        bc = bc + sfull[s, :, wide : wide + 256]
        shift = (wide // P_SIZE) * s
        own = sfull[s, :, 0:128]
        heads = heads + (pltpu.roll(own, shift, 1) if shift else own)
    sums_out[:, E : E + 256] = bc
    sums_out[:, E + 256 : E + 384] = heads
    for copy in to_pass + to_sib + to_far:
        copy.wait_send()
    for zp in range(4):
        com_to_sib(zp).wait_send()
    big.end()
    few.end()
    gather_pieces_end(at, gate_sum, gate_slot, gsem)
    gather_pieces_end(at, mown, x_slot, asem)
    keep_copy.wait()
    com_copy.wait_send()
    got = in_sum.at[other, pl.ds(2 * E, 384)]
    remote(csum, got, cx[4], cx[5], at.sib).wait_recv()


def finish_last(hid, d_gate, d_u, d_dt, w_main, w_com, gate_sum, small):
    length, depth = hid.shape
    piece, shard, half = length // 4, depth // 8, depth // 16
    wide = d_gate.shape[1]
    vm = pltpu.VMEM
    shards4 = lambda cuts: [dma(3, 4 * cuts), dma(4 * cuts), dma(4 * cuts), dma(4 * cuts)]
    return pl.pallas_call(
        last_kernel,
        in_specs=[pl.BlockSpec(memory_space=ANY)] * 7 + [pl.BlockSpec(memory_space=pltpu.VMEM)],
        out_specs=[
            pl.BlockSpec(memory_space=pltpu.VMEM),
            pl.BlockSpec(memory_space=ANY),
            pl.BlockSpec(memory_space=pltpu.VMEM),
        ],
        out_shape=[
            jax.ShapeDtypeStruct((piece, depth), f32),
            jax.ShapeDtypeStruct((shard, 2 * E + 384), bf16),
            jax.ShapeDtypeStruct((8, E + 384), f32),
        ],
        scratch_shapes=[vm(hid.shape, bf16), vm((length, 2 * wide + 384), bf16), vm((depth, 2 * wide + 384), bf16)]
        + [vm((piece, depth), bf16)] * 7
        + [vm((4, 2, shard, wide + 384), bf16)]
        + [vm((4, shard, wide), bf16)] * 4
        + [vm((shard, wide), bf16)]
        + [vm((4, 2, half, 384), bf16)] * 2
        + [vm((4, half, 384), bf16)] * 4
        + [vm((half, 384), bf16)] * 2
        + [vm((8,) + small.shape, f32), vm(small.shape, f32), vm((4,) + small.shape, f32), vm(gate_sum.shape, bf16)]
        + [dma(2), dma(4), dma(4), dma(4), dma(), dma()]
        + [dma(3, PARTS), dma(3, PARTS)]
        + shards4(2)
        + shards4(1)
        + [dma(4), dma(4), dma(), dma(), dma(), dma(), dma()]
        + [dma(8), dma(8)]
        + [dma(3), dma(3), dma()]
        + [dma(3, PARTS), dma(3, PARTS), dma()]
        + [dma(3, PARTS), dma(3, PARTS), dma()],
        compiler_params=pltpu.CompilerParams(
            collective_id=4, has_side_effects=True, vmem_limit_bytes=60 * 2**20
        ),
        name="finish_last",
    )(hid, d_gate, d_u, d_dt, w_main, w_com, gate_sum, small)


def over_rows(left, right):
    return lax.dot_general(
        left, right, (((0,), (0,)), ((), ())), preferred_element_type=jnp.float32
    )


def gather_plain(hid, main, com):
    hid_all = lax.all_gather(hid, "seq", axis=0)
    main_all = lax.all_gather(main, "wshard", axis=0)
    return hid_all, main_all, lax.all_gather(com, "wshard", axis=0)


def gather_more_plain(cot, rows, wide):
    cot_all = lax.all_gather(cot, "seq", axis=0)
    cols = lax.all_to_all(rows, "wshard", split_axis=1, concat_axis=0, tiled=True)
    own = lax.dynamic_slice_in_dim(cols, lax.axis_index("seq") * wide, wide, 0)
    return cot_all, lax.all_gather(own, "wshard", axis=1, tiled=True)


def reduce_scattered(v, axis):
    return lax.psum_scatter(v, axis, scatter_dimension=0, tiled=False)


def reduce_first_plain(layer, rows, gate):
    layer_sum = reduce_scattered(layer, "seq").astype(f32)
    rows = rows.reshape(-1, rows.shape[-1])
    part = lax.psum_scatter(rows, "wshard", scatter_dimension=1, tiled=True)
    part = lax.all_gather(part, "seq", axis=0, tiled=True)
    part = lax.all_to_all(part, "wshard", split_axis=0, concat_axis=1, tiled=True)
    return layer_sum, part, reduce_scattered(gate, "wshard")


def finish_plain(hid, d_gate, d_u, d_dt, w_main, w_com, gate_sum, small):
    groups, owners = lax.axis_size("seq"), lax.axis_size("wshard")
    wide = d_gate.shape[1]
    rest = jnp.concatenate([d_u, d_dt], axis=1)
    nt = lambda p, q: lax.dot_general(p, q, (((1,), (1,)), ((), ())), preferred_element_type=f32)
    back = nt(d_gate, w_main[:, :wide]) + nt(rest, jnp.concatenate([w_main[:, wide:], w_com], axis=1))
    back_sum = reduce_scattered(back.astype(bf16).reshape(groups, -1, D), "seq").astype(f32)
    part = reduce_scattered(over_rows(hid, rest).astype(bf16).reshape(owners, -1, rest.shape[1]), "wshard")
    part = lax.all_gather(jnp.concatenate([gate_sum, part], axis=1), "seq", axis=0)
    in_sum = jnp.concatenate(
        [part[i, :, :wide] for i in range(groups)]
        + [part[i, :, wide : 2 * wide] for i in range(groups)]
        + [jnp.sum(part[:, :, 2 * wide :].astype(f32), axis=0).astype(bf16)],
        axis=1,
    )
    full = lax.all_gather(lax.psum(small, "wshard"), "seq", axis=0)
    turned = [jnp.roll(full[i, :, :128], i * (wide // P_SIZE), axis=1) for i in range(groups)]
    sums = jnp.concatenate(
        [full[i, :, :wide] for i in range(groups)] + [jnp.sum(full[:, :, wide:], axis=0), sum(turned)], axis=1
    )
    return back_sum, in_sum, sums


def middle_plain(gate, mixed, cot_all, w_out, normed):
    mixed_wide = mixed.astype(f32)
    sg = jax.nn.sigmoid(gate)
    silu = gate * sg
    g = mixed_wide * silu
    g_low = g.astype(bf16)
    a = lax.dot_general(cot_all, w_out, (((1,), (1,)), ((), ())), preferred_element_type=f32)
    sums = lax.psum(jnp.stack([jnp.sum(g * g, axis=1), jnp.sum(a * g, axis=1)]), "seq")
    r = lax.rsqrt(sums[0] / E + eps)[:, None]
    pull = (r * r * r) * (sums[1] / E)[:, None]
    d_g = r * a - g * pull
    d_mixed = (d_g * silu).astype(bf16)
    d_gate = (d_g * mixed_wide * (sg * (1.0 + gate * (1.0 - sg)))).astype(bf16)
    layer_part = (jnp.dot(g_low, w_out, preferred_element_type=f32) * r).astype(bf16)
    cot_r = (cot_all.astype(f32) * r).astype(bf16)
    out_part = over_rows(g_low, cot_r).astype(bf16)

    gate_part = over_rows(normed, d_gate).astype(bf16)
    return d_mixed, d_gate, gate_part, out_part, layer_part


def shards(
    hidden,
    segments,
    norm_gain,
    in_weight,
    conv_weight,
    conv_bias,
    step_bias,
    decay_log,
    skip_scale,
    gate_gain,
    out_weight,
    cotangent,
):
    group = lax.axis_index("seq")
    groups, owners = lax.axis_size("seq"), lax.axis_size("wshard")
    direct = (groups, owners) == (4, 8)
    heads = H // groups
    wide = heads * P_SIZE
    length = segments.shape[1]
    hidden_own, cot_own = hidden[0], cotangent[0]
    main = jnp.concatenate(
        [
            lax.dynamic_slice_in_dim(in_weight, group * wide, wide, 1),
            lax.dynamic_slice_in_dim(in_weight, E + group * wide, wide, 1),
        ],
        axis=1,
    )
    com = jnp.concatenate([in_weight[:, 2 * E :], norm_gain[:, None]], axis=1)
    com = jnp.pad(com, ((0, 0), (0, 128 - H - 1)))
    out_gain = gate_gain.astype(f32)[:, None]
    out_scaled = (out_weight.astype(f32) * out_gain).astype(bf16)
    gather = gather_first if direct else gather_plain
    hidden_all, w_main, w_com = gather(hidden_own, main, com)
    hidden_all = hidden_all.reshape(length, D)
    w_main, w_com = w_main.reshape(D, 2 * wide), w_com.reshape(D, -1)
    gain_row = w_com[:, 2 * N + H].astype(f32)[None]

    seg = segments[0]
    seg_col = jnp.pad(seg, (8, 8), constant_values=-1)[:, None]
    segr = seg.reshape(length // Q, 1, Q)
    par = jnp.pad(jnp.stack([step_bias, decay_log]), ((0, 6), (0, 128 - H)))
    skip = jnp.repeat(skip_scale, P_SIZE)[None]
    facts = (seg_col, segr, conv_weight, conv_bias[None], par, skip)
    beside, more = (forward_traffic(cot_own, out_scaled), (cot_own, out_scaled)) if direct else (NoTraffic, ())
    u, dt, gate, normed, mixed, save, *got = mixer_fwd(beside, more, hidden_all, gain_row, w_main, w_com, *facts)
    cot_all, w_out = got if direct else gather_more_plain(cot_own, out_scaled, wide)
    cot_all, w_out = cot_all.reshape(length, D), w_out.reshape(wide, D)

    mid = middle if direct else middle_plain
    d_mixed, d_gate, gate_part, out_part, layer_part = mid(gate, mixed, cot_all, w_out, normed)
    own_wide = hidden_own.astype(f32)

    more = (layer_part.reshape(groups, -1, D), out_part.reshape(2, -1, D), gate_part.reshape(owners, -1, wide))
    beside = backward_traffic(*more) if direct else NoTraffic
    du, ddt, small, *got = mixer_bwd(
        beside, more if direct else (), u, dt, *facts, save, d_mixed
    )
    layer_sum, out_sum, gate_sum = got if direct else reduce_first_plain(*more)
    layer_output = own_wide + layer_sum
    finish = finish_last if direct else finish_plain
    back_sum, in_sum, sums = finish(normed, d_gate, du, ddt, w_main, w_com, gate_sum, small)

    own_scale = lax.rsqrt(jnp.mean(own_wide * own_wide, axis=-1, keepdims=True) + eps)
    b = back_sum * gain_row
    hidden_grad = (
        cot_own.astype(f32)
        + own_scale * b
        - own_wide * (own_scale * own_scale * own_scale) * jnp.mean(b * own_wide, axis=-1, keepdims=True)
    )
    in_weight_grad = in_sum[:, : 2 * E + 2 * N + H].astype(f32)
    norm_gain_grad = jnp.sum(in_weight_grad * in_weight.astype(f32), axis=1) / norm_gain.astype(f32)
    out_sum = out_sum.astype(f32)
    out_weight_grad = out_sum * out_gain
    gate_gain_grad = jnp.sum(out_sum * out_weight.astype(f32), axis=1)
    chan, per_head = sums[:, : E + 2 * N], sums[:, E + 2 * N : E + 2 * N + H]
    return (
        layer_output[None],
        hidden_grad[None],
        norm_gain_grad,
        in_weight_grad,
        chan[:4],
        chan[4],
        per_head[5],
        per_head[6],
        per_head[7],
        gate_gain_grad,
        out_weight_grad,
    )


def solution(mesh):
    in_specs = (
        P("wshard", "seq", None),
        P("wshard", None),
        P("wshard"),
        P("wshard", None),
        P(),
        P(),
        P(),
        P(),
        P(),
        P("wshard"),
        P("wshard", None),
        P("wshard", "seq", None),
    )
    out_specs = (
        P("wshard", "seq", None),
        P("wshard", "seq", None),
        P("wshard"),
        P("wshard", None),
        P(),
        P(),
        P(),
        P(),
        P(),
        P("wshard"),
        P("wshard", None),
    )
    return jax.shard_map(shards, mesh=mesh, in_specs=in_specs, out_specs=out_specs, check_vma=False)
```

```python
import functools

import jax
import jax.numpy as jnp
from jax import lax
from jax.experimental import pallas as pl
from jax.experimental.pallas import tpu as pltpu
from jax.sharding import PartitionSpec as P

D = 1536
H = 48
P_SIZE = 64
N = 128
E = 3072

eps = 1e-05
f32, bf16 = jnp.float32, jnp.bfloat16
Q = 128
NEG = -1e30


def dot(a, b):
    return jnp.dot(a, b, preferred_element_type=f32)


def dot_nt(a, b):
    return lax.dot_general(a, b, (((1,), (1,)), ((), ())), preferred_element_type=f32)


def dot3(tri, v):
    hi = v.astype(bf16)
    rest = v - hi.astype(f32)
    mid = rest.astype(bf16)
    low = (rest - mid.astype(f32)).astype(bf16)
    return dot(tri, hi) + dot(tri, mid) + dot(tri, low)


def sigmoid(v):
    return 1.0 / (1.0 + jnp.exp(-v))


def spread_col(v, col):
    return jnp.broadcast_to(v[:, col : col + 1], (Q, 128))


def softplus(v):
    return jnp.maximum(v, 0.0) + jnp.log1p(jnp.exp(-jnp.abs(v)))


def conv_pre(useen, flags, wk, bias, lanes, chans):
    pre = bias[:, chans] + wk[3:4, chans] * useen[8 : 8 + Q, lanes]
    for j in (1, 2, 3):
        pre = pre + wk[3 - j : 4 - j, chans] * (useen[8 - j : 8 - j + Q, lanes] * flags[j])
    return pre


class Facts:
    def __init__(self, chunk, seg_ref, par_ref, xw):
        self.group = lax.axis_index("seq")
        self.heads = xw // P_SIZE
        self.xw = xw
        near = seg_ref[pl.ds(pl.multiple_of(chunk * Q, 8), Q + 16), :]
        now = near[8 : 8 + Q]
        same = lambda other: jnp.broadcast_to(jnp.where(other == now, 1.0, 0.0), (Q, 128))
        self.before = [None] + [same(near[8 - j : 8 - j + Q]) for j in (1, 2, 3)]
        self.after = lambda j: same(near[8 + j : 8 + j + Q])
        self.carried = same(near[7:8])
        self.samelast = same(near[7 + Q : 8 + Q])
        self.now = now
        self.turn = self.heads * self.group
        lane = lax.broadcasted_iota(jnp.int32, (8, 128), 1)
        par = self.own(par_ref[...])
        self.bias = par[0:1]
        self.rate = jnp.where(lane < self.heads, -jnp.exp(par), 0.0)[1:2]

    def own(self, v):
        lane = lax.broadcasted_iota(jnp.int32, v.shape, 1)
        return jnp.where(lane < self.heads, pltpu.roll(v, lax.rem(128 - self.turn, 128), 1), 0.0)

    def back(self, v):
        return pltpu.roll(v, self.turn, 1)

    def chans(self, p):
        if p < self.xw // 128:
            return pl.ds(pl.multiple_of(self.group * self.xw + 128 * p, 128), 128)
        at = E + 128 * (p - self.xw // 128)
        return slice(at, at + 128)


class NoTraffic:
    inputs, outputs, scratch, collective_id = (), (), (), None

    def __init__(self, *refs):
        pass

    def step(self, i, last):
        pass


def fwd_kernel(traffic, hid_ref, gain_ref, main_ref, com_ref, seg_ref, segr_ref, wk_ref, bias_ref, par_ref, skip_ref, *rest):
    n_in, n_out = len(traffic.inputs), len(traffic.outputs)
    extra_in, rest = rest[:n_in], rest[n_in:]
    u_ref, dt_ref, gate_ref, normed_ref, mixed_ref, save_ref = rest[:6]
    extra_out, rest = rest[6 : 6 + n_out], rest[6 + n_out :]
    state, useen, act, next_u, next_dt = rest[:5]
    step_no = pl.program_id(0)
    traffic(*extra_in, *extra_out, *rest[5:]).step(step_no, pl.num_programs(0) - 1)
    xw = mixed_ref.shape[1]
    width = xw + 256
    pairs = xw // 128
    facts = Facts(jnp.maximum(step_no - 1, 0), seg_ref, par_ref, xw)

    @pl.when(step_no == 0)
    def _():
        next_u[...] = jnp.zeros_like(next_u)
        next_dt[...] = jnp.zeros_like(next_dt)

    @pl.when(step_no <= 1)
    def _():
        state[...] = jnp.zeros_like(state)
        useen[0:8, :] = jnp.zeros((8, width), f32)

    useen[8 : 8 + Q, :] = next_u[...]
    dt_now = next_dt[...]

    hid = hid_ref[...].astype(f32)
    depth = hid.shape[1]
    total = jnp.zeros((Q, 128), f32)
    for k in range(depth // 128):
        part = hid[:, 128 * k : 128 * k + 128]
        total = total + part * part
    scale = lax.rsqrt(jnp.sum(total, axis=1, keepdims=True) / depth + eps)
    normed_ref[...] = (hid * scale * gain_ref[...]).astype(bf16)
    low = normed_ref[...]
    for k in range(xw // 256):
        gate_ref[:, 256 * k : 256 * k + 256] = dot(low, main_ref[:, 256 * k : 256 * k + 256])
    for k in range(xw // 256):
        got = dot(low, main_ref[:, xw + 256 * k : xw + 256 * k + 256]).astype(bf16)
        u_ref[:, 256 * k : 256 * k + 256] = got
        next_u[:, 256 * k : 256 * k + 256] = got.astype(f32)
    got = dot(low, com_ref[:, 0:256]).astype(bf16)
    u_ref[:, xw : xw + 256] = got
    next_u[:, xw : xw + 256] = got.astype(f32)
    got = facts.own(dot(low, com_ref[:, 256:384]).astype(bf16).astype(f32))
    dt_ref[...] = got.astype(bf16)
    next_dt[...] = got

    carried, samelast = facts.carried, facts.samelast
    for p in range(width // 128):
        lanes = slice(128 * p, 128 * p + 128)
        pre = conv_pre(useen, facts.before, wk_ref, bias_ref, lanes, facts.chans(p))
        act[:, lanes] = pre * sigmoid(pre)
    tail = useen[Q : Q + 8, :]
    useen[0:8, :] = tail

    step = softplus(dt_now + facts.bias)
    row = lax.broadcasted_iota(jnp.int32, (Q, Q), 0)
    col = lax.broadcasted_iota(jnp.int32, (Q, Q), 1)
    tri = jnp.where(row >= col, 1.0, 0.0).astype(bf16)
    decay = dot3(tri, step * facts.rate)
    decay_t = decay.T
    madd = jnp.where((row >= col) & (facts.now == segr_ref[0]), 0.0, NEG)
    b_now = act[:, xw : xw + 128]
    c_low = act[:, xw + 128 : xw + 256].astype(bf16)
    gram = dot_nt(c_low, b_now.astype(bf16))
    b_t = b_now.T.astype(bf16)
    left = lax.broadcasted_iota(jnp.int32, (Q, 128), 1) < 64
    for p in range(pairs):
        lanes = slice(128 * p, 128 * p + 128)
        d0, d1 = spread_col(decay, 2 * p), spread_col(decay, 2 * p + 1)
        dp = jnp.where(left, d0, d1)
        sp = jnp.where(left, spread_col(step, 2 * p), spread_col(step, 2 * p + 1))
        xs = act[:, lanes]
        xp = xs * sp
        m0 = gram * jnp.exp(d0 - decay_t[2 * p : 2 * p + 1, :] + madd)
        m1 = gram * jnp.exp(d1 - decay_t[2 * p + 1 : 2 * p + 2, :] + madd)
        both = jnp.concatenate([m0.astype(bf16), m1.astype(bf16)], axis=1)
        stacked = jnp.concatenate(
            [jnp.where(left, xp, 0.0).astype(bf16), jnp.where(left, 0.0, xp).astype(bf16)], axis=0
        )
        st = state[:, lanes]
        st_low = st.astype(bf16)
        save_ref[0, :, lanes] = st_low
        y = dot(both, stacked) + dot(c_low, st_low) * (jnp.exp(dp) * carried)
        mixed_ref[:, lanes] = (y + skip_ref[:, facts.chans(p)] * xs).astype(bf16)
        last = dp[Q - 1 : Q, :]
        to_end = (xp * (jnp.exp(last - dp) * samelast)).astype(bf16)
        state[:, lanes] = st * (jnp.exp(last) * carried[Q - 1 : Q, :]) + dot(b_t, to_end)


def mixer_fwd(traffic, extra, hid, gain, main, com, seg, segr, wk, bias, par, skip):
    length, depth = hid.shape
    xw = main.shape[1] // 2
    width = xw + 256
    n = length // Q
    whole = lambda shape: pl.BlockSpec(shape, lambda i: (0,) * len(shape), pipeline_mode=pl.Buffered(1))
    ahead = lambda i: (jnp.minimum(i, n - 1), 0)
    now = lambda i: (jnp.maximum(i - 1, 0), 0)
    now3 = lambda i: (jnp.maximum(i - 1, 0), 0, 0)
    return pl.pallas_call(
        functools.partial(fwd_kernel, traffic),
        grid=(n + 1,),
        in_specs=[
            pl.BlockSpec((Q, depth), ahead),
            whole(gain.shape),
            whole(main.shape),
            whole(com.shape),
            whole(seg.shape),
            pl.BlockSpec((1, 1, Q), now3),
            whole(wk.shape),
            whole(bias.shape),
            whole(par.shape),
            whole(skip.shape),
        ]
        + [pl.BlockSpec(memory_space=pltpu.MemorySpace.HBM)] * len(extra),
        out_specs=[
            pl.BlockSpec((Q, width), ahead),
            pl.BlockSpec((Q, 128), ahead),
            pl.BlockSpec((Q, xw), ahead),
            pl.BlockSpec((Q, depth), ahead),
            pl.BlockSpec((Q, xw), now),
            pl.BlockSpec((1, 128, xw), now3),
        ]
        + [pl.BlockSpec(memory_space=pltpu.MemorySpace.HBM)] * len(traffic.outputs),
        out_shape=[
            jax.ShapeDtypeStruct((length, width), bf16),
            jax.ShapeDtypeStruct((length, 128), bf16),
            jax.ShapeDtypeStruct((length, xw), f32),
            jax.ShapeDtypeStruct((length, depth), bf16),
            jax.ShapeDtypeStruct((length, xw), bf16),
            jax.ShapeDtypeStruct((n, 128, xw), bf16),
            *traffic.outputs,
        ],
        scratch_shapes=[
            pltpu.VMEM((128, xw), f32),
            pltpu.VMEM((Q + 8, width), f32),
            pltpu.VMEM((Q, width), f32),
            pltpu.VMEM((Q, width), f32),
            pltpu.VMEM((Q, 128), f32),
            *traffic.scratch,
        ],
        compiler_params=pltpu.CompilerParams(
            vmem_limit_bytes=60 * 2**20,
            collective_id=traffic.collective_id,
            has_side_effects=traffic.collective_id is not None,
        ),
        name="mixer_forward",
    )(hid, gain, main, com, seg, segr, wk, bias, par, skip, *extra)


def bwd_kernel(traffic, u_ref, halo_ref, dt_ref, seg_ref, segr_ref, wk_ref, bias_ref, par_ref, skip_ref,
               save_ref, dy_ref, *rest):
    n_in, n_out = len(traffic.inputs), len(traffic.outputs)
    extra_in, rest = rest[:n_in], rest[n_in:]
    du_ref, ddt_ref, small_ref = rest[:3]
    extra_out, rest = rest[3 : 3 + n_out], rest[3 + n_out :]
    dstate, useen, act, slope, dpre, keep_y, keep_x, prod_a, prod_b, rows_a, held = rest[:11]
    wgrad_ref, hgrad_ref, sgrad_ref, spot_ref = rest[11:15]
    step_no = pl.program_id(0)
    last_step = pl.num_programs(0) - 1
    traffic(*extra_in, *extra_out, *rest[15:]).step(step_no, last_step)
    width = u_ref.shape[1]
    xw = width - 256
    pairs = xw // 128

    @pl.when(step_no == 0)
    def _():
        dstate[...] = jnp.zeros_like(dstate)
        dpre[Q : Q + 8, :] = jnp.zeros((8, width), f32)
        wgrad_ref[...] = jnp.zeros_like(wgrad_ref)
        hgrad_ref[...] = jnp.zeros_like(hgrad_ref)
        sgrad_ref[...] = jnp.zeros_like(sgrad_ref)
        rows_a[...] = jnp.zeros_like(rows_a)
        head_of = lax.broadcasted_iota(jnp.int32, (xw, 128), 0) // P_SIZE
        mark = head_of == lax.broadcasted_iota(jnp.int32, (xw, 128), 1)
        spot_ref[...] = jnp.where(mark, 1.0, 0.0).astype(bf16)

    useen[0:8, :] = halo_ref[...].astype(f32)[8:16, :]
    useen[8 : 8 + Q, :] = u_ref[...].astype(f32)
    facts = Facts(last_step - step_no, seg_ref, par_ref, xw)
    flags, carried, samelast = facts.before, facts.carried, facts.samelast
    for p in range(width // 128):
        lanes = slice(128 * p, 128 * p + 128)
        pre = conv_pre(useen, flags, wk_ref, bias_ref, lanes, facts.chans(p))
        sg = sigmoid(pre)
        act[:, lanes] = pre * sg
        slope[:, lanes] = sg * (1.0 + pre * (1.0 - sg))

    raw = dt_ref[...].astype(f32) + facts.bias
    step = softplus(raw)
    rate = facts.rate
    row = lax.broadcasted_iota(jnp.int32, (Q, Q), 0)
    col = lax.broadcasted_iota(jnp.int32, (Q, Q), 1)
    tri = jnp.where(row >= col, 1.0, 0.0).astype(bf16)
    upper = jnp.where(row <= col, 1.0, 0.0).astype(bf16)
    below = jnp.where(row > col, 1.0, 0.0).astype(bf16)
    decay = dot3(tri, step * rate)
    decay_t = decay.T
    madd = jnp.where((row <= col) & (facts.now == segr_ref[0]), 0.0, NEG)
    b_now, c_now = act[:, xw : xw + 128], act[:, xw + 128 : xw + 256]
    b_low, c_low = b_now.astype(bf16), c_now.astype(bf16)
    c_t = c_now.T.astype(bf16)
    gram = dot_nt(b_low, c_low)
    left = lax.broadcasted_iota(jnp.int32, (Q, 128), 1) < 64
    lane = lax.broadcasted_iota(jnp.int32, (Q, 128), 1)
    dgram = jnp.zeros((Q, Q), f32)
    cols_b = jnp.zeros((Q, 128), f32)
    for p in range(pairs):
        lanes = slice(128 * p, 128 * p + 128)
        d0, d1 = spread_col(decay, 2 * p), spread_col(decay, 2 * p + 1)
        dp = jnp.where(left, d0, d1)
        sp = jnp.where(left, spread_col(step, 2 * p), spread_col(step, 2 * p + 1))
        xs = act[:, lanes]
        xp = xs * sp
        dy_low = dy_ref[:, lanes]
        dy = dy_low.astype(f32)
        stacked = jnp.concatenate(
            [jnp.where(left, dy, 0.0).astype(bf16), jnp.where(left, 0.0, dy).astype(bf16)], axis=0
        )
        pair = dot_nt(xp.astype(bf16), stacked)
        mts = []
        for k, dk in ((0, d0), (1, d1)):
            h = 2 * p + k
            e = jnp.exp(decay_t[h : h + 1, :] - dk + madd)
            f = e * pair[:, 128 * k : 128 * k + 128]
            dgram = dgram + f
            w = gram * f
            mts.append((gram * e).astype(bf16))
            rows_a[h : h + 1, :] = jnp.sum(w, axis=0, keepdims=True)
            cols_b = jnp.where(lane == h, jnp.sum(w, axis=1, keepdims=True), cols_b)
        within = dot(jnp.concatenate(mts, axis=1), stacked)
        grow = jnp.exp(dp) * carried
        dy_in = dy * grow
        dy_in_low = dy_in.astype(bf16)
        keep_y[:, lanes] = dy_in_low
        st = save_ref[0, :, lanes]
        prod_a[:, lanes] = (dy_in * dot(c_low, st)).astype(bf16)
        last = dp[Q - 1 : Q, :]
        fade = jnp.exp(last - dp) * samelast
        ds = dstate[:, lanes]
        ds_low = ds.astype(bf16)
        xe = xp * fade
        keep_x[:, lanes] = xe.astype(bf16)
        later = dot(b_low, ds_low)
        prod_b[:, lanes] = (xe * later).astype(bf16)
        retain = jnp.exp(last) * carried[Q - 1 : Q, :]
        held[0:1, lanes] = jnp.sum(ds * st.astype(f32), axis=0, keepdims=True) * retain
        dxs = sp * (within + later * fade) + skip_ref[:, facts.chans(p)] * dy
        skp = xs * dy
        sgrad_ref[:, lanes] += jnp.sum(skp.reshape(Q // 8, 8, 128), axis=0)
        dpre[0:Q, lanes] = dxs * slope[:, lanes]
        dstate[:, lanes] = ds * retain + dot(c_t, dy_in_low)
        if p == 0:
            db_in, dc_in = dot_nt(keep_x[:, lanes], ds_low), dot_nt(dy_in_low, st)
        else:
            db_in, dc_in = db_in + dot_nt(keep_x[:, lanes], ds_low), dc_in + dot_nt(dy_in_low, st)

    dg_low = dgram.astype(bf16)
    db = dot(dg_low, c_low) + db_in
    dc = dot(dgram.T.astype(bf16), b_low) + dc_in
    dpre[0:Q, xw : xw + 128] = db * slope[:, xw : xw + 128]
    dpre[0:Q, xw + 128 : xw + 256] = dc * slope[:, xw + 128 : xw + 256]

    spot = spot_ref[...]
    a_in = dot(prod_a[...], spot)
    b_in = dot(prod_b[...], spot)
    hv = jnp.broadcast_to(held[0:1, :], (8, xw))
    h_hi = hv.astype(bf16)
    h_lo = (hv - h_hi.astype(f32)).astype(bf16)
    through = (dot(h_hi, spot) + dot(h_lo, spot))[0:1, :]
    a_own = rows_a[...].T
    cross = dot3(upper, a_own - cols_b + a_in) + dot3(below, b_in) + through
    total = cols_b + b_in
    sg = sigmoid(raw)
    ratio = jnp.where(step > 1e-30, sg / jnp.maximum(step, 1e-30), 1.0)
    draw = total * ratio + rate * cross * sg
    ddt_ref[...] = facts.back(draw).astype(bf16)
    hgrad_ref[0:8, :] += jnp.sum(draw.reshape(Q // 8, 8, 128), axis=0)
    hgrad_ref[8:16, :] += jnp.sum((step * cross).reshape(Q // 8, 8, 128), axis=0)

    ahead = [None] + [facts.after(j) for j in (1, 2, 3)]
    for p in range(width // 128):
        lanes = slice(128 * p, 128 * p + 128)
        own = dpre[0:Q, lanes]
        chans = facts.chans(p)
        du = wk_ref[3:4, chans] * own
        wgrad_ref[24:32, lanes] += jnp.sum((own * useen[8 : 8 + Q, lanes]).reshape(Q // 8, 8, 128), axis=0)
        wgrad_ref[32:40, lanes] += jnp.sum(own.reshape(Q // 8, 8, 128), axis=0)
        for j in (1, 2, 3):
            du = du + wk_ref[3 - j : 4 - j, chans] * (dpre[j : j + Q, lanes] * ahead[j])
            moved = own * (useen[8 - j : 8 - j + Q, lanes] * flags[j])
            k = 3 - j
            wgrad_ref[8 * k : 8 * k + 8, lanes] += jnp.sum(moved.reshape(Q // 8, 8, 128), axis=0)
        du_ref[:, lanes] = du.astype(bf16)
    first = dpre[0:8, :]
    dpre[Q : Q + 8, :] = first

    @pl.when(step_no == last_step)
    def _():
        small_ref[...] = jnp.zeros_like(small_ref)
        for k in range(5):
            small_ref[k : k + 1, :] = jnp.sum(wgrad_ref[8 * k : 8 * k + 8, :], axis=0, keepdims=True)
        small_ref[5:6, 0:128] = jnp.sum(hgrad_ref[0:8, :], axis=0, keepdims=True)
        small_ref[6:7, 0:128] = rate * jnp.sum(hgrad_ref[8:16, :], axis=0, keepdims=True)
        skips = sgrad_ref[...]
        hi = skips.astype(bf16)
        mid = (skips - hi.astype(f32)).astype(bf16)
        by_head = dot(hi, spot_ref[...]) + dot(mid, spot_ref[...])
        small_ref[7:8, 0:128] = jnp.sum(by_head, axis=0, keepdims=True)


def mixer_bwd(traffic, extra, u, dt, seg, segr, wk, bias, par, skip, save, dy):
    length, width = u.shape
    xw = width - 256
    n = length // Q
    whole = lambda shape: pl.BlockSpec(shape, lambda i: (0,) * len(shape))
    back = lambda i: (n - 1 - i, 0)
    return pl.pallas_call(
        functools.partial(bwd_kernel, traffic),
        grid=(n,),
        in_specs=[
            pl.BlockSpec((Q, width), back),
            pl.BlockSpec((16, width), lambda i: (jnp.maximum((n - 1 - i) * (Q // 16) - 1, 0), 0)),
            pl.BlockSpec((Q, 128), back),
            whole(seg.shape),
            pl.BlockSpec((1, 1, Q), lambda i: (n - 1 - i, 0, 0)),
            whole(wk.shape),
            whole(bias.shape),
            whole(par.shape),
            whole(skip.shape),
            pl.BlockSpec((1, 128, xw), lambda i: (n - 1 - i, 0, 0)),
            pl.BlockSpec((Q, xw), back),
        ]
        + [pl.BlockSpec(memory_space=pltpu.MemorySpace.HBM)] * len(extra),
        out_specs=[
            pl.BlockSpec((Q, width), back),
            pl.BlockSpec((Q, 128), back),
            whole((8, width)),
        ]
        + [pl.BlockSpec(memory_space=pltpu.MemorySpace.HBM)] * len(traffic.outputs),
        out_shape=[
            jax.ShapeDtypeStruct((length, width), bf16),
            jax.ShapeDtypeStruct((length, 128), bf16),
            jax.ShapeDtypeStruct((8, width), f32),
            *traffic.outputs,
        ],
        scratch_shapes=[
            pltpu.VMEM((128, xw), f32),
            pltpu.VMEM((Q + 8, width), f32),
            pltpu.VMEM((Q, width), f32),
            pltpu.VMEM((Q, width), f32),
            pltpu.VMEM((Q + 8, width), f32),
            pltpu.VMEM((Q, xw), bf16),
            pltpu.VMEM((Q, xw), bf16),
            pltpu.VMEM((Q, xw), bf16),
            pltpu.VMEM((Q, xw), bf16),
            pltpu.VMEM((128, 128), f32),
            pltpu.VMEM((8, xw), f32),
            pltpu.VMEM((40, width), f32),
            pltpu.VMEM((16, 128), f32),
            pltpu.VMEM((8, xw), f32),
            pltpu.VMEM((xw, 128), bf16),
            *traffic.scratch,
        ],
        compiler_params=pltpu.CompilerParams(
            vmem_limit_bytes=60 * 2**20,
            collective_id=traffic.collective_id,
            has_side_effects=traffic.collective_id is not None,
        ),
        name="mixer_backward",
    )(u, u, dt, seg, segr, wk, bias, par, skip, save, dy, *extra)


MESH = pl.DeviceIdType.MESH
ANY = pltpu.MemorySpace.HBM
PARTS = 4


def remote(src, dst, send_sem, recv_sem, device):
    return pltpu.make_async_remote_copy(
        src_ref=src, dst_ref=dst, send_sem=send_sem, recv_sem=recv_sem, device_id=device, device_id_type=MESH
    )


class Place:
    def __init__(self):
        self.w, self.s = lax.axis_index("wshard"), lax.axis_index("seq")
        self.z, self.x = self.w // 2, lax.rem(self.w, 2)
        self.y, self.c = self.s // 2, lax.rem(self.s, 2)
        self.s_sib = 2 * self.y + 1 - self.c
        self.s_far = 2 * (1 - self.y) + self.c
        self.s_diag = 2 * (1 - self.y) + 1 - self.c
        self.side = (2 * self.z + 1 - self.x, self.s)
        self.up = (lax.rem(self.w + 2, 8), self.s)
        self.down = (lax.rem(self.w + 6, 8), self.s)
        self.sib = (self.w, self.s_sib)
        self.far = (self.w, self.s_far)

    def greet(self, everyone=False, sequence=False):
        barrier = pltpu.get_barrier_semaphore()
        others = [(lax.rem(self.w + k, 8), self.s) for k in range(1, 8)] if everyone else []
        if everyone or sequence:
            others += [(self.w, lax.rem(self.s + k, 4)) for k in range(1, 4)]
        else:
            others = [self.side, self.up, self.down, self.sib, self.far]
        for other in others:
            pl.semaphore_signal(barrier, inc=1, device_id=other, device_id_type=MESH)
        pl.semaphore_wait(barrier, len(others))


def dma(*shape):
    return pltpu.SemaphoreType.DMA(shape)


def gather_pieces_start(at, own, slot, sems, stage=None):
    send, recv, local = sems[:3]
    rows = own.shape[0] // PARTS
    for k in range(PARTS):
        part = pl.ds(k * rows, rows)
        remote(own.at[part], slot(at.s).at[part], send.at[1, k], recv.at[1, k], at.far).start()
    for k in range(PARTS):
        part = pl.ds(k * rows, rows)
        remote(own.at[part], slot(at.s).at[part], send.at[0, k], recv.at[0, k], at.sib).start()
    if stage is not None:
        copy = pltpu.make_async_copy(own, stage, local)
        copy.start()
        copy.wait()
    pltpu.make_async_copy(own if stage is None else stage, slot(at.s), local).start()


def gather_pieces_pass(at, own, slot, sems):
    send, recv, _ = sems
    rows = own.shape[0] // PARTS
    for k in range(PARTS):
        part = pl.ds(k * rows, rows)
        theirs = slot(at.s_far).at[part]
        remote(theirs, theirs, send.at[1, k], recv.at[1, k], at.far).wait_recv()
        remote(theirs, theirs, send.at[2, k], recv.at[2, k], at.sib).start()


def gather_pieces_end(at, own, slot, sems):
    send, recv, local = sems
    rows = own.shape[0] // PARTS
    pltpu.make_async_copy(own, slot(at.s), local).wait()
    for k in range(PARTS):
        part = pl.ds(k * rows, rows)
        sib, diag, far = slot(at.s_sib).at[part], slot(at.s_diag).at[part], slot(at.s_far).at[part]
        remote(own.at[part], slot(at.s).at[part], send.at[0, k], recv.at[0, k], at.sib).wait_send()
        remote(own.at[part], slot(at.s).at[part], send.at[1, k], recv.at[1, k], at.far).wait_send()
        remote(far, far, send.at[2, k], recv.at[2, k], at.sib).wait_send()
        remote(sib, sib, send.at[0, k], recv.at[0, k], at.sib).wait_recv()
        remote(diag, diag, send.at[2, k], recv.at[2, k], at.sib).wait_recv()


CUTS = 6


def gather_shards(at, main, com, main_all, com_all, stage, sems, between):
    send, recv, csend, crecv, psend, precv, local, osend = sems
    half, cut = com.shape[0] // 2, main.shape[0] // CUTS
    mine = pl.ds(pl.multiple_of(at.c * half, half), half)
    load = pltpu.make_async_copy(main, stage[0], local.at[0])
    com_load = pltpu.make_async_copy(com, stage[1], local.at[1])
    keep = pltpu.make_async_copy(stage[0], main_all.at[at.w], local.at[0])
    com_keep = pltpu.make_async_copy(stage[1], com_all.at[at.w], local.at[1])

    def hop(zp, q, way, device, own=False):
        w, n, part = 2 * zp + at.x, zp * CUTS + q, pl.ds(q * cut, cut)
        slot, com_slot = main_all.at[w, part], com_all.at[w, mine]
        copies = [remote(main.at[part] if own else slot, slot, send.at[way, n], recv.at[w * CUTS + q], device)]
        if q == 1:
            copies.append(remote(com.at[mine] if own else com_slot, com_slot, csend.at[way, zp], crecv.at[w], device))
        return copies

    def cross(zp, way, device):
        w = 2 * zp + 1 - at.x
        slot = main_all.at[w, pl.ds(0, cut)]
        return [remote(slot, slot, osend.at[way, zp], recv.at[w * CUTS], device)]

    def begin(copies):
        for copy in copies:
            copy.start()

    def sent(copies):
        for copy in copies:
            copy.wait_send()

    def all_ways(act, q):
        act(hop(at.z, q, 0, at.side, True))

        @pl.when(at.z < 3)
        def _():
            act(hop(at.z, q, 1, at.up, True))

        @pl.when(at.z > 0)
        def _():
            act(hop(at.z, q, 2, at.down, True))

    def arrived(w, q):
        slot = main_all.at[w, pl.ds(q * cut, cut)]
        remote(slot, slot, send.at[0, 0], recv.at[w * CUTS + q], at.side).wait_recv()
        if q == 1:
            held = com_all.at[w, mine]
            remote(held, held, csend.at[0, 0], crecv.at[w], at.side).wait_recv()
            remote(held, held, psend.at[w], precv.at[w], at.sib).start()

    for q in range(CUTS):
        if q > 1:
            all_ways(sent, q - 2)
        all_ways(begin, q)
        if q == 0:
            load.start()
            com_load.start()
            load.wait()
            com_load.wait()
            keep.start()
            com_keep.start()
    arrived(2 * at.z + 1 - at.x, 0)

    @pl.when(at.z < 3)
    def _():
        begin(cross(at.z, 0, at.up))

    @pl.when(at.z > 0)
    def _():
        begin(cross(at.z, 1, at.down))

    for d in (1, 2, 3):
        if d == 3:
            between()
        for q in range(CUTS):

            @pl.when(at.z - d >= 0)
            def _():
                zp = at.z - d
                arrived(2 * zp + at.x, q)

                @pl.when(at.z < 3)
                def _():
                    begin(hop(zp, q, 1, at.up))

                if q > 0:
                    begin(hop(zp, q, 0, at.side))

            @pl.when(at.z + d <= 3)
            def _():
                zp = at.z + d
                arrived(2 * zp + at.x, q)

                @pl.when(at.z > 0)
                def _():
                    begin(hop(zp, q, 2, at.down))

                if q > 0:
                    begin(hop(zp, q, 0, at.side))

        @pl.when(at.z - d >= 0)
        def _():
            arrived(2 * (at.z - d) + 1 - at.x, 0)

            @pl.when(at.z < 3)
            def _():
                begin(cross(at.z - d, 0, at.up))

        @pl.when(at.z + d <= 3)
        def _():
            arrived(2 * (at.z + d) + 1 - at.x, 0)

            @pl.when(at.z > 0)
            def _():
                begin(cross(at.z + d, 1, at.down))

    for zp in range(4):
        for q in range(1, CUTS):
            arrived(2 * zp + 1 - at.x, q)
    keep.wait()
    com_keep.wait()
    all_ways(sent, CUTS - 2)
    all_ways(sent, CUTS - 1)
    for zp in range(4):

        @pl.when((at.z < 3) & (zp <= at.z))
        def _():
            sent(cross(zp, 0, at.up))

        @pl.when((at.z > 0) & (zp >= at.z))
        def _():
            sent(cross(zp, 1, at.down))

        for q in range(CUTS):
            if q > 0:

                @pl.when(at.z != zp)
                def _():
                    sent(hop(zp, q, 0, at.side))

            @pl.when((at.z < 3) & (zp < at.z))
            def _():
                sent(hop(zp, q, 1, at.up))

            @pl.when((at.z > 0) & (zp > at.z))
            def _():
                sent(hop(zp, q, 2, at.down))

    other = pl.ds(pl.multiple_of((1 - at.c) * half, half), half)
    for k in range(1, 8):
        w = lax.rem(at.w + k, 8)
        gone, got = com_all.at[w, mine], com_all.at[w, other]
        remote(gone, gone, psend.at[w], precv.at[w], at.sib).wait_send()
        remote(got, got, psend.at[w], precv.at[w], at.sib).wait_recv()


def gather_kernel(hid, main, com, hid_all, main_all, com_all, hid_v, main_v, com_v, *sems):
    at = Place()
    at.greet()
    slot = lambda s: hid_all.at[s]
    gather_pieces_start(at, hid, slot, sems[0:3], hid_v)
    pass_on = lambda: gather_pieces_pass(at, hid, slot, sems[0:3])
    gather_shards(at, main, com, main_all, com_all, (main_v, com_v), sems[3:11], pass_on)
    gather_pieces_end(at, hid, slot, sems[0:3])


def gather_first(hid, main, com):
    shape = lambda n, v: jax.ShapeDtypeStruct((n,) + v.shape, v.dtype)
    return pl.pallas_call(
        gather_kernel,
        in_specs=[pl.BlockSpec(memory_space=ANY)] * 3,
        out_specs=[pl.BlockSpec(memory_space=ANY)] * 3,
        out_shape=[shape(4, hid), shape(8, main), shape(8, com)],
        scratch_shapes=[pltpu.VMEM(v.shape, v.dtype) for v in (hid, main, com)]
        + [dma(3, PARTS), dma(3, PARTS), dma()]
        + [dma(3, 4 * CUTS), dma(8 * CUTS), dma(3, 4), dma(8), dma(8), dma(8), dma(2), dma(2, 4)],
        compiler_params=pltpu.CompilerParams(collective_id=1, has_side_effects=True),
        name="gather_first",
    )(hid, main, com)


SLICES = 8


def each_slice(body):
    def run(k, _):
        body(k)
        return 0

    lax.fori_loop(0, SLICES, run, 0)


def forward_traffic(cot, rows):
    class Traffic:
        inputs = (cot, rows)
        outputs = (
            jax.ShapeDtypeStruct((4,) + cot.shape, cot.dtype),
            jax.ShapeDtypeStruct((2,) + rows.shape, rows.dtype),
        )
        scratch = (
            pltpu.VMEM(cot.shape, cot.dtype),
            pltpu.VMEM(rows.shape, rows.dtype),
            dma(3, SLICES),
            dma(3, SLICES),
            dma(),
            dma(3, SLICES),
            dma(2, SLICES),
            dma(),
        )
        collective_id = 2

        def __init__(self, own, row_own, full, row_full, stage, rstage, send, recv, local, rsend, rrecv, rlocal):
            self.at = at = Place()
            self.own, self.full, self.row_own, self.row_full = own, full, row_own, row_full
            self.rrecv = rrecv
            cut, rcut = own.shape[0] // SLICES, row_own.shape[0] // SLICES
            part = lambda k: pl.ds(pl.multiple_of(k * cut, cut), cut)
            rpart = lambda k: pl.ds(pl.multiple_of(k * rcut, rcut), rcut)
            piece = lambda s, k: full.at[s, part(k)]
            self.load = pltpu.make_async_copy(own, stage, local)
            self.keep = pltpu.make_async_copy(stage, full.at[at.s], local)
            self.rload = pltpu.make_async_copy(row_own, rstage, rlocal)
            self.rkeep = pltpu.make_async_copy(rstage, row_full.at[at.x], rlocal)
            self.to_sib = lambda k: remote(own.at[part(k)], piece(at.s, k), send.at[0, k], recv.at[0, k], at.sib)
            self.to_far = lambda k: remote(own.at[part(k)], piece(at.s, k), send.at[1, k], recv.at[1, k], at.far)
            self.pass_on = lambda k: remote(piece(at.s_far, k), piece(at.s_far, k), send.at[2, k], recv.at[2, k], at.sib)
            here = lambda k, n, device: remote(
                row_full.at[at.x, rpart(k)], row_full.at[at.x, rpart(k)], rsend.at[n, k], rrecv.at[at.x, k], device
            )
            self.rows = (lambda k: here(k, 0, at.side), lambda k: here(k, 1, at.up), lambda k: here(k, 2, at.down))
            got = lambda s, n, k: remote(piece(s, k), piece(s, k), send.at[n, k], recv.at[n, k], at.sib)
            self.from_sib = lambda k: got(at.s_sib, 0, k)
            self.from_far = lambda k: got(at.s_far, 1, k)
            self.from_diag = lambda k: got(at.s_diag, 2, k)
            other = lambda k: row_full.at[1 - at.x, rpart(k)]
            self.from_side = lambda k: remote(other(k), other(k), rsend.at[0, k], rrecv.at[1 - at.x, k], at.side)

        def step(self, i, last):
            at = self.at
            upward, downward = (at.z >= at.s) & (at.z < 3), (at.z <= at.s) & (at.z > 0)
            side, up, down = self.rows

            @pl.when(i == 0)
            def _():
                at.greet()
                self.load.start()
                each_slice(lambda k: self.to_sib(k).start())

                @pl.when(at.z == at.s)
                def _():
                    self.rload.start()
                    self.rload.wait()
                    self.rkeep.start()
                    self.rkeep.wait()

                self.load.wait()
                self.keep.start()

            k = i - 1

            @pl.when((k >= 0) & (k < SLICES))
            def _():
                self.to_far(k).start()

            @pl.when((k >= SLICES) & (k < 2 * SLICES))
            def _():
                self.from_far(k - SLICES).wait_recv()
                self.pass_on(k - SLICES).start()

            far_away = jnp.where(at.z > at.s, at.z - at.s, at.s - at.z)
            v = 3 * i - 6 * far_away + 1
            r = jnp.where(v >= 0, lax.div(v, 4), -1)

            @pl.when((r >= 0) & (r < SLICES) & (4 * r < v))
            def _():
                @pl.when(at.z != at.s)
                def _():
                    side(r).wait_recv()

                side(r).start()

                @pl.when(upward)
                def _():
                    up(r).start()

                @pl.when(downward)
                def _():
                    down(r).start()

            @pl.when(i == last)
            def _():
                self.keep.wait()

                def finish(k):
                    self.to_sib(k).wait_send()
                    self.to_far(k).wait_send()
                    self.pass_on(k).wait_send()
                    self.from_sib(k).wait_recv()
                    self.from_diag(k).wait_recv()
                    side(k).wait_send()
                    self.from_side(k).wait_recv()

                    @pl.when(upward)
                    def _():
                        up(k).wait_send()

                    @pl.when(downward)
                    def _():
                        down(k).wait_send()

                each_slice(finish)

    return Traffic


def add_into(dst, src, rows):
    step = next(n for n in (64, 48, 32, 16) if rows % n == 0)

    def body(i, _):
        part = pl.ds(pl.multiple_of(i * step, 16), step)
        dst[part, :] = (dst[part, :].astype(f32) + src[part, :].astype(f32)).astype(bf16)
        return 0

    lax.fori_loop(0, rows // step, body, 0)


def far_first(at, i):
    inner = (at.z == 1) | (at.z == 2)
    i = jnp.where(inner & (i >= 2), 5 - i, i)
    return jnp.where(at.z < 2, 3 - i, i)


class ReduceShards:
    def __init__(self, at, partial, cuts, acc, from_side, from_down, from_up, sems):
        self.at, self.partial, self.cuts, self.acc = at, partial, cuts, acc
        self.from_side, self.from_down, self.from_up = from_side, from_down, from_up
        self.send, self.recv_side, self.recv_down, self.recv_up = sems
        self.rows = acc.shape[1] // cuts

    def unit(self, j):
        if isinstance(j, int):
            shard, cut = j // self.cuts, j % self.cuts
        else:
            shard, cut = lax.div(j, self.cuts), lax.rem(j, self.cuts)
        zp = far_first(self.at, shard)
        return zp, zp * self.cuts + cut, pl.ds(pl.multiple_of(cut * self.rows, self.rows), self.rows)

    def side_copy(self, j):
        at = self.at
        zp, n, part = self.unit(j)
        return remote(
            self.partial(zp).at[part], self.from_side.at[zp, part],
            self.send.at[0, n], self.recv_side.at[n], at.side,
        )

    def up_copy(self, j):
        zp, n, part = self.unit(j)
        return remote(
            self.acc.at[zp, part], self.from_down.at[zp, part], self.send.at[1, n], self.recv_down.at[n], self.at.up
        )

    def down_copy(self, j):
        zp, n, part = self.unit(j)
        return remote(
            self.acc.at[zp, part], self.from_up.at[zp, part], self.send.at[2, n], self.recv_up.at[n], self.at.down
        )

    def start(self):
        self.side_copy(0).start()
        self.side_copy(1).start()

    def step(self, j):
        at = self.at
        zp, _, part = self.unit(j)
        self.side_copy(j).wait()
        acc = self.acc.at[zp, part]
        add_into(acc, self.from_side.at[zp, part], self.rows)

        @pl.when((at.z > 0) & (zp >= at.z))
        def _():
            self.up_copy(j).wait_recv()
            add_into(acc, self.from_down.at[zp, part], self.rows)

        @pl.when((at.z < 3) & (zp <= at.z))
        def _():
            self.down_copy(j).wait_recv()
            add_into(acc, self.from_up.at[zp, part], self.rows)

        @pl.when(zp > at.z)
        def _():
            self.up_copy(j).start()

        @pl.when(zp < at.z)
        def _():
            self.down_copy(j).start()

    def end(self):
        at = self.at
        for j in range(4 * self.cuts):
            zp = self.unit(j)[0]

            @pl.when(zp > at.z)
            def _():
                self.up_copy(j).wait_send()

            @pl.when(zp < at.z)
            def _():
                self.down_copy(j).wait_send()


def backward_traffic(layer, rows, gate):
    piece, cols = layer.shape[1:]
    rrows = rows.shape[1]
    grows, gcols = gate.shape[1:]

    class Traffic:
        inputs = (layer, rows, gate)
        outputs = (
            jax.ShapeDtypeStruct((piece, cols), f32),
            jax.ShapeDtypeStruct((rrows, cols), bf16),
            jax.ShapeDtypeStruct((grows, gcols), bf16),
        )
        scratch = (
            *[pltpu.VMEM((piece, cols), bf16)] * 5,
            pltpu.VMEM((piece, cols), f32),
            *[pltpu.VMEM((rrows, cols), bf16)] * 4,
            dma(3, SLICES),
            dma(3, SLICES),
            dma(3),
            dma(3, SLICES),
            dma(3, SLICES),
            dma(2),
            dma(2, SLICES),
            dma(2, SLICES),
            *[pltpu.VMEM((4, grows, gcols), bf16)] * 4,
            dma(3, 8),
            dma(8),
            dma(8),
            dma(8),
            dma(5),
        )
        collective_id = 3

        def __init__(
            self, layer, rows, gate, out, rows_out, gate_out,
            own_v, far_v, sib_v, pass_v, got_v, sum_v, acc, side_v, low_v, high_v,
            send, recv, local, rsend, rrecv, rlocal, fsend, frecv,
            gacc, gside, glow, ghigh, gsend, grecv_side, grecv_low, grecv_high, glocal,
        ):
            self.at = at = Place()
            cut, rcut = piece // SLICES, rrows // SLICES
            part = lambda k: pl.ds(pl.multiple_of(k * cut, cut), cut)
            rpart = lambda k: pl.ds(pl.multiple_of(k * rcut, rcut), rcut)
            self.own, self.sib, self.passed, self.got, self.sum = own_v, sib_v, pass_v, got_v, sum_v
            self.part, self.rpart, self.cut, self.rcut = part, rpart, cut, rcut
            self.far_v, self.acc, self.side_v, self.low_v, self.high_v = far_v, acc, side_v, low_v, high_v
            self.load_far = pltpu.make_async_copy(layer.at[at.s_far], far_v, local.at[0])
            self.load_own = pltpu.make_async_copy(layer.at[at.s], own_v, local.at[1])
            self.store = pltpu.make_async_copy(sum_v, out, local.at[2])
            self.to_pass = lambda k: remote(
                layer.at[at.s_diag, part(k)], pass_v.at[part(k)], send.at[0, k], recv.at[0, k], at.sib
            )
            self.to_sib = lambda k: remote(
                layer.at[at.s_sib, part(k)], sib_v.at[part(k)], send.at[1, k], recv.at[1, k], at.sib
            )
            self.to_far = lambda k: remote(
                far_v.at[part(k)], got_v.at[part(k)], send.at[2, k], recv.at[2, k], at.far
            )
            self.load_acc = pltpu.make_async_copy(rows.at[at.x], acc, rlocal.at[0])
            self.store_acc = pltpu.make_async_copy(acc, rows_out, rlocal.at[1])
            spread = lambda k, n, device: remote(
                acc.at[rpart(k)], rows_out.at[rpart(k)], fsend.at[n, k], frecv.at[n, k], device
            )
            self.spread_far = lambda k: spread(k, 0, at.far)
            self.spread_sib = lambda k: spread(k, 1, at.sib)
            self.spread_on = lambda k: remote(
                rows_out.at[rpart(k)], rows_out.at[rpart(k)], fsend.at[1, k], frecv.at[1, k], at.sib
            )
            self.gates = ReduceShards(
                at, lambda zp: gate.at[2 * zp + 1 - at.x], 2, gacc, gside, glow, ghigh,
                (gsend, grecv_side, grecv_low, grecv_high),
            )
            self.load_gate = [
                pltpu.make_async_copy(gate.at[2 * zp + at.x], gacc.at[zp], glocal.at[zp]) for zp in range(4)
            ]
            self.store_gate = pltpu.make_async_copy(gacc.at[at.z], gate_out, glocal.at[4])
            self.to_side = lambda k: remote(
                rows.at[1 - at.x, rpart(k)], side_v.at[rpart(k)], rsend.at[0, k], rrecv.at[0, k], at.side
            )
            self.to_up = lambda k: remote(
                acc.at[rpart(k)], low_v.at[rpart(k)], rsend.at[1, k], rrecv.at[1, k], at.up
            )
            self.to_down = lambda k: remote(
                acc.at[rpart(k)], high_v.at[rpart(k)], rsend.at[2, k], rrecv.at[2, k], at.down
            )

        def step(self, i, last):
            at = self.at

            @pl.when(i == 0)
            def _():
                at.greet()
                self.load_far.start()
                self.load_own.start()
                self.load_acc.start()
                for copy in self.load_gate:
                    copy.start()
                each_slice(lambda k: self.to_pass(k).start())
                each_slice(lambda k: self.to_sib(k).start())

            @pl.when(i < SLICES)
            def _():
                self.to_side(i).start()

            @pl.when(i == 1)
            def _():
                self.load_far.wait()
                self.load_own.wait()
                self.load_acc.wait()
                for copy in self.load_gate:
                    copy.wait()

            k = i - 1

            @pl.when((k >= 0) & (k < SLICES))
            def _():
                self.to_pass(k).wait_recv()
                add_into(self.far_v.at[self.part(k)], self.passed.at[self.part(k)], self.cut)
                self.to_far(k).start()

            m = i - SLICES

            @pl.when((m >= 0) & (m < SLICES))
            def _():
                self.to_sib(m).wait_recv()
                self.to_far(m).wait_recv()
                p = self.part(m)
                self.sum[p, :] = (
                    self.own[p, :].astype(f32) + self.sib[p, :].astype(f32) + self.got[p, :].astype(f32)
                )

            ends = jnp.where(at.z > 3 - at.z, at.z, 3 - at.z)
            chain = jnp.where(at.z < at.s, at.z, jnp.where(at.z > at.s, 3 - at.z, ends))
            v = 10 * i - 17 * chain - 26 + 10
            r = jnp.where(v >= 0, lax.div(v, 11), -1)

            @pl.when((r >= 0) & (r < SLICES) & (11 * r < v))
            def _():
                acc = self.acc.at[self.rpart(r)]
                self.to_side(r).wait_recv()
                add_into(acc, self.side_v.at[self.rpart(r)], self.rcut)

                @pl.when((at.z <= at.s) & (at.z > 0))
                def _():
                    self.to_up(r).wait_recv()
                    add_into(acc, self.low_v.at[self.rpart(r)], self.rcut)

                @pl.when((at.z >= at.s) & (at.z < 3))
                def _():
                    self.to_down(r).wait_recv()
                    add_into(acc, self.high_v.at[self.rpart(r)], self.rcut)

                @pl.when(at.z < at.s)
                def _():
                    self.to_up(r).start()

                @pl.when(at.z > at.s)
                def _():
                    self.to_down(r).start()

                @pl.when(at.z == at.s)
                def _():
                    self.spread_far(r).start()
                    self.spread_sib(r).start()

            g = i - (last - 7)

            @pl.when(g >= 0)
            def _():
                self.gates.side_copy(g).start()

            inner = jnp.where((at.z == 1) | (at.z == 2), 1, 0)
            g = i - 11 - inner

            @pl.when(g >= 0)
            def _():
                self.gates.step(g)

            @pl.when(i == last)
            def _():
                def rest(k, _):
                    self.gates.step(k)
                    return 0

                lax.fori_loop(last - 10 - inner, 8, rest, 0)

                self.store.start()
                self.store_gate.start()

                @pl.when(at.s == at.z)
                def _():
                    self.store_acc.start()

                def forward(k):
                    @pl.when(at.s_far == at.z)
                    def _():
                        self.spread_far(k).wait_recv()
                        self.spread_on(k).start()

                each_slice(forward)

                def finish(k):
                    @pl.when(at.s == at.z)
                    def _():
                        self.spread_far(k).wait_send()
                        self.spread_sib(k).wait_send()

                    @pl.when(at.s_far == at.z)
                    def _():
                        self.spread_on(k).wait_send()

                    @pl.when((at.s_sib == at.z) | (at.s_diag == at.z))
                    def _():
                        self.spread_on(k).wait_recv()

                    self.to_pass(k).wait_send()
                    self.to_sib(k).wait_send()
                    self.to_far(k).wait_send()
                    self.to_side(k).wait_send()

                    @pl.when(at.z < at.s)
                    def _():
                        self.to_up(k).wait_send()

                    @pl.when(at.z > at.s)
                    def _():
                        self.to_down(k).wait_send()

                each_slice(finish)
                self.gates.end()
                self.store.wait()
                self.store_gate.wait()

                @pl.when(at.s == at.z)
                def _():
                    self.store_acc.wait()

    return Traffic


def mid_kernel(gate, mixed, cot, w_out, normed,
               d_mixed, d_gate, gate_part, out_part, layer_part,
               gate_v, mixed_v, cot_v, normed_v, w_v, a_v, low_v, dg_v, l_v, out_v, stats, got, *sems):
    at = Place()
    load, xsend, xrecv, store = sems
    length, wide = mixed_v.shape
    depth = cot_v.shape[1]
    piece = length // 4
    strips = wide // 128
    tiles = piece // 256
    part = lambda t: pl.ds(pl.multiple_of(t * 256, 256), 256)

    def loads(k):
        r = pl.ds(pl.multiple_of(k * piece, piece), piece)
        pairs = ((cot, cot_v), (gate, gate_v), (mixed, mixed_v))
        return [pltpu.make_async_copy(p.at[r], v.at[r], load.at[3 * k + n]) for n, (p, v) in enumerate(pairs)]

    w_load = pltpu.make_async_copy(w_out, w_v, load.at[12])
    normed_load = pltpu.make_async_copy(normed, normed_v, load.at[13])
    w_load.start()
    for k in range(4):
        for copy in loads(k):
            copy.start()
    normed_load.start()
    at.greet(sequence=True)

    stats[...] = jnp.zeros_like(stats)
    w_load.wait()

    def first(i, _):
        @pl.when(lax.rem(i, tiles) == 0)
        def _():
            for copy in loads(lax.div(i, tiles)):
                copy.wait()

        tile = part(i)
        a_v[tile, :] = dot_nt(cot_v[tile, :], w_v[...])
        sum_g, sum_a = jnp.zeros((256, 128), f32), jnp.zeros((256, 128), f32)
        for n in range(strips):
            col = slice(128 * n, 128 * n + 128)
            gt = gate_v[tile, col]
            g = mixed_v[tile, col].astype(f32) * (gt * sigmoid(gt))
            sum_g = sum_g + g * g
            sum_a = sum_a + a_v[tile, col] * g
        stats[0:1, tile] = jnp.sum(sum_g.T, axis=0, keepdims=True)
        stats[1:2, tile] = jnp.sum(sum_a.T, axis=0, keepdims=True)
        return 0

    lax.fori_loop(0, 4 * tiles, first, 0)

    peers = (at.s_sib, at.s_far, at.s_diag)
    swap = [remote(stats, got.at[k], xsend.at[k], xrecv.at[k], (at.w, s)) for k, s in enumerate(peers)]
    for copy in swap:
        copy.start()
    for copy in swap:
        copy.wait()
    total = stats[...] + got[0] + got[1] + got[2]
    r_row = lax.rsqrt(total[0:1] / E + eps)
    stats[0:1, :] = r_row
    stats[1:2, :] = r_row * r_row * r_row * (total[1:2] / E)

    def column(k, at_row):
        return jnp.broadcast_to(stats[k : k + 1, pl.ds(pl.multiple_of(at_row, 128), 256)], (128, 256)).T

    def second(i, _):
        tile = pl.ds(pl.multiple_of(i * 256, 256), 256)
        r, pull = column(0, i * 256), column(1, i * 256)
        for n in range(strips):
            col = slice(128 * n, 128 * n + 128)
            gt, mx = gate_v[tile, col], mixed_v[tile, col].astype(f32)
            sg = sigmoid(gt)
            silu = gt * sg
            g = mx * silu
            low_v[tile, col] = (g * r).astype(bf16)
            d_g = r * a_v[tile, col] - g * pull
            mixed_v[tile, col] = (d_g * silu).astype(bf16)
            dg_v[tile, col] = (d_g * mx * (sg * (1.0 + gt * (1.0 - sg)))).astype(bf16)
        l_v[tile, :] = dot(low_v[tile, :], w_v[...]).astype(bf16)
        layer_copy(i).start()
        return 0

    layer_copy = lambda i: pltpu.make_async_copy(l_v.at[part(i)], layer_part.at[part(i)], store.at[9 + i])
    lax.fori_loop(0, length // 256, second, 0)
    keep = [pltpu.make_async_copy(mixed_v, d_mixed, store.at[0]), pltpu.make_async_copy(dg_v, d_gate, store.at[1])]
    for copy in keep:
        copy.start()
    normed_load.wait()
    tn = lambda p, q: lax.dot_general(p, q, (((0,), (0,)), ((), ())), preferred_element_type=f32)

    def out_block(n):
        room = out_v.at[part(n)]
        return room, pltpu.make_async_copy(room, out_part.at[part(n)], store.at[2 + n])

    def out_grad(n, _):
        room, copy = out_block(n)
        room[...] = tn(low_v[:, part(n)], cot_v[...]).astype(bf16)
        copy.start()
        return 0

    lax.fori_loop(0, wide // 256, out_grad, 0)
    shard = depth // 4
    block = lambda n: pl.ds(pl.multiple_of(n * shard, shard), shard)
    gate_block = lambda n: pltpu.make_async_copy(low_v.at[block(n)], gate_part.at[block(n)], store.at[5 + n])

    def gate_grad(n, _):
        low_v[block(n), :] = tn(normed_v[:, block(n)], dg_v[...]).astype(bf16)
        gate_block(n).start()
        return 0

    lax.fori_loop(0, 4, gate_grad, 0)

    for copy in keep:
        copy.wait()
    for n in range(wide // 256):
        out_block(n)[1].wait()
    for n in range(4):
        gate_block(n).wait()
    for i in range(length // 256):
        layer_copy(i).wait()


def middle(gate, mixed, cot, w_out, normed):
    length, wide = mixed.shape
    depth = cot.shape[1]
    piece = length // 4
    vm = pltpu.VMEM
    low = lambda *shape: jax.ShapeDtypeStruct(shape, bf16)
    return pl.pallas_call(
        mid_kernel,
        in_specs=[pl.BlockSpec(memory_space=ANY)] * 5,
        out_specs=[pl.BlockSpec(memory_space=ANY)] * 5,
        out_shape=[
            low(length, wide),
            low(length, wide),
            low(depth, wide),
            low(wide, depth),
            low(length, depth),
        ],
        scratch_shapes=[
            vm((length, wide), f32),
            vm((length, wide), bf16),
            vm((length, depth), bf16),
            vm((length, depth), bf16),
            vm((wide, depth), bf16),
            vm((length, wide), f32),
            vm((length, wide), bf16),
            vm((length, wide), bf16),
            vm((length, depth), bf16),
            vm((wide, depth), bf16),
        ]
        + [vm((8, length), f32), vm((3, 8, length), f32)]
        + [dma(14), dma(3), dma(3), dma(17)],
        compiler_params=pltpu.CompilerParams(
            collective_id=5, has_side_effects=True, vmem_limit_bytes=61 * 2**20
        ),
        name="middle",
    )(gate, mixed, cot, w_out, normed)


def small_start(at, small, got, sems):
    send, recv = sems
    for k in range(1, 8):
        peer = (lax.rem(at.w + k, 8), at.s)
        remote(small, got.at[k], send.at[k], recv.at[k], peer).start()


def small_pass(at, small, got, total, full, sems, more):
    send, recv = sems
    send2, recv2, local = more
    value = small[...]
    for k in range(1, 8):
        remote(small, got.at[k], send.at[k], recv.at[k], at.side).wait_recv()
        value = value + got[k]
    total[...] = value
    pltpu.make_async_copy(total, full.at[at.s], local).start()
    for k, s in enumerate((at.s_sib, at.s_far, at.s_diag)):
        remote(total, full.at[at.s], send2.at[k], recv2.at[k], (at.w, s)).start()


def small_end(at, small, got, total, full, sems, more):
    send, recv = sems
    send2, recv2, local = more
    pltpu.make_async_copy(total, full.at[at.s], local).wait()
    for k in range(1, 8):
        remote(small, got.at[k], send.at[k], recv.at[k], at.side).wait_send()
    for k, s in enumerate((at.s_sib, at.s_far, at.s_diag)):
        remote(total, full.at[at.s], send2.at[k], recv2.at[k], (at.w, s)).wait_send()
        remote(total, full.at[s], send2.at[k], recv2.at[k], (at.w, s)).wait_recv()


def last_kernel(hid, d_gate, d_u, d_dt, w_main, w_com, gate_sum, small,
                back_sum, in_sum, sums_out,
                hid_v, dp_v, w_v,
                b_diag, b_sib, b_far, b_own, from_sib, pass_sib, from_far,
                part_v, mside, mlow, mhigh, macc, mown, csib, cown, cacc, cside, clow, chigh, cfar, csum,
                sgot, stotal, sfull, gate_v, *sems):
    at = Place()
    sems = list(sems)
    take = lambda n: [sems.pop(0) for _ in range(n)]
    load, bsem, msem, csem, cx, ssem, smore, asem, gsem = (
        take(6), take(2), take(4), take(4), take(7), take(2), take(3), take(3), take(3)
    )
    piece = hid_v.shape[0] // 4
    shard = hid_v.shape[1] // 8
    wide = d_gate.shape[1]
    half = shard // 2
    mine = pl.ds(pl.multiple_of(at.c * half, half), half)
    other = pl.ds(pl.multiple_of((1 - at.c) * half, half), half)
    at.greet(everyone=True)

    order = (at.s_diag, at.s_far, at.s_sib, at.s)
    rows_of = lambda s: pl.ds(pl.multiple_of(s * piece, piece), piece)
    weights = [
        pltpu.make_async_copy(w_main, w_v.at[:, pl.ds(0, 2 * wide)], load[0].at[0]),
        pltpu.make_async_copy(w_com, w_v.at[:, pl.ds(2 * wide, 384)], load[0].at[1]),
    ]
    loads = []
    for k, s in enumerate(order):
        r = rows_of(s)
        loads.append(
            [
                pltpu.make_async_copy(d_gate.at[r], dp_v.at[r, pl.ds(0, wide)], load[1].at[k]),
                pltpu.make_async_copy(d_u.at[r], dp_v.at[r, pl.ds(wide, wide + 256)], load[2].at[k]),
                pltpu.make_async_copy(d_dt.at[r], dp_v.at[r, pl.ds(2 * wide + 256, 128)], load[3].at[k]),
            ]
        )
    hid_load = pltpu.make_async_copy(hid, hid_v, load[4])
    soon, later = weights + loads[0] + loads[1], [hid_load] + loads[2] + loads[3]
    for copy in soon + later:
        copy.start()
    gate_slot = lambda s: in_sum.at[:, pl.ds(pl.multiple_of(s * wide, 128), wide)]
    x_slot = lambda s: in_sum.at[:, pl.ds(pl.multiple_of(E + s * wide, 128), wide)]
    gather_pieces_start(at, gate_sum, gate_slot, gsem, gate_v)
    small_start(at, small, sgot, ssem)

    send, recv = bsem
    rows = piece // PARTS
    parts = [pl.ds(k * rows, rows) for k in range(PARTS)]
    to_pass = [remote(b_diag.at[p], pass_sib.at[p], send.at[0, k], recv.at[0, k], at.sib) for k, p in enumerate(parts)]
    to_sib = [remote(b_sib.at[p], from_sib.at[p], send.at[1, k], recv.at[1, k], at.sib) for k, p in enumerate(parts)]
    to_far = [remote(b_far.at[p], from_far.at[p], send.at[2, k], recv.at[2, k], at.far) for k, p in enumerate(parts)]

    def back_tile(s, out, t):
        tile = pl.ds(pl.multiple_of(s * piece + t * 256, 256), 256)
        place = pl.ds(t * 256, 256)

        for n in range(hid_v.shape[1] // 256):
            col = slice(256 * n, 256 * n + 256)
            out[place, col] = dot_nt(dp_v[tile, :], w_v[col, :]).astype(bf16)

    big = ReduceShards(at, lambda zp: part_v.at[zp, 1 - at.x, :, pl.ds(0, wide)], 2, macc, mside, mlow, mhigh, msem)
    few = ReduceShards(at, lambda zp: cown.at[zp, 1 - at.x], 1, cacc, cside, clow, chigh, csem)
    com_cols = pl.ds(wide, 384)
    com_to_sib = lambda zp: remote(
        part_v.at[zp, :, other, com_cols], csib.at[zp], cx[0].at[zp], cx[1].at[zp], at.sib
    )

    def shard_pair(i):
        zp = far_first(at, i)
        lanes = pl.ds(pl.multiple_of(zp * 2 * shard, 128), 2 * shard)
        got = lax.dot_general(
            hid_v[:, lanes], dp_v[:, wide : 2 * wide + 384], (((0,), (0,)), ((), ())), preferred_element_type=f32
        ).astype(bf16)
        part_v[zp, 0] = got[0:shard]
        part_v[zp, 1] = got[shard : 2 * shard]
        macc[zp] = part_v[zp, at.x, :, 0:wide]
        big.side_copy(2 * i).start()
        com_to_sib(zp).start()

    def com_pair(i):
        zp = far_first(at, i)
        com_to_sib(zp).wait_recv()
        for x in range(2):
            cown[zp, x] = part_v[zp, x, mine, com_cols]
            add_into(cown.at[zp, x], csib.at[zp, x], half)
        cacc[zp] = cown[zp, at.x]
        few.side_copy(i).start()

    ends = (at.z == 0) | (at.z == 3)

    def step(j, who):
        @pl.when(who)
        def _():
            big.step(j)
            if j % 2:
                few.step(j // 2)

    tiles = piece // 256
    per = PARTS // tiles
    def far_tile(t):
        back_tile(at.s_far, b_far, t)
        for k in range(t * per, t * per + per):
            to_pass[k].wait_recv()
            add_into(b_far.at[parts[k]], pass_sib.at[parts[k]], rows)
            to_far[k].start()

    for copy in soon:
        copy.wait()
    for t in range(tiles):
        back_tile(at.s_diag, b_diag, t)
        for k in range(t * per, t * per + per):
            to_pass[k].start()
    far_tile(0)
    for copy in later:
        copy.wait()
    def sib_tile(t):
        back_tile(at.s_sib, b_sib, t)
        for k in range(t * per, t * per + per):
            to_sib[k].start()

    shard_pair(0)
    far_tile(1)
    big.side_copy(1).start()
    shard_pair(1)
    com_pair(0)
    shard_pair(2)
    big.side_copy(3).start()
    com_pair(1)
    step(0, ends)
    step(1, ends)
    shard_pair(3)
    big.side_copy(5).start()
    com_pair(2)
    step(0, ~ends)
    step(2, ends)
    gather_pieces_pass(at, gate_sum, gate_slot, gsem)
    sib_tile(0)
    big.side_copy(7).start()
    com_pair(3)
    step(1, ~ends)
    step(3, ends)
    sib_tile(1)
    step(2, ~ends)
    step(4, ends)
    back_tile(at.s, b_own, 0)
    step(3, ~ends)
    step(4, ~ends)
    step(5, ends)
    back_tile(at.s, b_own, 1)
    step(5, ~ends)
    small_pass(at, small, sgot, stotal, sfull, ssem, smore)
    for j in (6, 7):
        big.step(j)
    few.step(3)
    mown[...] = macc[at.z]
    gather_pieces_start(at, mown, x_slot, asem)
    csum[...] = cacc[at.z]
    far_copy = remote(csum, cfar, cx[2], cx[3], at.far)
    far_copy.start()
    for k, p in enumerate(parts):
        to_sib[k].wait_recv()
        to_far[k].wait_recv()

        def body(i, _):
            r = pl.ds(pl.multiple_of(k * rows + i * 32, 32), 32)
            back_sum[r, :] = b_own[r, :].astype(f32) + from_sib[r, :].astype(f32) + from_far[r, :].astype(f32)
            return 0

        lax.fori_loop(0, rows // 32, body, 0)
    far_copy.wait()
    add_into(csum, cfar, half)
    com_out = in_sum.at[mine, pl.ds(2 * E, 384)]
    com_copy = remote(csum, com_out, cx[4], cx[5], at.sib)
    com_copy.start()
    keep_copy = pltpu.make_async_copy(csum, com_out, cx[6])
    keep_copy.start()
    gather_pieces_pass(at, mown, x_slot, asem)
    small_end(at, small, sgot, stotal, sfull, ssem, smore)
    sums_out[...] = jnp.zeros_like(sums_out)
    bc, heads = jnp.zeros((8, 256), f32), jnp.zeros((8, 128), f32)
    for s in range(4):
        sums_out[:, wide * s : wide * s + wide] = sfull[s, :, 0:wide]
        bc = bc + sfull[s, :, wide : wide + 256]
        shift = (wide // P_SIZE) * s
        own = sfull[s, :, 0:128]
        heads = heads + (pltpu.roll(own, shift, 1) if shift else own)
    sums_out[:, E : E + 256] = bc
    sums_out[:, E + 256 : E + 384] = heads
    for copy in to_pass + to_sib + to_far:
        copy.wait_send()
    for zp in range(4):
        com_to_sib(zp).wait_send()
    big.end()
    few.end()
    gather_pieces_end(at, gate_sum, gate_slot, gsem)
    gather_pieces_end(at, mown, x_slot, asem)
    keep_copy.wait()
    com_copy.wait_send()
    got = in_sum.at[other, pl.ds(2 * E, 384)]
    remote(csum, got, cx[4], cx[5], at.sib).wait_recv()


def finish_last(hid, d_gate, d_u, d_dt, w_main, w_com, gate_sum, small):
    length, depth = hid.shape
    piece, shard, half = length // 4, depth // 8, depth // 16
    wide = d_gate.shape[1]
    vm = pltpu.VMEM
    shards4 = lambda cuts: [dma(3, 4 * cuts), dma(4 * cuts), dma(4 * cuts), dma(4 * cuts)]
    return pl.pallas_call(
        last_kernel,
        in_specs=[pl.BlockSpec(memory_space=ANY)] * 7 + [pl.BlockSpec(memory_space=pltpu.VMEM)],
        out_specs=[
            pl.BlockSpec(memory_space=pltpu.VMEM),
            pl.BlockSpec(memory_space=ANY),
            pl.BlockSpec(memory_space=pltpu.VMEM),
        ],
        out_shape=[
            jax.ShapeDtypeStruct((piece, depth), f32),
            jax.ShapeDtypeStruct((shard, 2 * E + 384), bf16),
            jax.ShapeDtypeStruct((8, E + 384), f32),
        ],
        scratch_shapes=[vm(hid.shape, bf16), vm((length, 2 * wide + 384), bf16), vm((depth, 2 * wide + 384), bf16)]
        + [vm((piece, depth), bf16)] * 7
        + [vm((4, 2, shard, wide + 384), bf16)]
        + [vm((4, shard, wide), bf16)] * 4
        + [vm((shard, wide), bf16)]
        + [vm((4, 2, half, 384), bf16)] * 2
        + [vm((4, half, 384), bf16)] * 4
        + [vm((half, 384), bf16)] * 2
        + [vm((8,) + small.shape, f32), vm(small.shape, f32), vm((4,) + small.shape, f32), vm(gate_sum.shape, bf16)]
        + [dma(2), dma(4), dma(4), dma(4), dma(), dma()]
        + [dma(3, PARTS), dma(3, PARTS)]
        + shards4(2)
        + shards4(1)
        + [dma(4), dma(4), dma(), dma(), dma(), dma(), dma()]
        + [dma(8), dma(8)]
        + [dma(3), dma(3), dma()]
        + [dma(3, PARTS), dma(3, PARTS), dma()]
        + [dma(3, PARTS), dma(3, PARTS), dma()],
        compiler_params=pltpu.CompilerParams(
            collective_id=4, has_side_effects=True, vmem_limit_bytes=60 * 2**20
        ),
        name="finish_last",
    )(hid, d_gate, d_u, d_dt, w_main, w_com, gate_sum, small)


def over_rows(left, right):
    return lax.dot_general(
        left, right, (((0,), (0,)), ((), ())), preferred_element_type=jnp.float32
    )


def gather_plain(hid, main, com):
    hid_all = lax.all_gather(hid, "seq", axis=0)
    main_all = lax.all_gather(main, "wshard", axis=0)
    return hid_all, main_all, lax.all_gather(com, "wshard", axis=0)


def gather_more_plain(cot, rows, wide):
    cot_all = lax.all_gather(cot, "seq", axis=0)
    cols = lax.all_to_all(rows, "wshard", split_axis=1, concat_axis=0, tiled=True)
    own = lax.dynamic_slice_in_dim(cols, lax.axis_index("seq") * wide, wide, 0)
    return cot_all, lax.all_gather(own, "wshard", axis=1, tiled=True)


def reduce_scattered(v, axis):
    return lax.psum_scatter(v, axis, scatter_dimension=0, tiled=False)


def reduce_first_plain(layer, rows, gate):
    layer_sum = reduce_scattered(layer, "seq").astype(f32)
    rows = rows.reshape(-1, rows.shape[-1])
    part = lax.psum_scatter(rows, "wshard", scatter_dimension=1, tiled=True)
    part = lax.all_gather(part, "seq", axis=0, tiled=True)
    part = lax.all_to_all(part, "wshard", split_axis=0, concat_axis=1, tiled=True)
    return layer_sum, part, reduce_scattered(gate, "wshard")


def finish_plain(hid, d_gate, d_u, d_dt, w_main, w_com, gate_sum, small):
    groups, owners = lax.axis_size("seq"), lax.axis_size("wshard")
    wide = d_gate.shape[1]
    rest = jnp.concatenate([d_u, d_dt], axis=1)
    nt = lambda p, q: lax.dot_general(p, q, (((1,), (1,)), ((), ())), preferred_element_type=f32)
    back = nt(d_gate, w_main[:, :wide]) + nt(rest, jnp.concatenate([w_main[:, wide:], w_com], axis=1))
    back_sum = reduce_scattered(back.astype(bf16).reshape(groups, -1, D), "seq").astype(f32)
    part = reduce_scattered(over_rows(hid, rest).astype(bf16).reshape(owners, -1, rest.shape[1]), "wshard")
    part = lax.all_gather(jnp.concatenate([gate_sum, part], axis=1), "seq", axis=0)
    in_sum = jnp.concatenate(
        [part[i, :, :wide] for i in range(groups)]
        + [part[i, :, wide : 2 * wide] for i in range(groups)]
        + [jnp.sum(part[:, :, 2 * wide :].astype(f32), axis=0).astype(bf16)],
        axis=1,
    )
    full = lax.all_gather(lax.psum(small, "wshard"), "seq", axis=0)
    turned = [jnp.roll(full[i, :, :128], i * (wide // P_SIZE), axis=1) for i in range(groups)]
    sums = jnp.concatenate(
        [full[i, :, :wide] for i in range(groups)] + [jnp.sum(full[:, :, wide:], axis=0), sum(turned)], axis=1
    )
    return back_sum, in_sum, sums


def middle_plain(gate, mixed, cot_all, w_out, normed):
    mixed_wide = mixed.astype(f32)
    sg = jax.nn.sigmoid(gate)
    silu = gate * sg
    g = mixed_wide * silu
    g_low = g.astype(bf16)
    a = lax.dot_general(cot_all, w_out, (((1,), (1,)), ((), ())), preferred_element_type=f32)
    sums = lax.psum(jnp.stack([jnp.sum(g * g, axis=1), jnp.sum(a * g, axis=1)]), "seq")
    r = lax.rsqrt(sums[0] / E + eps)[:, None]
    pull = (r * r * r) * (sums[1] / E)[:, None]
    d_g = r * a - g * pull
    d_mixed = (d_g * silu).astype(bf16)
    d_gate = (d_g * mixed_wide * (sg * (1.0 + gate * (1.0 - sg)))).astype(bf16)
    layer_part = (jnp.dot(g_low, w_out, preferred_element_type=f32) * r).astype(bf16)
    cot_r = (cot_all.astype(f32) * r).astype(bf16)
    out_part = over_rows(g_low, cot_r).astype(bf16)

    gate_part = over_rows(normed, d_gate).astype(bf16)
    return d_mixed, d_gate, gate_part, out_part, layer_part


def shards(
    hidden,
    segments,
    norm_gain,
    in_weight,
    conv_weight,
    conv_bias,
    step_bias,
    decay_log,
    skip_scale,
    gate_gain,
    out_weight,
    cotangent,
):
    group = lax.axis_index("seq")
    groups, owners = lax.axis_size("seq"), lax.axis_size("wshard")
    direct = (groups, owners) == (4, 8)
    heads = H // groups
    wide = heads * P_SIZE
    length = segments.shape[1]
    hidden_own, cot_own = hidden[0], cotangent[0]
    main = jnp.concatenate(
        [
            lax.dynamic_slice_in_dim(in_weight, group * wide, wide, 1),
            lax.dynamic_slice_in_dim(in_weight, E + group * wide, wide, 1),
        ],
        axis=1,
    )
    com = jnp.concatenate([in_weight[:, 2 * E :], norm_gain[:, None]], axis=1)
    com = jnp.pad(com, ((0, 0), (0, 128 - H - 1)))
    out_gain = gate_gain.astype(f32)[:, None]
    out_scaled = (out_weight.astype(f32) * out_gain).astype(bf16)
    gather = gather_first if direct else gather_plain
    hidden_all, w_main, w_com = gather(hidden_own, main, com)
    hidden_all = hidden_all.reshape(length, D)
    w_main, w_com = w_main.reshape(D, 2 * wide), w_com.reshape(D, -1)
    gain_row = w_com[:, 2 * N + H].astype(f32)[None]

    seg = segments[0]
    seg_col = jnp.pad(seg, (8, 8), constant_values=-1)[:, None]
    segr = seg.reshape(length // Q, 1, Q)
    par = jnp.pad(jnp.stack([step_bias, decay_log]), ((0, 6), (0, 128 - H)))
    skip = jnp.repeat(skip_scale, P_SIZE)[None]
    facts = (seg_col, segr, conv_weight, conv_bias[None], par, skip)
    beside, more = (forward_traffic(cot_own, out_scaled), (cot_own, out_scaled)) if direct else (NoTraffic, ())
    u, dt, gate, normed, mixed, save, *got = mixer_fwd(beside, more, hidden_all, gain_row, w_main, w_com, *facts)
    cot_all, w_out = got if direct else gather_more_plain(cot_own, out_scaled, wide)
    cot_all, w_out = cot_all.reshape(length, D), w_out.reshape(wide, D)

    mid = middle if direct else middle_plain
    d_mixed, d_gate, gate_part, out_part, layer_part = mid(gate, mixed, cot_all, w_out, normed)
    own_wide = hidden_own.astype(f32)

    more = (layer_part.reshape(groups, -1, D), out_part.reshape(2, -1, D), gate_part.reshape(owners, -1, wide))
    beside = backward_traffic(*more) if direct else NoTraffic
    du, ddt, small, *got = mixer_bwd(
        beside, more if direct else (), u, dt, *facts, save, d_mixed
    )
    layer_sum, out_sum, gate_sum = got if direct else reduce_first_plain(*more)
    layer_output = own_wide + layer_sum
    finish = finish_last if direct else finish_plain
    back_sum, in_sum, sums = finish(normed, d_gate, du, ddt, w_main, w_com, gate_sum, small)

    own_scale = lax.rsqrt(jnp.mean(own_wide * own_wide, axis=-1, keepdims=True) + eps)
    b = back_sum * gain_row
    hidden_grad = (
        cot_own.astype(f32)
        + own_scale * b
        - own_wide * (own_scale * own_scale * own_scale) * jnp.mean(b * own_wide, axis=-1, keepdims=True)
    )
    in_weight_grad = in_sum[:, : 2 * E + 2 * N + H].astype(f32)
    norm_gain_grad = jnp.sum(in_weight_grad * in_weight.astype(f32), axis=1) / norm_gain.astype(f32)
    out_sum = out_sum.astype(f32)
    out_weight_grad = out_sum * out_gain
    gate_gain_grad = jnp.sum(out_sum * out_weight.astype(f32), axis=1)
    chan, per_head = sums[:, : E + 2 * N], sums[:, E + 2 * N : E + 2 * N + H]
    return (
        layer_output[None],
        hidden_grad[None],
        norm_gain_grad,
        in_weight_grad,
        chan[:4],
        chan[4],
        per_head[5],
        per_head[6],
        per_head[7],
        gate_gain_grad,
        out_weight_grad,
    )


def solution(mesh):
    in_specs = (
        P("wshard", "seq", None),
        P("wshard", None),
        P("wshard"),
        P("wshard", None),
        P(),
        P(),
        P(),
        P(),
        P(),
        P("wshard"),
        P("wshard", None),
        P("wshard", "seq", None),
    )
    out_specs = (
        P("wshard", "seq", None),
        P("wshard", "seq", None),
        P("wshard"),
        P("wshard", None),
        P(),
        P(),
        P(),
        P(),
        P(),
        P("wshard"),
        P("wshard", None),
    )
    return jax.shard_map(shards, mesh=mesh, in_specs=in_specs, out_specs=out_specs, check_vma=False)
```

```python
import functools

import jax
import jax.numpy as jnp
from jax import lax
from jax.experimental import pallas as pl
from jax.experimental.pallas import tpu as pltpu
from jax.sharding import PartitionSpec as P

D = 1536
H = 48
P_SIZE = 64
N = 128
E = 3072

eps = 1e-05
f32, bf16 = jnp.float32, jnp.bfloat16
Q = 128
NEG = -1e30


def dot(a, b):
    return jnp.dot(a, b, preferred_element_type=f32)


def dot_nt(a, b):
    return lax.dot_general(a, b, (((1,), (1,)), ((), ())), preferred_element_type=f32)


def dot3(tri, v):
    hi = v.astype(bf16)
    rest = v - hi.astype(f32)
    mid = rest.astype(bf16)
    low = (rest - mid.astype(f32)).astype(bf16)
    return dot(tri, hi) + dot(tri, mid) + dot(tri, low)


def sigmoid(v):
    return 1.0 / (1.0 + jnp.exp(-v))


def spread_col(v, col):
    return jnp.broadcast_to(v[:, col : col + 1], (Q, 128))


def softplus(v):
    return jnp.maximum(v, 0.0) + jnp.log1p(jnp.exp(-jnp.abs(v)))


def conv_pre(useen, flags, wk, bias, lanes, chans):
    pre = bias[:, chans] + wk[3:4, chans] * useen[8 : 8 + Q, lanes]
    for j in (1, 2, 3):
        pre = pre + wk[3 - j : 4 - j, chans] * (useen[8 - j : 8 - j + Q, lanes] * flags[j])
    return pre


class Facts:
    def __init__(self, chunk, seg_ref, par_ref, xw):
        self.group = lax.axis_index("seq")
        self.heads = xw // P_SIZE
        self.xw = xw
        near = seg_ref[pl.ds(pl.multiple_of(chunk * Q, 8), Q + 16), :]
        now = near[8 : 8 + Q]
        same = lambda other: jnp.broadcast_to(jnp.where(other == now, 1.0, 0.0), (Q, 128))
        self.before = [None] + [same(near[8 - j : 8 - j + Q]) for j in (1, 2, 3)]
        self.after = lambda j: same(near[8 + j : 8 + j + Q])
        self.carried = same(near[7:8])
        self.samelast = same(near[7 + Q : 8 + Q])
        self.now = now
        self.turn = self.heads * self.group
        lane = lax.broadcasted_iota(jnp.int32, (8, 128), 1)
        par = self.own(par_ref[...])
        self.bias = par[0:1]
        self.rate = jnp.where(lane < self.heads, -jnp.exp(par), 0.0)[1:2]

    def own(self, v):
        lane = lax.broadcasted_iota(jnp.int32, v.shape, 1)
        return jnp.where(lane < self.heads, pltpu.roll(v, lax.rem(128 - self.turn, 128), 1), 0.0)

    def back(self, v):
        return pltpu.roll(v, self.turn, 1)

    def chans(self, p):
        if p < self.xw // 128:
            return pl.ds(pl.multiple_of(self.group * self.xw + 128 * p, 128), 128)
        at = E + 128 * (p - self.xw // 128)
        return slice(at, at + 128)


class NoTraffic:
    inputs, outputs, scratch, collective_id = (), (), (), None

    def __init__(self, *refs):
        pass

    def step(self, i, last):
        pass


def fwd_kernel(traffic, hid_ref, gain_ref, main_ref, com_ref, seg_ref, segr_ref, wk_ref, bias_ref, par_ref, skip_ref, *rest):
    n_in, n_out = len(traffic.inputs), len(traffic.outputs)
    extra_in, rest = rest[:n_in], rest[n_in:]
    u_ref, dt_ref, gate_ref, normed_ref, mixed_ref, save_ref = rest[:6]
    extra_out, rest = rest[6 : 6 + n_out], rest[6 + n_out :]
    state, useen, act, next_u, next_dt = rest[:5]
    step_no = pl.program_id(0)
    traffic(*extra_in, *extra_out, *rest[5:]).step(step_no, pl.num_programs(0) - 1)
    xw = mixed_ref.shape[1]
    width = xw + 256
    pairs = xw // 128
    facts = Facts(jnp.maximum(step_no - 1, 0), seg_ref, par_ref, xw)

    @pl.when(step_no == 0)
    def _():
        next_u[...] = jnp.zeros_like(next_u)
        next_dt[...] = jnp.zeros_like(next_dt)

    @pl.when(step_no <= 1)
    def _():
        state[...] = jnp.zeros_like(state)
        useen[0:8, :] = jnp.zeros((8, width), f32)

    useen[8 : 8 + Q, :] = next_u[...]
    dt_now = next_dt[...]

    hid = hid_ref[...].astype(f32)
    depth = hid.shape[1]
    total = jnp.zeros((Q, 128), f32)
    for k in range(depth // 128):
        part = hid[:, 128 * k : 128 * k + 128]
        total = total + part * part
    scale = lax.rsqrt(jnp.sum(total, axis=1, keepdims=True) / depth + eps)
    normed_ref[...] = (hid * scale * gain_ref[...]).astype(bf16)
    low = normed_ref[...]
    for k in range(xw // 256):
        gate_ref[:, 256 * k : 256 * k + 256] = dot(low, main_ref[:, 256 * k : 256 * k + 256])
    for k in range(xw // 256):
        got = dot(low, main_ref[:, xw + 256 * k : xw + 256 * k + 256]).astype(bf16)
        u_ref[:, 256 * k : 256 * k + 256] = got
        next_u[:, 256 * k : 256 * k + 256] = got.astype(f32)
    got = dot(low, com_ref[:, 0:256]).astype(bf16)
    u_ref[:, xw : xw + 256] = got
    next_u[:, xw : xw + 256] = got.astype(f32)
    got = facts.own(dot(low, com_ref[:, 256:384]).astype(bf16).astype(f32))
    dt_ref[...] = got.astype(bf16)
    next_dt[...] = got

    carried, samelast = facts.carried, facts.samelast
    for p in range(width // 128):
        lanes = slice(128 * p, 128 * p + 128)
        pre = conv_pre(useen, facts.before, wk_ref, bias_ref, lanes, facts.chans(p))
        act[:, lanes] = pre * sigmoid(pre)
    tail = useen[Q : Q + 8, :]
    useen[0:8, :] = tail

    step = softplus(dt_now + facts.bias)
    row = lax.broadcasted_iota(jnp.int32, (Q, Q), 0)
    col = lax.broadcasted_iota(jnp.int32, (Q, Q), 1)
    tri = jnp.where(row >= col, 1.0, 0.0).astype(bf16)
    decay = dot3(tri, step * facts.rate)
    decay_t = decay.T
    madd = jnp.where((row >= col) & (facts.now == segr_ref[0]), 0.0, NEG)
    b_now = act[:, xw : xw + 128]
    c_low = act[:, xw + 128 : xw + 256].astype(bf16)
    gram = dot_nt(c_low, b_now.astype(bf16))
    b_t = b_now.T.astype(bf16)
    left = lax.broadcasted_iota(jnp.int32, (Q, 128), 1) < 64
    for p in range(pairs):
        lanes = slice(128 * p, 128 * p + 128)
        d0, d1 = spread_col(decay, 2 * p), spread_col(decay, 2 * p + 1)
        dp = jnp.where(left, d0, d1)
        sp = jnp.where(left, spread_col(step, 2 * p), spread_col(step, 2 * p + 1))
        xs = act[:, lanes]
        xp = xs * sp
        m0 = gram * jnp.exp(d0 - decay_t[2 * p : 2 * p + 1, :] + madd)
        m1 = gram * jnp.exp(d1 - decay_t[2 * p + 1 : 2 * p + 2, :] + madd)
        both = jnp.concatenate([m0.astype(bf16), m1.astype(bf16)], axis=1)
        stacked = jnp.concatenate(
            [jnp.where(left, xp, 0.0).astype(bf16), jnp.where(left, 0.0, xp).astype(bf16)], axis=0
        )
        st = state[:, lanes]
        st_low = st.astype(bf16)
        save_ref[0, :, lanes] = st_low
        y = dot(both, stacked) + dot(c_low, st_low) * (jnp.exp(dp) * carried)
        mixed_ref[:, lanes] = (y + skip_ref[:, facts.chans(p)] * xs).astype(bf16)
        last = dp[Q - 1 : Q, :]
        to_end = (xp * (jnp.exp(last - dp) * samelast)).astype(bf16)
        state[:, lanes] = st * (jnp.exp(last) * carried[Q - 1 : Q, :]) + dot(b_t, to_end)


def mixer_fwd(traffic, extra, hid, gain, main, com, seg, segr, wk, bias, par, skip):
    length, depth = hid.shape
    xw = main.shape[1] // 2
    width = xw + 256
    n = length // Q
    whole = lambda shape: pl.BlockSpec(shape, lambda i: (0,) * len(shape), pipeline_mode=pl.Buffered(1))
    ahead = lambda i: (jnp.minimum(i, n - 1), 0)
    now = lambda i: (jnp.maximum(i - 1, 0), 0)
    now3 = lambda i: (jnp.maximum(i - 1, 0), 0, 0)
    return pl.pallas_call(
        functools.partial(fwd_kernel, traffic),
        grid=(n + 1,),
        in_specs=[
            pl.BlockSpec((Q, depth), ahead),
            whole(gain.shape),
            whole(main.shape),
            whole(com.shape),
            whole(seg.shape),
            pl.BlockSpec((1, 1, Q), now3),
            whole(wk.shape),
            whole(bias.shape),
            whole(par.shape),
            whole(skip.shape),
        ]
        + [pl.BlockSpec(memory_space=pltpu.MemorySpace.HBM)] * len(extra),
        out_specs=[
            pl.BlockSpec((Q, width), ahead),
            pl.BlockSpec((Q, 128), ahead),
            pl.BlockSpec((Q, xw), ahead),
            pl.BlockSpec((Q, depth), ahead),
            pl.BlockSpec((Q, xw), now),
            pl.BlockSpec((1, 128, xw), now3),
        ]
        + [pl.BlockSpec(memory_space=pltpu.MemorySpace.HBM)] * len(traffic.outputs),
        out_shape=[
            jax.ShapeDtypeStruct((length, width), bf16),
            jax.ShapeDtypeStruct((length, 128), bf16),
            jax.ShapeDtypeStruct((length, xw), f32),
            jax.ShapeDtypeStruct((length, depth), bf16),
            jax.ShapeDtypeStruct((length, xw), bf16),
            jax.ShapeDtypeStruct((n, 128, xw), bf16),
            *traffic.outputs,
        ],
        scratch_shapes=[
            pltpu.VMEM((128, xw), f32),
            pltpu.VMEM((Q + 8, width), f32),
            pltpu.VMEM((Q, width), f32),
            pltpu.VMEM((Q, width), f32),
            pltpu.VMEM((Q, 128), f32),
            *traffic.scratch,
        ],
        compiler_params=pltpu.CompilerParams(
            vmem_limit_bytes=60 * 2**20,
            collective_id=traffic.collective_id,
            has_side_effects=traffic.collective_id is not None,
        ),
        name="mixer_forward",
    )(hid, gain, main, com, seg, segr, wk, bias, par, skip, *extra)


def bwd_kernel(traffic, u_ref, halo_ref, dt_ref, seg_ref, segr_ref, wk_ref, bias_ref, par_ref, skip_ref,
               save_ref, dy_ref, *rest):
    n_in, n_out = len(traffic.inputs), len(traffic.outputs)
    extra_in, rest = rest[:n_in], rest[n_in:]
    du_ref, ddt_ref, small_ref = rest[:3]
    extra_out, rest = rest[3 : 3 + n_out], rest[3 + n_out :]
    dstate, useen, act, slope, dpre, keep_y, keep_x, prod_a, prod_b, rows_a, held = rest[:11]
    wgrad_ref, hgrad_ref, sgrad_ref, spot_ref = rest[11:15]
    step_no = pl.program_id(0)
    last_step = pl.num_programs(0) - 1
    traffic(*extra_in, *extra_out, *rest[15:]).step(step_no, last_step)
    width = u_ref.shape[1]
    xw = width - 256
    pairs = xw // 128

    @pl.when(step_no == 0)
    def _():
        dstate[...] = jnp.zeros_like(dstate)
        dpre[Q : Q + 8, :] = jnp.zeros((8, width), f32)
        wgrad_ref[...] = jnp.zeros_like(wgrad_ref)
        hgrad_ref[...] = jnp.zeros_like(hgrad_ref)
        sgrad_ref[...] = jnp.zeros_like(sgrad_ref)
        rows_a[...] = jnp.zeros_like(rows_a)
        head_of = lax.broadcasted_iota(jnp.int32, (xw, 128), 0) // P_SIZE
        mark = head_of == lax.broadcasted_iota(jnp.int32, (xw, 128), 1)
        spot_ref[...] = jnp.where(mark, 1.0, 0.0).astype(bf16)

    useen[0:8, :] = halo_ref[...].astype(f32)[8:16, :]
    useen[8 : 8 + Q, :] = u_ref[...].astype(f32)
    facts = Facts(last_step - step_no, seg_ref, par_ref, xw)
    flags, carried, samelast = facts.before, facts.carried, facts.samelast
    for p in range(width // 128):
        lanes = slice(128 * p, 128 * p + 128)
        pre = conv_pre(useen, flags, wk_ref, bias_ref, lanes, facts.chans(p))
        sg = sigmoid(pre)
        act[:, lanes] = pre * sg
        slope[:, lanes] = sg * (1.0 + pre * (1.0 - sg))

    raw = dt_ref[...].astype(f32) + facts.bias
    step = softplus(raw)
    rate = facts.rate
    row = lax.broadcasted_iota(jnp.int32, (Q, Q), 0)
    col = lax.broadcasted_iota(jnp.int32, (Q, Q), 1)
    tri = jnp.where(row >= col, 1.0, 0.0).astype(bf16)
    upper = jnp.where(row <= col, 1.0, 0.0).astype(bf16)
    below = jnp.where(row > col, 1.0, 0.0).astype(bf16)
    decay = dot3(tri, step * rate)
    decay_t = decay.T
    madd = jnp.where((row <= col) & (facts.now == segr_ref[0]), 0.0, NEG)
    b_now, c_now = act[:, xw : xw + 128], act[:, xw + 128 : xw + 256]
    b_low, c_low = b_now.astype(bf16), c_now.astype(bf16)
    c_t = c_now.T.astype(bf16)
    gram = dot_nt(b_low, c_low)
    left = lax.broadcasted_iota(jnp.int32, (Q, 128), 1) < 64
    lane = lax.broadcasted_iota(jnp.int32, (Q, 128), 1)
    dgram = jnp.zeros((Q, Q), f32)
    cols_b = jnp.zeros((Q, 128), f32)
    for p in range(pairs):
        lanes = slice(128 * p, 128 * p + 128)
        d0, d1 = spread_col(decay, 2 * p), spread_col(decay, 2 * p + 1)
        dp = jnp.where(left, d0, d1)
        sp = jnp.where(left, spread_col(step, 2 * p), spread_col(step, 2 * p + 1))
        xs = act[:, lanes]
        xp = xs * sp
        dy_low = dy_ref[:, lanes]
        dy = dy_low.astype(f32)
        stacked = jnp.concatenate(
            [jnp.where(left, dy, 0.0).astype(bf16), jnp.where(left, 0.0, dy).astype(bf16)], axis=0
        )
        pair = dot_nt(xp.astype(bf16), stacked)
        mts = []
        for k, dk in ((0, d0), (1, d1)):
            h = 2 * p + k
            e = jnp.exp(decay_t[h : h + 1, :] - dk + madd)
            f = e * pair[:, 128 * k : 128 * k + 128]
            dgram = dgram + f
            w = gram * f
            mts.append((gram * e).astype(bf16))
            rows_a[h : h + 1, :] = jnp.sum(w, axis=0, keepdims=True)
            cols_b = jnp.where(lane == h, jnp.sum(w, axis=1, keepdims=True), cols_b)
        within = dot(jnp.concatenate(mts, axis=1), stacked)
        grow = jnp.exp(dp) * carried
        dy_in = dy * grow
        dy_in_low = dy_in.astype(bf16)
        keep_y[:, lanes] = dy_in_low
        st = save_ref[0, :, lanes]
        prod_a[:, lanes] = (dy_in * dot(c_low, st)).astype(bf16)
        last = dp[Q - 1 : Q, :]
        fade = jnp.exp(last - dp) * samelast
        ds = dstate[:, lanes]
        ds_low = ds.astype(bf16)
        xe = xp * fade
        keep_x[:, lanes] = xe.astype(bf16)
        later = dot(b_low, ds_low)
        prod_b[:, lanes] = (xe * later).astype(bf16)
        retain = jnp.exp(last) * carried[Q - 1 : Q, :]
        held[0:1, lanes] = jnp.sum(ds * st.astype(f32), axis=0, keepdims=True) * retain
        dxs = sp * (within + later * fade) + skip_ref[:, facts.chans(p)] * dy
        skp = xs * dy
        sgrad_ref[:, lanes] += jnp.sum(skp.reshape(Q // 8, 8, 128), axis=0)
        dpre[0:Q, lanes] = dxs * slope[:, lanes]
        dstate[:, lanes] = ds * retain + dot(c_t, dy_in_low)
        if p == 0:
            db_in, dc_in = dot_nt(keep_x[:, lanes], ds_low), dot_nt(dy_in_low, st)
        else:
            db_in, dc_in = db_in + dot_nt(keep_x[:, lanes], ds_low), dc_in + dot_nt(dy_in_low, st)

    dg_low = dgram.astype(bf16)
    db = dot(dg_low, c_low) + db_in
    dc = dot(dgram.T.astype(bf16), b_low) + dc_in
    dpre[0:Q, xw : xw + 128] = db * slope[:, xw : xw + 128]
    dpre[0:Q, xw + 128 : xw + 256] = dc * slope[:, xw + 128 : xw + 256]

    spot = spot_ref[...]
    a_in = dot(prod_a[...], spot)
    b_in = dot(prod_b[...], spot)
    hv = jnp.broadcast_to(held[0:1, :], (8, xw))
    h_hi = hv.astype(bf16)
    h_lo = (hv - h_hi.astype(f32)).astype(bf16)
    through = (dot(h_hi, spot) + dot(h_lo, spot))[0:1, :]
    a_own = rows_a[...].T
    cross = dot3(upper, a_own - cols_b + a_in) + dot3(below, b_in) + through
    total = cols_b + b_in
    sg = sigmoid(raw)
    ratio = jnp.where(step > 1e-30, sg / jnp.maximum(step, 1e-30), 1.0)
    draw = total * ratio + rate * cross * sg
    ddt_ref[...] = facts.back(draw).astype(bf16)
    hgrad_ref[0:8, :] += jnp.sum(draw.reshape(Q // 8, 8, 128), axis=0)
    hgrad_ref[8:16, :] += jnp.sum((step * cross).reshape(Q // 8, 8, 128), axis=0)

    ahead = [None] + [facts.after(j) for j in (1, 2, 3)]
    for p in range(width // 128):
        lanes = slice(128 * p, 128 * p + 128)
        own = dpre[0:Q, lanes]
        chans = facts.chans(p)
        du = wk_ref[3:4, chans] * own
        wgrad_ref[24:32, lanes] += jnp.sum((own * useen[8 : 8 + Q, lanes]).reshape(Q // 8, 8, 128), axis=0)
        wgrad_ref[32:40, lanes] += jnp.sum(own.reshape(Q // 8, 8, 128), axis=0)
        for j in (1, 2, 3):
            du = du + wk_ref[3 - j : 4 - j, chans] * (dpre[j : j + Q, lanes] * ahead[j])
            moved = own * (useen[8 - j : 8 - j + Q, lanes] * flags[j])
            k = 3 - j
            wgrad_ref[8 * k : 8 * k + 8, lanes] += jnp.sum(moved.reshape(Q // 8, 8, 128), axis=0)
        du_ref[:, lanes] = du.astype(bf16)
    first = dpre[0:8, :]
    dpre[Q : Q + 8, :] = first

    @pl.when(step_no == last_step)
    def _():
        small_ref[...] = jnp.zeros_like(small_ref)
        for k in range(5):
            small_ref[k : k + 1, :] = jnp.sum(wgrad_ref[8 * k : 8 * k + 8, :], axis=0, keepdims=True)
        small_ref[5:6, 0:128] = jnp.sum(hgrad_ref[0:8, :], axis=0, keepdims=True)
        small_ref[6:7, 0:128] = rate * jnp.sum(hgrad_ref[8:16, :], axis=0, keepdims=True)
        skips = sgrad_ref[...]
        hi = skips.astype(bf16)
        mid = (skips - hi.astype(f32)).astype(bf16)
        by_head = dot(hi, spot_ref[...]) + dot(mid, spot_ref[...])
        small_ref[7:8, 0:128] = jnp.sum(by_head, axis=0, keepdims=True)


def mixer_bwd(traffic, extra, u, dt, seg, segr, wk, bias, par, skip, save, dy):
    length, width = u.shape
    xw = width - 256
    n = length // Q
    whole = lambda shape: pl.BlockSpec(shape, lambda i: (0,) * len(shape))
    back = lambda i: (n - 1 - i, 0)
    return pl.pallas_call(
        functools.partial(bwd_kernel, traffic),
        grid=(n,),
        in_specs=[
            pl.BlockSpec((Q, width), back),
            pl.BlockSpec((16, width), lambda i: (jnp.maximum((n - 1 - i) * (Q // 16) - 1, 0), 0)),
            pl.BlockSpec((Q, 128), back),
            whole(seg.shape),
            pl.BlockSpec((1, 1, Q), lambda i: (n - 1 - i, 0, 0)),
            whole(wk.shape),
            whole(bias.shape),
            whole(par.shape),
            whole(skip.shape),
            pl.BlockSpec((1, 128, xw), lambda i: (n - 1 - i, 0, 0)),
            pl.BlockSpec((Q, xw), back),
        ]
        + [pl.BlockSpec(memory_space=pltpu.MemorySpace.HBM)] * len(extra),
        out_specs=[
            pl.BlockSpec((Q, width), back),
            pl.BlockSpec((Q, 128), back),
            whole((8, width)),
        ]
        + [pl.BlockSpec(memory_space=pltpu.MemorySpace.HBM)] * len(traffic.outputs),
        out_shape=[
            jax.ShapeDtypeStruct((length, width), bf16),
            jax.ShapeDtypeStruct((length, 128), bf16),
            jax.ShapeDtypeStruct((8, width), f32),
            *traffic.outputs,
        ],
        scratch_shapes=[
            pltpu.VMEM((128, xw), f32),
            pltpu.VMEM((Q + 8, width), f32),
            pltpu.VMEM((Q, width), f32),
            pltpu.VMEM((Q, width), f32),
            pltpu.VMEM((Q + 8, width), f32),
            pltpu.VMEM((Q, xw), bf16),
            pltpu.VMEM((Q, xw), bf16),
            pltpu.VMEM((Q, xw), bf16),
            pltpu.VMEM((Q, xw), bf16),
            pltpu.VMEM((128, 128), f32),
            pltpu.VMEM((8, xw), f32),
            pltpu.VMEM((40, width), f32),
            pltpu.VMEM((16, 128), f32),
            pltpu.VMEM((8, xw), f32),
            pltpu.VMEM((xw, 128), bf16),
            *traffic.scratch,
        ],
        compiler_params=pltpu.CompilerParams(
            vmem_limit_bytes=60 * 2**20,
            collective_id=traffic.collective_id,
            has_side_effects=traffic.collective_id is not None,
        ),
        name="mixer_backward",
    )(u, u, dt, seg, segr, wk, bias, par, skip, save, dy, *extra)


MESH = pl.DeviceIdType.MESH
ANY = pltpu.MemorySpace.HBM
PARTS = 4


def remote(src, dst, send_sem, recv_sem, device):
    return pltpu.make_async_remote_copy(
        src_ref=src, dst_ref=dst, send_sem=send_sem, recv_sem=recv_sem, device_id=device, device_id_type=MESH
    )


class Place:
    def __init__(self):
        self.w, self.s = lax.axis_index("wshard"), lax.axis_index("seq")
        self.z, self.x = self.w // 2, lax.rem(self.w, 2)
        self.y, self.c = self.s // 2, lax.rem(self.s, 2)
        self.s_sib = 2 * self.y + 1 - self.c
        self.s_far = 2 * (1 - self.y) + self.c
        self.s_diag = 2 * (1 - self.y) + 1 - self.c
        self.side = (2 * self.z + 1 - self.x, self.s)
        self.up = (lax.rem(self.w + 2, 8), self.s)
        self.down = (lax.rem(self.w + 6, 8), self.s)
        self.sib = (self.w, self.s_sib)
        self.far = (self.w, self.s_far)

    def greet(self, everyone=False, sequence=False):
        barrier = pltpu.get_barrier_semaphore()
        others = [(lax.rem(self.w + k, 8), self.s) for k in range(1, 8)] if everyone else []
        if everyone or sequence:
            others += [(self.w, lax.rem(self.s + k, 4)) for k in range(1, 4)]
        else:
            others = [self.side, self.up, self.down, self.sib, self.far]
        for other in others:
            pl.semaphore_signal(barrier, inc=1, device_id=other, device_id_type=MESH)
        pl.semaphore_wait(barrier, len(others))


def dma(*shape):
    return pltpu.SemaphoreType.DMA(shape)


def gather_pieces_start(at, own, slot, sems, stage=None):
    send, recv, local = sems[:3]
    rows = own.shape[0] // PARTS
    for k in range(PARTS):
        part = pl.ds(k * rows, rows)
        remote(own.at[part], slot(at.s).at[part], send.at[1, k], recv.at[1, k], at.far).start()
    for k in range(PARTS):
        part = pl.ds(k * rows, rows)
        remote(own.at[part], slot(at.s).at[part], send.at[0, k], recv.at[0, k], at.sib).start()
    if stage is not None:
        copy = pltpu.make_async_copy(own, stage, local)
        copy.start()
        copy.wait()
    pltpu.make_async_copy(own if stage is None else stage, slot(at.s), local).start()


def gather_pieces_pass(at, own, slot, sems):
    send, recv, _ = sems
    rows = own.shape[0] // PARTS
    for k in range(PARTS):
        part = pl.ds(k * rows, rows)
        theirs = slot(at.s_far).at[part]
        remote(theirs, theirs, send.at[1, k], recv.at[1, k], at.far).wait_recv()
        remote(theirs, theirs, send.at[2, k], recv.at[2, k], at.sib).start()


def gather_pieces_end(at, own, slot, sems):
    send, recv, local = sems
    rows = own.shape[0] // PARTS
    pltpu.make_async_copy(own, slot(at.s), local).wait()
    for k in range(PARTS):
        part = pl.ds(k * rows, rows)
        sib, diag, far = slot(at.s_sib).at[part], slot(at.s_diag).at[part], slot(at.s_far).at[part]
        remote(own.at[part], slot(at.s).at[part], send.at[0, k], recv.at[0, k], at.sib).wait_send()
        remote(own.at[part], slot(at.s).at[part], send.at[1, k], recv.at[1, k], at.far).wait_send()
        remote(far, far, send.at[2, k], recv.at[2, k], at.sib).wait_send()
        remote(sib, sib, send.at[0, k], recv.at[0, k], at.sib).wait_recv()
        remote(diag, diag, send.at[2, k], recv.at[2, k], at.sib).wait_recv()


CUTS = 6


def gather_shards(at, main, com, main_all, com_all, stage, sems, between):
    send, recv, csend, crecv, psend, precv, local, osend = sems
    half, cut = com.shape[0] // 2, main.shape[0] // CUTS
    mine = pl.ds(pl.multiple_of(at.c * half, half), half)
    load = pltpu.make_async_copy(main, stage[0], local.at[0])
    com_load = pltpu.make_async_copy(com, stage[1], local.at[1])
    keep = pltpu.make_async_copy(stage[0], main_all.at[at.w], local.at[0])
    com_keep = pltpu.make_async_copy(stage[1], com_all.at[at.w], local.at[1])

    def hop(zp, q, way, device, own=False):
        w, n, part = 2 * zp + at.x, zp * CUTS + q, pl.ds(q * cut, cut)
        slot, com_slot = main_all.at[w, part], com_all.at[w, mine]
        copies = [remote(main.at[part] if own else slot, slot, send.at[way, n], recv.at[w * CUTS + q], device)]
        if q == 1:
            copies.append(remote(com.at[mine] if own else com_slot, com_slot, csend.at[way, zp], crecv.at[w], device))
        return copies

    def cross(zp, way, device):
        w = 2 * zp + 1 - at.x
        slot = main_all.at[w, pl.ds(0, cut)]
        return [remote(slot, slot, osend.at[way, zp], recv.at[w * CUTS], device)]

    def begin(copies):
        for copy in copies:
            copy.start()

    def sent(copies):
        for copy in copies:
            copy.wait_send()

    def all_ways(act, q):
        act(hop(at.z, q, 0, at.side, True))

        @pl.when(at.z < 3)
        def _():
            act(hop(at.z, q, 1, at.up, True))

        @pl.when(at.z > 0)
        def _():
            act(hop(at.z, q, 2, at.down, True))

    def arrived(w, q):
        slot = main_all.at[w, pl.ds(q * cut, cut)]
        remote(slot, slot, send.at[0, 0], recv.at[w * CUTS + q], at.side).wait_recv()
        if q == 1:
            held = com_all.at[w, mine]
            remote(held, held, csend.at[0, 0], crecv.at[w], at.side).wait_recv()
            remote(held, held, psend.at[w], precv.at[w], at.sib).start()

    for q in range(CUTS):
        if q > 1:
            all_ways(sent, q - 2)
        all_ways(begin, q)
        if q == 0:
            load.start()
            com_load.start()
            load.wait()
            com_load.wait()
            keep.start()
            com_keep.start()
    arrived(2 * at.z + 1 - at.x, 0)

    @pl.when(at.z < 3)
    def _():
        begin(cross(at.z, 0, at.up))

    @pl.when(at.z > 0)
    def _():
        begin(cross(at.z, 1, at.down))

    for d in (1, 2, 3):
        if d == 3:
            between()
        for q in range(CUTS):

            @pl.when(at.z - d >= 0)
            def _():
                zp = at.z - d
                arrived(2 * zp + at.x, q)

                @pl.when(at.z < 3)
                def _():
                    begin(hop(zp, q, 1, at.up))

                if q > 0:
                    begin(hop(zp, q, 0, at.side))

            @pl.when(at.z + d <= 3)
            def _():
                zp = at.z + d
                arrived(2 * zp + at.x, q)

                @pl.when(at.z > 0)
                def _():
                    begin(hop(zp, q, 2, at.down))

                if q > 0:
                    begin(hop(zp, q, 0, at.side))

        @pl.when(at.z - d >= 0)
        def _():
            arrived(2 * (at.z - d) + 1 - at.x, 0)

            @pl.when(at.z < 3)
            def _():
                begin(cross(at.z - d, 0, at.up))

        @pl.when(at.z + d <= 3)
        def _():
            arrived(2 * (at.z + d) + 1 - at.x, 0)

            @pl.when(at.z > 0)
            def _():
                begin(cross(at.z + d, 1, at.down))

    for zp in range(4):
        for q in range(1, CUTS):
            arrived(2 * zp + 1 - at.x, q)
    keep.wait()
    com_keep.wait()
    all_ways(sent, CUTS - 2)
    all_ways(sent, CUTS - 1)
    for zp in range(4):

        @pl.when((at.z < 3) & (zp <= at.z))
        def _():
            sent(cross(zp, 0, at.up))

        @pl.when((at.z > 0) & (zp >= at.z))
        def _():
            sent(cross(zp, 1, at.down))

        for q in range(CUTS):
            if q > 0:

                @pl.when(at.z != zp)
                def _():
                    sent(hop(zp, q, 0, at.side))

            @pl.when((at.z < 3) & (zp < at.z))
            def _():
                sent(hop(zp, q, 1, at.up))

            @pl.when((at.z > 0) & (zp > at.z))
            def _():
                sent(hop(zp, q, 2, at.down))

    other = pl.ds(pl.multiple_of((1 - at.c) * half, half), half)
    for k in range(1, 8):
        w = lax.rem(at.w + k, 8)
        gone, got = com_all.at[w, mine], com_all.at[w, other]
        remote(gone, gone, psend.at[w], precv.at[w], at.sib).wait_send()
        remote(got, got, psend.at[w], precv.at[w], at.sib).wait_recv()


def gather_kernel(hid, main, com, hid_all, main_all, com_all, hid_v, main_v, com_v, *sems):
    at = Place()
    at.greet()
    slot = lambda s: hid_all.at[s]
    gather_pieces_start(at, hid, slot, sems[0:3], hid_v)
    pass_on = lambda: gather_pieces_pass(at, hid, slot, sems[0:3])
    gather_shards(at, main, com, main_all, com_all, (main_v, com_v), sems[3:11], pass_on)
    gather_pieces_end(at, hid, slot, sems[0:3])


def gather_first(hid, main, com):
    shape = lambda n, v: jax.ShapeDtypeStruct((n,) + v.shape, v.dtype)
    return pl.pallas_call(
        gather_kernel,
        in_specs=[pl.BlockSpec(memory_space=ANY)] * 3,
        out_specs=[pl.BlockSpec(memory_space=ANY)] * 3,
        out_shape=[shape(4, hid), shape(8, main), shape(8, com)],
        scratch_shapes=[pltpu.VMEM(v.shape, v.dtype) for v in (hid, main, com)]
        + [dma(3, PARTS), dma(3, PARTS), dma()]
        + [dma(3, 4 * CUTS), dma(8 * CUTS), dma(3, 4), dma(8), dma(8), dma(8), dma(2), dma(2, 4)],
        compiler_params=pltpu.CompilerParams(collective_id=1, has_side_effects=True),
        name="gather_first",
    )(hid, main, com)


SLICES = 8


def each_slice(body):
    def run(k, _):
        body(k)
        return 0

    lax.fori_loop(0, SLICES, run, 0)


def forward_traffic(cot, rows):
    class Traffic:
        inputs = (cot, rows)
        outputs = (
            jax.ShapeDtypeStruct((4,) + cot.shape, cot.dtype),
            jax.ShapeDtypeStruct((2,) + rows.shape, rows.dtype),
        )
        scratch = (
            pltpu.VMEM(cot.shape, cot.dtype),
            pltpu.VMEM(rows.shape, rows.dtype),
            dma(3, SLICES),
            dma(3, SLICES),
            dma(),
            dma(3, SLICES),
            dma(2, SLICES),
            dma(),
        )
        collective_id = 2

        def __init__(self, own, row_own, full, row_full, stage, rstage, send, recv, local, rsend, rrecv, rlocal):
            self.at = at = Place()
            self.own, self.full, self.row_own, self.row_full = own, full, row_own, row_full
            self.rrecv = rrecv
            cut, rcut = own.shape[0] // SLICES, row_own.shape[0] // SLICES
            part = lambda k: pl.ds(pl.multiple_of(k * cut, cut), cut)
            rpart = lambda k: pl.ds(pl.multiple_of(k * rcut, rcut), rcut)
            piece = lambda s, k: full.at[s, part(k)]
            self.load = pltpu.make_async_copy(own, stage, local)
            self.keep = pltpu.make_async_copy(stage, full.at[at.s], local)
            self.rload = pltpu.make_async_copy(row_own, rstage, rlocal)
            self.rkeep = pltpu.make_async_copy(rstage, row_full.at[at.x], rlocal)
            self.to_sib = lambda k: remote(own.at[part(k)], piece(at.s, k), send.at[0, k], recv.at[0, k], at.sib)
            self.to_far = lambda k: remote(own.at[part(k)], piece(at.s, k), send.at[1, k], recv.at[1, k], at.far)
            self.pass_on = lambda k: remote(piece(at.s_far, k), piece(at.s_far, k), send.at[2, k], recv.at[2, k], at.sib)
            here = lambda k, n, device: remote(
                row_full.at[at.x, rpart(k)], row_full.at[at.x, rpart(k)], rsend.at[n, k], rrecv.at[at.x, k], device
            )
            self.rows = (lambda k: here(k, 0, at.side), lambda k: here(k, 1, at.up), lambda k: here(k, 2, at.down))
            got = lambda s, n, k: remote(piece(s, k), piece(s, k), send.at[n, k], recv.at[n, k], at.sib)
            self.from_sib = lambda k: got(at.s_sib, 0, k)
            self.from_far = lambda k: got(at.s_far, 1, k)
            self.from_diag = lambda k: got(at.s_diag, 2, k)
            other = lambda k: row_full.at[1 - at.x, rpart(k)]
            self.from_side = lambda k: remote(other(k), other(k), rsend.at[0, k], rrecv.at[1 - at.x, k], at.side)

        def step(self, i, last):
            at = self.at
            upward, downward = (at.z >= at.s) & (at.z < 3), (at.z <= at.s) & (at.z > 0)
            side, up, down = self.rows

            @pl.when(i == 0)
            def _():
                at.greet()
                self.load.start()
                each_slice(lambda k: self.to_sib(k).start())

                @pl.when(at.z == at.s)
                def _():
                    self.rload.start()
                    self.rload.wait()
                    self.rkeep.start()
                    self.rkeep.wait()

                self.load.wait()
                self.keep.start()

            k = i - 1

            @pl.when((k >= 0) & (k < SLICES))
            def _():
                self.to_far(k).start()

            @pl.when((k >= SLICES) & (k < 2 * SLICES))
            def _():
                self.from_far(k - SLICES).wait_recv()
                self.pass_on(k - SLICES).start()

            far_away = jnp.where(at.z > at.s, at.z - at.s, at.s - at.z)
            v = 3 * i - 6 * far_away + 1
            r = jnp.where(v >= 0, lax.div(v, 4), -1)

            @pl.when((r >= 0) & (r < SLICES) & (4 * r < v))
            def _():
                @pl.when(at.z != at.s)
                def _():
                    side(r).wait_recv()

                side(r).start()

                @pl.when(upward)
                def _():
                    up(r).start()

                @pl.when(downward)
                def _():
                    down(r).start()

            @pl.when(i == last)
            def _():
                self.keep.wait()

                def finish(k):
                    self.to_sib(k).wait_send()
                    self.to_far(k).wait_send()
                    self.pass_on(k).wait_send()
                    self.from_sib(k).wait_recv()
                    self.from_diag(k).wait_recv()
                    side(k).wait_send()
                    self.from_side(k).wait_recv()

                    @pl.when(upward)
                    def _():
                        up(k).wait_send()

                    @pl.when(downward)
                    def _():
                        down(k).wait_send()

                each_slice(finish)

    return Traffic


def add_into(dst, src, rows):
    step = next(n for n in (64, 48, 32, 16) if rows % n == 0)

    def body(i, _):
        part = pl.ds(pl.multiple_of(i * step, 16), step)
        dst[part, :] = (dst[part, :].astype(f32) + src[part, :].astype(f32)).astype(bf16)
        return 0

    lax.fori_loop(0, rows // step, body, 0)


def far_first(at, i):
    inner = (at.z == 1) | (at.z == 2)
    i = jnp.where(inner & (i >= 2), 5 - i, i)
    return jnp.where(at.z < 2, 3 - i, i)


class ReduceShards:
    def __init__(self, at, partial, cuts, acc, from_side, from_down, from_up, sems):
        self.at, self.partial, self.cuts, self.acc = at, partial, cuts, acc
        self.from_side, self.from_down, self.from_up = from_side, from_down, from_up
        self.send, self.recv_side, self.recv_down, self.recv_up = sems
        self.rows = acc.shape[1] // cuts

    def unit(self, j):
        if isinstance(j, int):
            shard, cut = j // self.cuts, j % self.cuts
        else:
            shard, cut = lax.div(j, self.cuts), lax.rem(j, self.cuts)
        zp = far_first(self.at, shard)
        return zp, zp * self.cuts + cut, pl.ds(pl.multiple_of(cut * self.rows, self.rows), self.rows)

    def side_copy(self, j):
        at = self.at
        zp, n, part = self.unit(j)
        return remote(
            self.partial(zp).at[part], self.from_side.at[zp, part],
            self.send.at[0, n], self.recv_side.at[n], at.side,
        )

    def up_copy(self, j):
        zp, n, part = self.unit(j)
        return remote(
            self.acc.at[zp, part], self.from_down.at[zp, part], self.send.at[1, n], self.recv_down.at[n], self.at.up
        )

    def down_copy(self, j):
        zp, n, part = self.unit(j)
        return remote(
            self.acc.at[zp, part], self.from_up.at[zp, part], self.send.at[2, n], self.recv_up.at[n], self.at.down
        )

    def start(self):
        self.side_copy(0).start()
        self.side_copy(1).start()

    def step(self, j):
        at = self.at
        zp, _, part = self.unit(j)
        self.side_copy(j).wait()
        acc = self.acc.at[zp, part]
        add_into(acc, self.from_side.at[zp, part], self.rows)

        @pl.when((at.z > 0) & (zp >= at.z))
        def _():
            self.up_copy(j).wait_recv()
            add_into(acc, self.from_down.at[zp, part], self.rows)

        @pl.when((at.z < 3) & (zp <= at.z))
        def _():
            self.down_copy(j).wait_recv()
            add_into(acc, self.from_up.at[zp, part], self.rows)

        @pl.when(zp > at.z)
        def _():
            self.up_copy(j).start()

        @pl.when(zp < at.z)
        def _():
            self.down_copy(j).start()

    def end(self):
        at = self.at
        for j in range(4 * self.cuts):
            zp = self.unit(j)[0]

            @pl.when(zp > at.z)
            def _():
                self.up_copy(j).wait_send()

            @pl.when(zp < at.z)
            def _():
                self.down_copy(j).wait_send()


def backward_traffic(layer, rows, gate):
    piece, cols = layer.shape[1:]
    rrows = rows.shape[1]
    grows, gcols = gate.shape[1:]

    class Traffic:
        inputs = (layer, rows, gate)
        outputs = (
            jax.ShapeDtypeStruct((piece, cols), f32),
            jax.ShapeDtypeStruct((rrows, cols), bf16),
            jax.ShapeDtypeStruct((grows, gcols), bf16),
        )
        scratch = (
            *[pltpu.VMEM((piece, cols), bf16)] * 5,
            pltpu.VMEM((piece, cols), f32),
            *[pltpu.VMEM((rrows, cols), bf16)] * 4,
            dma(3, SLICES),
            dma(3, SLICES),
            dma(3),
            dma(3, SLICES),
            dma(3, SLICES),
            dma(2),
            dma(2, SLICES),
            dma(2, SLICES),
            *[pltpu.VMEM((4, grows, gcols), bf16)] * 4,
            dma(3, 8),
            dma(8),
            dma(8),
            dma(8),
            dma(5),
        )
        collective_id = 3

        def __init__(
            self, layer, rows, gate, out, rows_out, gate_out,
            own_v, far_v, sib_v, pass_v, got_v, sum_v, acc, side_v, low_v, high_v,
            send, recv, local, rsend, rrecv, rlocal, fsend, frecv,
            gacc, gside, glow, ghigh, gsend, grecv_side, grecv_low, grecv_high, glocal,
        ):
            self.at = at = Place()
            cut, rcut = piece // SLICES, rrows // SLICES
            part = lambda k: pl.ds(pl.multiple_of(k * cut, cut), cut)
            rpart = lambda k: pl.ds(pl.multiple_of(k * rcut, rcut), rcut)
            self.own, self.sib, self.passed, self.got, self.sum = own_v, sib_v, pass_v, got_v, sum_v
            self.part, self.rpart, self.cut, self.rcut = part, rpart, cut, rcut
            self.far_v, self.acc, self.side_v, self.low_v, self.high_v = far_v, acc, side_v, low_v, high_v
            self.load_far = pltpu.make_async_copy(layer.at[at.s_far], far_v, local.at[0])
            self.load_own = pltpu.make_async_copy(layer.at[at.s], own_v, local.at[1])
            self.store = pltpu.make_async_copy(sum_v, out, local.at[2])
            self.to_pass = lambda k: remote(
                layer.at[at.s_diag, part(k)], pass_v.at[part(k)], send.at[0, k], recv.at[0, k], at.sib
            )
            self.to_sib = lambda k: remote(
                layer.at[at.s_sib, part(k)], sib_v.at[part(k)], send.at[1, k], recv.at[1, k], at.sib
            )
            self.to_far = lambda k: remote(
                far_v.at[part(k)], got_v.at[part(k)], send.at[2, k], recv.at[2, k], at.far
            )
            self.load_acc = pltpu.make_async_copy(rows.at[at.x], acc, rlocal.at[0])
            self.store_acc = pltpu.make_async_copy(acc, rows_out, rlocal.at[1])
            spread = lambda k, n, device: remote(
                acc.at[rpart(k)], rows_out.at[rpart(k)], fsend.at[n, k], frecv.at[n, k], device
            )
            self.spread_far = lambda k: spread(k, 0, at.far)
            self.spread_sib = lambda k: spread(k, 1, at.sib)
            self.spread_on = lambda k: remote(
                rows_out.at[rpart(k)], rows_out.at[rpart(k)], fsend.at[1, k], frecv.at[1, k], at.sib
            )
            self.gates = ReduceShards(
                at, lambda zp: gate.at[2 * zp + 1 - at.x], 2, gacc, gside, glow, ghigh,
                (gsend, grecv_side, grecv_low, grecv_high),
            )
            self.load_gate = [
                pltpu.make_async_copy(gate.at[2 * zp + at.x], gacc.at[zp], glocal.at[zp]) for zp in range(4)
            ]
            self.store_gate = pltpu.make_async_copy(gacc.at[at.z], gate_out, glocal.at[4])
            self.to_side = lambda k: remote(
                rows.at[1 - at.x, rpart(k)], side_v.at[rpart(k)], rsend.at[0, k], rrecv.at[0, k], at.side
            )
            self.to_up = lambda k: remote(
                acc.at[rpart(k)], low_v.at[rpart(k)], rsend.at[1, k], rrecv.at[1, k], at.up
            )
            self.to_down = lambda k: remote(
                acc.at[rpart(k)], high_v.at[rpart(k)], rsend.at[2, k], rrecv.at[2, k], at.down
            )

        def step(self, i, last):
            at = self.at

            @pl.when(i == 0)
            def _():
                at.greet()
                self.load_far.start()
                self.load_own.start()
                self.load_acc.start()
                for copy in self.load_gate:
                    copy.start()
                each_slice(lambda k: self.to_pass(k).start())
                each_slice(lambda k: self.to_sib(k).start())

            @pl.when(i < SLICES)
            def _():
                self.to_side(i).start()

            @pl.when(i == 1)
            def _():
                self.load_far.wait()
                self.load_own.wait()
                self.load_acc.wait()
                for copy in self.load_gate:
                    copy.wait()

            k = i - 1

            @pl.when((k >= 0) & (k < SLICES))
            def _():
                self.to_pass(k).wait_recv()
                add_into(self.far_v.at[self.part(k)], self.passed.at[self.part(k)], self.cut)
                self.to_far(k).start()

            m = i - SLICES

            @pl.when((m >= 0) & (m < SLICES))
            def _():
                self.to_sib(m).wait_recv()
                self.to_far(m).wait_recv()
                p = self.part(m)
                self.sum[p, :] = (
                    self.own[p, :].astype(f32) + self.sib[p, :].astype(f32) + self.got[p, :].astype(f32)
                )

            ends = jnp.where(at.z > 3 - at.z, at.z, 3 - at.z)
            chain = jnp.where(at.z < at.s, at.z, jnp.where(at.z > at.s, 3 - at.z, ends))
            v = 10 * i - 17 * chain - 26 + 10
            r = jnp.where(v >= 0, lax.div(v, 11), -1)

            @pl.when((r >= 0) & (r < SLICES) & (11 * r < v))
            def _():
                acc = self.acc.at[self.rpart(r)]
                self.to_side(r).wait_recv()
                add_into(acc, self.side_v.at[self.rpart(r)], self.rcut)

                @pl.when((at.z <= at.s) & (at.z > 0))
                def _():
                    self.to_up(r).wait_recv()
                    add_into(acc, self.low_v.at[self.rpart(r)], self.rcut)

                @pl.when((at.z >= at.s) & (at.z < 3))
                def _():
                    self.to_down(r).wait_recv()
                    add_into(acc, self.high_v.at[self.rpart(r)], self.rcut)

                @pl.when(at.z < at.s)
                def _():
                    self.to_up(r).start()

                @pl.when(at.z > at.s)
                def _():
                    self.to_down(r).start()

                @pl.when(at.z == at.s)
                def _():
                    self.spread_far(r).start()
                    self.spread_sib(r).start()

            g = i - (last - 7)

            @pl.when(g >= 0)
            def _():
                self.gates.side_copy(g).start()

            inner = jnp.where((at.z == 1) | (at.z == 2), 1, 0)
            g = i - 11 - inner

            @pl.when(g >= 0)
            def _():
                self.gates.step(g)

            @pl.when(i == last)
            def _():
                def rest(k, _):
                    self.gates.step(k)
                    return 0

                lax.fori_loop(last - 10 - inner, 8, rest, 0)

                self.store.start()
                self.store_gate.start()

                @pl.when(at.s == at.z)
                def _():
                    self.store_acc.start()

                def forward(k):
                    @pl.when(at.s_far == at.z)
                    def _():
                        self.spread_far(k).wait_recv()
                        self.spread_on(k).start()

                each_slice(forward)

                def finish(k):
                    @pl.when(at.s == at.z)
                    def _():
                        self.spread_far(k).wait_send()
                        self.spread_sib(k).wait_send()

                    @pl.when(at.s_far == at.z)
                    def _():
                        self.spread_on(k).wait_send()

                    @pl.when((at.s_sib == at.z) | (at.s_diag == at.z))
                    def _():
                        self.spread_on(k).wait_recv()

                    self.to_pass(k).wait_send()
                    self.to_sib(k).wait_send()
                    self.to_far(k).wait_send()
                    self.to_side(k).wait_send()

                    @pl.when(at.z < at.s)
                    def _():
                        self.to_up(k).wait_send()

                    @pl.when(at.z > at.s)
                    def _():
                        self.to_down(k).wait_send()

                each_slice(finish)
                self.gates.end()
                self.store.wait()
                self.store_gate.wait()

                @pl.when(at.s == at.z)
                def _():
                    self.store_acc.wait()

    return Traffic


def mid_kernel(gate, mixed, cot, w_out, normed,
               d_mixed, d_gate, gate_part, out_part, layer_part,
               gate_v, mixed_v, cot_v, normed_v, w_v, a_v, low_v, dg_v, l_v, out_v, stats, got, *sems):
    at = Place()
    load, xsend, xrecv, store = sems
    length, wide = mixed_v.shape
    depth = cot_v.shape[1]
    piece = length // 4
    strips = wide // 128
    tiles = piece // 256
    part = lambda t: pl.ds(pl.multiple_of(t * 256, 256), 256)

    def loads(k):
        r = pl.ds(pl.multiple_of(k * piece, piece), piece)
        pairs = ((cot, cot_v), (gate, gate_v), (mixed, mixed_v))
        return [pltpu.make_async_copy(p.at[r], v.at[r], load.at[3 * k + n]) for n, (p, v) in enumerate(pairs)]

    w_load = pltpu.make_async_copy(w_out, w_v, load.at[12])
    normed_load = pltpu.make_async_copy(normed, normed_v, load.at[13])
    w_load.start()
    for k in range(4):
        for copy in loads(k):
            copy.start()
    normed_load.start()
    at.greet(sequence=True)

    stats[...] = jnp.zeros_like(stats)
    w_load.wait()

    def first(i, _):
        @pl.when(lax.rem(i, tiles) == 0)
        def _():
            for copy in loads(lax.div(i, tiles)):
                copy.wait()

        tile = part(i)
        a_v[tile, :] = dot_nt(cot_v[tile, :], w_v[...])
        sum_g, sum_a = jnp.zeros((256, 128), f32), jnp.zeros((256, 128), f32)
        for n in range(strips):
            col = slice(128 * n, 128 * n + 128)
            gt = gate_v[tile, col]
            g = mixed_v[tile, col].astype(f32) * (gt * sigmoid(gt))
            sum_g = sum_g + g * g
            sum_a = sum_a + a_v[tile, col] * g
        stats[0:1, tile] = jnp.sum(sum_g.T, axis=0, keepdims=True)
        stats[1:2, tile] = jnp.sum(sum_a.T, axis=0, keepdims=True)
        return 0

    lax.fori_loop(0, 4 * tiles, first, 0)

    peers = (at.s_sib, at.s_far, at.s_diag)
    swap = [remote(stats, got.at[k], xsend.at[k], xrecv.at[k], (at.w, s)) for k, s in enumerate(peers)]
    for copy in swap:
        copy.start()
    for copy in swap:
        copy.wait()
    total = stats[...] + got[0] + got[1] + got[2]
    r_row = lax.rsqrt(total[0:1] / E + eps)
    stats[0:1, :] = r_row
    stats[1:2, :] = r_row * r_row * r_row * (total[1:2] / E)

    def column(k, at_row):
        return jnp.broadcast_to(stats[k : k + 1, pl.ds(pl.multiple_of(at_row, 128), 256)], (128, 256)).T

    def second(i, _):
        tile = pl.ds(pl.multiple_of(i * 256, 256), 256)
        r, pull = column(0, i * 256), column(1, i * 256)
        for n in range(strips):
            col = slice(128 * n, 128 * n + 128)
            gt, mx = gate_v[tile, col], mixed_v[tile, col].astype(f32)
            sg = sigmoid(gt)
            silu = gt * sg
            g = mx * silu
            low_v[tile, col] = (g * r).astype(bf16)
            d_g = r * a_v[tile, col] - g * pull
            mixed_v[tile, col] = (d_g * silu).astype(bf16)
            dg_v[tile, col] = (d_g * mx * (sg * (1.0 + gt * (1.0 - sg)))).astype(bf16)
        l_v[tile, :] = dot(low_v[tile, :], w_v[...]).astype(bf16)
        layer_copy(i).start()
        return 0

    layer_copy = lambda i: pltpu.make_async_copy(l_v.at[part(i)], layer_part.at[part(i)], store.at[9 + i])
    lax.fori_loop(0, length // 256, second, 0)
    keep = [pltpu.make_async_copy(mixed_v, d_mixed, store.at[0]), pltpu.make_async_copy(dg_v, d_gate, store.at[1])]
    for copy in keep:
        copy.start()
    normed_load.wait()
    tn = lambda p, q: lax.dot_general(p, q, (((0,), (0,)), ((), ())), preferred_element_type=f32)

    def out_block(n):
        room = out_v.at[part(n)]
        return room, pltpu.make_async_copy(room, out_part.at[part(n)], store.at[2 + n])

    def out_grad(n, _):
        room, copy = out_block(n)
        room[...] = tn(low_v[:, part(n)], cot_v[...]).astype(bf16)
        copy.start()
        return 0

    lax.fori_loop(0, wide // 256, out_grad, 0)
    shard = depth // 4
    block = lambda n: pl.ds(pl.multiple_of(n * shard, shard), shard)
    gate_block = lambda n: pltpu.make_async_copy(low_v.at[block(n)], gate_part.at[block(n)], store.at[5 + n])

    def gate_grad(n, _):
        low_v[block(n), :] = tn(normed_v[:, block(n)], dg_v[...]).astype(bf16)
        gate_block(n).start()
        return 0

    lax.fori_loop(0, 4, gate_grad, 0)

    for copy in keep:
        copy.wait()
    for n in range(wide // 256):
        out_block(n)[1].wait()
    for n in range(4):
        gate_block(n).wait()
    for i in range(length // 256):
        layer_copy(i).wait()


def middle(gate, mixed, cot, w_out, normed):
    length, wide = mixed.shape
    depth = cot.shape[1]
    piece = length // 4
    vm = pltpu.VMEM
    low = lambda *shape: jax.ShapeDtypeStruct(shape, bf16)
    return pl.pallas_call(
        mid_kernel,
        in_specs=[pl.BlockSpec(memory_space=ANY)] * 5,
        out_specs=[pl.BlockSpec(memory_space=ANY)] * 5,
        out_shape=[
            low(length, wide),
            low(length, wide),
            low(depth, wide),
            low(wide, depth),
            low(length, depth),
        ],
        scratch_shapes=[
            vm((length, wide), f32),
            vm((length, wide), bf16),
            vm((length, depth), bf16),
            vm((length, depth), bf16),
            vm((wide, depth), bf16),
            vm((length, wide), f32),
            vm((length, wide), bf16),
            vm((length, wide), bf16),
            vm((length, depth), bf16),
            vm((wide, depth), bf16),
        ]
        + [vm((8, length), f32), vm((3, 8, length), f32)]
        + [dma(14), dma(3), dma(3), dma(17)],
        compiler_params=pltpu.CompilerParams(
            collective_id=5, has_side_effects=True, vmem_limit_bytes=61 * 2**20
        ),
        name="middle",
    )(gate, mixed, cot, w_out, normed)


def small_start(at, small, got, sems):
    send, recv = sems
    for k in range(1, 8):
        peer = (lax.rem(at.w + k, 8), at.s)
        remote(small, got.at[k], send.at[k], recv.at[k], peer).start()


def small_pass(at, small, got, total, full, sems, more):
    send, recv = sems
    send2, recv2, local = more
    value = small[...]
    for k in range(1, 8):
        remote(small, got.at[k], send.at[k], recv.at[k], at.side).wait_recv()
        value = value + got[k]
    total[...] = value
    pltpu.make_async_copy(total, full.at[at.s], local).start()
    for k, s in enumerate((at.s_sib, at.s_far, at.s_diag)):
        remote(total, full.at[at.s], send2.at[k], recv2.at[k], (at.w, s)).start()


def small_end(at, small, got, total, full, sems, more):
    send, recv = sems
    send2, recv2, local = more
    pltpu.make_async_copy(total, full.at[at.s], local).wait()
    for k in range(1, 8):
        remote(small, got.at[k], send.at[k], recv.at[k], at.side).wait_send()
    for k, s in enumerate((at.s_sib, at.s_far, at.s_diag)):
        remote(total, full.at[at.s], send2.at[k], recv2.at[k], (at.w, s)).wait_send()
        remote(total, full.at[s], send2.at[k], recv2.at[k], (at.w, s)).wait_recv()


def last_kernel(hid, d_gate, d_u, d_dt, w_main, w_com, gate_sum, own, cot, small, gain_ref,
                hidden_grad, in_sum, sums_out,
                hid_v, dp_v, w_v,
                b_diag, b_sib, b_far, b_own, from_sib, pass_sib, from_far,
                part_v, mside, mlow, mhigh, macc, mown, csib, cown, cacc, cside, clow, chigh, cfar, csum,
                sgot, stotal, sfull, gate_v, own_v, cot_v, *sems):
    at = Place()
    sems = list(sems)
    take = lambda n: [sems.pop(0) for _ in range(n)]
    load, bsem, msem, csem, cx, ssem, smore, asem, gsem = (
        take(6), take(2), take(4), take(4), take(7), take(2), take(3), take(3), take(3)
    )
    piece = hid_v.shape[0] // 4
    shard = hid_v.shape[1] // 8
    wide = d_gate.shape[1]
    half = shard // 2
    mine = pl.ds(pl.multiple_of(at.c * half, half), half)
    other = pl.ds(pl.multiple_of((1 - at.c) * half, half), half)
    at.greet(everyone=True)

    order = (at.s_diag, at.s_far, at.s_sib, at.s)
    rows_of = lambda s: pl.ds(pl.multiple_of(s * piece, piece), piece)
    weights = [
        pltpu.make_async_copy(w_main, w_v.at[:, pl.ds(0, 2 * wide)], load[0].at[0]),
        pltpu.make_async_copy(w_com, w_v.at[:, pl.ds(2 * wide, 384)], load[0].at[1]),
    ]
    loads = []
    for k, s in enumerate(order):
        r = rows_of(s)
        loads.append(
            [
                pltpu.make_async_copy(d_gate.at[r], dp_v.at[r, pl.ds(0, wide)], load[1].at[k]),
                pltpu.make_async_copy(d_u.at[r], dp_v.at[r, pl.ds(wide, wide + 256)], load[2].at[k]),
                pltpu.make_async_copy(d_dt.at[r], dp_v.at[r, pl.ds(2 * wide + 256, 128)], load[3].at[k]),
            ]
        )
    hid_load = pltpu.make_async_copy(hid, hid_v, load[4])
    soon, later = weights + loads[0] + loads[1], [hid_load] + loads[2] + loads[3]
    ends_loads = [
        pltpu.make_async_copy(own, own_v, load[5].at[0]),
        pltpu.make_async_copy(cot, cot_v, load[5].at[1]),
    ]
    for copy in soon + later + ends_loads:
        copy.start()
    gate_slot = lambda s: in_sum.at[:, pl.ds(pl.multiple_of(s * wide, 128), wide)]
    x_slot = lambda s: in_sum.at[:, pl.ds(pl.multiple_of(E + s * wide, 128), wide)]
    gather_pieces_start(at, gate_sum, gate_slot, gsem, gate_v)
    small_start(at, small, sgot, ssem)

    send, recv = bsem
    rows = piece // PARTS
    parts = [pl.ds(k * rows, rows) for k in range(PARTS)]
    to_pass = [remote(b_diag.at[p], pass_sib.at[p], send.at[0, k], recv.at[0, k], at.sib) for k, p in enumerate(parts)]
    to_sib = [remote(b_sib.at[p], from_sib.at[p], send.at[1, k], recv.at[1, k], at.sib) for k, p in enumerate(parts)]
    to_far = [remote(b_far.at[p], from_far.at[p], send.at[2, k], recv.at[2, k], at.far) for k, p in enumerate(parts)]

    def back_tile(s, out, t):
        tile = pl.ds(pl.multiple_of(s * piece + t * 256, 256), 256)
        place = pl.ds(t * 256, 256)

        for n in range(hid_v.shape[1] // 256):
            col = slice(256 * n, 256 * n + 256)
            out[place, col] = dot_nt(dp_v[tile, :], w_v[col, :]).astype(bf16)

    big = ReduceShards(at, lambda zp: part_v.at[zp, 1 - at.x, :, pl.ds(0, wide)], 2, macc, mside, mlow, mhigh, msem)
    few = ReduceShards(at, lambda zp: cown.at[zp, 1 - at.x], 1, cacc, cside, clow, chigh, csem)
    com_cols = pl.ds(wide, 384)
    com_to_sib = lambda zp: remote(
        part_v.at[zp, :, other, com_cols], csib.at[zp], cx[0].at[zp], cx[1].at[zp], at.sib
    )

    def shard_pair(i):
        zp = far_first(at, i)
        lanes = pl.ds(pl.multiple_of(zp * 2 * shard, 128), 2 * shard)
        got = lax.dot_general(
            hid_v[:, lanes], dp_v[:, wide : 2 * wide + 384], (((0,), (0,)), ((), ())), preferred_element_type=f32
        ).astype(bf16)
        part_v[zp, 0] = got[0:shard]
        part_v[zp, 1] = got[shard : 2 * shard]
        macc[zp] = part_v[zp, at.x, :, 0:wide]
        big.side_copy(2 * i).start()
        com_to_sib(zp).start()

    def com_pair(i):
        zp = far_first(at, i)
        com_to_sib(zp).wait_recv()
        for x in range(2):
            cown[zp, x] = part_v[zp, x, mine, com_cols]
            add_into(cown.at[zp, x], csib.at[zp, x], half)
        cacc[zp] = cown[zp, at.x]
        few.side_copy(i).start()

    ends = (at.z == 0) | (at.z == 3)

    def step(j, who):
        @pl.when(who)
        def _():
            big.step(j)
            if j % 2:
                few.step(j // 2)

    tiles = piece // 256
    per = PARTS // tiles
    def far_tile(t):
        back_tile(at.s_far, b_far, t)
        for k in range(t * per, t * per + per):
            to_pass[k].wait_recv()
            add_into(b_far.at[parts[k]], pass_sib.at[parts[k]], rows)
            to_far[k].start()

    for copy in soon:
        copy.wait()
    for t in range(tiles):
        back_tile(at.s_diag, b_diag, t)
        for k in range(t * per, t * per + per):
            to_pass[k].start()
    far_tile(0)
    for copy in later:
        copy.wait()
    def sib_tile(t):
        back_tile(at.s_sib, b_sib, t)
        for k in range(t * per, t * per + per):
            to_sib[k].start()

    shard_pair(0)
    far_tile(1)
    big.side_copy(1).start()
    shard_pair(1)
    com_pair(0)
    shard_pair(2)
    big.side_copy(3).start()
    com_pair(1)
    step(0, ends)
    step(1, ends)
    shard_pair(3)
    big.side_copy(5).start()
    com_pair(2)
    step(0, ~ends)
    step(2, ends)
    gather_pieces_pass(at, gate_sum, gate_slot, gsem)
    sib_tile(0)
    big.side_copy(7).start()
    com_pair(3)
    step(1, ~ends)
    step(3, ends)
    sib_tile(1)
    step(2, ~ends)
    step(4, ends)
    back_tile(at.s, b_own, 0)
    step(3, ~ends)
    step(4, ~ends)
    step(5, ends)
    back_tile(at.s, b_own, 1)
    step(5, ~ends)
    small_pass(at, small, sgot, stotal, sfull, ssem, smore)
    for j in (6, 7):
        big.step(j)
    few.step(3)
    mown[...] = macc[at.z]
    gather_pieces_start(at, mown, x_slot, asem)
    csum[...] = cacc[at.z]
    far_copy = remote(csum, cfar, cx[2], cx[3], at.far)
    far_copy.start()
    for copy in ends_loads:
        copy.wait()
    for k, p in enumerate(parts):
        to_sib[k].wait_recv()
        to_far[k].wait_recv()

        def body(i, _):
            r = pl.ds(pl.multiple_of(k * rows + i * 32, 32), 32)
            total = b_own[r, :].astype(f32) + from_sib[r, :].astype(f32) + from_far[r, :].astype(f32)
            back, wide_own = total * gain_ref[...], own_v[r, :].astype(f32)
            depth = wide_own.shape[1]
            scale = lax.rsqrt(jnp.sum(wide_own * wide_own, axis=1, keepdims=True) / depth + eps)
            along = jnp.sum(back * wide_own, axis=1, keepdims=True) / depth
            hidden_grad[r, :] = (
                cot_v[r, :].astype(f32) + scale * back - wide_own * (scale * scale * scale * along)
            )
            return 0

        lax.fori_loop(0, rows // 32, body, 0)
    far_copy.wait()
    add_into(csum, cfar, half)
    com_out = in_sum.at[mine, pl.ds(2 * E, 384)]
    com_copy = remote(csum, com_out, cx[4], cx[5], at.sib)
    com_copy.start()
    keep_copy = pltpu.make_async_copy(csum, com_out, cx[6])
    keep_copy.start()
    gather_pieces_pass(at, mown, x_slot, asem)
    small_end(at, small, sgot, stotal, sfull, ssem, smore)
    sums_out[...] = jnp.zeros_like(sums_out)
    bc, heads = jnp.zeros((8, 256), f32), jnp.zeros((8, 128), f32)
    for s in range(4):
        sums_out[:, wide * s : wide * s + wide] = sfull[s, :, 0:wide]
        bc = bc + sfull[s, :, wide : wide + 256]
        shift = (wide // P_SIZE) * s
        own = sfull[s, :, 0:128]
        heads = heads + (pltpu.roll(own, shift, 1) if shift else own)
    sums_out[:, E : E + 256] = bc
    sums_out[:, E + 256 : E + 384] = heads
    for copy in to_pass + to_sib + to_far:
        copy.wait_send()
    for zp in range(4):
        com_to_sib(zp).wait_send()
    big.end()
    few.end()
    gather_pieces_end(at, gate_sum, gate_slot, gsem)
    gather_pieces_end(at, mown, x_slot, asem)
    keep_copy.wait()
    com_copy.wait_send()
    got = in_sum.at[other, pl.ds(2 * E, 384)]
    remote(csum, got, cx[4], cx[5], at.sib).wait_recv()


def finish_last(hid, d_gate, d_u, d_dt, w_main, w_com, gate_sum, own, cot, small, gain):
    length, depth = hid.shape
    piece, shard, half = length // 4, depth // 8, depth // 16
    wide = d_gate.shape[1]
    vm = pltpu.VMEM
    shards4 = lambda cuts: [dma(3, 4 * cuts), dma(4 * cuts), dma(4 * cuts), dma(4 * cuts)]
    return pl.pallas_call(
        last_kernel,
        in_specs=[pl.BlockSpec(memory_space=ANY)] * 9 + [pl.BlockSpec(memory_space=pltpu.VMEM)] * 2,
        out_specs=[
            pl.BlockSpec(memory_space=pltpu.VMEM),
            pl.BlockSpec(memory_space=ANY),
            pl.BlockSpec(memory_space=pltpu.VMEM),
        ],
        out_shape=[
            jax.ShapeDtypeStruct((piece, depth), f32),
            jax.ShapeDtypeStruct((shard, 2 * E + 384), bf16),
            jax.ShapeDtypeStruct((8, E + 384), f32),
        ],
        scratch_shapes=[vm(hid.shape, bf16), vm((length, 2 * wide + 384), bf16), vm((depth, 2 * wide + 384), bf16)]
        + [vm((piece, depth), bf16)] * 7
        + [vm((4, 2, shard, wide + 384), bf16)]
        + [vm((4, shard, wide), bf16)] * 4
        + [vm((shard, wide), bf16)]
        + [vm((4, 2, half, 384), bf16)] * 2
        + [vm((4, half, 384), bf16)] * 4
        + [vm((half, 384), bf16)] * 2
        + [vm((8,) + small.shape, f32), vm(small.shape, f32), vm((4,) + small.shape, f32), vm(gate_sum.shape, bf16)]
        + [vm((piece, depth), bf16)] * 2
        + [dma(2), dma(4), dma(4), dma(4), dma(), dma(2)]
        + [dma(3, PARTS), dma(3, PARTS)]
        + shards4(2)
        + shards4(1)
        + [dma(4), dma(4), dma(), dma(), dma(), dma(), dma()]
        + [dma(8), dma(8)]
        + [dma(3), dma(3), dma()]
        + [dma(3, PARTS), dma(3, PARTS), dma()]
        + [dma(3, PARTS), dma(3, PARTS), dma()],
        compiler_params=pltpu.CompilerParams(
            collective_id=4, has_side_effects=True, vmem_limit_bytes=60 * 2**20
        ),
        name="finish_last",
    )(hid, d_gate, d_u, d_dt, w_main, w_com, gate_sum, own, cot, small, gain)


def over_rows(left, right):
    return lax.dot_general(
        left, right, (((0,), (0,)), ((), ())), preferred_element_type=jnp.float32
    )


def gather_plain(hid, main, com):
    hid_all = lax.all_gather(hid, "seq", axis=0)
    main_all = lax.all_gather(main, "wshard", axis=0)
    return hid_all, main_all, lax.all_gather(com, "wshard", axis=0)


def gather_more_plain(cot, rows, wide):
    cot_all = lax.all_gather(cot, "seq", axis=0)
    cols = lax.all_to_all(rows, "wshard", split_axis=1, concat_axis=0, tiled=True)
    own = lax.dynamic_slice_in_dim(cols, lax.axis_index("seq") * wide, wide, 0)
    return cot_all, lax.all_gather(own, "wshard", axis=1, tiled=True)


def reduce_scattered(v, axis):
    return lax.psum_scatter(v, axis, scatter_dimension=0, tiled=False)


def reduce_first_plain(layer, rows, gate):
    layer_sum = reduce_scattered(layer, "seq").astype(f32)
    rows = rows.reshape(-1, rows.shape[-1])
    part = lax.psum_scatter(rows, "wshard", scatter_dimension=1, tiled=True)
    part = lax.all_gather(part, "seq", axis=0, tiled=True)
    part = lax.all_to_all(part, "wshard", split_axis=0, concat_axis=1, tiled=True)
    return layer_sum, part, reduce_scattered(gate, "wshard")


def finish_plain(hid, d_gate, d_u, d_dt, w_main, w_com, gate_sum, own, cot, small, gain):
    groups, owners = lax.axis_size("seq"), lax.axis_size("wshard")
    wide = d_gate.shape[1]
    rest = jnp.concatenate([d_u, d_dt], axis=1)
    nt = lambda p, q: lax.dot_general(p, q, (((1,), (1,)), ((), ())), preferred_element_type=f32)
    back = nt(d_gate, w_main[:, :wide]) + nt(rest, jnp.concatenate([w_main[:, wide:], w_com], axis=1))
    back_sum = reduce_scattered(back.astype(bf16).reshape(groups, -1, D), "seq").astype(f32)
    part = reduce_scattered(over_rows(hid, rest).astype(bf16).reshape(owners, -1, rest.shape[1]), "wshard")
    part = lax.all_gather(jnp.concatenate([gate_sum, part], axis=1), "seq", axis=0)
    in_sum = jnp.concatenate(
        [part[i, :, :wide] for i in range(groups)]
        + [part[i, :, wide : 2 * wide] for i in range(groups)]
        + [jnp.sum(part[:, :, 2 * wide :].astype(f32), axis=0).astype(bf16)],
        axis=1,
    )
    full = lax.all_gather(lax.psum(small, "wshard"), "seq", axis=0)
    turned = [jnp.roll(full[i, :, :128], i * (wide // P_SIZE), axis=1) for i in range(groups)]
    sums = jnp.concatenate(
        [full[i, :, :wide] for i in range(groups)] + [jnp.sum(full[:, :, wide:], axis=0), sum(turned)], axis=1
    )
    wide_own = own.astype(f32)
    own_scale = lax.rsqrt(jnp.mean(wide_own * wide_own, axis=-1, keepdims=True) + eps)
    b = back_sum * gain
    hidden_grad = (
        cot.astype(f32)
        + own_scale * b
        - wide_own * (own_scale * own_scale * own_scale) * jnp.mean(b * wide_own, axis=-1, keepdims=True)
    )
    return hidden_grad, in_sum, sums


def middle_plain(gate, mixed, cot_all, w_out, normed):
    mixed_wide = mixed.astype(f32)
    sg = jax.nn.sigmoid(gate)
    silu = gate * sg
    g = mixed_wide * silu
    g_low = g.astype(bf16)
    a = lax.dot_general(cot_all, w_out, (((1,), (1,)), ((), ())), preferred_element_type=f32)
    sums = lax.psum(jnp.stack([jnp.sum(g * g, axis=1), jnp.sum(a * g, axis=1)]), "seq")
    r = lax.rsqrt(sums[0] / E + eps)[:, None]
    pull = (r * r * r) * (sums[1] / E)[:, None]
    d_g = r * a - g * pull
    d_mixed = (d_g * silu).astype(bf16)
    d_gate = (d_g * mixed_wide * (sg * (1.0 + gate * (1.0 - sg)))).astype(bf16)
    layer_part = (jnp.dot(g_low, w_out, preferred_element_type=f32) * r).astype(bf16)
    cot_r = (cot_all.astype(f32) * r).astype(bf16)
    out_part = over_rows(g_low, cot_r).astype(bf16)

    gate_part = over_rows(normed, d_gate).astype(bf16)
    return d_mixed, d_gate, gate_part, out_part, layer_part


def shards(
    hidden,
    segments,
    norm_gain,
    in_weight,
    conv_weight,
    conv_bias,
    step_bias,
    decay_log,
    skip_scale,
    gate_gain,
    out_weight,
    cotangent,
):
    group = lax.axis_index("seq")
    groups, owners = lax.axis_size("seq"), lax.axis_size("wshard")
    direct = (groups, owners) == (4, 8)
    heads = H // groups
    wide = heads * P_SIZE
    length = segments.shape[1]
    hidden_own, cot_own = hidden[0], cotangent[0]
    main = jnp.concatenate(
        [
            lax.dynamic_slice_in_dim(in_weight, group * wide, wide, 1),
            lax.dynamic_slice_in_dim(in_weight, E + group * wide, wide, 1),
        ],
        axis=1,
    )
    com = jnp.concatenate([in_weight[:, 2 * E :], norm_gain[:, None]], axis=1)
    com = jnp.pad(com, ((0, 0), (0, 128 - H - 1)))
    out_gain = gate_gain.astype(f32)[:, None]
    out_scaled = (out_weight.astype(f32) * out_gain).astype(bf16)
    gather = gather_first if direct else gather_plain
    hidden_all, w_main, w_com = gather(hidden_own, main, com)
    hidden_all = hidden_all.reshape(length, D)
    w_main, w_com = w_main.reshape(D, 2 * wide), w_com.reshape(D, -1)
    gain_row = w_com[:, 2 * N + H].astype(f32)[None]

    seg = segments[0]
    seg_col = jnp.pad(seg, (8, 8), constant_values=-1)[:, None]
    segr = seg.reshape(length // Q, 1, Q)
    par = jnp.pad(jnp.stack([step_bias, decay_log]), ((0, 6), (0, 128 - H)))
    skip = jnp.repeat(skip_scale, P_SIZE)[None]
    facts = (seg_col, segr, conv_weight, conv_bias[None], par, skip)
    beside, more = (forward_traffic(cot_own, out_scaled), (cot_own, out_scaled)) if direct else (NoTraffic, ())
    u, dt, gate, normed, mixed, save, *got = mixer_fwd(beside, more, hidden_all, gain_row, w_main, w_com, *facts)
    cot_all, w_out = got if direct else gather_more_plain(cot_own, out_scaled, wide)
    cot_all, w_out = cot_all.reshape(length, D), w_out.reshape(wide, D)

    mid = middle if direct else middle_plain
    d_mixed, d_gate, gate_part, out_part, layer_part = mid(gate, mixed, cot_all, w_out, normed)
    own_wide = hidden_own.astype(f32)

    more = (layer_part.reshape(groups, -1, D), out_part.reshape(2, -1, D), gate_part.reshape(owners, -1, wide))
    beside = backward_traffic(*more) if direct else NoTraffic
    du, ddt, small, *got = mixer_bwd(
        beside, more if direct else (), u, dt, *facts, save, d_mixed
    )
    layer_sum, out_sum, gate_sum = got if direct else reduce_first_plain(*more)
    layer_output = own_wide + layer_sum
    finish = finish_last if direct else finish_plain
    hidden_grad, in_sum, sums = finish(
        normed, d_gate, du, ddt, w_main, w_com, gate_sum, hidden_own, cot_own, small, gain_row
    )

    in_weight_grad = in_sum[:, : 2 * E + 2 * N + H].astype(f32)
    norm_gain_grad = jnp.sum(in_weight_grad * in_weight.astype(f32), axis=1) / norm_gain.astype(f32)
    out_sum = out_sum.astype(f32)
    out_weight_grad = out_sum * out_gain
    gate_gain_grad = jnp.sum(out_sum * out_weight.astype(f32), axis=1)
    chan, per_head = sums[:, : E + 2 * N], sums[:, E + 2 * N : E + 2 * N + H]
    return (
        layer_output[None],
        hidden_grad[None],
        norm_gain_grad,
        in_weight_grad,
        chan[:4],
        chan[4],
        per_head[5],
        per_head[6],
        per_head[7],
        gate_gain_grad,
        out_weight_grad,
    )


def solution(mesh):
    in_specs = (
        P("wshard", "seq", None),
        P("wshard", None),
        P("wshard"),
        P("wshard", None),
        P(),
        P(),
        P(),
        P(),
        P(),
        P("wshard"),
        P("wshard", None),
        P("wshard", "seq", None),
    )
    out_specs = (
        P("wshard", "seq", None),
        P("wshard", "seq", None),
        P("wshard"),
        P("wshard", None),
        P(),
        P(),
        P(),
        P(),
        P(),
        P("wshard"),
        P("wshard", None),
    )
    return jax.shard_map(shards, mesh=mesh, in_specs=in_specs, out_specs=out_specs, check_vma=False)
```

```python
import functools

import jax
import jax.numpy as jnp
from jax import lax
from jax.experimental import pallas as pl
from jax.experimental.pallas import tpu as pltpu
from jax.sharding import PartitionSpec as P

D = 1536
H = 48
P_SIZE = 64
N = 128
E = 3072

eps = 1e-05
f32, bf16 = jnp.float32, jnp.bfloat16
Q = 128
NEG = -1e30


def dot(a, b):
    return jnp.dot(a, b, preferred_element_type=f32)


def dot_nt(a, b):
    return lax.dot_general(a, b, (((1,), (1,)), ((), ())), preferred_element_type=f32)


def dot3(tri, v):
    hi = v.astype(bf16)
    rest = v - hi.astype(f32)
    mid = rest.astype(bf16)
    low = (rest - mid.astype(f32)).astype(bf16)
    return dot(tri, hi) + dot(tri, mid) + dot(tri, low)


def sigmoid(v):
    return 1.0 / (1.0 + jnp.exp(-v))


def spread_col(v, col):
    return jnp.broadcast_to(v[:, col : col + 1], (Q, 128))


def softplus(v):
    return jnp.maximum(v, 0.0) + jnp.log1p(jnp.exp(-jnp.abs(v)))


def conv_pre(useen, flags, wk, bias, lanes, chans):
    pre = bias[:, chans] + wk[3:4, chans] * useen[8 : 8 + Q, lanes]
    for j in (1, 2, 3):
        pre = pre + wk[3 - j : 4 - j, chans] * (useen[8 - j : 8 - j + Q, lanes] * flags[j])
    return pre


class Facts:
    def __init__(self, chunk, seg_ref, par_ref, xw):
        self.group = lax.axis_index("seq")
        self.heads = xw // P_SIZE
        self.xw = xw
        near = seg_ref[pl.ds(pl.multiple_of(chunk * Q, 8), Q + 16), :]
        now = near[8 : 8 + Q]
        same = lambda other: jnp.broadcast_to(jnp.where(other == now, 1.0, 0.0), (Q, 128))
        self.before = [None] + [same(near[8 - j : 8 - j + Q]) for j in (1, 2, 3)]
        self.after = lambda j: same(near[8 + j : 8 + j + Q])
        self.carried = same(near[7:8])
        self.samelast = same(near[7 + Q : 8 + Q])
        self.now = now
        self.turn = self.heads * self.group
        lane = lax.broadcasted_iota(jnp.int32, (8, 128), 1)
        par = self.own(par_ref[...])
        self.bias = par[0:1]
        self.rate = jnp.where(lane < self.heads, -jnp.exp(par), 0.0)[1:2]

    def own(self, v):
        lane = lax.broadcasted_iota(jnp.int32, v.shape, 1)
        return jnp.where(lane < self.heads, pltpu.roll(v, lax.rem(128 - self.turn, 128), 1), 0.0)

    def back(self, v):
        return pltpu.roll(v, self.turn, 1)

    def chans(self, p):
        if p < self.xw // 128:
            return pl.ds(pl.multiple_of(self.group * self.xw + 128 * p, 128), 128)
        at = E + 128 * (p - self.xw // 128)
        return slice(at, at + 128)


class NoTraffic:
    inputs, outputs, scratch, collective_id = (), (), (), None

    def __init__(self, *refs):
        pass

    def step(self, i, last):
        pass


def fwd_kernel(traffic, hid_ref, gain_ref, main_ref, com_ref, seg_ref, segr_ref, wk_ref, bias_ref, par_ref, skip_ref, *rest):
    n_in, n_out = len(traffic.inputs), len(traffic.outputs)
    extra_in, rest = rest[:n_in], rest[n_in:]
    u_ref, dt_ref, gate_ref, normed_ref, mixed_ref, save_ref = rest[:6]
    extra_out, rest = rest[6 : 6 + n_out], rest[6 + n_out :]
    state, useen, act, next_u, next_dt = rest[:5]
    step_no = pl.program_id(0)
    traffic(*extra_in, *extra_out, *rest[5:]).step(step_no, pl.num_programs(0) - 1)
    xw = mixed_ref.shape[1]
    width = xw + 256
    pairs = xw // 128
    facts = Facts(jnp.maximum(step_no - 1, 0), seg_ref, par_ref, xw)

    @pl.when(step_no == 0)
    def _():
        next_u[...] = jnp.zeros_like(next_u)
        next_dt[...] = jnp.zeros_like(next_dt)

    @pl.when(step_no <= 1)
    def _():
        state[...] = jnp.zeros_like(state)
        useen[0:8, :] = jnp.zeros((8, width), f32)

    useen[8 : 8 + Q, :] = next_u[...]
    dt_now = next_dt[...]

    hid = hid_ref[...].astype(f32)
    depth = hid.shape[1]
    total = jnp.zeros((Q, 128), f32)
    for k in range(depth // 128):
        part = hid[:, 128 * k : 128 * k + 128]
        total = total + part * part
    scale = lax.rsqrt(jnp.sum(total, axis=1, keepdims=True) / depth + eps)
    normed_ref[...] = (hid * scale * gain_ref[...]).astype(bf16)
    low = normed_ref[...]
    for k in range(xw // 256):
        gate_ref[:, 256 * k : 256 * k + 256] = dot(low, main_ref[:, 256 * k : 256 * k + 256])
    for k in range(xw // 256):
        got = dot(low, main_ref[:, xw + 256 * k : xw + 256 * k + 256]).astype(bf16)
        u_ref[:, 256 * k : 256 * k + 256] = got
        next_u[:, 256 * k : 256 * k + 256] = got.astype(f32)
    got = dot(low, com_ref[:, 0:256]).astype(bf16)
    u_ref[:, xw : xw + 256] = got
    next_u[:, xw : xw + 256] = got.astype(f32)
    got = facts.own(dot(low, com_ref[:, 256:384]).astype(bf16).astype(f32))
    dt_ref[...] = got.astype(bf16)
    next_dt[...] = got

    carried, samelast = facts.carried, facts.samelast
    for p in range(width // 128):
        lanes = slice(128 * p, 128 * p + 128)
        pre = conv_pre(useen, facts.before, wk_ref, bias_ref, lanes, facts.chans(p))
        act[:, lanes] = pre * sigmoid(pre)
    tail = useen[Q : Q + 8, :]
    useen[0:8, :] = tail

    step = softplus(dt_now + facts.bias)
    row = lax.broadcasted_iota(jnp.int32, (Q, Q), 0)
    col = lax.broadcasted_iota(jnp.int32, (Q, Q), 1)
    tri = jnp.where(row >= col, 1.0, 0.0).astype(bf16)
    decay = dot3(tri, step * facts.rate)
    decay_t = decay.T
    madd = jnp.where((row >= col) & (facts.now == segr_ref[0]), 0.0, NEG)
    b_now = act[:, xw : xw + 128]
    c_low = act[:, xw + 128 : xw + 256].astype(bf16)
    gram = dot_nt(c_low, b_now.astype(bf16))
    b_t = b_now.T.astype(bf16)
    left = lax.broadcasted_iota(jnp.int32, (Q, 128), 1) < 64
    for p in range(pairs):
        lanes = slice(128 * p, 128 * p + 128)
        d0, d1 = spread_col(decay, 2 * p), spread_col(decay, 2 * p + 1)
        dp = jnp.where(left, d0, d1)
        sp = jnp.where(left, spread_col(step, 2 * p), spread_col(step, 2 * p + 1))
        xs = act[:, lanes]
        xp = xs * sp
        m0 = gram * jnp.exp(d0 - decay_t[2 * p : 2 * p + 1, :] + madd)
        m1 = gram * jnp.exp(d1 - decay_t[2 * p + 1 : 2 * p + 2, :] + madd)
        both = jnp.concatenate([m0.astype(bf16), m1.astype(bf16)], axis=1)
        stacked = jnp.concatenate(
            [jnp.where(left, xp, 0.0).astype(bf16), jnp.where(left, 0.0, xp).astype(bf16)], axis=0
        )
        st = state[:, lanes]
        st_low = st.astype(bf16)
        save_ref[0, :, lanes] = st_low
        y = dot(both, stacked) + dot(c_low, st_low) * (jnp.exp(dp) * carried)
        mixed_ref[:, lanes] = (y + skip_ref[:, facts.chans(p)] * xs).astype(bf16)
        last = dp[Q - 1 : Q, :]
        to_end = (xp * (jnp.exp(last - dp) * samelast)).astype(bf16)
        state[:, lanes] = st * (jnp.exp(last) * carried[Q - 1 : Q, :]) + dot(b_t, to_end)


def mixer_fwd(traffic, extra, hid, gain, main, com, seg, segr, wk, bias, par, skip):
    length, depth = hid.shape
    xw = main.shape[1] // 2
    width = xw + 256
    n = length // Q
    whole = lambda shape: pl.BlockSpec(shape, lambda i: (0,) * len(shape), pipeline_mode=pl.Buffered(1))
    ahead = lambda i: (jnp.minimum(i, n - 1), 0)
    now = lambda i: (jnp.maximum(i - 1, 0), 0)
    now3 = lambda i: (jnp.maximum(i - 1, 0), 0, 0)
    return pl.pallas_call(
        functools.partial(fwd_kernel, traffic),
        grid=(n + 1,),
        in_specs=[
            pl.BlockSpec((Q, depth), ahead),
            whole(gain.shape),
            whole(main.shape),
            whole(com.shape),
            whole(seg.shape),
            pl.BlockSpec((1, 1, Q), now3),
            whole(wk.shape),
            whole(bias.shape),
            whole(par.shape),
            whole(skip.shape),
        ]
        + [pl.BlockSpec(memory_space=pltpu.MemorySpace.HBM)] * len(extra),
        out_specs=[
            pl.BlockSpec((Q, width), ahead),
            pl.BlockSpec((Q, 128), ahead),
            pl.BlockSpec((Q, xw), ahead),
            pl.BlockSpec((Q, depth), ahead),
            pl.BlockSpec((Q, xw), now),
            pl.BlockSpec((1, 128, xw), now3),
        ]
        + [pl.BlockSpec(memory_space=pltpu.MemorySpace.HBM)] * len(traffic.outputs),
        out_shape=[
            jax.ShapeDtypeStruct((length, width), bf16),
            jax.ShapeDtypeStruct((length, 128), bf16),
            jax.ShapeDtypeStruct((length, xw), f32),
            jax.ShapeDtypeStruct((length, depth), bf16),
            jax.ShapeDtypeStruct((length, xw), bf16),
            jax.ShapeDtypeStruct((n, 128, xw), bf16),
            *traffic.outputs,
        ],
        scratch_shapes=[
            pltpu.VMEM((128, xw), f32),
            pltpu.VMEM((Q + 8, width), f32),
            pltpu.VMEM((Q, width), f32),
            pltpu.VMEM((Q, width), f32),
            pltpu.VMEM((Q, 128), f32),
            *traffic.scratch,
        ],
        compiler_params=pltpu.CompilerParams(
            vmem_limit_bytes=60 * 2**20,
            collective_id=traffic.collective_id,
            has_side_effects=traffic.collective_id is not None,
        ),
        name="mixer_forward",
    )(hid, gain, main, com, seg, segr, wk, bias, par, skip, *extra)


def bwd_kernel(traffic, u_ref, halo_ref, dt_ref, seg_ref, segr_ref, wk_ref, bias_ref, par_ref, skip_ref,
               save_ref, dy_ref, *rest):
    n_in, n_out = len(traffic.inputs), len(traffic.outputs)
    extra_in, rest = rest[:n_in], rest[n_in:]
    du_ref, ddt_ref, small_ref = rest[:3]
    extra_out, rest = rest[3 : 3 + n_out], rest[3 + n_out :]
    dstate, useen, act, slope, dpre, keep_y, keep_x, prod_a, prod_b, rows_a, held = rest[:11]
    wgrad_ref, hgrad_ref, sgrad_ref, spot_ref = rest[11:15]
    step_no = pl.program_id(0)
    last_step = pl.num_programs(0) - 1
    traffic(*extra_in, *extra_out, *rest[15:]).step(step_no, last_step)
    width = u_ref.shape[1]
    xw = width - 256
    pairs = xw // 128

    @pl.when(step_no == 0)
    def _():
        dstate[...] = jnp.zeros_like(dstate)
        dpre[Q : Q + 8, :] = jnp.zeros((8, width), f32)
        wgrad_ref[...] = jnp.zeros_like(wgrad_ref)
        hgrad_ref[...] = jnp.zeros_like(hgrad_ref)
        sgrad_ref[...] = jnp.zeros_like(sgrad_ref)
        rows_a[...] = jnp.zeros_like(rows_a)
        head_of = lax.broadcasted_iota(jnp.int32, (xw, 128), 0) // P_SIZE
        mark = head_of == lax.broadcasted_iota(jnp.int32, (xw, 128), 1)
        spot_ref[...] = jnp.where(mark, 1.0, 0.0).astype(bf16)

    useen[0:8, :] = halo_ref[...].astype(f32)[8:16, :]
    useen[8 : 8 + Q, :] = u_ref[...].astype(f32)
    facts = Facts(last_step - step_no, seg_ref, par_ref, xw)
    flags, carried, samelast = facts.before, facts.carried, facts.samelast
    for p in range(width // 128):
        lanes = slice(128 * p, 128 * p + 128)
        pre = conv_pre(useen, flags, wk_ref, bias_ref, lanes, facts.chans(p))
        sg = sigmoid(pre)
        act[:, lanes] = pre * sg
        slope[:, lanes] = sg * (1.0 + pre * (1.0 - sg))

    raw = dt_ref[...].astype(f32) + facts.bias
    step = softplus(raw)
    rate = facts.rate
    row = lax.broadcasted_iota(jnp.int32, (Q, Q), 0)
    col = lax.broadcasted_iota(jnp.int32, (Q, Q), 1)
    tri = jnp.where(row >= col, 1.0, 0.0).astype(bf16)
    upper = jnp.where(row <= col, 1.0, 0.0).astype(bf16)
    below = jnp.where(row > col, 1.0, 0.0).astype(bf16)
    decay = dot3(tri, step * rate)
    decay_t = decay.T
    madd = jnp.where((row <= col) & (facts.now == segr_ref[0]), 0.0, NEG)
    b_now, c_now = act[:, xw : xw + 128], act[:, xw + 128 : xw + 256]
    b_low, c_low = b_now.astype(bf16), c_now.astype(bf16)
    c_t = c_now.T.astype(bf16)
    gram = dot_nt(b_low, c_low)
    left = lax.broadcasted_iota(jnp.int32, (Q, 128), 1) < 64
    lane = lax.broadcasted_iota(jnp.int32, (Q, 128), 1)
    dgram = jnp.zeros((Q, Q), f32)
    cols_b = jnp.zeros((Q, 128), f32)
    for p in range(pairs):
        lanes = slice(128 * p, 128 * p + 128)
        d0, d1 = spread_col(decay, 2 * p), spread_col(decay, 2 * p + 1)
        dp = jnp.where(left, d0, d1)
        sp = jnp.where(left, spread_col(step, 2 * p), spread_col(step, 2 * p + 1))
        xs = act[:, lanes]
        xp = xs * sp
        dy_low = dy_ref[:, lanes]
        dy = dy_low.astype(f32)
        stacked = jnp.concatenate(
            [jnp.where(left, dy, 0.0).astype(bf16), jnp.where(left, 0.0, dy).astype(bf16)], axis=0
        )
        pair = dot_nt(xp.astype(bf16), stacked)
        mts = []
        for k, dk in ((0, d0), (1, d1)):
            h = 2 * p + k
            e = jnp.exp(decay_t[h : h + 1, :] - dk + madd)
            f = e * pair[:, 128 * k : 128 * k + 128]
            dgram = dgram + f
            w = gram * f
            mts.append((gram * e).astype(bf16))
            rows_a[h : h + 1, :] = jnp.sum(w, axis=0, keepdims=True)
            cols_b = jnp.where(lane == h, jnp.sum(w, axis=1, keepdims=True), cols_b)
        within = dot(jnp.concatenate(mts, axis=1), stacked)
        grow = jnp.exp(dp) * carried
        dy_in = dy * grow
        dy_in_low = dy_in.astype(bf16)
        keep_y[:, lanes] = dy_in_low
        st = save_ref[0, :, lanes]
        prod_a[:, lanes] = (dy_in * dot(c_low, st)).astype(bf16)
        last = dp[Q - 1 : Q, :]
        fade = jnp.exp(last - dp) * samelast
        ds = dstate[:, lanes]
        ds_low = ds.astype(bf16)
        xe = xp * fade
        keep_x[:, lanes] = xe.astype(bf16)
        later = dot(b_low, ds_low)
        prod_b[:, lanes] = (xe * later).astype(bf16)
        retain = jnp.exp(last) * carried[Q - 1 : Q, :]
        held[0:1, lanes] = jnp.sum(ds * st.astype(f32), axis=0, keepdims=True) * retain
        dxs = sp * (within + later * fade) + skip_ref[:, facts.chans(p)] * dy
        skp = xs * dy
        sgrad_ref[:, lanes] += jnp.sum(skp.reshape(Q // 8, 8, 128), axis=0)
        dpre[0:Q, lanes] = dxs * slope[:, lanes]
        dstate[:, lanes] = ds * retain + dot(c_t, dy_in_low)
        if p == 0:
            db_in, dc_in = dot_nt(keep_x[:, lanes], ds_low), dot_nt(dy_in_low, st)
        else:
            db_in, dc_in = db_in + dot_nt(keep_x[:, lanes], ds_low), dc_in + dot_nt(dy_in_low, st)

    dg_low = dgram.astype(bf16)
    db = dot(dg_low, c_low) + db_in
    dc = dot(dgram.T.astype(bf16), b_low) + dc_in
    dpre[0:Q, xw : xw + 128] = db * slope[:, xw : xw + 128]
    dpre[0:Q, xw + 128 : xw + 256] = dc * slope[:, xw + 128 : xw + 256]

    spot = spot_ref[...]
    a_in = dot(prod_a[...], spot)
    b_in = dot(prod_b[...], spot)
    hv = jnp.broadcast_to(held[0:1, :], (8, xw))
    h_hi = hv.astype(bf16)
    h_lo = (hv - h_hi.astype(f32)).astype(bf16)
    through = (dot(h_hi, spot) + dot(h_lo, spot))[0:1, :]
    a_own = rows_a[...].T
    cross = dot3(upper, a_own - cols_b + a_in) + dot3(below, b_in) + through
    total = cols_b + b_in
    sg = sigmoid(raw)
    ratio = jnp.where(step > 1e-30, sg / jnp.maximum(step, 1e-30), 1.0)
    draw = total * ratio + rate * cross * sg
    ddt_ref[...] = facts.back(draw).astype(bf16)
    hgrad_ref[0:8, :] += jnp.sum(draw.reshape(Q // 8, 8, 128), axis=0)
    hgrad_ref[8:16, :] += jnp.sum((step * cross).reshape(Q // 8, 8, 128), axis=0)

    ahead = [None] + [facts.after(j) for j in (1, 2, 3)]
    for p in range(width // 128):
        lanes = slice(128 * p, 128 * p + 128)
        own = dpre[0:Q, lanes]
        chans = facts.chans(p)
        du = wk_ref[3:4, chans] * own
        wgrad_ref[24:32, lanes] += jnp.sum((own * useen[8 : 8 + Q, lanes]).reshape(Q // 8, 8, 128), axis=0)
        wgrad_ref[32:40, lanes] += jnp.sum(own.reshape(Q // 8, 8, 128), axis=0)
        for j in (1, 2, 3):
            du = du + wk_ref[3 - j : 4 - j, chans] * (dpre[j : j + Q, lanes] * ahead[j])
            moved = own * (useen[8 - j : 8 - j + Q, lanes] * flags[j])
            k = 3 - j
            wgrad_ref[8 * k : 8 * k + 8, lanes] += jnp.sum(moved.reshape(Q // 8, 8, 128), axis=0)
        du_ref[:, lanes] = du.astype(bf16)
    first = dpre[0:8, :]
    dpre[Q : Q + 8, :] = first

    @pl.when(step_no == last_step)
    def _():
        small_ref[...] = jnp.zeros_like(small_ref)
        for k in range(5):
            small_ref[k : k + 1, :] = jnp.sum(wgrad_ref[8 * k : 8 * k + 8, :], axis=0, keepdims=True)
        small_ref[5:6, 0:128] = jnp.sum(hgrad_ref[0:8, :], axis=0, keepdims=True)
        small_ref[6:7, 0:128] = rate * jnp.sum(hgrad_ref[8:16, :], axis=0, keepdims=True)
        skips = sgrad_ref[...]
        hi = skips.astype(bf16)
        mid = (skips - hi.astype(f32)).astype(bf16)
        by_head = dot(hi, spot_ref[...]) + dot(mid, spot_ref[...])
        small_ref[7:8, 0:128] = jnp.sum(by_head, axis=0, keepdims=True)


def mixer_bwd(traffic, extra, u, dt, seg, segr, wk, bias, par, skip, save, dy):
    length, width = u.shape
    xw = width - 256
    n = length // Q
    whole = lambda shape: pl.BlockSpec(shape, lambda i: (0,) * len(shape))
    back = lambda i: (n - 1 - i, 0)
    return pl.pallas_call(
        functools.partial(bwd_kernel, traffic),
        grid=(n,),
        in_specs=[
            pl.BlockSpec((Q, width), back),
            pl.BlockSpec((16, width), lambda i: (jnp.maximum((n - 1 - i) * (Q // 16) - 1, 0), 0)),
            pl.BlockSpec((Q, 128), back),
            whole(seg.shape),
            pl.BlockSpec((1, 1, Q), lambda i: (n - 1 - i, 0, 0)),
            whole(wk.shape),
            whole(bias.shape),
            whole(par.shape),
            whole(skip.shape),
            pl.BlockSpec((1, 128, xw), lambda i: (n - 1 - i, 0, 0)),
            pl.BlockSpec((Q, xw), back),
        ]
        + [pl.BlockSpec(memory_space=pltpu.MemorySpace.HBM)] * len(extra),
        out_specs=[
            pl.BlockSpec((Q, width), back),
            pl.BlockSpec((Q, 128), back),
            whole((8, width)),
        ]
        + [pl.BlockSpec(memory_space=pltpu.MemorySpace.HBM)] * len(traffic.outputs),
        out_shape=[
            jax.ShapeDtypeStruct((length, width), bf16),
            jax.ShapeDtypeStruct((length, 128), bf16),
            jax.ShapeDtypeStruct((8, width), f32),
            *traffic.outputs,
        ],
        scratch_shapes=[
            pltpu.VMEM((128, xw), f32),
            pltpu.VMEM((Q + 8, width), f32),
            pltpu.VMEM((Q, width), f32),
            pltpu.VMEM((Q, width), f32),
            pltpu.VMEM((Q + 8, width), f32),
            pltpu.VMEM((Q, xw), bf16),
            pltpu.VMEM((Q, xw), bf16),
            pltpu.VMEM((Q, xw), bf16),
            pltpu.VMEM((Q, xw), bf16),
            pltpu.VMEM((128, 128), f32),
            pltpu.VMEM((8, xw), f32),
            pltpu.VMEM((40, width), f32),
            pltpu.VMEM((16, 128), f32),
            pltpu.VMEM((8, xw), f32),
            pltpu.VMEM((xw, 128), bf16),
            *traffic.scratch,
        ],
        compiler_params=pltpu.CompilerParams(
            vmem_limit_bytes=60 * 2**20,
            collective_id=traffic.collective_id,
            has_side_effects=traffic.collective_id is not None,
        ),
        name="mixer_backward",
    )(u, u, dt, seg, segr, wk, bias, par, skip, save, dy, *extra)


MESH = pl.DeviceIdType.MESH
ANY = pltpu.MemorySpace.HBM
PARTS = 4


def remote(src, dst, send_sem, recv_sem, device):
    return pltpu.make_async_remote_copy(
        src_ref=src, dst_ref=dst, send_sem=send_sem, recv_sem=recv_sem, device_id=device, device_id_type=MESH
    )


class Place:
    def __init__(self):
        self.w, self.s = lax.axis_index("wshard"), lax.axis_index("seq")
        self.z, self.x = self.w // 2, lax.rem(self.w, 2)
        self.y, self.c = self.s // 2, lax.rem(self.s, 2)
        self.s_sib = 2 * self.y + 1 - self.c
        self.s_far = 2 * (1 - self.y) + self.c
        self.s_diag = 2 * (1 - self.y) + 1 - self.c
        self.side = (2 * self.z + 1 - self.x, self.s)
        self.up = (lax.rem(self.w + 2, 8), self.s)
        self.down = (lax.rem(self.w + 6, 8), self.s)
        self.sib = (self.w, self.s_sib)
        self.far = (self.w, self.s_far)

    def greet(self, everyone=False, sequence=False):
        barrier = pltpu.get_barrier_semaphore()
        others = [(lax.rem(self.w + k, 8), self.s) for k in range(1, 8)] if everyone else []
        if everyone or sequence:
            others += [(self.w, lax.rem(self.s + k, 4)) for k in range(1, 4)]
        else:
            others = [self.side, self.up, self.down, self.sib, self.far]
        for other in others:
            pl.semaphore_signal(barrier, inc=1, device_id=other, device_id_type=MESH)
        pl.semaphore_wait(barrier, len(others))


def dma(*shape):
    return pltpu.SemaphoreType.DMA(shape)


def gather_pieces_start(at, own, slot, sems, stage=None):
    send, recv, local = sems[:3]
    rows = own.shape[0] // PARTS
    for k in range(PARTS):
        part = pl.ds(k * rows, rows)
        remote(own.at[part], slot(at.s).at[part], send.at[1, k], recv.at[1, k], at.far).start()
    for k in range(PARTS):
        part = pl.ds(k * rows, rows)
        remote(own.at[part], slot(at.s).at[part], send.at[0, k], recv.at[0, k], at.sib).start()
    if stage is not None:
        copy = pltpu.make_async_copy(own, stage, local)
        copy.start()
        copy.wait()
    pltpu.make_async_copy(own if stage is None else stage, slot(at.s), local).start()


def gather_pieces_pass(at, own, slot, sems):
    send, recv, _ = sems
    rows = own.shape[0] // PARTS
    for k in range(PARTS):
        part = pl.ds(k * rows, rows)
        theirs = slot(at.s_far).at[part]
        remote(theirs, theirs, send.at[1, k], recv.at[1, k], at.far).wait_recv()
        remote(theirs, theirs, send.at[2, k], recv.at[2, k], at.sib).start()


def gather_pieces_end(at, own, slot, sems):
    send, recv, local = sems
    rows = own.shape[0] // PARTS
    pltpu.make_async_copy(own, slot(at.s), local).wait()
    for k in range(PARTS):
        part = pl.ds(k * rows, rows)
        sib, diag, far = slot(at.s_sib).at[part], slot(at.s_diag).at[part], slot(at.s_far).at[part]
        remote(own.at[part], slot(at.s).at[part], send.at[0, k], recv.at[0, k], at.sib).wait_send()
        remote(own.at[part], slot(at.s).at[part], send.at[1, k], recv.at[1, k], at.far).wait_send()
        remote(far, far, send.at[2, k], recv.at[2, k], at.sib).wait_send()
        remote(sib, sib, send.at[0, k], recv.at[0, k], at.sib).wait_recv()
        remote(diag, diag, send.at[2, k], recv.at[2, k], at.sib).wait_recv()


CUTS = 6


def gather_shards(at, main, com, main_all, com_all, stage, sems, between):
    send, recv, csend, crecv, psend, precv, local, osend = sems
    half, cut = com.shape[0] // 2, main.shape[0] // CUTS
    mine = pl.ds(pl.multiple_of(at.c * half, half), half)
    load = pltpu.make_async_copy(main, stage[0], local.at[0])
    com_load = pltpu.make_async_copy(com, stage[1], local.at[1])
    keep = pltpu.make_async_copy(stage[0], main_all.at[at.w], local.at[0])
    com_keep = pltpu.make_async_copy(stage[1], com_all.at[at.w], local.at[1])

    def hop(zp, q, way, device, own=False):
        w, n, part = 2 * zp + at.x, zp * CUTS + q, pl.ds(q * cut, cut)
        slot, com_slot = main_all.at[w, part], com_all.at[w, mine]
        copies = [remote(main.at[part] if own else slot, slot, send.at[way, n], recv.at[w * CUTS + q], device)]
        if q == 1:
            copies.append(remote(com.at[mine] if own else com_slot, com_slot, csend.at[way, zp], crecv.at[w], device))
        return copies

    def cross(zp, way, device):
        w = 2 * zp + 1 - at.x
        slot = main_all.at[w, pl.ds(0, cut)]
        return [remote(slot, slot, osend.at[way, zp], recv.at[w * CUTS], device)]

    def begin(copies):
        for copy in copies:
            copy.start()

    def sent(copies):
        for copy in copies:
            copy.wait_send()

    def all_ways(act, q):
        act(hop(at.z, q, 0, at.side, True))

        @pl.when(at.z < 3)
        def _():
            act(hop(at.z, q, 1, at.up, True))

        @pl.when(at.z > 0)
        def _():
            act(hop(at.z, q, 2, at.down, True))

    def arrived(w, q):
        slot = main_all.at[w, pl.ds(q * cut, cut)]
        remote(slot, slot, send.at[0, 0], recv.at[w * CUTS + q], at.side).wait_recv()
        if q == 1:
            held = com_all.at[w, mine]
            remote(held, held, csend.at[0, 0], crecv.at[w], at.side).wait_recv()
            remote(held, held, psend.at[w], precv.at[w], at.sib).start()

    for q in range(CUTS):
        if q > 1:
            all_ways(sent, q - 2)
        all_ways(begin, q)
        if q == 0:
            load.start()
            com_load.start()
            load.wait()
            com_load.wait()
            keep.start()
            com_keep.start()
    arrived(2 * at.z + 1 - at.x, 0)

    @pl.when(at.z < 3)
    def _():
        begin(cross(at.z, 0, at.up))

    @pl.when(at.z > 0)
    def _():
        begin(cross(at.z, 1, at.down))

    for d in (1, 2, 3):
        if d == 3:
            between()
        for q in range(CUTS):

            @pl.when(at.z - d >= 0)
            def _():
                zp = at.z - d
                arrived(2 * zp + at.x, q)

                @pl.when(at.z < 3)
                def _():
                    begin(hop(zp, q, 1, at.up))

                if q > 0:
                    begin(hop(zp, q, 0, at.side))

            @pl.when(at.z + d <= 3)
            def _():
                zp = at.z + d
                arrived(2 * zp + at.x, q)

                @pl.when(at.z > 0)
                def _():
                    begin(hop(zp, q, 2, at.down))

                if q > 0:
                    begin(hop(zp, q, 0, at.side))

        @pl.when(at.z - d >= 0)
        def _():
            arrived(2 * (at.z - d) + 1 - at.x, 0)

            @pl.when(at.z < 3)
            def _():
                begin(cross(at.z - d, 0, at.up))

        @pl.when(at.z + d <= 3)
        def _():
            arrived(2 * (at.z + d) + 1 - at.x, 0)

            @pl.when(at.z > 0)
            def _():
                begin(cross(at.z + d, 1, at.down))

    for zp in range(4):
        for q in range(1, CUTS):
            arrived(2 * zp + 1 - at.x, q)
    keep.wait()
    com_keep.wait()
    all_ways(sent, CUTS - 2)
    all_ways(sent, CUTS - 1)
    for zp in range(4):

        @pl.when((at.z < 3) & (zp <= at.z))
        def _():
            sent(cross(zp, 0, at.up))

        @pl.when((at.z > 0) & (zp >= at.z))
        def _():
            sent(cross(zp, 1, at.down))

        for q in range(CUTS):
            if q > 0:

                @pl.when(at.z != zp)
                def _():
                    sent(hop(zp, q, 0, at.side))

            @pl.when((at.z < 3) & (zp < at.z))
            def _():
                sent(hop(zp, q, 1, at.up))

            @pl.when((at.z > 0) & (zp > at.z))
            def _():
                sent(hop(zp, q, 2, at.down))

    other = pl.ds(pl.multiple_of((1 - at.c) * half, half), half)
    for k in range(1, 8):
        w = lax.rem(at.w + k, 8)
        gone, got = com_all.at[w, mine], com_all.at[w, other]
        remote(gone, gone, psend.at[w], precv.at[w], at.sib).wait_send()
        remote(got, got, psend.at[w], precv.at[w], at.sib).wait_recv()


def gather_kernel(hid, main, com, hid_all, main_all, com_all, hid_v, main_v, com_v, *sems):
    at = Place()
    at.greet()
    slot = lambda s: hid_all.at[s]
    gather_pieces_start(at, hid, slot, sems[0:3], hid_v)
    pass_on = lambda: gather_pieces_pass(at, hid, slot, sems[0:3])
    gather_shards(at, main, com, main_all, com_all, (main_v, com_v), sems[3:11], pass_on)
    gather_pieces_end(at, hid, slot, sems[0:3])


def gather_first(hid, main, com):
    shape = lambda n, v: jax.ShapeDtypeStruct((n,) + v.shape, v.dtype)
    return pl.pallas_call(
        gather_kernel,
        in_specs=[pl.BlockSpec(memory_space=ANY)] * 3,
        out_specs=[pl.BlockSpec(memory_space=ANY)] * 3,
        out_shape=[shape(4, hid), shape(8, main), shape(8, com)],
        scratch_shapes=[pltpu.VMEM(v.shape, v.dtype) for v in (hid, main, com)]
        + [dma(3, PARTS), dma(3, PARTS), dma()]
        + [dma(3, 4 * CUTS), dma(8 * CUTS), dma(3, 4), dma(8), dma(8), dma(8), dma(2), dma(2, 4)],
        compiler_params=pltpu.CompilerParams(collective_id=1, has_side_effects=True),
        name="gather_first",
    )(hid, main, com)


SLICES = 8


def each_slice(body):
    def run(k, _):
        body(k)
        return 0

    lax.fori_loop(0, SLICES, run, 0)


def forward_traffic(cot, rows):
    class Traffic:
        inputs = (cot, rows)
        outputs = (
            jax.ShapeDtypeStruct((4,) + cot.shape, cot.dtype),
            jax.ShapeDtypeStruct((2,) + rows.shape, rows.dtype),
        )
        scratch = (
            pltpu.VMEM(cot.shape, cot.dtype),
            pltpu.VMEM(rows.shape, rows.dtype),
            dma(3, SLICES),
            dma(3, SLICES),
            dma(),
            dma(3, SLICES),
            dma(2, SLICES),
            dma(),
        )
        collective_id = 2

        def __init__(self, own, row_own, full, row_full, stage, rstage, send, recv, local, rsend, rrecv, rlocal):
            self.at = at = Place()
            self.own, self.full, self.row_own, self.row_full = own, full, row_own, row_full
            self.rrecv = rrecv
            cut, rcut = own.shape[0] // SLICES, row_own.shape[0] // SLICES
            part = lambda k: pl.ds(pl.multiple_of(k * cut, cut), cut)
            rpart = lambda k: pl.ds(pl.multiple_of(k * rcut, rcut), rcut)
            piece = lambda s, k: full.at[s, part(k)]
            self.load = pltpu.make_async_copy(own, stage, local)
            self.keep = pltpu.make_async_copy(stage, full.at[at.s], local)
            self.rload = pltpu.make_async_copy(row_own, rstage, rlocal)
            self.rkeep = pltpu.make_async_copy(rstage, row_full.at[at.x], rlocal)
            self.to_sib = lambda k: remote(own.at[part(k)], piece(at.s, k), send.at[0, k], recv.at[0, k], at.sib)
            self.to_far = lambda k: remote(own.at[part(k)], piece(at.s, k), send.at[1, k], recv.at[1, k], at.far)
            self.pass_on = lambda k: remote(piece(at.s_far, k), piece(at.s_far, k), send.at[2, k], recv.at[2, k], at.sib)
            here = lambda k, n, device: remote(
                row_full.at[at.x, rpart(k)], row_full.at[at.x, rpart(k)], rsend.at[n, k], rrecv.at[at.x, k], device
            )
            self.rows = (lambda k: here(k, 0, at.side), lambda k: here(k, 1, at.up), lambda k: here(k, 2, at.down))
            got = lambda s, n, k: remote(piece(s, k), piece(s, k), send.at[n, k], recv.at[n, k], at.sib)
            self.from_sib = lambda k: got(at.s_sib, 0, k)
            self.from_far = lambda k: got(at.s_far, 1, k)
            self.from_diag = lambda k: got(at.s_diag, 2, k)
            other = lambda k: row_full.at[1 - at.x, rpart(k)]
            self.from_side = lambda k: remote(other(k), other(k), rsend.at[0, k], rrecv.at[1 - at.x, k], at.side)

        def step(self, i, last):
            at = self.at
            upward, downward = (at.z >= at.s) & (at.z < 3), (at.z <= at.s) & (at.z > 0)
            side, up, down = self.rows

            @pl.when(i == 0)
            def _():
                at.greet()
                self.load.start()
                each_slice(lambda k: self.to_sib(k).start())

                @pl.when(at.z == at.s)
                def _():
                    self.rload.start()
                    self.rload.wait()
                    self.rkeep.start()
                    self.rkeep.wait()

                self.load.wait()
                self.keep.start()

            k = i - 1

            @pl.when((k >= 0) & (k < SLICES))
            def _():
                self.to_far(k).start()

            @pl.when((k >= SLICES) & (k < 2 * SLICES))
            def _():
                self.from_far(k - SLICES).wait_recv()
                self.pass_on(k - SLICES).start()

            far_away = jnp.where(at.z > at.s, at.z - at.s, at.s - at.z)
            v = 3 * i - 6 * far_away + 1
            r = jnp.where(v >= 0, lax.div(v, 4), -1)

            @pl.when((r >= 0) & (r < SLICES) & (4 * r < v))
            def _():
                @pl.when(at.z != at.s)
                def _():
                    side(r).wait_recv()

                side(r).start()

                @pl.when(upward)
                def _():
                    up(r).start()

                @pl.when(downward)
                def _():
                    down(r).start()

            @pl.when(i == last)
            def _():
                self.keep.wait()

                def finish(k):
                    self.to_sib(k).wait_send()
                    self.to_far(k).wait_send()
                    self.pass_on(k).wait_send()
                    self.from_sib(k).wait_recv()
                    self.from_diag(k).wait_recv()
                    side(k).wait_send()
                    self.from_side(k).wait_recv()

                    @pl.when(upward)
                    def _():
                        up(k).wait_send()

                    @pl.when(downward)
                    def _():
                        down(k).wait_send()

                each_slice(finish)

    return Traffic


def add_into(dst, src, rows):
    step = next(n for n in (64, 48, 32, 16) if rows % n == 0)

    def body(i, _):
        part = pl.ds(pl.multiple_of(i * step, 16), step)
        dst[part, :] = (dst[part, :].astype(f32) + src[part, :].astype(f32)).astype(bf16)
        return 0

    lax.fori_loop(0, rows // step, body, 0)


def far_first(at, i):
    inner = (at.z == 1) | (at.z == 2)
    i = jnp.where(inner & (i >= 2), 5 - i, i)
    return jnp.where(at.z < 2, 3 - i, i)


class ReduceShards:
    def __init__(self, at, partial, cuts, acc, from_side, from_down, from_up, sems):
        self.at, self.partial, self.cuts, self.acc = at, partial, cuts, acc
        self.from_side, self.from_down, self.from_up = from_side, from_down, from_up
        self.send, self.recv_side, self.recv_down, self.recv_up = sems
        self.rows = acc.shape[1] // cuts

    def unit(self, j):
        if isinstance(j, int):
            shard, cut = j // self.cuts, j % self.cuts
        else:
            shard, cut = lax.div(j, self.cuts), lax.rem(j, self.cuts)
        zp = far_first(self.at, shard)
        return zp, zp * self.cuts + cut, pl.ds(pl.multiple_of(cut * self.rows, self.rows), self.rows)

    def side_copy(self, j):
        at = self.at
        zp, n, part = self.unit(j)
        return remote(
            self.partial(zp).at[part], self.from_side.at[zp, part],
            self.send.at[0, n], self.recv_side.at[n], at.side,
        )

    def up_copy(self, j):
        zp, n, part = self.unit(j)
        return remote(
            self.acc.at[zp, part], self.from_down.at[zp, part], self.send.at[1, n], self.recv_down.at[n], self.at.up
        )

    def down_copy(self, j):
        zp, n, part = self.unit(j)
        return remote(
            self.acc.at[zp, part], self.from_up.at[zp, part], self.send.at[2, n], self.recv_up.at[n], self.at.down
        )

    def start(self):
        self.side_copy(0).start()
        self.side_copy(1).start()

    def step(self, j):
        at = self.at
        zp, _, part = self.unit(j)
        self.side_copy(j).wait()
        acc = self.acc.at[zp, part]
        add_into(acc, self.from_side.at[zp, part], self.rows)

        @pl.when((at.z > 0) & (zp >= at.z))
        def _():
            self.up_copy(j).wait_recv()
            add_into(acc, self.from_down.at[zp, part], self.rows)

        @pl.when((at.z < 3) & (zp <= at.z))
        def _():
            self.down_copy(j).wait_recv()
            add_into(acc, self.from_up.at[zp, part], self.rows)

        @pl.when(zp > at.z)
        def _():
            self.up_copy(j).start()

        @pl.when(zp < at.z)
        def _():
            self.down_copy(j).start()

    def end(self):
        at = self.at
        for j in range(4 * self.cuts):
            zp = self.unit(j)[0]

            @pl.when(zp > at.z)
            def _():
                self.up_copy(j).wait_send()

            @pl.when(zp < at.z)
            def _():
                self.down_copy(j).wait_send()


def backward_traffic(layer, rows, gate):
    piece, cols = layer.shape[1:]
    rrows = rows.shape[1]
    grows, gcols = gate.shape[1:]

    class Traffic:
        inputs = (layer, rows, gate)
        outputs = (
            jax.ShapeDtypeStruct((piece, cols), f32),
            jax.ShapeDtypeStruct((rrows, cols), bf16),
            jax.ShapeDtypeStruct((grows, gcols), bf16),
        )
        scratch = (
            *[pltpu.VMEM((piece, cols), bf16)] * 5,
            pltpu.VMEM((piece, cols), f32),
            *[pltpu.VMEM((rrows, cols), bf16)] * 4,
            dma(3, SLICES),
            dma(3, SLICES),
            dma(3),
            dma(3, SLICES),
            dma(3, SLICES),
            dma(2),
            dma(2, SLICES),
            dma(2, SLICES),
            *[pltpu.VMEM((4, grows, gcols), bf16)] * 4,
            dma(3, 8),
            dma(8),
            dma(8),
            dma(8),
            dma(5),
        )
        collective_id = 3

        def __init__(
            self, layer, rows, gate, out, rows_out, gate_out,
            own_v, far_v, sib_v, pass_v, got_v, sum_v, acc, side_v, low_v, high_v,
            send, recv, local, rsend, rrecv, rlocal, fsend, frecv,
            gacc, gside, glow, ghigh, gsend, grecv_side, grecv_low, grecv_high, glocal,
        ):
            self.at = at = Place()
            cut, rcut = piece // SLICES, rrows // SLICES
            part = lambda k: pl.ds(pl.multiple_of(k * cut, cut), cut)
            rpart = lambda k: pl.ds(pl.multiple_of(k * rcut, rcut), rcut)
            self.own, self.sib, self.passed, self.got, self.sum = own_v, sib_v, pass_v, got_v, sum_v
            self.part, self.rpart, self.cut, self.rcut = part, rpart, cut, rcut
            self.far_v, self.acc, self.side_v, self.low_v, self.high_v = far_v, acc, side_v, low_v, high_v
            self.load_far = pltpu.make_async_copy(layer.at[at.s_far], far_v, local.at[0])
            self.load_own = pltpu.make_async_copy(layer.at[at.s], own_v, local.at[1])
            self.store = pltpu.make_async_copy(sum_v, out, local.at[2])
            self.to_pass = lambda k: remote(
                layer.at[at.s_diag, part(k)], pass_v.at[part(k)], send.at[0, k], recv.at[0, k], at.sib
            )
            self.to_sib = lambda k: remote(
                layer.at[at.s_sib, part(k)], sib_v.at[part(k)], send.at[1, k], recv.at[1, k], at.sib
            )
            self.to_far = lambda k: remote(
                far_v.at[part(k)], got_v.at[part(k)], send.at[2, k], recv.at[2, k], at.far
            )
            self.load_acc = pltpu.make_async_copy(rows.at[at.x], acc, rlocal.at[0])
            self.store_acc = pltpu.make_async_copy(acc, rows_out, rlocal.at[1])
            spread = lambda k, n, device: remote(
                acc.at[rpart(k)], rows_out.at[rpart(k)], fsend.at[n, k], frecv.at[n, k], device
            )
            self.spread_far = lambda k: spread(k, 0, at.far)
            self.spread_sib = lambda k: spread(k, 1, at.sib)
            self.spread_on = lambda k: remote(
                rows_out.at[rpart(k)], rows_out.at[rpart(k)], fsend.at[1, k], frecv.at[1, k], at.sib
            )
            self.gates = ReduceShards(
                at, lambda zp: gate.at[2 * zp + 1 - at.x], 2, gacc, gside, glow, ghigh,
                (gsend, grecv_side, grecv_low, grecv_high),
            )
            self.load_gate = [
                pltpu.make_async_copy(gate.at[2 * zp + at.x], gacc.at[zp], glocal.at[zp]) for zp in range(4)
            ]
            self.store_gate = pltpu.make_async_copy(gacc.at[at.z], gate_out, glocal.at[4])
            self.to_side = lambda k: remote(
                rows.at[1 - at.x, rpart(k)], side_v.at[rpart(k)], rsend.at[0, k], rrecv.at[0, k], at.side
            )
            self.to_up = lambda k: remote(
                acc.at[rpart(k)], low_v.at[rpart(k)], rsend.at[1, k], rrecv.at[1, k], at.up
            )
            self.to_down = lambda k: remote(
                acc.at[rpart(k)], high_v.at[rpart(k)], rsend.at[2, k], rrecv.at[2, k], at.down
            )

        def step(self, i, last):
            at = self.at

            @pl.when(i == 0)
            def _():
                at.greet()
                self.load_far.start()
                self.load_own.start()
                self.load_acc.start()
                for copy in self.load_gate:
                    copy.start()
                each_slice(lambda k: self.to_pass(k).start())
                each_slice(lambda k: self.to_sib(k).start())

            @pl.when(i < SLICES)
            def _():
                self.to_side(i).start()

            @pl.when(i == 1)
            def _():
                self.load_far.wait()
                self.load_own.wait()
                self.load_acc.wait()
                for copy in self.load_gate:
                    copy.wait()

            k = i - 1

            @pl.when((k >= 0) & (k < SLICES))
            def _():
                self.to_pass(k).wait_recv()
                add_into(self.far_v.at[self.part(k)], self.passed.at[self.part(k)], self.cut)
                self.to_far(k).start()

            m = i - SLICES

            @pl.when((m >= 0) & (m < SLICES))
            def _():
                self.to_sib(m).wait_recv()
                self.to_far(m).wait_recv()
                p = self.part(m)
                self.sum[p, :] = (
                    self.own[p, :].astype(f32) + self.sib[p, :].astype(f32) + self.got[p, :].astype(f32)
                )

            ends = jnp.where(at.z > 3 - at.z, at.z, 3 - at.z)
            chain = jnp.where(at.z < at.s, at.z, jnp.where(at.z > at.s, 3 - at.z, ends))
            v = 10 * i - 17 * chain - 26 + 10
            r = jnp.where(v >= 0, lax.div(v, 11), -1)

            @pl.when((r >= 0) & (r < SLICES) & (11 * r < v))
            def _():
                acc = self.acc.at[self.rpart(r)]
                self.to_side(r).wait_recv()
                add_into(acc, self.side_v.at[self.rpart(r)], self.rcut)

                @pl.when((at.z <= at.s) & (at.z > 0))
                def _():
                    self.to_up(r).wait_recv()
                    add_into(acc, self.low_v.at[self.rpart(r)], self.rcut)

                @pl.when((at.z >= at.s) & (at.z < 3))
                def _():
                    self.to_down(r).wait_recv()
                    add_into(acc, self.high_v.at[self.rpart(r)], self.rcut)

                @pl.when(at.z < at.s)
                def _():
                    self.to_up(r).start()

                @pl.when(at.z > at.s)
                def _():
                    self.to_down(r).start()

                @pl.when(at.z == at.s)
                def _():
                    self.spread_far(r).start()
                    self.spread_sib(r).start()

            g = i - (last - 7)

            @pl.when(g >= 0)
            def _():
                self.gates.side_copy(g).start()

            inner = jnp.where((at.z == 1) | (at.z == 2), 1, 0)
            g = i - 12 - inner

            @pl.when(g >= 0)
            def _():
                self.gates.step(g)

            @pl.when(i == last)
            def _():
                def rest(k, _):
                    self.gates.step(k)
                    return 0

                lax.fori_loop(last - 11 - inner, 8, rest, 0)

                self.store.start()
                self.store_gate.start()

                @pl.when(at.s == at.z)
                def _():
                    self.store_acc.start()

                def forward(k):
                    @pl.when(at.s_far == at.z)
                    def _():
                        self.spread_far(k).wait_recv()
                        self.spread_on(k).start()

                each_slice(forward)

                def finish(k):
                    @pl.when(at.s == at.z)
                    def _():
                        self.spread_far(k).wait_send()
                        self.spread_sib(k).wait_send()

                    @pl.when(at.s_far == at.z)
                    def _():
                        self.spread_on(k).wait_send()

                    @pl.when((at.s_sib == at.z) | (at.s_diag == at.z))
                    def _():
                        self.spread_on(k).wait_recv()

                    self.to_pass(k).wait_send()
                    self.to_sib(k).wait_send()
                    self.to_far(k).wait_send()
                    self.to_side(k).wait_send()

                    @pl.when(at.z < at.s)
                    def _():
                        self.to_up(k).wait_send()

                    @pl.when(at.z > at.s)
                    def _():
                        self.to_down(k).wait_send()

                each_slice(finish)
                self.gates.end()
                self.store.wait()
                self.store_gate.wait()

                @pl.when(at.s == at.z)
                def _():
                    self.store_acc.wait()

    return Traffic


def mid_kernel(gate, mixed, cot, w_out, normed,
               d_mixed, d_gate, gate_part, out_part, layer_part,
               gate_v, mixed_v, cot_v, normed_v, w_v, a_v, low_v, dg_v, l_v, out_v, stats, got, *sems):
    at = Place()
    load, xsend, xrecv, store = sems
    length, wide = mixed_v.shape
    depth = cot_v.shape[1]
    piece = length // 4
    strips = wide // 128
    tiles = piece // 256
    part = lambda t: pl.ds(pl.multiple_of(t * 256, 256), 256)

    def loads(k):
        r = pl.ds(pl.multiple_of(k * piece, piece), piece)
        pairs = ((cot, cot_v), (gate, gate_v), (mixed, mixed_v))
        return [pltpu.make_async_copy(p.at[r], v.at[r], load.at[3 * k + n]) for n, (p, v) in enumerate(pairs)]

    w_load = pltpu.make_async_copy(w_out, w_v, load.at[12])
    normed_load = pltpu.make_async_copy(normed, normed_v, load.at[13])
    w_load.start()
    for k in range(4):
        for copy in loads(k):
            copy.start()
    normed_load.start()
    at.greet(sequence=True)

    stats[...] = jnp.zeros_like(stats)
    w_load.wait()

    def first(i, _):
        @pl.when(lax.rem(i, tiles) == 0)
        def _():
            for copy in loads(lax.div(i, tiles)):
                copy.wait()

        tile = part(i)
        a_v[tile, :] = dot_nt(cot_v[tile, :], w_v[...])
        sum_g, sum_a = jnp.zeros((256, 128), f32), jnp.zeros((256, 128), f32)
        for n in range(strips):
            col = slice(128 * n, 128 * n + 128)
            gt = gate_v[tile, col]
            g = mixed_v[tile, col].astype(f32) * (gt * sigmoid(gt))
            sum_g = sum_g + g * g
            sum_a = sum_a + a_v[tile, col] * g
        stats[0:1, tile] = jnp.sum(sum_g.T, axis=0, keepdims=True)
        stats[1:2, tile] = jnp.sum(sum_a.T, axis=0, keepdims=True)
        return 0

    lax.fori_loop(0, 4 * tiles, first, 0)

    peers = (at.s_sib, at.s_far, at.s_diag)
    swap = [remote(stats, got.at[k], xsend.at[k], xrecv.at[k], (at.w, s)) for k, s in enumerate(peers)]
    for copy in swap:
        copy.start()
    for copy in swap:
        copy.wait()
    total = stats[...] + got[0] + got[1] + got[2]
    r_row = lax.rsqrt(total[0:1] / E + eps)
    stats[0:1, :] = r_row
    stats[1:2, :] = r_row * r_row * r_row * (total[1:2] / E)

    def column(k, at_row):
        return jnp.broadcast_to(stats[k : k + 1, pl.ds(pl.multiple_of(at_row, 128), 256)], (128, 256)).T

    def second(i, _):
        tile = pl.ds(pl.multiple_of(i * 256, 256), 256)
        r, pull = column(0, i * 256), column(1, i * 256)
        for n in range(strips):
            col = slice(128 * n, 128 * n + 128)
            gt, mx = gate_v[tile, col], mixed_v[tile, col].astype(f32)
            sg = sigmoid(gt)
            silu = gt * sg
            g = mx * silu
            low_v[tile, col] = (g * r).astype(bf16)
            d_g = r * a_v[tile, col] - g * pull
            mixed_v[tile, col] = (d_g * silu).astype(bf16)
            dg_v[tile, col] = (d_g * mx * (sg * (1.0 + gt * (1.0 - sg)))).astype(bf16)
        l_v[tile, :] = dot(low_v[tile, :], w_v[...]).astype(bf16)
        layer_copy(i).start()
        return 0

    layer_copy = lambda i: pltpu.make_async_copy(l_v.at[part(i)], layer_part.at[part(i)], store.at[9 + i])
    lax.fori_loop(0, length // 256, second, 0)
    keep = [pltpu.make_async_copy(mixed_v, d_mixed, store.at[0]), pltpu.make_async_copy(dg_v, d_gate, store.at[1])]
    for copy in keep:
        copy.start()
    normed_load.wait()
    tn = lambda p, q: lax.dot_general(p, q, (((0,), (0,)), ((), ())), preferred_element_type=f32)

    def out_block(n):
        room = out_v.at[part(n)]
        return room, pltpu.make_async_copy(room, out_part.at[part(n)], store.at[2 + n])

    def out_grad(n, _):
        room, copy = out_block(n)
        room[...] = tn(low_v[:, part(n)], cot_v[...]).astype(bf16)
        copy.start()
        return 0

    lax.fori_loop(0, wide // 256, out_grad, 0)
    shard = depth // 4
    block = lambda n: pl.ds(pl.multiple_of(n * shard, shard), shard)
    gate_block = lambda n: pltpu.make_async_copy(low_v.at[block(n)], gate_part.at[block(n)], store.at[5 + n])

    def gate_grad(n, _):
        low_v[block(n), :] = tn(normed_v[:, block(n)], dg_v[...]).astype(bf16)
        gate_block(n).start()
        return 0

    lax.fori_loop(0, 4, gate_grad, 0)

    for copy in keep:
        copy.wait()
    for n in range(wide // 256):
        out_block(n)[1].wait()
    for n in range(4):
        gate_block(n).wait()
    for i in range(length // 256):
        layer_copy(i).wait()


def middle(gate, mixed, cot, w_out, normed):
    length, wide = mixed.shape
    depth = cot.shape[1]
    piece = length // 4
    vm = pltpu.VMEM
    low = lambda *shape: jax.ShapeDtypeStruct(shape, bf16)
    return pl.pallas_call(
        mid_kernel,
        in_specs=[pl.BlockSpec(memory_space=ANY)] * 5,
        out_specs=[pl.BlockSpec(memory_space=ANY)] * 5,
        out_shape=[
            low(length, wide),
            low(length, wide),
            low(depth, wide),
            low(wide, depth),
            low(length, depth),
        ],
        scratch_shapes=[
            vm((length, wide), f32),
            vm((length, wide), bf16),
            vm((length, depth), bf16),
            vm((length, depth), bf16),
            vm((wide, depth), bf16),
            vm((length, wide), f32),
            vm((length, wide), bf16),
            vm((length, wide), bf16),
            vm((length, depth), bf16),
            vm((wide, depth), bf16),
        ]
        + [vm((8, length), f32), vm((3, 8, length), f32)]
        + [dma(14), dma(3), dma(3), dma(17)],
        compiler_params=pltpu.CompilerParams(
            collective_id=5, has_side_effects=True, vmem_limit_bytes=61 * 2**20
        ),
        name="middle",
    )(gate, mixed, cot, w_out, normed)


def small_start(at, small, got, sems):
    send, recv = sems
    for k in range(1, 8):
        peer = (lax.rem(at.w + k, 8), at.s)
        remote(small, got.at[k], send.at[k], recv.at[k], peer).start()


def small_pass(at, small, got, total, full, sems, more):
    send, recv = sems
    send2, recv2, local = more
    value = small[...]
    for k in range(1, 8):
        remote(small, got.at[k], send.at[k], recv.at[k], at.side).wait_recv()
        value = value + got[k]
    total[...] = value
    pltpu.make_async_copy(total, full.at[at.s], local).start()
    for k, s in enumerate((at.s_sib, at.s_far, at.s_diag)):
        remote(total, full.at[at.s], send2.at[k], recv2.at[k], (at.w, s)).start()


def small_end(at, small, got, total, full, sems, more):
    send, recv = sems
    send2, recv2, local = more
    pltpu.make_async_copy(total, full.at[at.s], local).wait()
    for k in range(1, 8):
        remote(small, got.at[k], send.at[k], recv.at[k], at.side).wait_send()
    for k, s in enumerate((at.s_sib, at.s_far, at.s_diag)):
        remote(total, full.at[at.s], send2.at[k], recv2.at[k], (at.w, s)).wait_send()
        remote(total, full.at[s], send2.at[k], recv2.at[k], (at.w, s)).wait_recv()


def last_kernel(hid, d_gate, d_u, d_dt, w_main, w_com, gate_sum, own, cot, small, gain_ref,
                hidden_grad, in_sum, sums_out,
                hid_v, dp_v, w_v,
                b_diag, b_sib, b_far, b_own, from_sib, pass_sib, from_far,
                part_v, mside, mlow, mhigh, macc, mown, csib, cown, cacc, cside, clow, chigh, cfar, csum,
                sgot, stotal, sfull, gate_v, own_v, cot_v, *sems):
    at = Place()
    sems = list(sems)
    take = lambda n: [sems.pop(0) for _ in range(n)]
    load, bsem, msem, csem, cx, ssem, smore, asem, gsem = (
        take(6), take(2), take(4), take(4), take(7), take(2), take(3), take(3), take(3)
    )
    piece = hid_v.shape[0] // 4
    shard = hid_v.shape[1] // 8
    wide = d_gate.shape[1]
    half = shard // 2
    mine = pl.ds(pl.multiple_of(at.c * half, half), half)
    other = pl.ds(pl.multiple_of((1 - at.c) * half, half), half)
    at.greet(everyone=True)

    order = (at.s_diag, at.s_far, at.s_sib, at.s)
    rows_of = lambda s: pl.ds(pl.multiple_of(s * piece, piece), piece)
    weights = [
        pltpu.make_async_copy(w_main, w_v.at[:, pl.ds(0, 2 * wide)], load[0].at[0]),
        pltpu.make_async_copy(w_com, w_v.at[:, pl.ds(2 * wide, 384)], load[0].at[1]),
    ]
    loads = []
    for k, s in enumerate(order):
        r = rows_of(s)
        loads.append(
            [
                pltpu.make_async_copy(d_gate.at[r], dp_v.at[r, pl.ds(0, wide)], load[1].at[k]),
                pltpu.make_async_copy(d_u.at[r], dp_v.at[r, pl.ds(wide, wide + 256)], load[2].at[k]),
                pltpu.make_async_copy(d_dt.at[r], dp_v.at[r, pl.ds(2 * wide + 256, 128)], load[3].at[k]),
            ]
        )
    hid_load = pltpu.make_async_copy(hid, hid_v, load[4])
    soon, later = weights + loads[0] + loads[1], [hid_load] + loads[2] + loads[3]
    ends_loads = [
        pltpu.make_async_copy(own, own_v, load[5].at[0]),
        pltpu.make_async_copy(cot, cot_v, load[5].at[1]),
    ]
    for copy in soon + later + ends_loads:
        copy.start()
    gate_slot = lambda s: in_sum.at[:, pl.ds(pl.multiple_of(s * wide, 128), wide)]
    x_slot = lambda s: in_sum.at[:, pl.ds(pl.multiple_of(E + s * wide, 128), wide)]
    gather_pieces_start(at, gate_sum, gate_slot, gsem, gate_v)
    small_start(at, small, sgot, ssem)

    send, recv = bsem
    rows = piece // PARTS
    parts = [pl.ds(k * rows, rows) for k in range(PARTS)]
    to_pass = [remote(b_diag.at[p], pass_sib.at[p], send.at[0, k], recv.at[0, k], at.sib) for k, p in enumerate(parts)]
    to_sib = [remote(b_sib.at[p], from_sib.at[p], send.at[1, k], recv.at[1, k], at.sib) for k, p in enumerate(parts)]
    to_far = [remote(b_far.at[p], from_far.at[p], send.at[2, k], recv.at[2, k], at.far) for k, p in enumerate(parts)]

    def back_tile(s, out, t):
        tile = pl.ds(pl.multiple_of(s * piece + t * 256, 256), 256)
        place = pl.ds(t * 256, 256)

        for n in range(hid_v.shape[1] // 256):
            col = slice(256 * n, 256 * n + 256)
            out[place, col] = dot_nt(dp_v[tile, :], w_v[col, :]).astype(bf16)

    big = ReduceShards(at, lambda zp: part_v.at[zp, 1 - at.x, :, pl.ds(0, wide)], 2, macc, mside, mlow, mhigh, msem)
    few = ReduceShards(at, lambda zp: cown.at[zp, 1 - at.x], 1, cacc, cside, clow, chigh, csem)
    com_cols = pl.ds(wide, 384)
    com_to_sib = lambda zp: remote(
        part_v.at[zp, :, other, com_cols], csib.at[zp], cx[0].at[zp], cx[1].at[zp], at.sib
    )

    def shard_pair(i):
        zp = far_first(at, i)
        lanes = pl.ds(pl.multiple_of(zp * 2 * shard, 128), 2 * shard)
        got = lax.dot_general(
            hid_v[:, lanes], dp_v[:, wide : 2 * wide + 384], (((0,), (0,)), ((), ())), preferred_element_type=f32
        ).astype(bf16)
        part_v[zp, 0] = got[0:shard]
        part_v[zp, 1] = got[shard : 2 * shard]
        macc[zp] = part_v[zp, at.x, :, 0:wide]
        big.side_copy(2 * i).start()
        com_to_sib(zp).start()

    def com_pair(i):
        zp = far_first(at, i)
        com_to_sib(zp).wait_recv()
        for x in range(2):
            cown[zp, x] = part_v[zp, x, mine, com_cols]
            add_into(cown.at[zp, x], csib.at[zp, x], half)
        cacc[zp] = cown[zp, at.x]
        few.side_copy(i).start()

    ends = (at.z == 0) | (at.z == 3)

    def step(j, who):
        @pl.when(who)
        def _():
            big.step(j)
            if j % 2:
                few.step(j // 2)

    tiles = piece // 256
    per = PARTS // tiles
    def far_tile(t):
        back_tile(at.s_far, b_far, t)
        for k in range(t * per, t * per + per):
            to_pass[k].wait_recv()
            add_into(b_far.at[parts[k]], pass_sib.at[parts[k]], rows)
            to_far[k].start()

    for copy in soon:
        copy.wait()
    for t in range(tiles):
        back_tile(at.s_diag, b_diag, t)
        for k in range(t * per, t * per + per):
            to_pass[k].start()
    far_tile(0)
    for copy in later:
        copy.wait()
    def sib_tile(t):
        back_tile(at.s_sib, b_sib, t)
        for k in range(t * per, t * per + per):
            to_sib[k].start()

    shard_pair(0)
    far_tile(1)
    big.side_copy(1).start()
    shard_pair(1)
    com_pair(0)
    shard_pair(2)
    big.side_copy(3).start()
    com_pair(1)
    step(0, ends)
    step(1, ends)
    shard_pair(3)
    big.side_copy(5).start()
    com_pair(2)
    step(0, ~ends)
    step(2, ends)
    gather_pieces_pass(at, gate_sum, gate_slot, gsem)
    sib_tile(0)
    big.side_copy(7).start()
    com_pair(3)
    step(1, ~ends)
    step(3, ends)
    sib_tile(1)
    step(2, ~ends)
    step(4, ends)
    back_tile(at.s, b_own, 0)
    step(3, ~ends)
    step(4, ~ends)
    step(5, ends)
    back_tile(at.s, b_own, 1)
    step(5, ~ends)
    small_pass(at, small, sgot, stotal, sfull, ssem, smore)
    for j in (6, 7):
        big.step(j)
    few.step(3)
    mown[...] = macc[at.z]
    gather_pieces_start(at, mown, x_slot, asem)
    csum[...] = cacc[at.z]
    far_copy = remote(csum, cfar, cx[2], cx[3], at.far)
    far_copy.start()
    for copy in ends_loads:
        copy.wait()
    for k, p in enumerate(parts):
        to_sib[k].wait_recv()
        to_far[k].wait_recv()

        def body(i, _):
            r = pl.ds(pl.multiple_of(k * rows + i * 32, 32), 32)
            total = b_own[r, :].astype(f32) + from_sib[r, :].astype(f32) + from_far[r, :].astype(f32)
            back, wide_own = total * gain_ref[...], own_v[r, :].astype(f32)
            depth = wide_own.shape[1]
            scale = lax.rsqrt(jnp.sum(wide_own * wide_own, axis=1, keepdims=True) / depth + eps)
            along = jnp.sum(back * wide_own, axis=1, keepdims=True) / depth
            hidden_grad[r, :] = (
                cot_v[r, :].astype(f32) + scale * back - wide_own * (scale * scale * scale * along)
            )
            return 0

        lax.fori_loop(0, rows // 32, body, 0)
    far_copy.wait()
    add_into(csum, cfar, half)
    com_out = in_sum.at[mine, pl.ds(2 * E, 384)]
    com_copy = remote(csum, com_out, cx[4], cx[5], at.sib)
    com_copy.start()
    keep_copy = pltpu.make_async_copy(csum, com_out, cx[6])
    keep_copy.start()
    gather_pieces_pass(at, mown, x_slot, asem)
    small_end(at, small, sgot, stotal, sfull, ssem, smore)
    sums_out[...] = jnp.zeros_like(sums_out)
    bc, heads = jnp.zeros((8, 256), f32), jnp.zeros((8, 128), f32)
    for s in range(4):
        sums_out[:, wide * s : wide * s + wide] = sfull[s, :, 0:wide]
        bc = bc + sfull[s, :, wide : wide + 256]
        shift = (wide // P_SIZE) * s
        own = sfull[s, :, 0:128]
        heads = heads + (pltpu.roll(own, shift, 1) if shift else own)
    sums_out[:, E : E + 256] = bc
    sums_out[:, E + 256 : E + 384] = heads
    for copy in to_pass + to_sib + to_far:
        copy.wait_send()
    for zp in range(4):
        com_to_sib(zp).wait_send()
    big.end()
    few.end()
    gather_pieces_end(at, gate_sum, gate_slot, gsem)
    gather_pieces_end(at, mown, x_slot, asem)
    keep_copy.wait()
    com_copy.wait_send()
    got = in_sum.at[other, pl.ds(2 * E, 384)]
    remote(csum, got, cx[4], cx[5], at.sib).wait_recv()


def finish_last(hid, d_gate, d_u, d_dt, w_main, w_com, gate_sum, own, cot, small, gain):
    length, depth = hid.shape
    piece, shard, half = length // 4, depth // 8, depth // 16
    wide = d_gate.shape[1]
    vm = pltpu.VMEM
    shards4 = lambda cuts: [dma(3, 4 * cuts), dma(4 * cuts), dma(4 * cuts), dma(4 * cuts)]
    return pl.pallas_call(
        last_kernel,
        in_specs=[pl.BlockSpec(memory_space=ANY)] * 9 + [pl.BlockSpec(memory_space=pltpu.VMEM)] * 2,
        out_specs=[
            pl.BlockSpec(memory_space=pltpu.VMEM),
            pl.BlockSpec(memory_space=ANY),
            pl.BlockSpec(memory_space=pltpu.VMEM),
        ],
        out_shape=[
            jax.ShapeDtypeStruct((piece, depth), f32),
            jax.ShapeDtypeStruct((shard, 2 * E + 384), bf16),
            jax.ShapeDtypeStruct((8, E + 384), f32),
        ],
        scratch_shapes=[vm(hid.shape, bf16), vm((length, 2 * wide + 384), bf16), vm((depth, 2 * wide + 384), bf16)]
        + [vm((piece, depth), bf16)] * 7
        + [vm((4, 2, shard, wide + 384), bf16)]
        + [vm((4, shard, wide), bf16)] * 4
        + [vm((shard, wide), bf16)]
        + [vm((4, 2, half, 384), bf16)] * 2
        + [vm((4, half, 384), bf16)] * 4
        + [vm((half, 384), bf16)] * 2
        + [vm((8,) + small.shape, f32), vm(small.shape, f32), vm((4,) + small.shape, f32), vm(gate_sum.shape, bf16)]
        + [vm((piece, depth), bf16)] * 2
        + [dma(2), dma(4), dma(4), dma(4), dma(), dma(2)]
        + [dma(3, PARTS), dma(3, PARTS)]
        + shards4(2)
        + shards4(1)
        + [dma(4), dma(4), dma(), dma(), dma(), dma(), dma()]
        + [dma(8), dma(8)]
        + [dma(3), dma(3), dma()]
        + [dma(3, PARTS), dma(3, PARTS), dma()]
        + [dma(3, PARTS), dma(3, PARTS), dma()],
        compiler_params=pltpu.CompilerParams(
            collective_id=4, has_side_effects=True, vmem_limit_bytes=60 * 2**20
        ),
        name="finish_last",
    )(hid, d_gate, d_u, d_dt, w_main, w_com, gate_sum, own, cot, small, gain)


def over_rows(left, right):
    return lax.dot_general(
        left, right, (((0,), (0,)), ((), ())), preferred_element_type=jnp.float32
    )


def gather_plain(hid, main, com):
    hid_all = lax.all_gather(hid, "seq", axis=0)
    main_all = lax.all_gather(main, "wshard", axis=0)
    return hid_all, main_all, lax.all_gather(com, "wshard", axis=0)


def gather_more_plain(cot, rows, wide):
    cot_all = lax.all_gather(cot, "seq", axis=0)
    cols = lax.all_to_all(rows, "wshard", split_axis=1, concat_axis=0, tiled=True)
    own = lax.dynamic_slice_in_dim(cols, lax.axis_index("seq") * wide, wide, 0)
    return cot_all, lax.all_gather(own, "wshard", axis=1, tiled=True)


def reduce_scattered(v, axis):
    return lax.psum_scatter(v, axis, scatter_dimension=0, tiled=False)


def reduce_first_plain(layer, rows, gate):
    layer_sum = reduce_scattered(layer, "seq").astype(f32)
    rows = rows.reshape(-1, rows.shape[-1])
    part = lax.psum_scatter(rows, "wshard", scatter_dimension=1, tiled=True)
    part = lax.all_gather(part, "seq", axis=0, tiled=True)
    part = lax.all_to_all(part, "wshard", split_axis=0, concat_axis=1, tiled=True)
    return layer_sum, part, reduce_scattered(gate, "wshard")


def finish_plain(hid, d_gate, d_u, d_dt, w_main, w_com, gate_sum, own, cot, small, gain):
    groups, owners = lax.axis_size("seq"), lax.axis_size("wshard")
    wide = d_gate.shape[1]
    rest = jnp.concatenate([d_u, d_dt], axis=1)
    nt = lambda p, q: lax.dot_general(p, q, (((1,), (1,)), ((), ())), preferred_element_type=f32)
    back = nt(d_gate, w_main[:, :wide]) + nt(rest, jnp.concatenate([w_main[:, wide:], w_com], axis=1))
    back_sum = reduce_scattered(back.astype(bf16).reshape(groups, -1, D), "seq").astype(f32)
    part = reduce_scattered(over_rows(hid, rest).astype(bf16).reshape(owners, -1, rest.shape[1]), "wshard")
    part = lax.all_gather(jnp.concatenate([gate_sum, part], axis=1), "seq", axis=0)
    in_sum = jnp.concatenate(
        [part[i, :, :wide] for i in range(groups)]
        + [part[i, :, wide : 2 * wide] for i in range(groups)]
        + [jnp.sum(part[:, :, 2 * wide :].astype(f32), axis=0).astype(bf16)],
        axis=1,
    )
    full = lax.all_gather(lax.psum(small, "wshard"), "seq", axis=0)
    turned = [jnp.roll(full[i, :, :128], i * (wide // P_SIZE), axis=1) for i in range(groups)]
    sums = jnp.concatenate(
        [full[i, :, :wide] for i in range(groups)] + [jnp.sum(full[:, :, wide:], axis=0), sum(turned)], axis=1
    )
    wide_own = own.astype(f32)
    own_scale = lax.rsqrt(jnp.mean(wide_own * wide_own, axis=-1, keepdims=True) + eps)
    b = back_sum * gain
    hidden_grad = (
        cot.astype(f32)
        + own_scale * b
        - wide_own * (own_scale * own_scale * own_scale) * jnp.mean(b * wide_own, axis=-1, keepdims=True)
    )
    return hidden_grad, in_sum, sums


def middle_plain(gate, mixed, cot_all, w_out, normed):
    mixed_wide = mixed.astype(f32)
    sg = jax.nn.sigmoid(gate)
    silu = gate * sg
    g = mixed_wide * silu
    g_low = g.astype(bf16)
    a = lax.dot_general(cot_all, w_out, (((1,), (1,)), ((), ())), preferred_element_type=f32)
    sums = lax.psum(jnp.stack([jnp.sum(g * g, axis=1), jnp.sum(a * g, axis=1)]), "seq")
    r = lax.rsqrt(sums[0] / E + eps)[:, None]
    pull = (r * r * r) * (sums[1] / E)[:, None]
    d_g = r * a - g * pull
    d_mixed = (d_g * silu).astype(bf16)
    d_gate = (d_g * mixed_wide * (sg * (1.0 + gate * (1.0 - sg)))).astype(bf16)
    layer_part = (jnp.dot(g_low, w_out, preferred_element_type=f32) * r).astype(bf16)
    cot_r = (cot_all.astype(f32) * r).astype(bf16)
    out_part = over_rows(g_low, cot_r).astype(bf16)

    gate_part = over_rows(normed, d_gate).astype(bf16)
    return d_mixed, d_gate, gate_part, out_part, layer_part


def shards(
    hidden,
    segments,
    norm_gain,
    in_weight,
    conv_weight,
    conv_bias,
    step_bias,
    decay_log,
    skip_scale,
    gate_gain,
    out_weight,
    cotangent,
):
    group = lax.axis_index("seq")
    groups, owners = lax.axis_size("seq"), lax.axis_size("wshard")
    direct = (groups, owners) == (4, 8)
    heads = H // groups
    wide = heads * P_SIZE
    length = segments.shape[1]
    hidden_own, cot_own = hidden[0], cotangent[0]
    main = jnp.concatenate(
        [
            lax.dynamic_slice_in_dim(in_weight, group * wide, wide, 1),
            lax.dynamic_slice_in_dim(in_weight, E + group * wide, wide, 1),
        ],
        axis=1,
    )
    com = jnp.concatenate([in_weight[:, 2 * E :], norm_gain[:, None]], axis=1)
    com = jnp.pad(com, ((0, 0), (0, 128 - H - 1)))
    out_gain = gate_gain.astype(f32)[:, None]
    out_scaled = (out_weight.astype(f32) * out_gain).astype(bf16)
    gather = gather_first if direct else gather_plain
    hidden_all, w_main, w_com = gather(hidden_own, main, com)
    hidden_all = hidden_all.reshape(length, D)
    w_main, w_com = w_main.reshape(D, 2 * wide), w_com.reshape(D, -1)
    gain_row = w_com[:, 2 * N + H].astype(f32)[None]

    seg = segments[0]
    seg_col = jnp.pad(seg, (8, 8), constant_values=-1)[:, None]
    segr = seg.reshape(length // Q, 1, Q)
    par = jnp.pad(jnp.stack([step_bias, decay_log]), ((0, 6), (0, 128 - H)))
    skip = jnp.repeat(skip_scale, P_SIZE)[None]
    facts = (seg_col, segr, conv_weight, conv_bias[None], par, skip)
    beside, more = (forward_traffic(cot_own, out_scaled), (cot_own, out_scaled)) if direct else (NoTraffic, ())
    u, dt, gate, normed, mixed, save, *got = mixer_fwd(beside, more, hidden_all, gain_row, w_main, w_com, *facts)
    cot_all, w_out = got if direct else gather_more_plain(cot_own, out_scaled, wide)
    cot_all, w_out = cot_all.reshape(length, D), w_out.reshape(wide, D)

    mid = middle if direct else middle_plain
    d_mixed, d_gate, gate_part, out_part, layer_part = mid(gate, mixed, cot_all, w_out, normed)
    own_wide = hidden_own.astype(f32)

    more = (layer_part.reshape(groups, -1, D), out_part.reshape(2, -1, D), gate_part.reshape(owners, -1, wide))
    beside = backward_traffic(*more) if direct else NoTraffic
    du, ddt, small, *got = mixer_bwd(
        beside, more if direct else (), u, dt, *facts, save, d_mixed
    )
    layer_sum, out_sum, gate_sum = got if direct else reduce_first_plain(*more)
    layer_output = own_wide + layer_sum
    finish = finish_last if direct else finish_plain
    hidden_grad, in_sum, sums = finish(
        normed, d_gate, du, ddt, w_main, w_com, gate_sum, hidden_own, cot_own, small, gain_row
    )

    in_weight_grad = in_sum[:, : 2 * E + 2 * N + H].astype(f32)
    norm_gain_grad = jnp.sum(in_weight_grad * in_weight.astype(f32), axis=1) / norm_gain.astype(f32)
    out_sum = out_sum.astype(f32)
    out_weight_grad = out_sum * out_gain
    gate_gain_grad = jnp.sum(out_sum * out_weight.astype(f32), axis=1)
    chan, per_head = sums[:, : E + 2 * N], sums[:, E + 2 * N : E + 2 * N + H]
    return (
        layer_output[None],
        hidden_grad[None],
        norm_gain_grad,
        in_weight_grad,
        chan[:4],
        chan[4],
        per_head[5],
        per_head[6],
        per_head[7],
        gate_gain_grad,
        out_weight_grad,
    )


def solution(mesh):
    in_specs = (
        P("wshard", "seq", None),
        P("wshard", None),
        P("wshard"),
        P("wshard", None),
        P(),
        P(),
        P(),
        P(),
        P(),
        P("wshard"),
        P("wshard", None),
        P("wshard", "seq", None),
    )
    out_specs = (
        P("wshard", "seq", None),
        P("wshard", "seq", None),
        P("wshard"),
        P("wshard", None),
        P(),
        P(),
        P(),
        P(),
        P(),
        P("wshard"),
        P("wshard", None),
    )
    return jax.shard_map(shards, mesh=mesh, in_specs=in_specs, out_specs=out_specs, check_vma=False)
```
